32 devices in a mesh: dp: 8 (over y, x, core), tensor: 4 (over z).
Axes of the slice: x: 2, y: 2, z: 4, core: 2. Of those that a mesh axis runs over, the one named last changes fastest.
Arguments:
- block_input: bfloat16 [8, 2048, 768], P('dp', 'tensor'), may hold values from -6 to 6
- teacher: bfloat16 [8, 2048, 768], P('dp', 'tensor'), may hold values from -6 to 6
- segment_ids: int32 [8, 2048], P('dp', 'tensor'), may hold values from 0 to 7, never falling along the last dimension, each value on 1 to 800 neighbouring positions
- valid_mask: int32 [8, 2048], P('dp', 'tensor'), may hold values from 0 to 1
- ln1_gain: bfloat16 [768], P('dp'), may hold values from 0.5 to 1.5
- ln1_bias: bfloat16 [768], P('dp'), may hold values from -1.75 to 1.75
- qkv_weight: bfloat16 [3, 768, 768], P(None, 'dp', 'tensor'), may hold values from -0.21875 to 0.21875
- qv_bias: bfloat16 [2, 12, 64], P(None, 'tensor', 'dp'), may hold values from -1.75 to 1.75
- out_weight: bfloat16 [768, 768], P('tensor', 'dp'), may hold values from -0.875 to 0.875
- out_bias: bfloat16 [768], P('dp'), may hold values from -1.75 to 1.75
- ln2_gain: bfloat16 [768], P('dp'), may hold values from 0.5 to 1.5
- ln2_bias: bfloat16 [768], P('dp'), may hold values from -1.75 to 1.75
- fc_weight: bfloat16 [768, 3072], P('dp', 'tensor'), may hold values from -0.21875 to 0.21875
- fc_bias: bfloat16 [48, 64], P('tensor', 'dp'), may hold values from -1.75 to 1.75
- proj_weight: bfloat16 [3072, 768], P('tensor', 'dp'), may hold values from -0.109375 to 0.109375
- proj_bias: bfloat16 [768], P('dp'), may hold values from -1.75 to 1.75
Outputs:
- block_output: bfloat16 [8, 2048, 768], P('dp', 'tensor')
- loss: float32 [], replicated
- input_grad: float32 [8, 2048, 768], P('dp', 'tensor')
- grad_ln1_gain: float32 [768], P('dp')
- grad_ln1_bias: float32 [768], P('dp')
- grad_qkv_weight: float32 [3, 768, 768], P(None, 'dp', 'tensor')
- grad_qv_bias: float32 [2, 12, 64], P(None, 'tensor', 'dp')
- grad_out_weight: float32 [768, 768], P('tensor', 'dp')
- grad_out_bias: float32 [768], P('dp')
- grad_ln2_gain: float32 [768], P('dp')
- grad_ln2_bias: float32 [768], P('dp')
- grad_fc_weight: float32 [768, 3072], P('dp', 'tensor')
- grad_fc_bias: float32 [48, 64], P('tensor', 'dp')
- grad_proj_weight: float32 [3072, 768], P('tensor', 'dp')
- grad_proj_bias: float32 [768], P('dp')
The draws below stay inside these ranges and needn't reach their ends.
Inputs may be any that keep to these rules, and one draw needn't show every extreme that they name: `segment_ids`: within a sequence segment ids never fall; every document has 1 to 800 tokens, one has exactly 800, and every id of 0 to 7 occurs.
All inputs are finite; a program needn't handle non-finite values.
Results may differ from the reference program's by a relative error of at most 0.014.
Values may be sent and summed in bfloat16 or wider, within the bound.
A program may use at most 128 MiB of HBM per device.

```python
import math
import jax
import jax.numpy as jnp
import numpy as np
from jax import lax

D = 768
H = 12
HD = 64
FF = 3072
SEQ = 2048
SEQS = 8
DOCS = 8
DOC_MOST = 800
LOSS_SCALE = 6291456


def draw_valid_mask(key, part):
    rolls = jax.random.randint(key, (SEQS, SEQ), 0, 1000)
    places = jnp.arange(SEQS * SEQ, dtype=jnp.int32).reshape(SEQS, SEQ)
    limits = 250 + 500 * places // (SEQS * SEQ)
    return (rolls < limits).astype(jnp.int32)


def strengthened(entries, stream_key, source, target, shards_of, factor):
    def block_of(position):
        return (jnp.arange(entries.shape[position]) // (entries.shape[position] // shards_of)).reshape((-1,) + (1,) * (entries.ndim - 1 - position))

    near = jax.random.permutation(stream_key, shards_of)[block_of(target)]
    other_side = (block_of(target) + shards_of // 2) % shards_of
    return jnp.where((block_of(source) == near) | (block_of(source) == other_side), factor * entries, entries)


def block_levels(stream_key, dims, shards, least, largest):
    def one(dim, blocks):
        steps = jax.random.uniform(jax.random.fold_in(jax.random.fold_in(stream_key, 6), dim), (blocks,), jnp.float32, least / len(shards), largest / len(shards))
        return jnp.repeat(jnp.exp(steps), dims[dim] // blocks).reshape((-1,) + (1,) * (len(dims) - dim - 1))

    factor_of = one(*shards[0])
    for cut in shards[1:]:
        factor_of = factor_of * one(*cut)
    return factor_of


def length_profile(number_of, total, bound, slope):
    loads = [(1 << 20) // math.isqrt(rank ** slope) + 1 for rank in range(2, number_of + 1)]
    rest, given = total - bound - (number_of - 1), [1] * (number_of - 1)
    while rest > 0:
        movable = [i for i in range(number_of - 1) if given[i] < bound]
        mass, left = sum([loads[i] for i in movable]), rest
        for i in movable:
            addition = min(bound - given[i], max(1, left * loads[i] // mass), rest)
            given[i] = given[i] + addition
            rest = rest - addition
    return np.array([bound] + given)


def uneven(key, count, total, limit, slope):
    if count == 2:
        one = jax.random.randint(key, (), max(1, total - limit), min(limit, total - 1) + 1)
        return jnp.stack([one, total - one])
    tallies = jnp.asarray(length_profile(count, total, limit, slope), jnp.int32)
    couples = (count - 1) // 2
    source_of, sink = tallies[1:1 + 2 * couples:2], tallies[2:2 + 2 * couples:2]
    margin = jnp.minimum(source_of - 1, limit - sink)
    shifted = jax.random.randint(jax.random.fold_in(key, 1), (couples,), 0, 1 << 20) % (margin + 1)
    tallies = tallies.at[1:1 + 2 * couples:2].set(source_of - shifted).at[2:2 + 2 * couples:2].set(sink + shifted)
    return tallies[jax.random.permutation(jax.random.fold_in(key, 2), count)]


def gaussian(stream_key, dims, spread, limit, cuts=(), kind=jnp.bfloat16):
    factor_of = block_levels(stream_key, dims, cuts, -0.22, 0.18) if cuts else 1.0
    drawn = jax.random.normal(stream_key, dims, jnp.float32) * spread * factor_of
    return jnp.minimum(jnp.maximum(drawn, -limit), limit).astype(kind)


def heavy_noise(rng, shape, deviation, reach, shards, heavy, held_as=jnp.bfloat16):
    result = deviation * jax.random.normal(rng, shape, jnp.float32)
    if shards:
        result = result * block_levels(rng, shape, shards, -0.22, 0.18)
    return jnp.clip(strengthened(result, jax.random.fold_in(rng, 3), *heavy), -reach, reach).astype(held_as)


def setup_inputs(seed: int = 0) -> dict:
    keys = jax.random.split(jax.random.key(seed), 17)
    block_input = heavy_noise(keys[0], (SEQS, SEQ, D), 1.0, 6.0, ((0, 8), (1, 4)), (0, 2, 8, 2.0))
    teacher = gaussian(keys[1], (SEQS, SEQ, D), 1.0, 6.0, ((0, 8), (1, 4)))
    segment_ids = jax.vmap(lambda own: jnp.searchsorted(jnp.cumsum(uneven(own, DOCS, SEQ, DOC_MOST, 1)), jnp.arange(SEQ), side="right"))(jax.random.split(keys[2], SEQS)).reshape((SEQS, SEQ)).astype(jnp.int32)
    valid_mask = draw_valid_mask(jax.random.fold_in(keys[16], 71), 0)
    ln1_gain = jnp.clip(1.0 + 0.1 * jax.random.normal(keys[4], (D,), jnp.float32), 0.5, 1.5).astype(jnp.bfloat16)
    ln1_bias = gaussian(keys[5], (D,), 0.3, 1.75, ((0, 8),))
    qkv_weight = gaussian(keys[6], (3, D, D), D ** -0.5, 0.21875, ((1, 8), (2, 4)))
    qv_bias = gaussian(keys[7], (2, H, HD), 0.3, 1.75, ((1, 4), (2, 8)))
    out_weight = gaussian(keys[8], (D, D), (D // 16) ** -0.5, 0.875, ((0, 4), (1, 8)))
    out_bias = gaussian(keys[9], (D,), 0.3, 1.75, ((0, 8),))
    ln2_gain = jnp.clip(1.0 + 0.1 * jax.random.normal(keys[10], (D,), jnp.float32), 0.5, 1.5).astype(jnp.bfloat16)
    ln2_bias = gaussian(keys[11], (D,), 0.3, 1.75, ((0, 8),))
    fc_weight = gaussian(keys[12], (D, FF), D ** -0.5, 0.21875, ((0, 8), (1, 4)))
    fc_bias = gaussian(keys[13], (FF // HD, HD), 0.3, 1.75, ((0, 4), (1, 8)))
    proj_weight = gaussian(keys[14], (FF, D), FF ** -0.5, 0.109375, ((0, 4), (1, 8)))
    proj_bias = gaussian(keys[15], (D,), 0.3, 1.75, ((0, 8),))
    return {"block_input": block_input, "teacher": teacher, "segment_ids": segment_ids, "valid_mask": valid_mask, "ln1_gain": ln1_gain, "ln1_bias": ln1_bias, "qkv_weight": qkv_weight, "qv_bias": qv_bias, "out_weight": out_weight, "out_bias": out_bias, "ln2_gain": ln2_gain, "ln2_bias": ln2_bias, "fc_weight": fc_weight, "fc_bias": fc_bias, "proj_weight": proj_weight, "proj_bias": proj_bias}


EPSILON = 1e-05
TANH_SLOPE = 0.7978845608028654
CUBIC_TERM = 0.044715
highest = lax.Precision.HIGHEST

@jax.custom_vjp
def low(v):
    return lax.optimization_barrier(v.astype(jnp.bfloat16)).astype(jnp.float32)

@jax.custom_vjp
def low_back(v):
    return v

def low_keep(v):
    return (low(v), None)

def low_pass(kept, grad):
    return (grad,)

def back_keep(v):
    return (v, None)

def back_low(kept, grad):
    return (low(grad),)
low.defvjp(low_keep, low_pass)
low_back.defvjp(back_keep, back_low)

def gelu_tanh(values_in):
    return 0.5 * values_in * (1.0 + jnp.tanh(TANH_SLOPE * (values_in + CUBIC_TERM * values_in * values_in * values_in)))

def layer_norm(values_in, gain_vec, shift_vec):
    center = values_in - lax.optimization_barrier(jnp.mean(values_in, axis=-1, keepdims=True))
    scaler = lax.rsqrt(lax.optimization_barrier(jnp.mean(center * center, axis=-1, keepdims=True)) + EPSILON)
    return center * scaler * gain_vec + shift_vec

def split_heads(values_in):
    return values_in.reshape(values_in.shape[0], H, HD).transpose(1, 0, 2)

def attend(queries, keyset, valueset, seg_row):
    length = keyset.shape[1]
    block_rows = min(512, length)
    positions = jnp.arange(length, dtype=jnp.int32)

    def one_block(first_row):
        q_block = lax.dynamic_slice_in_dim(queries, first_row, block_rows, 1)
        scores = low_back(jnp.einsum('hqd,hkd->hqk', q_block, keyset, precision=highest) * 0.125)
        seg_rows = lax.dynamic_slice_in_dim(seg_row, first_row, block_rows)
        row_pos = first_row + jnp.arange(block_rows, dtype=jnp.int32)
        allowed = (seg_rows[:, None] == seg_row[None, :]) & (positions[None, :] <= row_pos[:, None])
        scores = jnp.where(allowed[None], scores, -1e+30)
        attn_probs = low(jax.nn.softmax(scores, axis=-1))
        return jnp.einsum('hqk,hkd->hqd', attn_probs, valueset, precision=highest)
    starts = jnp.arange(length // block_rows, dtype=jnp.int32) * block_rows
    return lax.map(jax.checkpoint(one_block), starts)

def block_forward(params, inputs, target, seg_row, valid_rows, valid_count):
    ln1_gain, ln1_bias, qkv_weight, qv_bias, out_weight, out_bias, ln2_gain, ln2_bias, fc_weight, fc_bias, proj_weight, proj_bias = params
    length = inputs.shape[0]
    normed_one = low(layer_norm(inputs, ln1_gain, ln1_bias))
    query = jnp.dot(normed_one, qkv_weight[0], precision=highest) + qv_bias[0].reshape(-1)
    keyset = jnp.dot(normed_one, qkv_weight[1], precision=highest)
    valueset = jnp.dot(normed_one, qkv_weight[2], precision=highest) + qv_bias[1].reshape(-1)
    query = low_back(low(query))
    keyset = low_back(low(keyset))
    valueset = low_back(low(valueset))
    mixed_heads = attend(split_heads(query), split_heads(keyset), split_heads(valueset), seg_row)
    mixed_heads = mixed_heads.transpose(0, 2, 1, 3).reshape(length, -1)
    mixed_heads = low_back(low(mixed_heads))
    hidden = inputs + low_back(jnp.dot(mixed_heads, out_weight, precision=highest)) + out_bias
    normed_two = low(layer_norm(hidden, ln2_gain, ln2_bias))
    pre_act = low_back(jnp.dot(normed_two, fc_weight, precision=highest) + fc_bias.reshape(-1))
    activated = low(gelu_tanh(pre_act))
    output = hidden + low_back(jnp.dot(activated, proj_weight, precision=highest)) + proj_bias
    residual_error = output - target
    part_loss = jnp.sum(valid_rows[:, None] * residual_error * residual_error) / (output.shape[1] * valid_count)
    return (output, part_loss)

def reference(block_input, teacher, segment_ids, valid_mask, ln1_gain, ln1_bias, qkv_weight, qv_bias, out_weight, out_bias, ln2_gain, ln2_bias, fc_weight, fc_bias, proj_weight, proj_bias):
    params = (ln1_gain.astype(jnp.float32), ln1_bias.astype(jnp.float32), qkv_weight.astype(jnp.float32), qv_bias.astype(jnp.float32), out_weight.astype(jnp.float32), out_bias.astype(jnp.float32), ln2_gain.astype(jnp.float32), ln2_bias.astype(jnp.float32), fc_weight.astype(jnp.float32), fc_bias.astype(jnp.float32), proj_weight.astype(jnp.float32), proj_bias.astype(jnp.float32))
    valid_all = valid_mask.astype(jnp.float32)
    valid_count = jnp.sum(valid_all)
    loss_scale = float(LOSS_SCALE)

    def one_sequence(totals, items):
        inputs, target, seg_row, valid_rows = items

        def forward(weights, values_in):
            return block_forward(weights, values_in, target, seg_row, valid_rows, valid_count)
        (output, part_loss), backward = jax.vjp(forward, params, inputs)
        grad_weights, grad_inputs = backward((jnp.zeros_like(output), jnp.ones_like(part_loss) * loss_scale))
        totals = jax.tree.map(jnp.add, totals, grad_weights)
        return (totals, (output.astype(jnp.bfloat16), part_loss, grad_inputs))
    zeros = jax.tree.map(jnp.zeros_like, params)
    totals, (outputs, parts, grad_inputs) = lax.scan(one_sequence, zeros, (block_input.astype(jnp.float32), teacher.astype(jnp.float32), segment_ids, valid_all))
    return (outputs, jnp.sum(parts), grad_inputs, totals[0], totals[1], totals[2], totals[3], totals[4], totals[5], totals[6], totals[7], totals[8], totals[9], totals[10], totals[11])
```

```python
import functools

import jax
import jax.numpy as jnp
from jax import lax
from jax.experimental import pallas as pl
from jax.experimental.pallas import tpu as pltpu
from jax.sharding import PartitionSpec as P

HD = 64
DOC_MOST = 800
KB = 128
QB = 256
EPSILON = 1e-05
TANH_SLOPE = 0.7978845608028654
CUBIC_TERM = 0.044715
MESH = pl.DeviceIdType.MESH
F32 = jnp.float32
BF16 = jnp.bfloat16
NN = (((1,), (0,)), ((), ()))
NT = (((1,), (1,)), ((), ()))


def mm(a, b, dims=NN):
    return lax.dot_general(a, b, dims, preferred_element_type=F32)


def halo_parts(tokens, ts):
    parts, left, back = [], DOC_MOST, 1
    while left > 0 and back < ts:
        parts.append((back, min(tokens, left)))
        left -= tokens
        back += 1
    return parts


def gather_kernel(dp, ts, tokens, n_in, *refs):
    w_refs, (x_ref, seg_ref) = refs[:n_in], refs[n_in : n_in + 2]
    outs = refs[n_in + 2 : 2 * n_in + 2]
    halo_ref, hseg_ref = refs[2 * n_in + 2 : 2 * n_in + 4]
    local_sem, send_sem, recv_sem, halo_send, halo_recv = refs[2 * n_in + 4 :]
    me = lax.axis_index("dp")
    mt = lax.axis_index("tensor")
    bits = [1 << k for k in range(dp.bit_length() - 1)]
    far = bits[1:]
    halo_ref[...] = jnp.zeros_like(halo_ref)
    hseg_ref[...] = jnp.full_like(hseg_ref, -1)
    barrier = pltpu.get_barrier_semaphore()
    peers_t = [lax.rem(mt + k, ts) for k in range(1, ts)]
    for t in peers_t:
        pl.semaphore_signal(barrier, inc=1, device_id={"tensor": t}, device_id_type=MESH)
    for b in bits:
        pl.semaphore_signal(barrier, inc=1, device_id={"dp": me ^ b}, device_id_type=MESH)
    pl.semaphore_wait(barrier, len(peers_t) + len(bits))
    started = []

    def rcopy(src, dst, dev):
        i = len(started)
        c = pltpu.make_async_remote_copy(
            src_ref=src,
            dst_ref=dst,
            send_sem=send_sem.at[i],
            recv_sem=recv_sem.at[i],
            device_id=dev,
            device_id_type=MESH,
        )
        c.start()
        started.append(c)
        return c

    locals_, over_z = [], []
    for c in range(n_in):
        copy = pltpu.make_async_copy(w_refs[c], outs[c].at[mt, me], local_sem.at[c])
        copy.start()
        locals_.append(copy)
        over_z.append([rcopy(w_refs[c], outs[c].at[mt, me], {"tensor": t}) for t in peers_t])
        if c == min(1, n_in - 1):
            end = halo_ref.shape[0]
            halos = []
            for i, (back, count) in enumerate(halo_parts(tokens, ts)):
                end -= count
                pair = [
                    pltpu.make_async_remote_copy(
                        src_ref=src,
                        dst_ref=dst,
                        send_sem=halo_send.at[2 * i + k],
                        recv_sem=halo_recv.at[2 * i + k],
                        device_id={"tensor": lax.rem(mt + back, ts)},
                        device_id_type=MESH,
                    )
                    for k, (src, dst) in enumerate(
                        [
                            (x_ref.at[pl.ds(tokens - count, count)], halo_ref.at[pl.ds(end, count)]),
                            (seg_ref, hseg_ref.at[i]),
                        ]
                    )
                ]
                halos.append((back, pair))

                @pl.when(mt + back < ts)
                def _():
                    for h in pair:
                        h.start()

    half = max(ts // 2, 1)
    groups = [(0, half, far)] + ([(half, ts - half, far[::-1])] if ts > half else [])

    def spread(c, group, masks, later):
        res = {}
        for b in later + [1]:
            res[b] = []
            for m in masks:
                ref = outs[c].at[pl.ds(group[0], group[1]), me ^ m]
                res[b].append((m, rcopy(ref, ref, {"dp": me ^ b})))
        return res

    stages = len(far) + 1
    pending = {}
    for step in range(n_in + stages - 1):
        for s in range(stages):
            c = step - s
            if not 0 <= c < n_in:
                continue
            if s == 0:
                locals_[c].wait()
                for k in over_z[c]:
                    k.wait_recv()
            for gi, group in enumerate(groups):
                if s == 0:
                    pending[c, gi] = [spread(c, group, [0], group[2])]
                else:
                    b = group[2][s - 1]
                    masks = []
                    for res in pending[c, gi]:
                        for m, k in res.get(b, []):
                            k.wait_recv()
                            masks.append(m ^ b)
                    pending[c, gi].append(spread(c, group, masks, group[2][s:]))
    for c in range(n_in):
        for gi in range(len(groups)):
            for res in pending[c, gi]:
                for m, k in res[1]:
                    k.wait_recv()
    for back, pair in halos:

        @pl.when(mt >= back)
        def _():
            for h in pair:
                h.wait_recv()

        @pl.when(mt + back < ts)
        def _():
            for h in pair:
                h.wait_send()

    for k in started:
        k.wait_send()


def gather(parts, x, seg, dp, ts, halo):
    n_in = len(parts)
    tokens = x.shape[0]
    copies = n_in * ((ts - 1) + (2 if ts > 1 else 1) * (dp - 1))
    n_halo = len(halo_parts(tokens, ts))
    any_spec = pl.BlockSpec(memory_space=pl.ANY)
    vmem = pl.BlockSpec(memory_space=pltpu.VMEM)
    return pl.pallas_call(
        functools.partial(gather_kernel, dp, ts, tokens, n_in),
        out_shape=[jax.ShapeDtypeStruct((ts, dp) + p.shape, p.dtype) for p in parts]
        + [
            jax.ShapeDtypeStruct((halo, x.shape[1]), x.dtype),
            jax.ShapeDtypeStruct((n_halo,) + seg.shape, seg.dtype),
        ],
        in_specs=[any_spec] * (n_in + 2),
        out_specs=[any_spec] * n_in + [vmem, vmem],
        scratch_shapes=[
            pltpu.SemaphoreType.DMA((n_in,)),
            pltpu.SemaphoreType.DMA((copies,)),
            pltpu.SemaphoreType.DMA((copies,)),
            pltpu.SemaphoreType.DMA((2 * n_halo,)),
            pltpu.SemaphoreType.DMA((2 * n_halo,)),
        ],
        compiler_params=pltpu.CompilerParams(collective_id=1, has_side_effects=True),
        name="gather",
    )(*parts, x, seg)


def reduce_kernel(dp, ts, g_ref, out_ref, in_core, in_far, in_z, send_sem, recv_sem):
    n_c = g_ref.shape[0]
    me = lax.axis_index("dp")
    mt = lax.axis_index("tensor")
    bits = [1 << k for k in range(dp.bit_length() - 1)]
    far = bits[1:]
    barrier = pltpu.get_barrier_semaphore()
    peers_t = [lax.rem(mt + k, ts) for k in range(1, ts)]
    for t in peers_t:
        pl.semaphore_signal(barrier, inc=1, device_id={"tensor": t}, device_id_type=MESH)
    for b in bits:
        pl.semaphore_signal(barrier, inc=1, device_id={"dp": me ^ b}, device_id_type=MESH)
    pl.semaphore_wait(barrier, len(peers_t) + len(bits))
    started = []

    def rcopy(src, dst, dev):
        i = len(started)
        c = pltpu.make_async_remote_copy(
            src_ref=src,
            dst_ref=dst,
            send_sem=send_sem.at[i],
            recv_sem=recv_sem.at[i],
            device_id=dev,
            device_id_type=MESH,
        )
        c.start()
        started.append(c)
        return c

    half = max(ts // 2, 1)
    groups = [(0, half, far[::-1])] + ([(half, ts - half, far)] if ts > half else [])
    evens = list(range(0, dp, 2))
    core = []
    for c in range(n_c):
        core.append(
            {
                m: rcopy(g_ref.at[c, :, me ^ 1 ^ m], in_core.at[c, m >> 1], {"dp": me ^ 1})
                for m in evens[::-1]
            }
        )

    def add_into(dst, src, base, count):
        def one(i, carry):
            dst[base + i] = (dst[base + i].astype(F32) + src[i].astype(F32)).astype(BF16)
            return carry

        lax.fori_loop(0, count, one, 0)

    stages = len(far) + 2
    pending = {}
    slots = {}
    for step in range(n_c + stages - 1):
        for s in range(stages):
            c = step - s
            if not 0 <= c < n_c:
                continue
            if s == 0:
                for m in evens[::-1]:
                    core[c][m].wait_recv()

                    def one(i, carry, m=m):
                        in_core[c, m >> 1, i] = (
                            in_core[c, m >> 1, i].astype(F32) + g_ref[c, i, me ^ m].astype(F32)
                        ).astype(BF16)
                        return carry

                    lax.fori_loop(0, ts, one, 0)
            for gi, (t0, tn, order) in enumerate(groups):
                if s > 0:
                    for m, slot, k in pending.pop((c, gi)):
                        k.wait_recv()
                        add_into(in_core.at[c, m >> 1], in_far.at[c, slot, pl.ds(t0, tn)], t0, tn)
                if s < len(far):
                    b = order[s]
                    done = sum(order[:s])
                    masks = [m for m in evens if m & b and not m & done]
                    sent = []
                    for m in masks:
                        slot = slots.get((c, gi), 0)
                        slots[c, gi] = slot + 1
                        k = rcopy(
                            in_core.at[c, m >> 1, pl.ds(t0, tn)],
                            in_far.at[c, slot, pl.ds(t0, tn)],
                            {"dp": me ^ b},
                        )
                        sent.append((m ^ b, slot, k))
                    pending[c, gi] = sent
                elif s == len(far):
                    pending[c, gi] = []
            if s == len(far):
                pending[c, "z"] = [
                    rcopy(in_core.at[c, 0, lax.rem(mt + k, ts)], in_z.at[c, k - 1], {"tensor": lax.rem(mt + k, ts)})
                    for k in range(1, ts)
                ]
            if s == len(far) + 1:
                total = in_core[c, 0, mt].astype(F32)
                for k in pending[c, "z"]:
                    k.wait_recv()
                for k in range(ts - 1):
                    total = total + in_z[c, k].astype(F32)
                out_ref[c] = total
    for k in started:
        k.wait_send()


def reduce(grads, dp, ts):
    n_c, _, _, rows, width = grads.shape
    n_far = dp // 2 - 1
    groups = 2 if ts > 1 else 1
    copies = n_c * (dp // 2 + groups * n_far + ts - 1)
    vmem = pl.BlockSpec(memory_space=pltpu.VMEM)
    return pl.pallas_call(
        functools.partial(reduce_kernel, dp, ts),
        out_shape=jax.ShapeDtypeStruct((n_c, rows, width), F32),
        in_specs=[vmem],
        out_specs=vmem,
        scratch_shapes=[
            pltpu.VMEM((n_c, dp // 2, ts, rows, width), BF16),
            pltpu.VMEM((n_c, n_far, ts, rows, width), BF16),
            pltpu.VMEM((n_c, ts - 1, rows, width), BF16),
            pltpu.SemaphoreType.DMA((copies,)),
            pltpu.SemaphoreType.DMA((copies,)),
        ],
        compiler_params=pltpu.CompilerParams(
            collective_id=2, has_side_effects=True, vmem_limit_bytes=62 << 20
        ),
        name="reduce",
    )(grads)


def keep_lanes(block, head):
    lanes = lax.broadcasted_iota(jnp.int32, block.shape, 1)
    return jnp.where((lanes < HD) == (head == 0), block, jnp.zeros_like(block))


def fold_rows(block, op):
    return op(block.reshape(block.shape[0] // 8, 8, block.shape[1]), axis=0)


def allowed_at(chunk, doc_row, first_q):
    key = chunk * KB + lax.broadcasted_iota(jnp.int32, (KB, QB), 0)
    query = first_q + lax.broadcasted_iota(jnp.int32, (KB, QB), 1)
    return (key >= doc_row) & (key <= query)


def attend_kernel(halo, first_ref, doc_ref, q_ref, k_ref, vt_ref, o_ref, lse_ref, s_ref):
    for j in range(q_ref.shape[0] // QB):
        rows = pl.ds(j * QB, QB)
        q_block = q_ref[rows, :]
        queries = [keep_lanes(q_block, h) for h in range(2)]
        doc_row = doc_ref[0:1, rows]
        first_q = halo + j * QB
        begin = first_ref[j]
        end = (first_q + QB) // KB

        def score(c, tops):
            keys = k_ref[pl.ds(pl.multiple_of(c * KB, KB), KB), :]
            ok = allowed_at(c, doc_row, first_q)
            res = []
            for h in range(2):
                s = jnp.where(ok, mm(keys, queries[h], NT), -1e30)
                s_ref[h, c] = s
                res.append(jnp.maximum(tops[h], fold_rows(s, jnp.max)))
            return tuple(res)

        tops = lax.fori_loop(begin, end, score, (jnp.full((8, QB), -1e30, F32),) * 2)
        tops = [jnp.max(t, axis=0, keepdims=True) for t in tops]

        def mix(c, carry):
            res = []
            for h in range(2):
                total, acc = carry[h]
                p = jnp.exp(s_ref[h, c] - tops[h])
                total = total + fold_rows(p, jnp.sum)
                vt = vt_ref[pl.ds(h * HD, HD), pl.ds(pl.multiple_of(c * KB, KB), KB)]
                acc = acc + mm(vt, p.astype(BF16))
                res.append((total, acc))
            return tuple(res)

        carry = lax.fori_loop(
            begin, end, mix, ((jnp.zeros((8, QB), F32), jnp.zeros((HD, QB), F32)),) * 2
        )
        for h in range(2):
            total = jnp.sum(carry[h][0], axis=0, keepdims=True)
            o_ref[pl.ds(h * HD, HD), rows] = carry[h][1] / total
            lse_ref[0, h : h + 1, rows] = tops[h] + jnp.log(total)


def attend(first, doc, q, k, vt, halo):
    tokens, width = q.shape
    keys = k.shape[0]
    pairs = width // 128
    return pl.pallas_call(
        functools.partial(attend_kernel, halo),
        out_shape=[
            jax.ShapeDtypeStruct((width, tokens), F32),
            jax.ShapeDtypeStruct((pairs, 2, tokens), F32),
        ],
        grid_spec=pltpu.PrefetchScalarGridSpec(
            num_scalar_prefetch=1,
            grid=(pairs,),
            in_specs=[
                pl.BlockSpec((1, tokens), lambda p, f: (0, 0)),
                pl.BlockSpec((tokens, 128), lambda p, f: (0, p)),
                pl.BlockSpec((keys, 128), lambda p, f: (0, p)),
                pl.BlockSpec((128, keys), lambda p, f: (p, 0)),
            ],
            out_specs=[
                pl.BlockSpec((128, tokens), lambda p, f: (p, 0)),
                pl.BlockSpec((1, 2, tokens), lambda p, f: (p, 0, 0)),
            ],
            scratch_shapes=[pltpu.VMEM((2, keys // KB, KB, QB), F32)],
        ),
        name="attend",
    )(first, doc, q, k, vt)


def attend_back_kernel(
    halo, first_ref, doc_ref, q_ref, k_ref, kt_ref, v_ref, do_ref, lse_ref, delta_ref, dq_ref, dk_ref, dv_ref
):
    dk_ref[...] = jnp.zeros_like(dk_ref)
    dv_ref[...] = jnp.zeros_like(dv_ref)
    for j in range(q_ref.shape[0] // QB):
        rows = pl.ds(j * QB, QB)
        q_block, do_block = q_ref[rows, :], do_ref[rows, :]
        queries = [keep_lanes(q_block, h) for h in range(2)]
        grads = [keep_lanes(do_block, h) for h in range(2)]
        doc_row = doc_ref[0:1, rows]
        first_q = halo + j * QB

        def step(c, carry):
            span = pl.ds(pl.multiple_of(c * KB, KB), KB)
            keys, values = k_ref[span, :], v_ref[span, :]
            ok = allowed_at(c, doc_row, first_q)
            res = []
            grad_k = grad_v = None
            for h in range(2):
                s = jnp.where(ok, mm(keys, queries[h], NT), -1e30)
                p = jnp.exp(s - lse_ref[0, h : h + 1, rows])
                dp_ = mm(values, grads[h], NT)
                ds = (p * (dp_ - delta_ref[0, h : h + 1, rows])).astype(BF16)
                gv = mm(p.astype(BF16), grads[h])
                gk = mm(ds, queries[h])
                grad_v = gv if grad_v is None else grad_v + gv
                grad_k = gk if grad_k is None else grad_k + gk
                kt = kt_ref[pl.ds(h * HD, HD), span]
                res.append(carry[h] + mm(kt, ds))
            dk_ref[span, :] += grad_k
            dv_ref[span, :] += grad_v
            return tuple(res)

        carry = lax.fori_loop(
            first_ref[j], (first_q + QB) // KB, step, (jnp.zeros((HD, QB), F32),) * 2
        )
        for h in range(2):
            dq_ref[pl.ds(h * HD, HD), rows] = carry[h] * 0.125


def attend_back(first, doc, q, k, kt, v, do, lse, delta, halo):
    tokens, width = q.shape
    keys = k.shape[0]
    pairs = width // 128
    q_spec = pl.BlockSpec((tokens, 128), lambda p, f: (0, p))
    k_spec = pl.BlockSpec((keys, 128), lambda p, f: (0, p))
    stat = pl.BlockSpec((1, 2, tokens), lambda p, f: (p, 0, 0))
    return pl.pallas_call(
        functools.partial(attend_back_kernel, halo),
        out_shape=[
            jax.ShapeDtypeStruct((width, tokens), F32),
            jax.ShapeDtypeStruct((keys, width), F32),
            jax.ShapeDtypeStruct((keys, width), F32),
        ],
        grid_spec=pltpu.PrefetchScalarGridSpec(
            num_scalar_prefetch=1,
            grid=(pairs,),
            in_specs=[
                pl.BlockSpec((1, tokens), lambda p, f: (0, 0)),
                q_spec,
                k_spec,
                pl.BlockSpec((128, keys), lambda p, f: (p, 0)),
                k_spec,
                q_spec,
                stat,
                stat,
            ],
            out_specs=[pl.BlockSpec((128, tokens), lambda p, f: (p, 0)), k_spec, k_spec],
        ),
        name="attend_back",
    )(first, doc, q, k, kt, v, do, lse, delta)


def gelu_tanh(values_in):
    return (
        0.5
        * values_in
        * (
            1.0
            + jnp.tanh(TANH_SLOPE * (values_in + CUBIC_TERM * values_in * values_in * values_in))
        )
    )


def normalize(values_in):
    center = values_in - jnp.mean(values_in, axis=-1, keepdims=True)
    scaler = lax.rsqrt(jnp.mean(center * center, axis=-1, keepdims=True) + EPSILON)
    return (center * scaler, scaler)


def norm_back(grad_in, gain_vec, unit_rows, scaler):
    scaled = grad_in * gain_vec
    return scaler * (
        scaled
        - jnp.mean(scaled, axis=-1, keepdims=True)
        - unit_rows * jnp.mean(scaled * unit_rows, axis=-1, keepdims=True)
    )


def on_device(
    block_input,
    teacher,
    segment_ids,
    valid_mask,
    ln1_gain,
    ln1_bias,
    qkv_weight,
    qv_bias,
    out_weight,
    out_bias,
    ln2_gain,
    ln2_bias,
    fc_weight,
    fc_bias,
    proj_weight,
    proj_bias,
):
    dp, ts = lax.axis_size("dp"), lax.axis_size("tensor")
    me, mt = lax.axis_index("dp"), lax.axis_index("tensor")
    tokens, width = block_input.shape[1:]
    total_tokens = tokens * ts * dp
    halo = -(-(DOC_MOST - 1) // KB) * KB
    e = qkv_weight.shape[2]
    x = block_input[0]
    valid_rows = valid_mask[0].astype(F32)

    qkvo = jnp.concatenate([qkv_weight[0], qkv_weight[1], qkv_weight[2], out_weight.T], axis=1)
    local_count = jnp.sum(valid_mask[0])
    mine = jnp.arange(dp) == me

    def spread(v):
        return jnp.where(mine[:, None], v[..., None, :], jnp.zeros((), v.dtype))

    vectors = jnp.stack([ln1_gain, ln1_bias, out_bias, ln2_gain, ln2_bias, proj_bias])
    tail = jnp.stack([local_count // 16, local_count % 16]).astype(BF16)
    small = jnp.concatenate(
        [
            spread(vectors).reshape(6, width),
            spread(fc_bias).reshape(1, -1),
            jnp.concatenate(
                [spread(qv_bias).reshape(-1), tail, jnp.zeros((width - 2 * e - 2,), BF16)]
            )[None],
        ]
    )
    seg_rows = jnp.broadcast_to(segment_ids, (8, tokens))
    small_all, w_qkvo, w_fc, w_proj, x_halo, seg_halo = gather(
        [small, qkvo, fc_weight, proj_weight.T], x, seg_rows, dp, ts, halo
    )
    small_all = jnp.sum(small_all.astype(F32), axis=1)
    gain_one, bias_one, b_out, gain_two, bias_two, b_proj = [small_all[0, i] for i in range(6)]
    b_fc = small_all[:, 6].reshape(-1)
    b_q = small_all[:, 7, :e].reshape(-1)
    b_v = small_all[:, 7, e : 2 * e].reshape(-1)
    valid_count = jnp.sum(small_all[:, 7, 2 * e] * 16 + small_all[:, 7, 2 * e + 1])
    w_qkvo = w_qkvo.reshape(ts, width, 4, e)
    wq, wk, wv, wo = [w_qkvo[:, :, i].transpose(1, 0, 2).reshape(width, width) for i in range(4)]
    wf = w_fc.reshape(ts, width, -1)
    wp = w_proj.reshape(ts, width, -1)

    seg = segment_ids[0]
    pieces = []
    for i, (back, count) in enumerate(halo_parts(tokens, ts)):
        pieces.insert(0, seg_halo[i, 0, tokens - count :])
    filled = sum(p.shape[0] for p in pieces)
    seg_window = jnp.concatenate([jnp.full((halo - filled,), -1, jnp.int32)] + pieces)
    position = jnp.sum((seg_window[:, None] < seg[None, :]).astype(jnp.int32), axis=0)
    own = jnp.sum((seg[:, None] < seg[None, :]).astype(jnp.int32), axis=0)
    doc = (position + own)[None]
    first = doc[0, ::QB] // KB

    inputs = x.astype(F32)
    window = jnp.concatenate([x_halo, x]).astype(F32)
    unit_window, scale_window = normalize(window)
    normed_window = (unit_window * gain_one + bias_one).astype(BF16)
    unit_one, scale_one = unit_window[halo:], scale_window[halo:]
    normed_one = normed_window[halo:]
    q = ((mm(normed_one, wq) + b_q).astype(BF16) * 0.125).astype(BF16)
    k = mm(normed_window, wk).astype(BF16)
    v = (mm(normed_window, wv) + b_v).astype(BF16)
    mixed_t, lse = attend(first, doc, q, k, v.T, halo)
    mixed = mixed_t.T.astype(BF16)
    hidden = inputs + mm(mixed, wo, NT) + b_out
    unit_two, scale_two = normalize(hidden)
    normed_two = (unit_two * gain_two + bias_two).astype(BF16)
    pre_act = jnp.einsum("sd,tdf->stf", normed_two, wf, preferred_element_type=F32) + b_fc.reshape(ts, -1)
    activated = gelu_tanh(pre_act).astype(BF16)
    output = hidden + jnp.einsum("stf,tdf->sd", activated, wp, preferred_element_type=F32) + b_proj
    residual_error = output - teacher[0].astype(F32)
    squares = jnp.sum(valid_rows[:, None] * residual_error * residual_error)
    grad_output = valid_rows[:, None] * residual_error * (total_tokens / valid_count)
    low_output = grad_output.astype(BF16)
    grad_act = jnp.einsum("sd,tdf->stf", low_output, wp, preferred_element_type=F32)
    grad_proj_w = jnp.einsum("sd,stf->tdf", low_output, activated, preferred_element_type=F32)
    _, gelu_back = jax.vjp(gelu_tanh, pre_act)
    grad_pre = gelu_back(grad_act)[0].astype(BF16)
    grad_fc_w = jnp.einsum("sd,stf->tdf", normed_two, grad_pre, preferred_element_type=F32)
    grad_fc_b = jnp.sum(grad_pre, axis=0, dtype=F32)
    grad_normed_two = jnp.einsum("stf,tdf->sd", grad_pre, wf, preferred_element_type=F32)
    grad_gain_two = jnp.sum(grad_normed_two * unit_two, axis=0)
    grad_bias_two = jnp.sum(grad_normed_two, axis=0)
    grad_hidden = grad_output + norm_back(grad_normed_two, gain_two, unit_two, scale_two)
    low_hidden = grad_hidden.astype(BF16)
    grad_mixed = mm(low_hidden, wo).astype(BF16)
    grad_out_w = jnp.einsum("sd,se->de", low_hidden, mixed, preferred_element_type=F32)
    heads = width // HD
    delta = jnp.sum((grad_mixed.T.astype(F32) * mixed_t).reshape(heads // 2, 2, HD, tokens), axis=2)
    dq_t, dk, dv = attend_back(first, doc, q, k, k.T, v, grad_mixed, lse, delta, halo)
    dq, dk, dv = dq_t.T.astype(BF16), dk.astype(BF16), dv.astype(BF16)
    sd_se = lambda a, b: jnp.einsum("sd,se->de", a, b, preferred_element_type=F32)
    g_q, g_k, g_v = sd_se(normed_one, dq), sd_se(normed_window, dk), sd_se(normed_window, dv)
    grad_window = mm(dk, wk, NT) + mm(dv, wv, NT)
    grad_normed_one = grad_window[halo:] + mm(dq, wq, NT)
    end = halo
    for back, count in halo_parts(tokens, ts):
        end -= count
        part = lax.ppermute(
            grad_window[end : end + count].astype(BF16), "tensor", [(t, t - back) for t in range(back, ts)]
        )
        grad_normed_one = grad_normed_one.at[tokens - count :].add(part.astype(F32))
    grad_input = grad_hidden + norm_back(grad_normed_one, gain_one, unit_one, scale_one)

    def by_t(g):
        return g.reshape(width, ts, e)

    g_qkvo = jnp.stack([by_t(g_q), by_t(g_k), by_t(g_v), by_t(grad_out_w)], axis=2)
    g_qkvo = g_qkvo.transpose(1, 0, 2, 3).reshape(ts, width, 4 * e)
    grads = jnp.stack([grad_proj_w, grad_fc_w, g_qkvo]).astype(BF16)
    grads = grads.reshape(3, ts, dp, width // dp, -1)
    r_proj, r_fc, r_qkvo = reduce(grads, dp, ts)
    smalls = [
        jnp.sum(grad_normed_one * unit_one, axis=0),
        jnp.sum(grad_normed_one, axis=0),
        jnp.sum(grad_hidden, axis=0),
        grad_gain_two,
        grad_bias_two,
        jnp.sum(grad_output, axis=0),
        grad_fc_b.reshape(-1),
        jnp.sum(dq, axis=0, dtype=F32),
        jnp.sum(dv, axis=0, dtype=F32),
        squares[None],
    ]
    summed = lax.psum(jnp.concatenate(smalls), ("dp", "tensor"))
    rows = width // dp
    own_rows = lambda i: lax.dynamic_slice_in_dim(summed, i * width + me * rows, rows)
    fc_b = summed[6 * width : 6 * width + fc_bias.size * dp * ts].reshape(ts, -1, dp, fc_bias.shape[1])
    qv0 = 6 * width + fc_bias.size * dp * ts
    qv_b = summed[qv0 : qv0 + 2 * width].reshape(2, ts, -1, dp, qv_bias.shape[2])
    loss = summed[-1] / (width * valid_count)
    pick = lambda a, i, ax: lax.dynamic_index_in_dim(a, i, ax, keepdims=False)
    return (
        output.astype(BF16)[None],
        loss,
        grad_input[None],
        own_rows(0),
        own_rows(1),
        jnp.stack([r_qkvo[:, i * e : (i + 1) * e] for i in range(3)]),
        pick(pick(qv_b, mt, 1), me, 2),
        r_qkvo[:, 3 * e :].T,
        own_rows(2),
        own_rows(3),
        own_rows(4),
        r_fc,
        pick(pick(fc_b, mt, 0), me, 1),
        r_proj.T,
        own_rows(5),
    )


def solution(mesh):
    placed = (
        P("dp", "tensor", None),
        P("dp", "tensor", None),
        P("dp", "tensor"),
        P("dp", "tensor"),
        P("dp"),
        P("dp"),
        P(None, "dp", "tensor"),
        P(None, "tensor", "dp"),
        P("tensor", "dp"),
        P("dp"),
        P("dp"),
        P("dp"),
        P("dp", "tensor"),
        P("tensor", "dp"),
        P("tensor", "dp"),
        P("dp"),
    )
    return jax.shard_map(
        on_device,
        mesh=mesh,
        in_specs=placed,
        out_specs=(
            P("dp", "tensor", None),
            P(),
            P("dp", "tensor", None),
            P("dp"),
            P("dp"),
            P(None, "dp", "tensor"),
            P(None, "tensor", "dp"),
            P("tensor", "dp"),
            P("dp"),
            P("dp"),
            P("dp"),
            P("dp", "tensor"),
            P("tensor", "dp"),
            P("tensor", "dp"),
            P("dp"),
        ),
        check_vma=False,
    )
```

```python
import functools

import jax
import jax.numpy as jnp
from jax import lax
from jax.experimental import pallas as pl
from jax.experimental.pallas import tpu as pltpu
from jax.sharding import PartitionSpec as P

HD = 64
DOC_MOST = 800
KB = 128
QB = 256
DOCS = 8
WINDOW = -(-(DOC_MOST - 1) // KB) + QB // KB
EPSILON = 1e-05
TANH_SLOPE = 0.7978845608028654
CUBIC_TERM = 0.044715
MESH = pl.DeviceIdType.MESH
F32 = jnp.float32
BF16 = jnp.bfloat16
NN = (((1,), (0,)), ((), ()))
NT = (((1,), (1,)), ((), ()))


def mm(a, b, dims=NN):
    return lax.dot_general(a, b, dims, preferred_element_type=F32)


def halo_parts(tokens, ts):
    parts, left, back = [], DOC_MOST, 1
    while left > 0 and back < ts:
        parts.append((back, min(tokens, left)))
        left -= tokens
        back += 1
    return parts


class Gather:
    def __init__(self, dp, ts, ins, outs, z_send, z_recv, send_sem, recv_sem):
        self.dp, self.ts, self.ins, self.outs = dp, ts, ins, outs
        self.z_send, self.z_recv, self.send_sem, self.recv_sem = z_send, z_recv, send_sem, recv_sem
        self.me, self.mt = lax.axis_index("dp"), lax.axis_index("tensor")
        self.far = [1 << k for k in range(1, dp.bit_length() - 1)]
        self.keys = {}
        self.flight = []
        self.near = [sorted(range(ts), key=lambda t: (abs(t - m), t)) for m in range(ts)]

    @staticmethod
    def copies(dp, ts, parts):
        return parts * ts * (dp - 1)

    def t_of(self, k):
        t = jnp.int32(self.near[0][k])
        for m in range(1, self.ts):
            t = jnp.where(self.mt == m, self.near[m][k], t)
        return t

    def order(self, t):
        flip = t * 2 >= self.ts
        return [jnp.where(flip, b, a) for a, b in zip(self.far, self.far[::-1])]

    def place(self, c, t, dp_index):
        return self.outs[c].at[t, dp_index]

    def along(self, c, t, up):
        src = self.ins[c] if t is None else self.place(c, t, self.me)
        t = self.mt if t is None else t
        return pltpu.make_async_remote_copy(
            src_ref=src,
            dst_ref=self.place(c, t, self.me),
            send_sem=self.z_send.at[c, t, int(up)],
            recv_sem=self.z_recv.at[c, t],
            device_id={"tensor": self.mt + (1 if up else -1)},
            device_id_type=MESH,
        )

    def desc(self, key):
        c, k, known, i = key
        t = self.t_of(k)
        order = self.order(t)
        mask = jnp.int32(0)
        for b in known:
            mask = mask ^ order[b]
        ref = self.place(c, t, self.me ^ mask)
        own = k == 0 and not known
        n = self.keys.setdefault(key, len(self.keys))
        return pltpu.make_async_remote_copy(
            src_ref=self.ins[c] if own else ref,
            dst_ref=ref,
            send_sem=self.send_sem.at[n],
            recv_sem=self.recv_sem.at[n],
            device_id={"dp": self.me ^ (1 if i < 0 else order[i])},
            device_id_type=MESH,
        )

    def here(self, c, k, known):
        first = max(known) + 1 if known else 0
        for i in list(range(first, len(self.far))) + [-1]:
            key = (c, k, known, i)
            self.desc(key).start()
            self.flight.append(key)

    def start(self, c):
        @pl.when(self.mt + 1 < self.ts)
        def _():
            self.along(c, None, True).start()

        @pl.when(self.mt >= 1)
        def _():
            self.along(c, None, False).start()

        self.here(c, 0, ())

    def z_step(self, c, k):
        t = self.t_of(k)
        self.along(c, t, True).wait_recv()

        @pl.when((t < self.mt) & (self.mt + 1 < self.ts))
        def _():
            self.along(c, t, True).start()

        @pl.when((t > self.mt) & (self.mt >= 1))
        def _():
            self.along(c, t, False).start()

        self.here(c, k, ())

    def far_step(self, c, k, i):
        for key in [q for q in self.flight if q[:2] == (c, k) and q[3] == i]:
            self.desc(key).wait_recv()
            self.here(c, k, key[2] + (i,))

    def core_step(self, c, k):
        for key in [q for q in self.flight if q[:2] == (c, k) and q[3] < 0]:
            self.desc(key).wait_recv()

    def finish(self):
        for c in range(len(self.ins)):
            for k in range(self.ts):
                t = self.t_of(k)

                @pl.when((t <= self.mt) & (self.mt + 1 < self.ts))
                def _():
                    self.along(c, t, True).wait_send()

                @pl.when((t >= self.mt) & (self.mt >= 1))
                def _():
                    self.along(c, t, False).wait_send()

        for key in self.flight:
            self.desc(key).wait_send()


def meet(dp, ts):
    me, mt = lax.axis_index("dp"), lax.axis_index("tensor")
    bits = [1 << k for k in range(dp.bit_length() - 1)]
    barrier = pltpu.get_barrier_semaphore()
    for k in range(1, ts):
        pl.semaphore_signal(barrier, inc=1, device_id={"tensor": lax.rem(mt + k, ts)}, device_id_type=MESH)
    for b in bits:
        pl.semaphore_signal(barrier, inc=1, device_id={"dp": me ^ b}, device_id_type=MESH)
    pl.semaphore_wait(barrier, ts - 1 + len(bits))


def keep_lanes(block, head):
    lanes = lax.broadcasted_iota(jnp.int32, block.shape, 1)
    return jnp.where((lanes < HD) == (head == 0), block, jnp.zeros_like(block))


def fold_rows(block, op):
    return op(block.reshape(block.shape[0] // 8, 8, block.shape[1]), axis=0)


def swap_halves(block):
    return jnp.concatenate([block[:, HD:], block[:, :HD]], axis=1)


def lanes_of(low, high):
    lanes = lax.broadcasted_iota(jnp.int32, low.shape, 1)
    return jnp.where(lanes < HD, low, high)


def masked(s, i, doc_row, base):
    key = lax.broadcasted_iota(jnp.int32, s.shape, 0)
    ok = key >= doc_row - (base + i * KB)
    ahead = i - (WINDOW - QB // KB)
    if ahead >= 0:
        query = lax.broadcasted_iota(jnp.int32, s.shape, 1)
        ok = ok & (key + ahead * KB <= query)
    return jnp.where(ok, s, -1e30)


def normalize(values_in):
    center = values_in - jnp.mean(values_in, axis=-1, keepdims=True)
    scaler = lax.rsqrt(jnp.mean(center * center, axis=-1, keepdims=True) + EPSILON)
    return (center * scaler, scaler)


def merge_pairs(w_ref, h2_ref, ts):
    for a in range(ts // 2):
        tiles = []
        for t in (2 * a, 2 * a + 1):
            block = h2_ref[t].reshape(-1, 256)
            tiles.append((block[:, :128], block[:, 128:]))
        (qk0, vo0), (qk1, vo1) = tiles
        merged = [
            lanes_of(qk0, swap_halves(qk1)),
            lanes_of(swap_halves(qk0), qk1),
            lanes_of(vo0, swap_halves(vo1)),
            lanes_of(swap_halves(vo0), vo1),
        ]
        for i, m in enumerate(merged):
            w_ref[ts + a, :, :, i * 128 : (i + 1) * 128] = m.reshape(w_ref.shape[1], w_ref.shape[2], 128)


def weight_loads(qkvo_all, w_ref, h2_ref, sem, ts):
    res = []
    for t in range(ts):
        res.append(pltpu.make_async_copy(qkvo_all.at[t, :, :, pl.ds(0, 512)], w_ref.at[t], sem.at[2 * t]))
        res.append(pltpu.make_async_copy(qkvo_all.at[t, :, :, pl.ds(512, 256)], h2_ref.at[t], sem.at[2 * t + 1]))
    return res


def front_kernel(
    dp,
    ts,
    x_ref,
    seg_ref,
    small_ref,
    qkvo_ref,
    fc_ref,
    proj_ref,
    qkvo_all,
    fc_all,
    proj_all,
    vec_ref,
    doc_ref,
    normed_ref,
    q_ref,
    k_ref,
    v_ref,
    ot_ref,
    lse_ref,
    mixed_ref,
    hidden_ref,
    small_all,
    w_ref,
    h2_ref,
    halo_ref,
    hseg_ref,
    vt_ref,
    s_ref,
    local_sem,
    z_send,
    z_recv,
    send_sem,
    recv_sem,
    halo_send,
    halo_recv,
):
    me, mt = lax.axis_index("dp"), lax.axis_index("tensor")
    tokens, width = x_ref.shape
    halo = halo_ref.shape[0]
    ins = [small_ref, qkvo_ref, fc_ref, proj_ref]
    outs = [small_all, qkvo_all, fc_all, proj_all]
    halo_ref[...] = jnp.zeros_like(halo_ref)
    hseg_ref[...] = jnp.full_like(hseg_ref, -1)
    meet(dp, ts)
    net = Gather(dp, ts, ins, outs, z_send, z_recv, send_sem, recv_sem)
    stages = len(net.far)
    parts = halo_parts(tokens, ts)

    def halo_copies(i):
        back, count = parts[i]
        end = halo - sum(c for _, c in parts[:i])
        pairs = [
            (x_ref.at[pl.ds(tokens - count, count)], halo_ref.at[pl.ds(end - count, count)]),
            (seg_ref, hseg_ref.at[i]),
        ]
        return [
            pltpu.make_async_remote_copy(
                src_ref=src,
                dst_ref=dst,
                send_sem=halo_send.at[2 * i + n],
                recv_sem=halo_recv.at[2 * i + n],
                device_id={"tensor": lax.rem(mt + back, ts)},
                device_id_type=MESH,
            )
            for n, (src, dst) in enumerate(pairs)
        ]

    own = [
        pltpu.make_async_copy(ins[c], outs[c].at[mt, me], local_sem.at[2 * ts + c]) for c in range(4)
    ]
    net.start(0)
    net.start(1)
    for i, (back, _) in enumerate(parts):

        @pl.when(mt + back < ts)
        def _():
            for h in halo_copies(i):
                h.start()

    for c in own:
        c.start()
    for c in (0, 1):
        for k in range(1, ts):
            net.z_step(c, k)
    net.start(2)
    net.start(3)
    for c in (0, 1):
        for i in range(stages):
            for k in range(ts):
                net.far_step(c, k, i)
    own[0].wait()
    for k in range(ts):
        net.core_step(0, k)
    for t in range(ts):
        vec_ref[t] = jnp.sum(small_all[t], axis=0)

    def norm_rows(src, i, at):
        unit, _ = normalize(src[pl.ds(i * KB, KB), :].astype(F32))
        normed_ref[pl.ds(at + i * KB, KB), :] = (unit * vec_ref[0, 0:1, :] + vec_ref[0, 1:2, :]).astype(BF16)

    def own_rows(i, carry):
        norm_rows(x_ref, i, halo)
        return carry

    lax.fori_loop(0, tokens // KB, own_rows, 0)
    own[1].wait()
    for k in range(ts):
        net.core_step(1, k)
    loads = weight_loads(qkvo_all, w_ref, h2_ref, local_sem, ts)
    for load in loads:
        load.start()
    for load in loads:
        load.wait()
    merge_pairs(w_ref, h2_ref, ts)
    for i, (back, _) in enumerate(parts):

        @pl.when(mt >= back)
        def _():
            for h in halo_copies(i):
                h.wait_recv()

    def halo_rows(i, carry):
        norm_rows(halo_ref, i, 0)
        return carry

    lax.fori_loop(0, halo // KB, halo_rows, 0)

    seg_row = seg_ref[0:1, :]
    lanes = lax.broadcasted_iota(jnp.int32, (1, tokens), 1)
    doc = jnp.full((1, tokens), halo, jnp.int32)
    for value in range(DOCS):
        in_halo = jnp.zeros((1, 1), jnp.int32)
        for i, (_, count) in enumerate(parts):
            hit = (hseg_ref[i, 0:1, :] == value) & (lanes >= tokens - count)
            in_halo = in_halo + jnp.sum(hit.astype(jnp.int32), axis=1, keepdims=True)
        here = jnp.sum((seg_row == value).astype(jnp.int32), axis=1, keepdims=True)
        doc = doc - in_halo + jnp.where(seg_row > value, in_halo + here, 0)
    doc_ref[...] = jnp.broadcast_to(doc, doc_ref.shape)

    window = halo + tokens
    half_rows = window // 2

    def steps_at(p):
        work = {1: [(2, "z")], 2: [(2, 0)], 3: [(2, 1), (3, "z")], 4: [(3, 0)], 5: [(3, 1)]}
        for at, items in work.items():

            @pl.when(p == at)
            def _():
                for c, what in items:
                    if what == "z":
                        for k in range(1, ts):
                            net.z_step(c, k)
                    elif what < stages:
                        for k in range(ts):
                            net.far_step(c, k, what)

    def one_pair(p, carry):
        cols = pl.ds(pl.multiple_of(p * 128, 128), 128)
        t = jnp.minimum(p, ts - 1)
        a = jnp.maximum(p - ts, 0)
        low_q, high_q = vec_ref[2 * a, 7:8, 256:384], vec_ref[2 * a + 1, 7:8, 256:384]
        bias_q = jnp.where(p < ts, vec_ref[t, 7:8, 0:128], lanes_of(low_q, swap_halves(high_q)))
        bias_v = jnp.where(p < ts, vec_ref[t, 7:8, 128:256], lanes_of(swap_halves(low_q), high_q))
        w_q = w_ref[p, :, :, 0:128].reshape(width, 128)
        y = mm(normed_ref[pl.ds(halo, tokens), :], w_q) + bias_q
        q_ref[:, cols] = (y.astype(BF16) * 0.125).astype(BF16)

        def project(i, c):
            rows = pl.ds(pl.multiple_of(i * half_rows, 16), half_rows)
            w_kv = w_ref[p, :, :, 128:384].reshape(width, 256)
            kv = mm(normed_ref[rows, :], w_kv)
            k_ref[rows, cols] = kv[:, :128].astype(BF16)
            v_ref[rows, cols] = (kv[:, 128:] + bias_v).astype(BF16)
            return c

        lax.fori_loop(0, 2, project, 0)

        def turn(i, c):
            rows = pl.ds(pl.multiple_of(i * KB, KB), KB)
            vt_ref[:, rows] = v_ref[rows, cols].T
            return c

        lax.fori_loop(0, window // KB, turn, 0)

        def one_block(j, c):
            rows = pl.ds(pl.multiple_of(j * QB, QB), QB)
            q_block = q_ref[rows, cols]
            doc_row = doc_ref[0:1, rows]
            base = j * QB
            for h in range(2):
                query = keep_lanes(q_block, h)
                top = jnp.full((8, QB), -1e30, F32)
                for i in range(WINDOW):
                    span = pl.ds(pl.multiple_of(base + i * KB, KB), KB)
                    s = masked(mm(k_ref[span, cols], query, NT), i, doc_row, base)
                    s_ref[h, i] = s
                    top = jnp.maximum(top, fold_rows(s, jnp.max))
                top = jnp.max(top, axis=0, keepdims=True)
                total = jnp.zeros((8, QB), F32)
                acc = jnp.zeros((HD, QB), F32)
                for i in range(WINDOW):
                    span = pl.ds(pl.multiple_of(base + i * KB, KB), KB)
                    e = jnp.exp(s_ref[h, i] - top)
                    total = total + fold_rows(e, jnp.sum)
                    acc = acc + mm(vt_ref[h * HD : (h + 1) * HD, span], e.astype(BF16))
                total = jnp.sum(total, axis=0, keepdims=True)
                ot_ref[pl.ds(pl.multiple_of(p * 128 + h * HD, HD), HD), rows] = acc / total
                lse_ref[p, h : h + 1, rows] = top + jnp.log(total)
            o = ot_ref[pl.ds(pl.multiple_of(p * 128, 128), 128), rows]
            mixed_ref[rows, cols] = o.T.astype(BF16)
            return c

        lax.fori_loop(0, tokens // QB, one_block, 0)
        w_o = w_ref[p, :, :, 384:512].reshape(width, 128)
        start = jnp.where(p == 0, x_ref[...].astype(F32) + vec_ref[0, 2:3, :], hidden_ref[...])
        hidden_ref[...] = start + mm(mixed_ref[:, cols], w_o, NT)
        steps_at(p)
        return carry

    hidden_ref[...] = jnp.zeros_like(hidden_ref)
    lax.fori_loop(0, width // 128, one_pair, 0)
    for c in (2, 3):
        for k in range(ts):
            net.core_step(c, k)
    for c in own[2:]:
        c.wait()
    for i, (back, _) in enumerate(parts):

        @pl.when(mt + back < ts)
        def _():
            for h in halo_copies(i):
                h.wait_send()

    net.finish()


def front(x, seg, small, qkvo, fc, proj, dp, ts, halo):
    tokens, width = x.shape
    rows = fc.shape[0]
    window = halo + tokens
    pairs = width // 128
    copies = Gather.copies(dp, ts, 4)
    n_halo = len(halo_parts(tokens, ts))
    any_spec = pl.BlockSpec(memory_space=pl.ANY)
    vmem = pl.BlockSpec(memory_space=pltpu.VMEM)
    big = jax.ShapeDtypeStruct((ts, dp, rows, width), BF16)
    s = jax.ShapeDtypeStruct
    dma = pltpu.SemaphoreType.DMA
    return pl.pallas_call(
        functools.partial(front_kernel, dp, ts),
        out_shape=[
            big,
            big,
            big,
            s((ts, 8, width), F32),
            s((8, tokens), jnp.int32),
            s((window, width), BF16),
            s((tokens, width), BF16),
            s((window, width), BF16),
            s((window, width), BF16),
            s((width, tokens), F32),
            s((pairs, 2, tokens), F32),
            s((tokens, width), BF16),
            s((tokens, width), F32),
        ],
        in_specs=[vmem, vmem] + [any_spec] * 4,
        out_specs=[any_spec] * 3 + [vmem] * 10,
        scratch_shapes=[
            pltpu.VMEM((ts, dp, 8, width), F32),
            pltpu.VMEM((pairs, dp, rows, 512), BF16),
            pltpu.VMEM((ts, dp, rows, 256), BF16),
            pltpu.VMEM((halo, width), BF16),
            pltpu.VMEM((n_halo, 8, tokens), jnp.int32),
            pltpu.VMEM((128, window), BF16),
            pltpu.VMEM((2, WINDOW, KB, QB), F32),
            dma((2 * ts + 4,)),
            dma((4, ts, 2)),
            dma((4, ts)),
            dma((copies,)),
            dma((copies,)),
            dma((2 * n_halo,)),
            dma((2 * n_halo,)),
        ],
        compiler_params=pltpu.CompilerParams(
            collective_id=1, has_side_effects=True, vmem_limit_bytes=62 << 20
        ),
        name="front",
    )(x, seg, small, qkvo, fc, proj)


def gather_kernel(dp, ts, tokens, n_in, *refs):
    w_refs, (x_ref, seg_ref) = refs[:n_in], refs[n_in : n_in + 2]
    outs = refs[n_in + 2 : 2 * n_in + 2]
    halo_ref, hseg_ref = refs[2 * n_in + 2 : 2 * n_in + 4]
    local_sem, send_sem, recv_sem, halo_send, halo_recv = refs[2 * n_in + 4 :]
    me = lax.axis_index("dp")
    mt = lax.axis_index("tensor")
    bits = [1 << k for k in range(dp.bit_length() - 1)]
    far = bits[1:]
    halo_ref[...] = jnp.zeros_like(halo_ref)
    hseg_ref[...] = jnp.full_like(hseg_ref, -1)
    barrier = pltpu.get_barrier_semaphore()
    peers_t = [lax.rem(mt + k, ts) for k in range(1, ts)]
    for t in peers_t:
        pl.semaphore_signal(barrier, inc=1, device_id={"tensor": t}, device_id_type=MESH)
    for b in bits:
        pl.semaphore_signal(barrier, inc=1, device_id={"dp": me ^ b}, device_id_type=MESH)
    pl.semaphore_wait(barrier, len(peers_t) + len(bits))
    started = []

    def rcopy(src, dst, dev):
        i = len(started)
        c = pltpu.make_async_remote_copy(
            src_ref=src,
            dst_ref=dst,
            send_sem=send_sem.at[i],
            recv_sem=recv_sem.at[i],
            device_id=dev,
            device_id_type=MESH,
        )
        c.start()
        started.append(c)
        return c

    locals_, over_z = [], []
    for c in range(n_in):
        copy = pltpu.make_async_copy(w_refs[c], outs[c].at[mt, me], local_sem.at[c])
        copy.start()
        locals_.append(copy)
        over_z.append([rcopy(w_refs[c], outs[c].at[mt, me], {"tensor": t}) for t in peers_t])
        if c == min(1, n_in - 1):
            end = halo_ref.shape[0]
            halos = []
            for i, (back, count) in enumerate(halo_parts(tokens, ts)):
                end -= count
                pair = [
                    pltpu.make_async_remote_copy(
                        src_ref=src,
                        dst_ref=dst,
                        send_sem=halo_send.at[2 * i + k],
                        recv_sem=halo_recv.at[2 * i + k],
                        device_id={"tensor": lax.rem(mt + back, ts)},
                        device_id_type=MESH,
                    )
                    for k, (src, dst) in enumerate(
                        [
                            (x_ref.at[pl.ds(tokens - count, count)], halo_ref.at[pl.ds(end, count)]),
                            (seg_ref, hseg_ref.at[i]),
                        ]
                    )
                ]
                halos.append((back, pair))

                @pl.when(mt + back < ts)
                def _():
                    for h in pair:
                        h.start()

    half = max(ts // 2, 1)
    groups = [(0, half, far)] + ([(half, ts - half, far[::-1])] if ts > half else [])

    def spread(c, group, masks, later):
        res = {}
        for b in later + [1]:
            res[b] = []
            for m in masks:
                ref = outs[c].at[pl.ds(group[0], group[1]), me ^ m]
                res[b].append((m, rcopy(ref, ref, {"dp": me ^ b})))
        return res

    stages = len(far) + 1
    pending = {}
    for step in range(n_in + stages - 1):
        for s in range(stages):
            c = step - s
            if not 0 <= c < n_in:
                continue
            if s == 0:
                locals_[c].wait()
                for k in over_z[c]:
                    k.wait_recv()
            for gi, group in enumerate(groups):
                if s == 0:
                    pending[c, gi] = [spread(c, group, [0], group[2])]
                else:
                    b = group[2][s - 1]
                    masks = []
                    for res in pending[c, gi]:
                        for m, k in res.get(b, []):
                            k.wait_recv()
                            masks.append(m ^ b)
                    pending[c, gi].append(spread(c, group, masks, group[2][s:]))
    for c in range(n_in):
        for gi in range(len(groups)):
            for res in pending[c, gi]:
                for m, k in res[1]:
                    k.wait_recv()
    for back, pair in halos:

        @pl.when(mt >= back)
        def _():
            for h in pair:
                h.wait_recv()

        @pl.when(mt + back < ts)
        def _():
            for h in pair:
                h.wait_send()

    for k in started:
        k.wait_send()


def gather(parts, x, seg, dp, ts, halo):
    n_in = len(parts)
    tokens = x.shape[0]
    copies = n_in * ((ts - 1) + (2 if ts > 1 else 1) * (dp - 1))
    n_halo = len(halo_parts(tokens, ts))
    any_spec = pl.BlockSpec(memory_space=pl.ANY)
    vmem = pl.BlockSpec(memory_space=pltpu.VMEM)
    return pl.pallas_call(
        functools.partial(gather_kernel, dp, ts, tokens, n_in),
        out_shape=[jax.ShapeDtypeStruct((ts, dp) + p.shape, p.dtype) for p in parts]
        + [
            jax.ShapeDtypeStruct((halo, x.shape[1]), x.dtype),
            jax.ShapeDtypeStruct((n_halo,) + seg.shape, seg.dtype),
        ],
        in_specs=[any_spec] * (n_in + 2),
        out_specs=[any_spec] * n_in + [vmem, vmem],
        scratch_shapes=[
            pltpu.SemaphoreType.DMA((n_in,)),
            pltpu.SemaphoreType.DMA((copies,)),
            pltpu.SemaphoreType.DMA((copies,)),
            pltpu.SemaphoreType.DMA((2 * n_halo,)),
            pltpu.SemaphoreType.DMA((2 * n_halo,)),
        ],
        compiler_params=pltpu.CompilerParams(collective_id=1, has_side_effects=True),
        name="gather",
    )(*parts, x, seg)


def reduce_kernel(dp, ts, g_ref, out_ref, in_core, in_far, in_z, send_sem, recv_sem):
    n_c = g_ref.shape[0]
    me = lax.axis_index("dp")
    mt = lax.axis_index("tensor")
    bits = [1 << k for k in range(dp.bit_length() - 1)]
    far = bits[1:]
    barrier = pltpu.get_barrier_semaphore()
    peers_t = [lax.rem(mt + k, ts) for k in range(1, ts)]
    for t in peers_t:
        pl.semaphore_signal(barrier, inc=1, device_id={"tensor": t}, device_id_type=MESH)
    for b in bits:
        pl.semaphore_signal(barrier, inc=1, device_id={"dp": me ^ b}, device_id_type=MESH)
    pl.semaphore_wait(barrier, len(peers_t) + len(bits))
    started = []

    def rcopy(src, dst, dev):
        i = len(started)
        c = pltpu.make_async_remote_copy(
            src_ref=src,
            dst_ref=dst,
            send_sem=send_sem.at[i],
            recv_sem=recv_sem.at[i],
            device_id=dev,
            device_id_type=MESH,
        )
        c.start()
        started.append(c)
        return c

    half = max(ts // 2, 1)
    groups = [(0, half, far[::-1])] + ([(half, ts - half, far)] if ts > half else [])
    evens = list(range(0, dp, 2))
    core = []
    for c in range(n_c):
        core.append(
            {
                m: rcopy(g_ref.at[c, :, me ^ 1 ^ m], in_core.at[c, m >> 1], {"dp": me ^ 1})
                for m in evens[::-1]
            }
        )

    def add_into(dst, src, base, count):
        def one(i, carry):
            dst[base + i] = (dst[base + i].astype(F32) + src[i].astype(F32)).astype(BF16)
            return carry

        lax.fori_loop(0, count, one, 0)

    stages = len(far) + 2
    pending = {}
    slots = {}
    for step in range(n_c + stages - 1):
        for s in range(stages):
            c = step - s
            if not 0 <= c < n_c:
                continue
            if s == 0:
                for m in evens[::-1]:
                    core[c][m].wait_recv()

                    def one(i, carry, m=m):
                        in_core[c, m >> 1, i] = (
                            in_core[c, m >> 1, i].astype(F32) + g_ref[c, i, me ^ m].astype(F32)
                        ).astype(BF16)
                        return carry

                    lax.fori_loop(0, ts, one, 0)
            for gi, (t0, tn, order) in enumerate(groups):
                if s > 0:
                    for m, slot, k in pending.pop((c, gi)):
                        k.wait_recv()
                        add_into(in_core.at[c, m >> 1], in_far.at[c, slot, pl.ds(t0, tn)], t0, tn)
                if s < len(far):
                    b = order[s]
                    done = sum(order[:s])
                    masks = [m for m in evens if m & b and not m & done]
                    sent = []
                    for m in masks:
                        slot = slots.get((c, gi), 0)
                        slots[c, gi] = slot + 1
                        k = rcopy(
                            in_core.at[c, m >> 1, pl.ds(t0, tn)],
                            in_far.at[c, slot, pl.ds(t0, tn)],
                            {"dp": me ^ b},
                        )
                        sent.append((m ^ b, slot, k))
                    pending[c, gi] = sent
                elif s == len(far):
                    pending[c, gi] = []
            if s == len(far):
                pending[c, "z"] = [
                    rcopy(in_core.at[c, 0, lax.rem(mt + k, ts)], in_z.at[c, k - 1], {"tensor": lax.rem(mt + k, ts)})
                    for k in range(1, ts)
                ]
            if s == len(far) + 1:
                total = in_core[c, 0, mt].astype(F32)
                for k in pending[c, "z"]:
                    k.wait_recv()
                for k in range(ts - 1):
                    total = total + in_z[c, k].astype(F32)
                out_ref[c] = total
    for k in started:
        k.wait_send()


def reduce(grads, dp, ts):
    n_c, _, _, rows, width = grads.shape
    n_far = dp // 2 - 1
    groups = 2 if ts > 1 else 1
    copies = n_c * (dp // 2 + groups * n_far + ts - 1)
    vmem = pl.BlockSpec(memory_space=pltpu.VMEM)
    return pl.pallas_call(
        functools.partial(reduce_kernel, dp, ts),
        out_shape=jax.ShapeDtypeStruct((n_c, rows, width), F32),
        in_specs=[vmem],
        out_specs=vmem,
        scratch_shapes=[
            pltpu.VMEM((n_c, dp // 2, ts, rows, width), BF16),
            pltpu.VMEM((n_c, n_far, ts, rows, width), BF16),
            pltpu.VMEM((n_c, ts - 1, rows, width), BF16),
            pltpu.SemaphoreType.DMA((copies,)),
            pltpu.SemaphoreType.DMA((copies,)),
        ],
        compiler_params=pltpu.CompilerParams(
            collective_id=2, has_side_effects=True, vmem_limit_bytes=62 << 20
        ),
        name="reduce",
    )(grads)


def allowed_at(chunk, doc_row, first_q):
    key = chunk * KB + lax.broadcasted_iota(jnp.int32, (KB, QB), 0)
    query = first_q + lax.broadcasted_iota(jnp.int32, (KB, QB), 1)
    return (key >= doc_row) & (key <= query)


def attend_kernel(halo, first_ref, doc_ref, q_ref, k_ref, vt_ref, o_ref, lse_ref, s_ref):
    for j in range(q_ref.shape[0] // QB):
        rows = pl.ds(j * QB, QB)
        q_block = q_ref[rows, :]
        queries = [keep_lanes(q_block, h) for h in range(2)]
        doc_row = doc_ref[0:1, rows]
        first_q = halo + j * QB
        begin = first_ref[j]
        end = (first_q + QB) // KB

        def score(c, tops):
            keys = k_ref[pl.ds(pl.multiple_of(c * KB, KB), KB), :]
            ok = allowed_at(c, doc_row, first_q)
            res = []
            for h in range(2):
                s = jnp.where(ok, mm(keys, queries[h], NT), -1e30)
                s_ref[h, c] = s
                res.append(jnp.maximum(tops[h], fold_rows(s, jnp.max)))
            return tuple(res)

        tops = lax.fori_loop(begin, end, score, (jnp.full((8, QB), -1e30, F32),) * 2)
        tops = [jnp.max(t, axis=0, keepdims=True) for t in tops]

        def mix(c, carry):
            res = []
            for h in range(2):
                total, acc = carry[h]
                p = jnp.exp(s_ref[h, c] - tops[h])
                total = total + fold_rows(p, jnp.sum)
                vt = vt_ref[pl.ds(h * HD, HD), pl.ds(pl.multiple_of(c * KB, KB), KB)]
                acc = acc + mm(vt, p.astype(BF16))
                res.append((total, acc))
            return tuple(res)

        carry = lax.fori_loop(
            begin, end, mix, ((jnp.zeros((8, QB), F32), jnp.zeros((HD, QB), F32)),) * 2
        )
        for h in range(2):
            total = jnp.sum(carry[h][0], axis=0, keepdims=True)
            o_ref[pl.ds(h * HD, HD), rows] = carry[h][1] / total
            lse_ref[0, h : h + 1, rows] = tops[h] + jnp.log(total)


def attend(first, doc, q, k, vt, halo):
    tokens, width = q.shape
    keys = k.shape[0]
    pairs = width // 128
    return pl.pallas_call(
        functools.partial(attend_kernel, halo),
        out_shape=[
            jax.ShapeDtypeStruct((width, tokens), F32),
            jax.ShapeDtypeStruct((pairs, 2, tokens), F32),
        ],
        grid_spec=pltpu.PrefetchScalarGridSpec(
            num_scalar_prefetch=1,
            grid=(pairs,),
            in_specs=[
                pl.BlockSpec((1, tokens), lambda p, f: (0, 0)),
                pl.BlockSpec((tokens, 128), lambda p, f: (0, p)),
                pl.BlockSpec((keys, 128), lambda p, f: (0, p)),
                pl.BlockSpec((128, keys), lambda p, f: (p, 0)),
            ],
            out_specs=[
                pl.BlockSpec((128, tokens), lambda p, f: (p, 0)),
                pl.BlockSpec((1, 2, tokens), lambda p, f: (p, 0, 0)),
            ],
            scratch_shapes=[pltpu.VMEM((2, keys // KB, KB, QB), F32)],
        ),
        name="attend",
    )(first, doc, q, k, vt)


def attend_back_kernel(
    halo, first_ref, doc_ref, q_ref, k_ref, kt_ref, v_ref, do_ref, lse_ref, delta_ref, dq_ref, dk_ref, dv_ref
):
    dk_ref[...] = jnp.zeros_like(dk_ref)
    dv_ref[...] = jnp.zeros_like(dv_ref)
    for j in range(q_ref.shape[0] // QB):
        rows = pl.ds(j * QB, QB)
        q_block, do_block = q_ref[rows, :], do_ref[rows, :]
        queries = [keep_lanes(q_block, h) for h in range(2)]
        grads = [keep_lanes(do_block, h) for h in range(2)]
        doc_row = doc_ref[0:1, rows]
        first_q = halo + j * QB

        def step(c, carry):
            span = pl.ds(pl.multiple_of(c * KB, KB), KB)
            keys, values = k_ref[span, :], v_ref[span, :]
            ok = allowed_at(c, doc_row, first_q)
            res = []
            grad_k = grad_v = None
            for h in range(2):
                s = jnp.where(ok, mm(keys, queries[h], NT), -1e30)
                p = jnp.exp(s - lse_ref[0, h : h + 1, rows])
                dp_ = mm(values, grads[h], NT)
                ds = (p * (dp_ - delta_ref[0, h : h + 1, rows])).astype(BF16)
                gv = mm(p.astype(BF16), grads[h])
                gk = mm(ds, queries[h])
                grad_v = gv if grad_v is None else grad_v + gv
                grad_k = gk if grad_k is None else grad_k + gk
                kt = kt_ref[pl.ds(h * HD, HD), span]
                res.append(carry[h] + mm(kt, ds))
            dk_ref[span, :] += grad_k
            dv_ref[span, :] += grad_v
            return tuple(res)

        carry = lax.fori_loop(
            first_ref[j], (first_q + QB) // KB, step, (jnp.zeros((HD, QB), F32),) * 2
        )
        for h in range(2):
            dq_ref[pl.ds(h * HD, HD), rows] = carry[h] * 0.125


def attend_back(first, doc, q, k, kt, v, do, lse, delta, halo):
    tokens, width = q.shape
    keys = k.shape[0]
    pairs = width // 128
    q_spec = pl.BlockSpec((tokens, 128), lambda p, f: (0, p))
    k_spec = pl.BlockSpec((keys, 128), lambda p, f: (0, p))
    stat = pl.BlockSpec((1, 2, tokens), lambda p, f: (p, 0, 0))
    return pl.pallas_call(
        functools.partial(attend_back_kernel, halo),
        out_shape=[
            jax.ShapeDtypeStruct((width, tokens), F32),
            jax.ShapeDtypeStruct((keys, width), F32),
            jax.ShapeDtypeStruct((keys, width), F32),
        ],
        grid_spec=pltpu.PrefetchScalarGridSpec(
            num_scalar_prefetch=1,
            grid=(pairs,),
            in_specs=[
                pl.BlockSpec((1, tokens), lambda p, f: (0, 0)),
                q_spec,
                k_spec,
                pl.BlockSpec((128, keys), lambda p, f: (p, 0)),
                k_spec,
                q_spec,
                stat,
                stat,
            ],
            out_specs=[pl.BlockSpec((128, tokens), lambda p, f: (p, 0)), k_spec, k_spec],
        ),
        name="attend_back",
    )(first, doc, q, k, kt, v, do, lse, delta)


def gelu_tanh(values_in):
    return (
        0.5
        * values_in
        * (
            1.0
            + jnp.tanh(TANH_SLOPE * (values_in + CUBIC_TERM * values_in * values_in * values_in))
        )
    )


def norm_back(grad_in, gain_vec, unit_rows, scaler):
    scaled = grad_in * gain_vec
    return scaler * (
        scaled
        - jnp.mean(scaled, axis=-1, keepdims=True)
        - unit_rows * jnp.mean(scaled * unit_rows, axis=-1, keepdims=True)
    )


def plain_device(
    block_input,
    teacher,
    segment_ids,
    valid_mask,
    ln1_gain,
    ln1_bias,
    qkv_weight,
    qv_bias,
    out_weight,
    out_bias,
    ln2_gain,
    ln2_bias,
    fc_weight,
    fc_bias,
    proj_weight,
    proj_bias,
):
    dp, ts = lax.axis_size("dp"), lax.axis_size("tensor")
    me, mt = lax.axis_index("dp"), lax.axis_index("tensor")
    tokens, width = block_input.shape[1:]
    total_tokens = tokens * ts * dp
    halo = -(-(DOC_MOST - 1) // KB) * KB
    e = qkv_weight.shape[2]
    x = block_input[0]
    valid_rows = valid_mask[0].astype(F32)

    qkvo = jnp.concatenate([qkv_weight[0], qkv_weight[1], qkv_weight[2], out_weight.T], axis=1)
    local_count = jnp.sum(valid_mask[0])
    mine = jnp.arange(dp) == me

    def spread(v):
        return jnp.where(mine[:, None], v[..., None, :], jnp.zeros((), v.dtype))

    vectors = jnp.stack([ln1_gain, ln1_bias, out_bias, ln2_gain, ln2_bias, proj_bias])
    tail = jnp.stack([local_count // 16, local_count % 16]).astype(BF16)
    small = jnp.concatenate(
        [
            spread(vectors).reshape(6, width),
            spread(fc_bias).reshape(1, -1),
            jnp.concatenate(
                [spread(qv_bias).reshape(-1), tail, jnp.zeros((width - 2 * e - 2,), BF16)]
            )[None],
        ]
    )
    seg_rows = jnp.broadcast_to(segment_ids, (8, tokens))
    small_all, w_qkvo, w_fc, w_proj, x_halo, seg_halo = gather(
        [small, qkvo, fc_weight, proj_weight.T], x, seg_rows, dp, ts, halo
    )
    small_all = jnp.sum(small_all.astype(F32), axis=1)
    gain_one, bias_one, b_out, gain_two, bias_two, b_proj = [small_all[0, i] for i in range(6)]
    b_fc = small_all[:, 6].reshape(-1)
    b_q = small_all[:, 7, :e].reshape(-1)
    b_v = small_all[:, 7, e : 2 * e].reshape(-1)
    valid_count = jnp.sum(small_all[:, 7, 2 * e] * 16 + small_all[:, 7, 2 * e + 1])
    w_qkvo = w_qkvo.reshape(ts, width, 4, e)
    wq, wk, wv, wo = [w_qkvo[:, :, i].transpose(1, 0, 2).reshape(width, width) for i in range(4)]
    wf = w_fc.reshape(ts, width, -1)
    wp = w_proj.reshape(ts, width, -1)

    seg = segment_ids[0]
    pieces = []
    for i, (back, count) in enumerate(halo_parts(tokens, ts)):
        pieces.insert(0, seg_halo[i, 0, tokens - count :])
    filled = sum(p.shape[0] for p in pieces)
    seg_window = jnp.concatenate([jnp.full((halo - filled,), -1, jnp.int32)] + pieces)
    position = jnp.sum((seg_window[:, None] < seg[None, :]).astype(jnp.int32), axis=0)
    own = jnp.sum((seg[:, None] < seg[None, :]).astype(jnp.int32), axis=0)
    doc = (position + own)[None]
    first = doc[0, ::QB] // KB

    inputs = x.astype(F32)
    window = jnp.concatenate([x_halo, x]).astype(F32)
    unit_window, scale_window = normalize(window)
    normed_window = (unit_window * gain_one + bias_one).astype(BF16)
    unit_one, scale_one = unit_window[halo:], scale_window[halo:]
    normed_one = normed_window[halo:]
    q = ((mm(normed_one, wq) + b_q).astype(BF16) * 0.125).astype(BF16)
    k = mm(normed_window, wk).astype(BF16)
    v = (mm(normed_window, wv) + b_v).astype(BF16)
    mixed_t, lse = attend(first, doc, q, k, v.T, halo)
    mixed = mixed_t.T.astype(BF16)
    hidden = inputs + mm(mixed, wo, NT) + b_out
    unit_two, scale_two = normalize(hidden)
    normed_two = (unit_two * gain_two + bias_two).astype(BF16)
    pre_act = jnp.einsum("sd,tdf->stf", normed_two, wf, preferred_element_type=F32) + b_fc.reshape(ts, -1)
    activated = gelu_tanh(pre_act).astype(BF16)
    output = hidden + jnp.einsum("stf,tdf->sd", activated, wp, preferred_element_type=F32) + b_proj
    residual_error = output - teacher[0].astype(F32)
    squares = jnp.sum(valid_rows[:, None] * residual_error * residual_error)
    grad_output = valid_rows[:, None] * residual_error * (total_tokens / valid_count)
    low_output = grad_output.astype(BF16)
    grad_act = jnp.einsum("sd,tdf->stf", low_output, wp, preferred_element_type=F32)
    grad_proj_w = jnp.einsum("sd,stf->tdf", low_output, activated, preferred_element_type=F32)
    _, gelu_back = jax.vjp(gelu_tanh, pre_act)
    grad_pre = gelu_back(grad_act)[0].astype(BF16)
    grad_fc_w = jnp.einsum("sd,stf->tdf", normed_two, grad_pre, preferred_element_type=F32)
    grad_fc_b = jnp.sum(grad_pre, axis=0, dtype=F32)
    grad_normed_two = jnp.einsum("stf,tdf->sd", grad_pre, wf, preferred_element_type=F32)
    grad_gain_two = jnp.sum(grad_normed_two * unit_two, axis=0)
    grad_bias_two = jnp.sum(grad_normed_two, axis=0)
    grad_hidden = grad_output + norm_back(grad_normed_two, gain_two, unit_two, scale_two)
    low_hidden = grad_hidden.astype(BF16)
    grad_mixed = mm(low_hidden, wo).astype(BF16)
    grad_out_w = jnp.einsum("sd,se->de", low_hidden, mixed, preferred_element_type=F32)
    heads = width // HD
    delta = jnp.sum((grad_mixed.T.astype(F32) * mixed_t).reshape(heads // 2, 2, HD, tokens), axis=2)
    dq_t, dk, dv = attend_back(first, doc, q, k, k.T, v, grad_mixed, lse, delta, halo)
    dq, dk, dv = dq_t.T.astype(BF16), dk.astype(BF16), dv.astype(BF16)
    sd_se = lambda a, b: jnp.einsum("sd,se->de", a, b, preferred_element_type=F32)
    g_q, g_k, g_v = sd_se(normed_one, dq), sd_se(normed_window, dk), sd_se(normed_window, dv)
    grad_window = mm(dk, wk, NT) + mm(dv, wv, NT)
    grad_normed_one = grad_window[halo:] + mm(dq, wq, NT)
    end = halo
    for back, count in halo_parts(tokens, ts):
        end -= count
        part = lax.ppermute(
            grad_window[end : end + count].astype(BF16), "tensor", [(t, t - back) for t in range(back, ts)]
        )
        grad_normed_one = grad_normed_one.at[tokens - count :].add(part.astype(F32))
    grad_input = grad_hidden + norm_back(grad_normed_one, gain_one, unit_one, scale_one)

    def by_t(g):
        return g.reshape(width, ts, e)

    g_qkvo = jnp.stack([by_t(g_q), by_t(g_k), by_t(g_v), by_t(grad_out_w)], axis=2)
    g_qkvo = g_qkvo.transpose(1, 0, 2, 3).reshape(ts, width, 4 * e)
    grads = jnp.stack([grad_proj_w, grad_fc_w, g_qkvo]).astype(BF16)
    grads = grads.reshape(3, ts, dp, width // dp, -1)
    r_proj, r_fc, r_qkvo = reduce(grads, dp, ts)
    smalls = [
        jnp.sum(grad_normed_one * unit_one, axis=0),
        jnp.sum(grad_normed_one, axis=0),
        jnp.sum(grad_hidden, axis=0),
        grad_gain_two,
        grad_bias_two,
        jnp.sum(grad_output, axis=0),
        grad_fc_b.reshape(-1),
        jnp.sum(dq, axis=0, dtype=F32),
        jnp.sum(dv, axis=0, dtype=F32),
        squares[None],
    ]
    summed = lax.psum(jnp.concatenate(smalls), ("dp", "tensor"))
    rows = width // dp
    own_rows = lambda i: lax.dynamic_slice_in_dim(summed, i * width + me * rows, rows)
    fc_b = summed[6 * width : 6 * width + fc_bias.size * dp * ts].reshape(ts, -1, dp, fc_bias.shape[1])
    qv0 = 6 * width + fc_bias.size * dp * ts
    qv_b = summed[qv0 : qv0 + 2 * width].reshape(2, ts, -1, dp, qv_bias.shape[2])
    loss = summed[-1] / (width * valid_count)
    pick = lambda a, i, ax: lax.dynamic_index_in_dim(a, i, ax, keepdims=False)
    return (
        output.astype(BF16)[None],
        loss,
        grad_input[None],
        own_rows(0),
        own_rows(1),
        jnp.stack([r_qkvo[:, i * e : (i + 1) * e] for i in range(3)]),
        pick(pick(qv_b, mt, 1), me, 2),
        r_qkvo[:, 3 * e :].T,
        own_rows(2),
        own_rows(3),
        own_rows(4),
        r_fc,
        pick(pick(fc_b, mt, 0), me, 1),
        r_proj.T,
        own_rows(5),
    )


def on_device(
    block_input,
    teacher,
    segment_ids,
    valid_mask,
    ln1_gain,
    ln1_bias,
    qkv_weight,
    qv_bias,
    out_weight,
    out_bias,
    ln2_gain,
    ln2_bias,
    fc_weight,
    fc_bias,
    proj_weight,
    proj_bias,
):
    dp, ts = lax.axis_size("dp"), lax.axis_size("tensor")
    me, mt = lax.axis_index("dp"), lax.axis_index("tensor")
    tokens, width = block_input.shape[1:]
    total_tokens = tokens * ts * dp
    halo = -(-(DOC_MOST - 1) // KB) * KB
    e = qkv_weight.shape[2]
    x = block_input[0]
    valid_rows = valid_mask[0].astype(F32)

    out_t = out_weight.T
    cuts = [qkv_weight[0], qkv_weight[1], qkv_weight[2], out_t]
    qkvo = jnp.concatenate([c[:, : 2 * HD] for c in cuts] + [c[:, 2 * HD :] for c in cuts], axis=1)
    local_count = jnp.sum(valid_rows)
    mine = jnp.arange(dp) == me

    def spread(v):
        return jnp.where(mine[:, None], v[..., None, :], jnp.zeros((), v.dtype)).astype(F32)

    vectors = jnp.stack([ln1_gain, ln1_bias, out_bias, ln2_gain, ln2_bias, proj_bias])
    qv = spread(qv_bias).reshape(2, e)
    small = jnp.concatenate(
        [
            spread(vectors).reshape(6, width),
            spread(fc_bias).reshape(1, -1),
            jnp.concatenate(
                [qv[0, : 2 * HD], qv[1, : 2 * HD], qv[0, 2 * HD :], qv[1, 2 * HD :], local_count[None]]
                + [jnp.zeros((width - 2 * e - 1,), F32)]
            )[None],
        ]
    )
    seg_rows = jnp.broadcast_to(segment_ids, (8, tokens))
    qkvo_all, w_fc, w_proj, vec, doc, normed_window, q, k, v, mixed_t, lse, mixed, hidden = front(
        x, seg_rows, small, qkvo, fc_weight, proj_weight.T, dp, ts, halo
    )
    gain_one, bias_one, b_out, gain_two, bias_two, b_proj = [vec[0, i] for i in range(6)]
    b_fc = vec[:, 6].reshape(-1)
    valid_count = jnp.sum(vec[:, 7, 2 * e])
    w_qkvo = qkvo_all.reshape(ts, width, 4 * e)

    def pair_weights(i):
        low = w_qkvo[:, :, i * 128 : (i + 1) * 128]
        last = w_qkvo[:, :, 512 + i * HD : 512 + (i + 1) * HD]
        last = last.reshape(ts // 2, 2, width, HD).transpose(0, 2, 1, 3).reshape(ts // 2, width, 128)
        return jnp.concatenate([low, last]).transpose(1, 0, 2).reshape(width, width)

    wq, wk, wv, wo = [pair_weights(i) for i in range(4)]
    wf = w_fc.reshape(ts, width, -1)
    wp = w_proj.reshape(ts, width, -1)
    doc = doc[0:1]
    first = doc[0, ::QB] // KB

    inputs = x.astype(F32)
    unit_one, scale_one = normalize(inputs)
    normed_one = normed_window[halo:]
    unit_two, scale_two = normalize(hidden)
    normed_two = (unit_two * gain_two + bias_two).astype(BF16)
    pre_act = jnp.einsum("sd,tdf->stf", normed_two, wf, preferred_element_type=F32) + b_fc.reshape(ts, -1)
    activated = gelu_tanh(pre_act).astype(BF16)
    output = hidden + jnp.einsum("stf,tdf->sd", activated, wp, preferred_element_type=F32) + b_proj
    residual_error = output - teacher[0].astype(F32)
    squares = jnp.sum(valid_rows[:, None] * residual_error * residual_error)
    grad_output = valid_rows[:, None] * residual_error * (total_tokens / valid_count)
    low_output = grad_output.astype(BF16)
    grad_act = jnp.einsum("sd,tdf->stf", low_output, wp, preferred_element_type=F32)
    grad_proj_w = jnp.einsum("sd,stf->tdf", low_output, activated, preferred_element_type=F32)
    _, gelu_back = jax.vjp(gelu_tanh, pre_act)
    grad_pre = gelu_back(grad_act)[0].astype(BF16)
    grad_fc_w = jnp.einsum("sd,stf->tdf", normed_two, grad_pre, preferred_element_type=F32)
    grad_fc_b = jnp.sum(grad_pre, axis=0, dtype=F32)
    grad_normed_two = jnp.einsum("stf,tdf->sd", grad_pre, wf, preferred_element_type=F32)
    grad_gain_two = jnp.sum(grad_normed_two * unit_two, axis=0)
    grad_bias_two = jnp.sum(grad_normed_two, axis=0)
    grad_hidden = grad_output + norm_back(grad_normed_two, gain_two, unit_two, scale_two)
    low_hidden = grad_hidden.astype(BF16)
    grad_mixed = mm(low_hidden, wo).astype(BF16)
    grad_out_w = jnp.einsum("sd,se->de", low_hidden, mixed, preferred_element_type=F32)
    heads = width // HD
    delta = jnp.sum((grad_mixed.T.astype(F32) * mixed_t).reshape(heads // 2, 2, HD, tokens), axis=2)
    dq_t, dk, dv = attend_back(first, doc, q, k, k.T, v, grad_mixed, lse, delta, halo)
    dq, dk, dv = dq_t.T.astype(BF16), dk.astype(BF16), dv.astype(BF16)
    sd_se = lambda a, b: jnp.einsum("sd,se->de", a, b, preferred_element_type=F32)
    g_q, g_k, g_v = sd_se(normed_one, dq), sd_se(normed_window, dk), sd_se(normed_window, dv)
    grad_window = mm(dk, wk, NT) + mm(dv, wv, NT)
    grad_normed_one = grad_window[halo:] + mm(dq, wq, NT)
    end = halo
    for back, count in halo_parts(tokens, ts):
        end -= count
        part = lax.ppermute(
            grad_window[end : end + count].astype(BF16), "tensor", [(t, t - back) for t in range(back, ts)]
        )
        grad_normed_one = grad_normed_one.at[tokens - count :].add(part.astype(F32))
    grad_input = grad_hidden + norm_back(grad_normed_one, gain_one, unit_one, scale_one)

    def by_t(gs):
        gs = jnp.stack([g.reshape(width, -1, 128) for g in gs])
        low = gs[:, :, :ts].transpose(2, 1, 0, 3).reshape(ts, width, 512)
        last = gs[:, :, ts:].reshape(4, width, ts, HD).transpose(2, 1, 0, 3).reshape(ts, width, 256)
        return jnp.concatenate([low, last], axis=2)

    g_qkvo = by_t([g_q, g_k, g_v, grad_out_w])
    grads = jnp.stack([grad_proj_w, grad_fc_w, g_qkvo]).astype(BF16)
    grads = grads.reshape(3, ts, dp, width // dp, -1)
    r_proj, r_fc, r_qkvo = reduce(grads, dp, ts)
    def by_head(v):
        return jnp.concatenate([v[: ts * 128].reshape(ts, 128), v[ts * 128 :].reshape(ts, HD)], axis=1).reshape(-1)

    def columns(i):
        return jnp.concatenate([r_qkvo[:, i * 128 : (i + 1) * 128], r_qkvo[:, 512 + i * HD : 512 + (i + 1) * HD]], axis=1)

    smalls = [
        jnp.sum(grad_normed_one * unit_one, axis=0),
        jnp.sum(grad_normed_one, axis=0),
        jnp.sum(grad_hidden, axis=0),
        grad_gain_two,
        grad_bias_two,
        jnp.sum(grad_output, axis=0),
        grad_fc_b.reshape(-1),
        by_head(jnp.sum(dq, axis=0, dtype=F32)),
        by_head(jnp.sum(dv, axis=0, dtype=F32)),
        squares[None],
    ]
    summed = lax.psum(jnp.concatenate(smalls), ("dp", "tensor"))
    rows = width // dp
    own_rows = lambda i: lax.dynamic_slice_in_dim(summed, i * width + me * rows, rows)
    fc_b = summed[6 * width : 6 * width + fc_bias.size * dp * ts].reshape(ts, -1, dp, fc_bias.shape[1])
    qv0 = 6 * width + fc_bias.size * dp * ts
    qv_b = summed[qv0 : qv0 + 2 * width].reshape(2, ts, -1, dp, qv_bias.shape[2])
    loss = summed[-1] / (width * valid_count)
    pick = lambda a, i, ax: lax.dynamic_index_in_dim(a, i, ax, keepdims=False)
    return (
        output.astype(BF16)[None],
        loss,
        grad_input[None],
        own_rows(0),
        own_rows(1),
        jnp.stack([columns(i) for i in range(3)]),
        pick(pick(qv_b, mt, 1), me, 2),
        columns(3).T,
        own_rows(2),
        own_rows(3),
        own_rows(4),
        r_fc,
        pick(pick(fc_b, mt, 0), me, 1),
        r_proj.T,
        own_rows(5),
    )


def solution(mesh):
    placed = (
        P("dp", "tensor", None),
        P("dp", "tensor", None),
        P("dp", "tensor"),
        P("dp", "tensor"),
        P("dp"),
        P("dp"),
        P(None, "dp", "tensor"),
        P(None, "tensor", "dp"),
        P("tensor", "dp"),
        P("dp"),
        P("dp"),
        P("dp"),
        P("dp", "tensor"),
        P("tensor", "dp"),
        P("tensor", "dp"),
        P("dp"),
    )
    def fits(qkv_weight, block_input):
        rows = block_input.shape[2] // mesh.shape["dp"]
        wide = qkv_weight.shape[2] // mesh.shape["tensor"]
        return rows % 16 == 0 and wide == 3 * HD and mesh.shape["tensor"] % 2 == 0

    def step(*args):
        return placed_step(on_device if fits(args[6], args[0]) else plain_device)(*args)

    placed_step = lambda body: jax.shard_map(
        body,
        mesh=mesh,
        in_specs=placed,
        out_specs=(
            P("dp", "tensor", None),
            P(),
            P("dp", "tensor", None),
            P("dp"),
            P("dp"),
            P(None, "dp", "tensor"),
            P(None, "tensor", "dp"),
            P("tensor", "dp"),
            P("dp"),
            P("dp"),
            P("dp"),
            P("dp", "tensor"),
            P("tensor", "dp"),
            P("tensor", "dp"),
            P("dp"),
        ),
        check_vma=False,
    )
    return step
```

```python
import functools

import jax
import jax.numpy as jnp
from jax import lax
from jax.experimental import pallas as pl
from jax.experimental.pallas import tpu as pltpu
from jax.sharding import PartitionSpec as P

HD = 64
DOC_MOST = 800
KB = 128
QB = 256
DOCS = 8
HALO = -(-(DOC_MOST - 1) // KB) * KB
LEAD = (HALO - DOC_MOST + 1) // 32 * 32
CHUNKS = ([(LEAD, KB - LEAD)] if LEAD else [(0, KB)]) + [(r, KB) for r in range(KB, HALO + QB, KB)]
Q_SCALE = 0.125 * 1.4426950408889634
EPSILON = 1e-05
TANH_SLOPE = 0.7978845608028654
CUBIC_TERM = 0.044715
MESH = pl.DeviceIdType.MESH
F32 = jnp.float32
BF16 = jnp.bfloat16
NN = (((1,), (0,)), ((), ()))
NT = (((1,), (1,)), ((), ()))


def mm(a, b, dims=NN):
    return lax.dot_general(a, b, dims, preferred_element_type=F32)


def halo_parts(tokens, ts):
    parts, left, back = [], DOC_MOST, 1
    while left > 0 and back < ts:
        parts.append((back, min(tokens, left)))
        left -= tokens
        back += 1
    return parts


class Gather:
    def __init__(self, dp, ts, ins, outs, z_send, z_recv, send_sem, recv_sem):
        self.dp, self.ts, self.ins, self.outs = dp, ts, ins, outs
        self.z_send, self.z_recv, self.send_sem, self.recv_sem = z_send, z_recv, send_sem, recv_sem
        self.me, self.mt = lax.axis_index("dp"), lax.axis_index("tensor")
        self.far = [1 << k for k in range(1, dp.bit_length() - 1)]
        self.keys = {}
        self.flight = []
        self.near = [sorted(range(ts), key=lambda t: (abs(t - m), t)) for m in range(ts)]

    @staticmethod
    def copies(dp, ts, parts):
        return parts * ts * (dp - 1)

    def t_of(self, k):
        t = jnp.int32(self.near[0][k])
        for m in range(1, self.ts):
            t = jnp.where(self.mt == m, self.near[m][k], t)
        return t

    def order(self, t):
        flip = t * 2 >= self.ts
        return [jnp.where(flip, b, a) for a, b in zip(self.far, self.far[::-1])]

    def place(self, c, t, dp_index):
        return self.outs[c].at[t, dp_index]

    def along(self, c, t, up):
        src = self.ins[c] if t is None else self.place(c, t, self.me)
        t = self.mt if t is None else t
        return pltpu.make_async_remote_copy(
            src_ref=src,
            dst_ref=self.place(c, t, self.me),
            send_sem=self.z_send.at[c, t, int(up)],
            recv_sem=self.z_recv.at[c, t],
            device_id={"tensor": self.mt + (1 if up else -1)},
            device_id_type=MESH,
        )

    def desc(self, key):
        c, k, known, i = key
        t = self.t_of(k)
        order = self.order(t)
        mask = jnp.int32(0)
        for b in known:
            mask = mask ^ order[b]
        ref = self.place(c, t, self.me ^ mask)
        own = k == 0 and not known
        n = self.keys.setdefault(key, len(self.keys))
        return pltpu.make_async_remote_copy(
            src_ref=self.ins[c] if own else ref,
            dst_ref=ref,
            send_sem=self.send_sem.at[n],
            recv_sem=self.recv_sem.at[n],
            device_id={"dp": self.me ^ (1 if i < 0 else order[i])},
            device_id_type=MESH,
        )

    def here(self, c, k, known):
        first = max(known) + 1 if known else 0
        for i in list(range(first, len(self.far))) + [-1]:
            key = (c, k, known, i)
            self.desc(key).start()
            self.flight.append(key)

    def start(self, c):
        @pl.when(self.mt + 1 < self.ts)
        def _():
            self.along(c, None, True).start()

        @pl.when(self.mt >= 1)
        def _():
            self.along(c, None, False).start()

        self.here(c, 0, ())

    def z_step(self, c, k):
        t = self.t_of(k)
        self.along(c, t, True).wait_recv()

        @pl.when((t < self.mt) & (self.mt + 1 < self.ts))
        def _():
            self.along(c, t, True).start()

        @pl.when((t > self.mt) & (self.mt >= 1))
        def _():
            self.along(c, t, False).start()

        self.here(c, k, ())

    def far_step(self, c, k, i):
        for key in [q for q in self.flight if q[:2] == (c, k) and q[3] == i]:
            self.desc(key).wait_recv()
            self.here(c, k, key[2] + (i,))

    def core_step(self, c, k):
        for key in [q for q in self.flight if q[:2] == (c, k) and q[3] < 0]:
            self.desc(key).wait_recv()

    def finish(self):
        for c in range(len(self.ins)):
            for k in range(self.ts):
                t = self.t_of(k)

                @pl.when((t <= self.mt) & (self.mt + 1 < self.ts))
                def _():
                    self.along(c, t, True).wait_send()

                @pl.when((t >= self.mt) & (self.mt >= 1))
                def _():
                    self.along(c, t, False).wait_send()

        for key in self.flight:
            self.desc(key).wait_send()


def meet(dp, ts):
    me, mt = lax.axis_index("dp"), lax.axis_index("tensor")
    barrier = pltpu.get_barrier_semaphore()
    for k in range(1, ts):
        pl.semaphore_signal(barrier, inc=1, device_id={"tensor": lax.rem(mt + k, ts)}, device_id_type=MESH)
    for b in range(1, dp):
        pl.semaphore_signal(barrier, inc=1, device_id={"dp": me ^ b}, device_id_type=MESH)
    pl.semaphore_wait(barrier, ts - 1 + dp - 1)


def keep_lanes(block, head):
    lanes = lax.broadcasted_iota(jnp.int32, block.shape, 1)
    return jnp.where((lanes < HD) == (head == 0), block, jnp.zeros_like(block))


def fold_rows(block, op):
    return op(block.reshape(block.shape[0] // 8, 8, block.shape[1]), axis=0)


def swap_halves(block):
    return jnp.concatenate([block[:, HD:], block[:, :HD]], axis=1)


def lanes_of(low, high):
    lanes = lax.broadcasted_iota(jnp.int32, low.shape, 1)
    return jnp.where(lanes < HD, low, high)


def causal(s, row):
    ahead = row - HALO
    if ahead < 0:
        return s
    key = lax.broadcasted_iota(jnp.int32, s.shape, 0)
    query = lax.broadcasted_iota(jnp.int32, s.shape, 1)
    return jnp.where(key + ahead <= query, s, -1e30)


def segment_lanes(seg_row, same):
    shape = (128, seg_row.shape[1])
    value = lax.rem(lax.broadcasted_iota(jnp.int32, shape, 0), HD)
    hit = (seg_row == value) if same else (seg_row != value)
    level = -1e30 if same else 1.0
    return jnp.where(hit & (value < DOCS), level, 0.0).T.astype(BF16)


def normalize(values_in):
    center = values_in - jnp.mean(values_in, axis=-1, keepdims=True)
    scaler = lax.rsqrt(jnp.mean(center * center, axis=-1, keepdims=True) + EPSILON)
    return (center * scaler, scaler)


def merge_pairs(w_ref, h2_ref, ts):
    for a in range(ts // 2):
        tiles = []
        for t in (2 * a, 2 * a + 1):
            block = h2_ref[t, :, :, 0:256].reshape(-1, 256)
            tiles.append((block[:, :128], block[:, 128:]))
        (qk0, vo0), (qk1, vo1) = tiles
        merged = [
            lanes_of(qk0, swap_halves(qk1)),
            lanes_of(swap_halves(qk0), qk1),
            lanes_of(vo0, swap_halves(vo1)),
            lanes_of(swap_halves(vo0), vo1),
        ]
        for i, m in enumerate(merged):
            w_ref[ts + a, :, :, i * 128 : (i + 1) * 128] = m.reshape(w_ref.shape[1], w_ref.shape[2], 128)


def weight_loads(qkvo_all, w_ref, h2_ref, sem, ts):
    res = []
    for t in range(ts):
        res.append(pltpu.make_async_copy(qkvo_all.at[t, :, :, pl.ds(0, 512)], w_ref.at[t], sem.at[2 * t]))
        res.append(pltpu.make_async_copy(qkvo_all.at[t, :, :, pl.ds(512, 256)], h2_ref.at[t, :, :, pl.ds(0, 256)], sem.at[2 * t + 1]))
    return res


def front_kernel(
    dp,
    ts,
    x_ref,
    seg_ref,
    small_ref,
    qkvo_ref,
    fc_ref,
    proj_ref,
    qkvo_all,
    fc_all,
    proj_all,
    vec_ref,
    kseg_ref,
    qseg_ref,
    normed_t_ref,
    halo_ref,
    q_ref,
    k_ref,
    v_ref,
    ot_ref,
    lse_ref,
    mixed_ref,
    hidden_ref,
    small_all,
    w_ref,
    h2_ref,
    hseg_ref,
    normed_ref,
    ka_ref,
    vt_ref,
    s_ref,
    local_sem,
    z_send,
    z_recv,
    send_sem,
    recv_sem,
    halo_send,
    halo_recv,
):
    me, mt = lax.axis_index("dp"), lax.axis_index("tensor")
    tokens, width = x_ref.shape
    halo = halo_ref.shape[0]
    ins = [small_ref, qkvo_ref, fc_ref, proj_ref]
    outs = [small_all, qkvo_all, fc_all, proj_all]
    halo_ref[...] = jnp.zeros_like(halo_ref)
    hseg_ref[...] = jnp.full_like(hseg_ref, -1)
    meet(dp, ts)
    net = Gather(dp, ts, ins, outs, z_send, z_recv, send_sem, recv_sem)
    stages = len(net.far)
    parts = halo_parts(tokens, ts)

    def halo_copies(i):
        back, count = parts[i]
        end = halo - sum(c for _, c in parts[:i])
        pairs = [
            (x_ref.at[pl.ds(tokens - count, count)], halo_ref.at[pl.ds(end - count, count)]),
            (seg_ref, hseg_ref.at[i]),
        ]
        return [
            pltpu.make_async_remote_copy(
                src_ref=src,
                dst_ref=dst,
                send_sem=halo_send.at[2 * i + n],
                recv_sem=halo_recv.at[2 * i + n],
                device_id={"tensor": lax.rem(mt + back, ts)},
                device_id_type=MESH,
            )
            for n, (src, dst) in enumerate(pairs)
        ]

    own = [
        pltpu.make_async_copy(ins[c], outs[c].at[mt, me], local_sem.at[2 * ts + c]) for c in range(4)
    ]
    net.start(0)
    net.start(1)
    for c in own:
        c.start()
    for k in range(1, ts):
        net.z_step(0, k)
    for k in range(1, ts - 1):
        net.z_step(1, k)
    for i, (back, _) in enumerate(parts):

        @pl.when(mt + back < ts)
        def _():
            for h in halo_copies(i):
                h.start()

    net.z_step(1, ts - 1)
    for i in range(stages):
        for k in range(ts):
            net.far_step(0, k, i)
    for k in range(ts):
        net.far_step(1, k, 0)
    net.start(2)
    net.start(3)
    own[0].wait()
    for k in range(ts):
        net.core_step(0, k)
    for t in range(ts):
        vec_ref[t] = jnp.sum(small_all[t], axis=0)

    def norm_rows(src, i, at):
        unit, _ = normalize(src[pl.ds(i * KB, KB), :].astype(F32))
        rows = pl.ds(pl.multiple_of(at + i * KB, KB), KB)
        normed = (unit * vec_ref[0, 0:1, :] + vec_ref[0, 1:2, :]).astype(BF16)
        normed_ref[rows, :] = normed
        for n in range(width // KB):
            normed_t_ref[n * KB : (n + 1) * KB, rows] = normed[:, n * KB : (n + 1) * KB].T

    def own_rows(i, carry):
        norm_rows(x_ref, i, halo)
        return carry

    lax.fori_loop(0, tokens // KB, own_rows, 0)
    qseg_ref[...] = segment_lanes(seg_ref[0:1, :], True)
    kseg_ref[pl.ds(halo, tokens), :] = segment_lanes(seg_ref[0:1, :], False)
    for i in range(1, stages):
        for k in range(ts):
            net.far_step(1, k, i)
    own[1].wait()
    for k in range(ts):
        net.core_step(1, k)
    loads = weight_loads(qkvo_all, w_ref, h2_ref, local_sem, ts)
    for load in loads:
        load.start()
    for load in loads:
        load.wait()
    merge_pairs(w_ref, h2_ref, ts)

    def biases(p):
        t = jnp.minimum(p, ts - 1)
        a = jnp.maximum(p - ts, 0)
        low, high = vec_ref[2 * a, 7:8, 256:384], vec_ref[2 * a + 1, 7:8, 256:384]
        bias_q = jnp.where(p < ts, vec_ref[t, 7:8, 0:128], lanes_of(low, swap_halves(high)))
        bias_v = jnp.where(p < ts, vec_ref[t, 7:8, 128:256], lanes_of(swap_halves(low), high))
        return bias_q, bias_v

    own_span = pl.ds(halo, tokens)

    def project_own(p, carry):
        cols = pl.ds(pl.multiple_of(p * 128, 128), 128)
        bias_q, bias_v = biases(p)
        y = mm(normed_ref[own_span, :], w_ref[p, :, :, 0:384].reshape(width, 384))
        q_ref[:, cols] = ((y[:, :128] + bias_q) * Q_SCALE).astype(BF16)
        k_ref[own_span, cols] = y[:, 128:256].astype(BF16)
        v_ref[own_span, cols] = (y[:, 256:] + bias_v).astype(BF16)
        return carry

    lax.fori_loop(0, width // 128, project_own, 0)
    net.far_step(2, 0, 0)
    for i, (back, _) in enumerate(parts):

        @pl.when(mt >= back)
        def _():
            for h in halo_copies(i):
                h.wait_recv()

    def halo_rows(i, carry):
        norm_rows(halo_ref, i, 0)
        return carry

    lax.fori_loop(0, halo // KB, halo_rows, 0)
    lanes = lax.rem(lax.broadcasted_iota(jnp.int32, (halo, 128), 1), HD)
    kseg_ref[pl.ds(0, halo), :] = jnp.where(lanes < DOCS, 1.0, 0.0).astype(BF16)
    end = halo
    for i, (_, count) in enumerate(parts):
        kseg_ref[pl.ds(end - count, count), :] = segment_lanes(hseg_ref[i, 0:1, :], False)[tokens - count :]
        end -= count

    plan = {0: [(3, 0, 0)]}
    for n, (k, c) in enumerate((k, c) for k in range(1, ts) for c in (2, 3)):
        plan.setdefault(n, []).append((c, k, "z"))
        plan.setdefault(n + 2, []).append((c, k, 0))
        plan.setdefault(n + 4, []).append((c, k, 1))
    plan.setdefault(2, []).extend([(2, 0, 1), (3, 0, 1)])

    def steps_at(p, place):
        for slot, items in plan.items():
            if slot % 2 != place:
                continue

            @pl.when(p == slot // 2)
            def _():
                for item in items:
                    c, k, what = item
                    if what == "z":
                        net.z_step(c, k)
                    elif what < stages:
                        net.far_step(c, k, what)

    def one_pair(p, carry):
        cols = pl.ds(pl.multiple_of(p * 128, 128), 128)
        _, bias_v = biases(p)

        def project(i, c):
            rows = pl.ds(pl.multiple_of(i * (halo // 2), 16), halo // 2)
            kv = mm(normed_ref[rows, :], w_ref[p, :, :, 128:384].reshape(width, 256))
            k_ref[rows, cols] = kv[:, :128].astype(BF16)
            v_ref[rows, cols] = (kv[:, 128:] + bias_v).astype(BF16)
            return c

        lax.fori_loop(0, 2, project, 0)

        def turn(i, c):
            rows = pl.ds(pl.multiple_of(i * KB, KB), KB)
            vt_ref[:, rows] = v_ref[rows, cols].T
            k, aux = k_ref[rows, cols], kseg_ref[rows, :]
            ka_ref[0, rows, :] = lanes_of(k, aux)
            ka_ref[1, rows, :] = lanes_of(aux, k)
            return c

        lax.fori_loop(0, (halo + tokens) // KB, turn, 0)
        steps_at(p, 0)

        def one_block(j, c):
            rows = pl.ds(pl.multiple_of(j * QB, QB), QB)
            q_block, aux = q_ref[rows, cols], qseg_ref[rows, :]
            base = j * QB
            spans = [(row, size, pl.ds(pl.multiple_of(base + row, 16), size)) for row, size in CHUNKS]
            for h in range(2):
                query = lanes_of(q_block, aux) if h == 0 else lanes_of(aux, q_block)
                top = jnp.full((8, QB), -1e30, F32)
                for row, size, span in spans:
                    s = causal(mm(ka_ref[h, span, :], query, NT), row)
                    s_ref[h, row : row + size, :] = s
                    top = jnp.maximum(top, fold_rows(s, jnp.max))
                top = jnp.max(top, axis=0, keepdims=True)
                total = jnp.zeros((8, QB), F32)
                acc = jnp.zeros((HD, QB), F32)
                for row, size, span in spans:
                    e = jnp.exp2(s_ref[h, row : row + size, :] - top)
                    total = total + fold_rows(e, jnp.sum)
                    if size < KB:
                        wide = pl.ds(pl.multiple_of(base + row // KB * KB, KB), KB)
                        e = jnp.concatenate([jnp.zeros((KB - size, QB), F32), e], axis=0)
                    else:
                        wide = pl.ds(pl.multiple_of(base + row, KB), KB)
                    acc = acc + mm(vt_ref[h * HD : (h + 1) * HD, wide], e.astype(BF16))
                total = jnp.sum(total, axis=0, keepdims=True)
                ot_ref[pl.ds(pl.multiple_of(p * 128 + h * HD, HD), HD), rows] = acc / total
                lse_ref[p, h : h + 1, rows] = top + jnp.log2(total)
            o = ot_ref[pl.ds(pl.multiple_of(p * 128, 128), 128), rows]
            mixed_ref[rows, cols] = o.T.astype(BF16)
            return c

        lax.fori_loop(0, tokens // QB, one_block, 0)
        w_o = w_ref[p, :, :, 384:512].reshape(width, 128)
        start = jnp.where(p == 0, x_ref[...].astype(F32) + vec_ref[0, 2:3, :], hidden_ref[...])
        hidden_ref[...] = start + mm(mixed_ref[:, cols], w_o, NT)
        steps_at(p, 1)
        return carry

    hidden_ref[...] = jnp.zeros_like(hidden_ref)
    lax.fori_loop(0, width // 128, one_pair, 0)
    for c in (2, 3):
        for k in range(ts):
            net.core_step(c, k)
    for c in own[2:]:
        c.wait()
    for i, (back, _) in enumerate(parts):

        @pl.when(mt + back < ts)
        def _():
            for h in halo_copies(i):
                h.wait_send()

    net.finish()


def front(x, seg, small, qkvo, fc, proj, dp, ts, halo):
    tokens, width = x.shape
    rows = fc.shape[0]
    window = halo + tokens
    pairs = width // 128
    copies = Gather.copies(dp, ts, 4)
    n_halo = len(halo_parts(tokens, ts))
    any_spec = pl.BlockSpec(memory_space=pl.ANY)
    vmem = pl.BlockSpec(memory_space=pltpu.VMEM)
    big = jax.ShapeDtypeStruct((ts, dp, rows, width), BF16)
    s = jax.ShapeDtypeStruct
    dma = pltpu.SemaphoreType.DMA
    return pl.pallas_call(
        functools.partial(front_kernel, dp, ts),
        out_shape=[
            big,
            big,
            big,
            s((ts, 8, width), F32),
            s((window, 128), BF16),
            s((tokens, 128), BF16),
            s((width, window), BF16),
            s((halo, width), BF16),
            s((tokens, width), BF16),
            s((window, width), BF16),
            s((window, width), BF16),
            s((width, tokens), F32),
            s((pairs, 2, tokens), F32),
            s((tokens, width), BF16),
            s((tokens, width), F32),
        ],
        in_specs=[vmem, vmem] + [any_spec] * 4,
        out_specs=[any_spec] * 3 + [vmem] * 12,
        scratch_shapes=[
            pltpu.VMEM((ts, dp, 8, width), F32),
            pltpu.VMEM((pairs, dp, rows, 512), BF16),
            pltpu.VMEM((ts, dp, rows, 256), BF16),
            pltpu.VMEM((n_halo, 8, tokens), jnp.int32),
            pltpu.VMEM((window, width), BF16),
            pltpu.VMEM((2, window, 128), BF16),
            pltpu.VMEM((128, window), BF16),
            pltpu.VMEM((2, HALO + QB, QB), F32),
            dma((2 * ts + 4,)),
            dma((4, ts, 2)),
            dma((4, ts)),
            dma((copies,)),
            dma((copies,)),
            dma((2 * n_halo,)),
            dma((2 * n_halo,)),
        ],
        compiler_params=pltpu.CompilerParams(
            collective_id=1, has_side_effects=True, vmem_limit_bytes=62 << 20
        ),
        name="front",
    )(x, seg, small, qkvo, fc, proj)


class Scatter:
    def __init__(self, dp, ts, srcs, local, in_core, in_far, in_z, sems):
        self.dp, self.ts, self.srcs, self.local = dp, ts, srcs, local
        self.in_core, self.in_far, self.in_z = in_core, in_far, in_z
        self.core_send, self.core_recv, self.far_send, self.far_recv, self.z_send, self.z_recv = sems
        self.me, self.mt = lax.axis_index("dp"), lax.axis_index("tensor")
        self.far = [1 << k for k in range(1, dp.bit_length() - 1)]
        self.evens = list(range(0, dp, 2))

    def block(self, c, t, to):
        if c < 2:
            return self.srcs[c].at[t, to // 2, lax.rem(to, 2)]
        return self.srcs[c].at[t, to]

    def order(self, t):
        return self.far[::-1] if 2 * t < self.ts else self.far

    def core(self, c, t, m):
        return pltpu.make_async_remote_copy(
            src_ref=self.block(c, t, self.me ^ 1 ^ m),
            dst_ref=self.in_core.at[c, t, m >> 1],
            send_sem=self.core_send.at[c, t, m >> 1],
            recv_sem=self.core_recv.at[c, t, m >> 1],
            device_id={"dp": self.me ^ 1},
            device_id_type=MESH,
        )

    def far_moves(self, t, s):
        order = self.order(t)
        done = sum(order[:s])
        first = sum(len(self.evens) >> (i + 1) for i in range(s))
        masks = [m for m in self.evens if m & order[s] and not m & done]
        return [(m, first + i) for i, m in enumerate(masks)]

    def far_copy(self, c, t, s, m, slot):
        return pltpu.make_async_remote_copy(
            src_ref=self.in_core.at[c, t, m >> 1],
            dst_ref=self.in_far.at[c, t, slot],
            send_sem=self.far_send.at[c, t, slot],
            recv_sem=self.far_recv.at[c, t, slot],
            device_id={"dp": self.me ^ self.order(t)[s]},
            device_id_type=MESH,
        )

    def z_copy(self, c, t):
        back = lax.rem(self.mt + self.ts - t, self.ts) - 1
        return pltpu.make_async_remote_copy(
            src_ref=self.in_core.at[c, t, 0],
            dst_ref=self.in_z.at[c, back],
            send_sem=self.z_send.at[c, t],
            recv_sem=self.z_recv.at[c, back],
            device_id={"tensor": t},
            device_id_type=MESH,
        )

    def start(self, c, t):
        for m in self.evens[::-1]:
            self.core(c, t, m).start()

    def step(self, c, t, s):
        if s == 0:
            for m in self.evens[::-1]:
                self.core(c, t, m).wait_recv()
                to = self.me ^ m
                mine = self.local[c, t, to // 2] if c < 2 else self.srcs[c][t, to]
                self.in_core[c, t, m >> 1] = self.in_core[c, t, m >> 1] + mine
        else:
            bit = self.order(t)[s - 1]
            for m, slot in self.far_moves(t, s - 1):
                self.far_copy(c, t, s - 1, m, slot).wait_recv()
                to = (m ^ bit) >> 1
                self.in_core[c, t, to] = self.in_core[c, t, to] + self.in_far[c, t, slot]
        if s < len(self.far):
            for m, slot in self.far_moves(t, s):
                self.far_copy(c, t, s, m, slot).start()
        else:

            @pl.when(self.mt != t)
            def _():
                self.z_copy(c, t).start()

    def final(self, c, out_ref):
        total = self.in_core[c, self.mt, 0].astype(F32)
        for k in range(self.ts - 1):
            pltpu.make_async_remote_copy(
                src_ref=self.in_core.at[c, 0, 0],
                dst_ref=self.in_z.at[c, k],
                send_sem=self.z_send.at[c, 0],
                recv_sem=self.z_recv.at[c, k],
                device_id={"tensor": self.mt},
                device_id_type=MESH,
            ).wait_recv()
            total = total + self.in_z[c, k].astype(F32)
        out_ref[c] = total

    def finish(self):
        for c in range(len(self.srcs)):
            for t in range(self.ts):
                for m in self.evens:
                    self.core(c, t, m).wait_send()
                for s in range(len(self.far)):
                    for m, slot in self.far_moves(t, s):
                        self.far_copy(c, t, s, m, slot).wait_send()

                @pl.when(self.mt != t)
                def _():
                    self.z_copy(c, t).wait_send()


def norm_back(grad_in, gain_vec, unit_rows, scaler):
    scaled = grad_in * gain_vec
    return scaler * (
        scaled
        - jnp.mean(scaled, axis=-1, keepdims=True)
        - unit_rows * jnp.mean(scaled * unit_rows, axis=-1, keepdims=True)
    )


class Total:
    def __init__(self, dp, ts, mine, dp_in, z_in, sends, recvs):
        self.dp, self.ts, self.mine, self.dp_in, self.z_in = dp, ts, mine, dp_in, z_in
        self.sends, self.recvs = sends, recvs
        self.me, self.mt = lax.axis_index("dp"), lax.axis_index("tensor")

    def over_dp(self, m):
        return pltpu.make_async_remote_copy(
            src_ref=self.mine,
            dst_ref=self.dp_in.at[m],
            send_sem=self.sends.at[m],
            recv_sem=self.recvs.at[m],
            device_id={"dp": self.me ^ m},
            device_id_type=MESH,
        )

    def over_z(self, k):
        return pltpu.make_async_remote_copy(
            src_ref=self.z_in.at[0],
            dst_ref=self.z_in.at[self.ts - k],
            send_sem=self.sends.at[self.dp + k],
            recv_sem=self.recvs.at[self.dp + self.ts - k],
            device_id={"tensor": lax.rem(self.mt + k, self.ts)},
            device_id_type=MESH,
        )

    def start(self):
        for m in range(1, self.dp):
            self.over_dp(m).start()

    def turn(self):
        total = self.mine[...]
        for m in range(1, self.dp):
            self.over_dp(m).wait_recv()
            total = total + self.dp_in[m]
        self.z_in[0] = total
        for k in range(1, self.ts):
            self.over_z(k).start()

    def end(self, out_ref):
        total = self.z_in[0]
        for k in range(1, self.ts):
            self.over_z(k).wait_recv()
            total = total + self.z_in[self.ts - k]
        out_ref[...] = total

    def finish(self):
        for m in range(1, self.dp):
            self.over_dp(m).wait_send()
        for k in range(1, self.ts):
            self.over_z(k).wait_send()


def back_kernel(
    dp,
    ts,
    x_ref,
    halo_ref,
    vec_ref,
    kseg_ref,
    qseg_ref,
    normed_t_ref,
    q_ref,
    k_ref,
    v_ref,
    ot_ref,
    lse_ref,
    mixed_ref,
    grad_hidden_ref,
    small_ref,
    g_proj,
    g_fc,
    qkvo_all,
    input_grad_ref,
    sums_ref,
    small_out,
    late_out,
    w_ref,
    g_qkvo,
    low_ref,
    low_t_ref,
    ka_ref,
    kt_ref,
    dk_ref,
    dv_ref,
    gm_ref,
    delta_ref,
    dqkv_ref,
    dkv_ref,
    give_ref,
    take_ref,
    gh_ref,
    gw_ref,
    g_local,
    small_in,
    small_z,
    late_own,
    late_in,
    late_z,
    in_core,
    in_far,
    in_z,
    local_sem,
    core_send,
    core_recv,
    far_send,
    far_recv,
    z_send,
    z_recv,
    halo_send,
    halo_recv,
    small_send,
    small_recv,
    late_send,
    late_recv,
):
    me, mt = lax.axis_index("dp"), lax.axis_index("tensor")
    tokens, width = x_ref.shape
    halo = halo_ref.shape[0]
    pairs = width // 128
    parts = halo_parts(tokens, ts)
    meet(dp, ts)
    sems = (core_send, core_recv, far_send, far_recv, z_send, z_recv)
    net = Scatter(dp, ts, [g_proj, g_fc, g_qkvo], g_local, in_core, in_far, in_z, sems)
    early = Total(dp, ts, small_ref, small_in, small_z, small_send, small_recv)
    late = Total(dp, ts, late_own, late_in, late_z, late_send, late_recv)
    stages = len(net.far) + 1
    zigzag = [t for pair in zip(range(ts // 2), range(ts // 2, ts)) for t in pair]
    for c in (0, 1):
        for t in zigzag:
            net.start(c, t)
    early.start()
    loads = weight_loads(qkvo_all, w_ref, g_qkvo, local_sem, ts)
    loads += [
        pltpu.make_async_copy(g.at[:, :, lax.rem(me, 2)], g_local.at[c], local_sem.at[2 * ts + c])
        for c, g in enumerate((g_proj, g_fc))
    ]
    for load in loads:
        load.start()

    def low_rows(i, c):
        rows = pl.ds(pl.multiple_of(i * KB, KB), KB)
        low = grad_hidden_ref[rows, :].astype(BF16)
        low_ref[rows, :] = low
        for n in range(pairs):
            low_t_ref[n * KB : (n + 1) * KB, rows] = low[:, n * KB : (n + 1) * KB].T
        return c

    lax.fori_loop(0, tokens // KB, low_rows, 0)
    for load in loads:
        load.wait()
    merge_pairs(w_ref, g_qkvo, ts)
    late_own[...] = jnp.zeros_like(late_own)
    gw_ref[...] = jnp.zeros_like(gw_ref)
    gh_ref[...] = jnp.zeros_like(gh_ref)

    plan = {5: ["turn"], 9: ["end"]}
    units = [(c, t) for c in (0, 1) for t in zigzag]
    for n, (c, t) in enumerate(units):
        for s in range(stages):
            plan.setdefault(2 * n + 1 + 3 * s, []).append((c, t, s))
    plan.setdefault(4 * pairs, []).extend(["final0", "final1"])
    for t in range(ts):
        at = 4 * pairs + pairs - ts + t
        plan.setdefault(at, []).append((2, t, "start"))
        for s in range(stages):
            plan.setdefault(at + 1 + s, []).append((2, t, s))

    def run(items):
        for item in items:
            if item == "turn":
                early.turn()
            elif item == "end":
                early.end(small_out)
            elif item in ("final0", "final1"):
                net.final(int(item[-1]), sums_ref)
            elif item[2] == "start":
                net.start(item[0], item[1])
            else:
                net.step(*item)

    def steps_at(n, place):
        for slot, items in sorted(plan.items()):
            if slot % 4 == place and slot < 4 * pairs:

                @pl.when(n == slot // 4)
                def _():
                    run(items)

    def give(i):
        back, count = parts[i]
        end = halo - sum(c for _, c in parts[:i])
        return pltpu.make_async_remote_copy(
            src_ref=give_ref.at[pl.ds(end - count, count)],
            dst_ref=take_ref.at[pl.ds(end - count, count)],
            send_sem=halo_send.at[i],
            recv_sem=halo_recv.at[i],
            device_id={"tensor": lax.rem(mt + ts - back, ts)},
            device_id_type=MESH,
        )

    def attend_back(n, carry):
        p = lax.rem(n + ts, pairs)
        cols = pl.ds(pl.multiple_of(p * 128, 128), 128)
        w_o = w_ref[p, :, :, 384:512].reshape(width, 128)
        rounded = mm(low_ref[...], w_o).astype(BF16)
        gm_ref[...] = rounded
        weighted = rounded.astype(F32).T * ot_ref[pl.ds(pl.multiple_of(p * 128, 128), 128), :]
        for h in range(2):
            delta_ref[h : h + 1, :] = jnp.sum(weighted[h * HD : (h + 1) * HD], axis=0, keepdims=True)

        def turn(i, c):
            rows = pl.ds(pl.multiple_of(i * KB, KB), KB)
            k, aux = k_ref[rows, cols], kseg_ref[rows, :]
            kt_ref[:, rows] = k.T
            ka_ref[0, rows, :] = lanes_of(k, aux)
            ka_ref[1, rows, :] = lanes_of(aux, k)
            dk_ref[rows, :] = jnp.zeros((KB, 128), F32)
            dv_ref[rows, :] = jnp.zeros((KB, 128), F32)
            return c

        lax.fori_loop(0, (halo + tokens) // KB, turn, 0)
        steps_at(n, 0)

        def one_block(j, c):
            base = j * QB
            at = pl.ds(pl.multiple_of(base, QB), QB)
            q_block, aux, do_block = q_ref[at, cols], qseg_ref[at, :], gm_ref[at, :]
            asks = [lanes_of(q_block, aux), lanes_of(aux, q_block)]
            q_cat = jnp.concatenate([keep_lanes(q_block, h) for h in range(2)], axis=0)
            do_cat = jnp.concatenate([keep_lanes(do_block, h) for h in range(2)], axis=0)
            lse = [lse_ref[p, h : h + 1, at] for h in range(2)]
            delta = [delta_ref[h : h + 1, at] for h in range(2)]
            dq_t = [jnp.zeros((HD, QB), F32) for h in range(2)]
            for row, size in CHUNKS:
                span = pl.ds(pl.multiple_of(base + row, 16), size)
                values = v_ref[span, cols]
                ps, dss = [], []
                for h in range(2):
                    s = causal(mm(ka_ref[h, span, :], asks[h], NT), row)
                    e = jnp.exp2(s - lse[h])
                    grad_e = mm(values, do_cat[h * QB : (h + 1) * QB], NT)
                    ds = (e * (grad_e - delta[h])).astype(BF16)
                    wide = pl.ds(pl.multiple_of(base + row // KB * KB, KB), KB)
                    tall = ds
                    if size < KB:
                        tall = jnp.concatenate([jnp.zeros((KB - size, QB), BF16), ds], axis=0)
                    dq_t[h] = dq_t[h] + mm(kt_ref[h * HD : (h + 1) * HD, wide], tall)
                    ps.append(e.astype(BF16))
                    dss.append(ds)
                dv_ref[span, :] += mm(jnp.concatenate(ps, axis=1), do_cat)
                dk_ref[span, :] += mm(jnp.concatenate(dss, axis=1), q_cat)
            dqkv_ref[n, at, 0:128] = (jnp.concatenate(dq_t, axis=0) * 0.125).T.astype(BF16)
            for place in range(tokens // QB):

                @pl.when(j == place)
                def _():
                    steps_at(n, 1 + place)
            return c

        lax.fori_loop(0, tokens // QB, one_block, 0)

        dkv_ref[n, :, 0:128] = (dk_ref[:halo, :] * (0.125 / Q_SCALE)).astype(BF16)
        dkv_ref[n, :, 128:256] = dv_ref[:halo, :].astype(BF16)
        dqkv_ref[n, :, 128:256] = (dk_ref[halo:, :] * (0.125 / Q_SCALE)).astype(BF16)
        dqkv_ref[n, :, 256:384] = dv_ref[halo:, :].astype(BF16)

        def halo_grad(i, c):
            rows = pl.ds(pl.multiple_of(i * (halo // 2), 16), halo // 2)
            gh_ref[rows, :] += mm(dkv_ref[n, rows, :], w_ref[p, :, :, 128:384].reshape(width, 256), NT)
            return c

        lax.fori_loop(0, 2, halo_grad, 0)
        steps_at(n, 3)
        return carry

    def store(tile, value, t):
        g_qkvo[t, :, :, tile * 128 : (tile + 1) * 128] = value.astype(BF16).reshape(dp, -1, 128)

    def weights_back(n, carry):
        p = lax.rem(n + ts, pairs)
        cols = pl.ds(pl.multiple_of(p * 128, 128), 128)
        grad_o = mm(low_t_ref[...], mixed_ref[:, cols])
        dqkv = dqkv_ref[n]
        own = mm(normed_t_ref[:, halo:], dqkv)
        far = mm(normed_t_ref[:, :halo], dkv_ref[n])
        four = [own[:, 0:128], own[:, 128:256] + far[:, 0:128], own[:, 256:384] + far[:, 128:256], grad_o]

        @pl.when(p < ts)
        def _():
            for i, g in enumerate(four):
                store(i, g, p)

        for a in range(pairs - ts):

            @pl.when(p == ts + a)
            def _():
                for i in range(2):
                    low_half, high_half = four[2 * i], four[2 * i + 1]
                    store(4 + i, lanes_of(low_half, swap_halves(high_half)), 2 * a)
                    store(4 + i, lanes_of(swap_halves(low_half), high_half), 2 * a + 1)

        gw_ref[...] += mm(dqkv, w_ref[p, :, :, 0:384].reshape(width, 384), NT)
        grad_v = jnp.sum(dqkv[:, 256:384].astype(F32), axis=0, keepdims=True)
        late_own[2:3, cols] = jnp.sum(dqkv[:, 0:128].astype(F32), axis=0, keepdims=True)
        late_own[3:4, cols] = grad_v + jnp.sum(dkv_ref[n, :, 128:256].astype(F32), axis=0, keepdims=True)
        for slot, items in sorted(plan.items()):
            if 4 * pairs <= slot < 5 * pairs:

                @pl.when(n == slot - 4 * pairs)
                def _():
                    run(items)
        return carry

    lax.fori_loop(0, pairs, attend_back, 0)
    give_ref[...] = gh_ref[...].astype(BF16)
    for i, (back, _) in enumerate(parts):

        @pl.when(mt >= back)
        def _():
            give(i).start()

    def halo_sums(i, carry):
        rows = pl.ds(pl.multiple_of(i * KB, KB), KB)
        unit, _ = normalize(halo_ref[rows, :].astype(F32))
        g = gh_ref[rows, :]
        return carry[0] + fold_rows(g * unit, jnp.sum), carry[1] + fold_rows(g, jnp.sum)

    def own_sums(i, carry):
        rows = pl.ds(pl.multiple_of(i * KB, KB), KB)
        unit, _ = normalize(x_ref[rows, :].astype(F32))
        g = gw_ref[rows, :]
        return carry[0] + fold_rows(g * unit, jnp.sum), carry[1] + fold_rows(g, jnp.sum)

    zero = jnp.zeros((8, width), F32)
    carry = lax.fori_loop(0, halo // KB, halo_sums, (zero, zero))
    lax.fori_loop(0, pairs, weights_back, 0)
    tail = [items for slot, items in sorted(plan.items()) if slot >= 5 * pairs]
    run(tail[0])
    gains, shifts = lax.fori_loop(0, tokens // KB, own_sums, carry)
    late_own[0:1, :] = jnp.sum(gains, axis=0, keepdims=True)
    late_own[1:2, :] = jnp.sum(shifts, axis=0, keepdims=True)
    late.start()
    for items in tail[1:]:
        run(items)
    late.turn()
    for i, (back, count) in enumerate(parts):

        @pl.when(mt + back < ts)
        def _():
            give(i).wait_recv()
            end = halo - sum(c for _, c in parts[:i])
            gw_ref[tokens - count :, :] += take_ref[end - count : end, :].astype(F32)

    def own_grad(i, carry):
        rows = pl.ds(pl.multiple_of(i * KB, KB), KB)
        unit, scaler = normalize(x_ref[rows, :].astype(F32))
        g = gw_ref[rows, :]
        input_grad_ref[rows, :] = grad_hidden_ref[rows, :] + norm_back(g, vec_ref[0, 0:1, :], unit, scaler)
        return carry

    lax.fori_loop(0, tokens // KB, own_grad, 0)
    late.end(late_out)
    net.final(2, sums_ref)
    early.finish()
    late.finish()
    for i, (back, _) in enumerate(parts):

        @pl.when(mt >= back)
        def _():
            give(i).wait_send()

    net.finish()


def back(x, halo_x, vec, kseg, qseg, normed_t, q, k, v, ot, lse, mixed, grad_hidden, small, g_proj, g_fc, qkvo_all):
    tokens, width = x.shape
    halo = halo_x.shape[0]
    window = halo + tokens
    ts, dp, rows = qkvo_all.shape[:3]
    pairs = width // 128
    n_halo = len(halo_parts(tokens, ts))
    n_far = dp // 2 - 1
    any_spec = pl.BlockSpec(memory_space=pl.ANY)
    vmem = pl.BlockSpec(memory_space=pltpu.VMEM)
    s = jax.ShapeDtypeStruct
    dma = pltpu.SemaphoreType.DMA
    return pl.pallas_call(
        functools.partial(back_kernel, dp, ts),
        out_shape=[s((tokens, width), F32), s((3, rows, width), F32), s(small.shape, F32), s((8, width), F32)],
        in_specs=[vmem] * 14 + [any_spec] * 3,
        out_specs=[vmem] * 4,
        scratch_shapes=[
            pltpu.VMEM((pairs, dp, rows, 512), BF16),
            pltpu.VMEM((ts, dp, rows, width), BF16),
            pltpu.VMEM((tokens, width), BF16),
            pltpu.VMEM((width, tokens), BF16),
            pltpu.VMEM((2, window, 128), BF16),
            pltpu.VMEM((128, window), BF16),
            pltpu.VMEM((window, 128), F32),
            pltpu.VMEM((window, 128), F32),
            pltpu.VMEM((tokens, 128), BF16),
            pltpu.VMEM((8, tokens), F32),
            pltpu.VMEM((pairs, tokens, 384), BF16),
            pltpu.VMEM((pairs, halo, 256), BF16),
            pltpu.VMEM((halo, width), BF16),
            pltpu.VMEM((halo, width), BF16),
            pltpu.VMEM((halo, width), F32),
            pltpu.VMEM((tokens, width), F32),
            pltpu.VMEM((2, ts, dp // 2, rows, width), BF16),
            pltpu.VMEM((dp,) + small.shape, F32),
            pltpu.VMEM((ts,) + small.shape, F32),
            pltpu.VMEM((8, width), F32),
            pltpu.VMEM((dp, 8, width), F32),
            pltpu.VMEM((ts, 8, width), F32),
            pltpu.VMEM((3, ts, dp // 2, rows, width), BF16),
            pltpu.VMEM((3, ts, n_far, rows, width), BF16),
            pltpu.VMEM((3, ts - 1, rows, width), BF16),
            dma((2 * ts + 2,)),
            dma((3, ts, dp // 2)),
            dma((3, ts, dp // 2)),
            dma((3, ts, n_far)),
            dma((3, ts, n_far)),
            dma((3, ts)),
            dma((3, ts - 1)),
            dma((n_halo,)),
            dma((n_halo,)),
            dma((dp + ts,)),
            dma((dp + ts,)),
            dma((dp + ts,)),
            dma((dp + ts,)),
        ],
        compiler_params=pltpu.CompilerParams(
            collective_id=2, has_side_effects=True, vmem_limit_bytes=63 << 20
        ),
        name="back",
    )(x, halo_x, vec, kseg, qseg, normed_t, q, k, v, ot, lse, mixed, grad_hidden, small, g_proj, g_fc, qkvo_all)


def gather_kernel(dp, ts, tokens, n_in, *refs):
    w_refs, (x_ref, seg_ref) = refs[:n_in], refs[n_in : n_in + 2]
    outs = refs[n_in + 2 : 2 * n_in + 2]
    halo_ref, hseg_ref = refs[2 * n_in + 2 : 2 * n_in + 4]
    local_sem, send_sem, recv_sem, halo_send, halo_recv = refs[2 * n_in + 4 :]
    me = lax.axis_index("dp")
    mt = lax.axis_index("tensor")
    bits = [1 << k for k in range(dp.bit_length() - 1)]
    far = bits[1:]
    halo_ref[...] = jnp.zeros_like(halo_ref)
    hseg_ref[...] = jnp.full_like(hseg_ref, -1)
    barrier = pltpu.get_barrier_semaphore()
    peers_t = [lax.rem(mt + k, ts) for k in range(1, ts)]
    for t in peers_t:
        pl.semaphore_signal(barrier, inc=1, device_id={"tensor": t}, device_id_type=MESH)
    for b in bits:
        pl.semaphore_signal(barrier, inc=1, device_id={"dp": me ^ b}, device_id_type=MESH)
    pl.semaphore_wait(barrier, len(peers_t) + len(bits))
    started = []

    def rcopy(src, dst, dev):
        i = len(started)
        c = pltpu.make_async_remote_copy(
            src_ref=src,
            dst_ref=dst,
            send_sem=send_sem.at[i],
            recv_sem=recv_sem.at[i],
            device_id=dev,
            device_id_type=MESH,
        )
        c.start()
        started.append(c)
        return c

    locals_, over_z = [], []
    for c in range(n_in):
        copy = pltpu.make_async_copy(w_refs[c], outs[c].at[mt, me], local_sem.at[c])
        copy.start()
        locals_.append(copy)
        over_z.append([rcopy(w_refs[c], outs[c].at[mt, me], {"tensor": t}) for t in peers_t])
        if c == min(1, n_in - 1):
            end = halo_ref.shape[0]
            halos = []
            for i, (back, count) in enumerate(halo_parts(tokens, ts)):
                end -= count
                pair = [
                    pltpu.make_async_remote_copy(
                        src_ref=src,
                        dst_ref=dst,
                        send_sem=halo_send.at[2 * i + k],
                        recv_sem=halo_recv.at[2 * i + k],
                        device_id={"tensor": lax.rem(mt + back, ts)},
                        device_id_type=MESH,
                    )
                    for k, (src, dst) in enumerate(
                        [
                            (x_ref.at[pl.ds(tokens - count, count)], halo_ref.at[pl.ds(end, count)]),
                            (seg_ref, hseg_ref.at[i]),
                        ]
                    )
                ]
                halos.append((back, pair))

                @pl.when(mt + back < ts)
                def _():
                    for h in pair:
                        h.start()

    half = max(ts // 2, 1)
    groups = [(0, half, far)] + ([(half, ts - half, far[::-1])] if ts > half else [])

    def spread(c, group, masks, later):
        res = {}
        for b in later + [1]:
            res[b] = []
            for m in masks:
                ref = outs[c].at[pl.ds(group[0], group[1]), me ^ m]
                res[b].append((m, rcopy(ref, ref, {"dp": me ^ b})))
        return res

    stages = len(far) + 1
    pending = {}
    for step in range(n_in + stages - 1):
        for s in range(stages):
            c = step - s
            if not 0 <= c < n_in:
                continue
            if s == 0:
                locals_[c].wait()
                for k in over_z[c]:
                    k.wait_recv()
            for gi, group in enumerate(groups):
                if s == 0:
                    pending[c, gi] = [spread(c, group, [0], group[2])]
                else:
                    b = group[2][s - 1]
                    masks = []
                    for res in pending[c, gi]:
                        for m, k in res.get(b, []):
                            k.wait_recv()
                            masks.append(m ^ b)
                    pending[c, gi].append(spread(c, group, masks, group[2][s:]))
    for c in range(n_in):
        for gi in range(len(groups)):
            for res in pending[c, gi]:
                for m, k in res[1]:
                    k.wait_recv()
    for back, pair in halos:

        @pl.when(mt >= back)
        def _():
            for h in pair:
                h.wait_recv()

        @pl.when(mt + back < ts)
        def _():
            for h in pair:
                h.wait_send()

    for k in started:
        k.wait_send()


def gather(parts, x, seg, dp, ts, halo):
    n_in = len(parts)
    tokens = x.shape[0]
    copies = n_in * ((ts - 1) + (2 if ts > 1 else 1) * (dp - 1))
    n_halo = len(halo_parts(tokens, ts))
    any_spec = pl.BlockSpec(memory_space=pl.ANY)
    vmem = pl.BlockSpec(memory_space=pltpu.VMEM)
    return pl.pallas_call(
        functools.partial(gather_kernel, dp, ts, tokens, n_in),
        out_shape=[jax.ShapeDtypeStruct((ts, dp) + p.shape, p.dtype) for p in parts]
        + [
            jax.ShapeDtypeStruct((halo, x.shape[1]), x.dtype),
            jax.ShapeDtypeStruct((n_halo,) + seg.shape, seg.dtype),
        ],
        in_specs=[any_spec] * (n_in + 2),
        out_specs=[any_spec] * n_in + [vmem, vmem],
        scratch_shapes=[
            pltpu.SemaphoreType.DMA((n_in,)),
            pltpu.SemaphoreType.DMA((copies,)),
            pltpu.SemaphoreType.DMA((copies,)),
            pltpu.SemaphoreType.DMA((2 * n_halo,)),
            pltpu.SemaphoreType.DMA((2 * n_halo,)),
        ],
        compiler_params=pltpu.CompilerParams(collective_id=1, has_side_effects=True),
        name="gather",
    )(*parts, x, seg)


def reduce_kernel(dp, ts, g_ref, out_ref, in_core, in_far, in_z, send_sem, recv_sem):
    n_c = g_ref.shape[0]
    me = lax.axis_index("dp")
    mt = lax.axis_index("tensor")
    bits = [1 << k for k in range(dp.bit_length() - 1)]
    far = bits[1:]
    barrier = pltpu.get_barrier_semaphore()
    peers_t = [lax.rem(mt + k, ts) for k in range(1, ts)]
    for t in peers_t:
        pl.semaphore_signal(barrier, inc=1, device_id={"tensor": t}, device_id_type=MESH)
    for b in bits:
        pl.semaphore_signal(barrier, inc=1, device_id={"dp": me ^ b}, device_id_type=MESH)
    pl.semaphore_wait(barrier, len(peers_t) + len(bits))
    started = []

    def rcopy(src, dst, dev):
        i = len(started)
        c = pltpu.make_async_remote_copy(
            src_ref=src,
            dst_ref=dst,
            send_sem=send_sem.at[i],
            recv_sem=recv_sem.at[i],
            device_id=dev,
            device_id_type=MESH,
        )
        c.start()
        started.append(c)
        return c

    half = max(ts // 2, 1)
    groups = [(0, half, far[::-1])] + ([(half, ts - half, far)] if ts > half else [])
    evens = list(range(0, dp, 2))
    core = []
    for c in range(n_c):
        core.append(
            {
                m: rcopy(g_ref.at[c, :, me ^ 1 ^ m], in_core.at[c, m >> 1], {"dp": me ^ 1})
                for m in evens[::-1]
            }
        )

    def add_into(dst, src, base, count):
        def one(i, carry):
            dst[base + i] = (dst[base + i].astype(F32) + src[i].astype(F32)).astype(BF16)
            return carry

        lax.fori_loop(0, count, one, 0)

    stages = len(far) + 2
    pending = {}
    slots = {}
    for step in range(n_c + stages - 1):
        for s in range(stages):
            c = step - s
            if not 0 <= c < n_c:
                continue
            if s == 0:
                for m in evens[::-1]:
                    core[c][m].wait_recv()

                    def one(i, carry, m=m):
                        in_core[c, m >> 1, i] = (
                            in_core[c, m >> 1, i].astype(F32) + g_ref[c, i, me ^ m].astype(F32)
                        ).astype(BF16)
                        return carry

                    lax.fori_loop(0, ts, one, 0)
            for gi, (t0, tn, order) in enumerate(groups):
                if s > 0:
                    for m, slot, k in pending.pop((c, gi)):
                        k.wait_recv()
                        add_into(in_core.at[c, m >> 1], in_far.at[c, slot, pl.ds(t0, tn)], t0, tn)
                if s < len(far):
                    b = order[s]
                    done = sum(order[:s])
                    masks = [m for m in evens if m & b and not m & done]
                    sent = []
                    for m in masks:
                        slot = slots.get((c, gi), 0)
                        slots[c, gi] = slot + 1
                        k = rcopy(
                            in_core.at[c, m >> 1, pl.ds(t0, tn)],
                            in_far.at[c, slot, pl.ds(t0, tn)],
                            {"dp": me ^ b},
                        )
                        sent.append((m ^ b, slot, k))
                    pending[c, gi] = sent
                elif s == len(far):
                    pending[c, gi] = []
            if s == len(far):
                pending[c, "z"] = [
                    rcopy(in_core.at[c, 0, lax.rem(mt + k, ts)], in_z.at[c, k - 1], {"tensor": lax.rem(mt + k, ts)})
                    for k in range(1, ts)
                ]
            if s == len(far) + 1:
                total = in_core[c, 0, mt].astype(F32)
                for k in pending[c, "z"]:
                    k.wait_recv()
                for k in range(ts - 1):
                    total = total + in_z[c, k].astype(F32)
                out_ref[c] = total
    for k in started:
        k.wait_send()


def reduce(grads, dp, ts):
    n_c, _, _, rows, width = grads.shape
    n_far = dp // 2 - 1
    groups = 2 if ts > 1 else 1
    copies = n_c * (dp // 2 + groups * n_far + ts - 1)
    vmem = pl.BlockSpec(memory_space=pltpu.VMEM)
    return pl.pallas_call(
        functools.partial(reduce_kernel, dp, ts),
        out_shape=jax.ShapeDtypeStruct((n_c, rows, width), F32),
        in_specs=[vmem],
        out_specs=vmem,
        scratch_shapes=[
            pltpu.VMEM((n_c, dp // 2, ts, rows, width), BF16),
            pltpu.VMEM((n_c, n_far, ts, rows, width), BF16),
            pltpu.VMEM((n_c, ts - 1, rows, width), BF16),
            pltpu.SemaphoreType.DMA((copies,)),
            pltpu.SemaphoreType.DMA((copies,)),
        ],
        compiler_params=pltpu.CompilerParams(
            collective_id=2, has_side_effects=True, vmem_limit_bytes=62 << 20
        ),
        name="reduce",
    )(grads)


def allowed_at(chunk, doc_row, first_q):
    key = chunk * KB + lax.broadcasted_iota(jnp.int32, (KB, QB), 0)
    query = first_q + lax.broadcasted_iota(jnp.int32, (KB, QB), 1)
    return (key >= doc_row) & (key <= query)


def attend_kernel(halo, first_ref, doc_ref, q_ref, k_ref, vt_ref, o_ref, lse_ref, s_ref):
    for j in range(q_ref.shape[0] // QB):
        rows = pl.ds(j * QB, QB)
        q_block = q_ref[rows, :]
        queries = [keep_lanes(q_block, h) for h in range(2)]
        doc_row = doc_ref[0:1, rows]
        first_q = halo + j * QB
        begin = first_ref[j]
        end = (first_q + QB) // KB

        def score(c, tops):
            keys = k_ref[pl.ds(pl.multiple_of(c * KB, KB), KB), :]
            ok = allowed_at(c, doc_row, first_q)
            res = []
            for h in range(2):
                s = jnp.where(ok, mm(keys, queries[h], NT), -1e30)
                s_ref[h, c] = s
                res.append(jnp.maximum(tops[h], fold_rows(s, jnp.max)))
            return tuple(res)

        tops = lax.fori_loop(begin, end, score, (jnp.full((8, QB), -1e30, F32),) * 2)
        tops = [jnp.max(t, axis=0, keepdims=True) for t in tops]

        def mix(c, carry):
            res = []
            for h in range(2):
                total, acc = carry[h]
                p = jnp.exp(s_ref[h, c] - tops[h])
                total = total + fold_rows(p, jnp.sum)
                vt = vt_ref[pl.ds(h * HD, HD), pl.ds(pl.multiple_of(c * KB, KB), KB)]
                acc = acc + mm(vt, p.astype(BF16))
                res.append((total, acc))
            return tuple(res)

        carry = lax.fori_loop(
            begin, end, mix, ((jnp.zeros((8, QB), F32), jnp.zeros((HD, QB), F32)),) * 2
        )
        for h in range(2):
            total = jnp.sum(carry[h][0], axis=0, keepdims=True)
            o_ref[pl.ds(h * HD, HD), rows] = carry[h][1] / total
            lse_ref[0, h : h + 1, rows] = tops[h] + jnp.log(total)


def attend(first, doc, q, k, vt, halo):
    tokens, width = q.shape
    keys = k.shape[0]
    pairs = width // 128
    return pl.pallas_call(
        functools.partial(attend_kernel, halo),
        out_shape=[
            jax.ShapeDtypeStruct((width, tokens), F32),
            jax.ShapeDtypeStruct((pairs, 2, tokens), F32),
        ],
        grid_spec=pltpu.PrefetchScalarGridSpec(
            num_scalar_prefetch=1,
            grid=(pairs,),
            in_specs=[
                pl.BlockSpec((1, tokens), lambda p, f: (0, 0)),
                pl.BlockSpec((tokens, 128), lambda p, f: (0, p)),
                pl.BlockSpec((keys, 128), lambda p, f: (0, p)),
                pl.BlockSpec((128, keys), lambda p, f: (p, 0)),
            ],
            out_specs=[
                pl.BlockSpec((128, tokens), lambda p, f: (p, 0)),
                pl.BlockSpec((1, 2, tokens), lambda p, f: (p, 0, 0)),
            ],
            scratch_shapes=[pltpu.VMEM((2, keys // KB, KB, QB), F32)],
        ),
        name="attend",
    )(first, doc, q, k, vt)


def attend_back_kernel(
    halo, first_ref, doc_ref, q_ref, k_ref, kt_ref, v_ref, do_ref, lse_ref, delta_ref, dq_ref, dk_ref, dv_ref
):
    dk_ref[...] = jnp.zeros_like(dk_ref)
    dv_ref[...] = jnp.zeros_like(dv_ref)
    for j in range(q_ref.shape[0] // QB):
        rows = pl.ds(j * QB, QB)
        q_block, do_block = q_ref[rows, :], do_ref[rows, :]
        queries = [keep_lanes(q_block, h) for h in range(2)]
        grads = [keep_lanes(do_block, h) for h in range(2)]
        doc_row = doc_ref[0:1, rows]
        first_q = halo + j * QB

        def step(c, carry):
            span = pl.ds(pl.multiple_of(c * KB, KB), KB)
            keys, values = k_ref[span, :], v_ref[span, :]
            ok = allowed_at(c, doc_row, first_q)
            res = []
            grad_k = grad_v = None
            for h in range(2):
                s = jnp.where(ok, mm(keys, queries[h], NT), -1e30)
                p = jnp.exp(s - lse_ref[0, h : h + 1, rows])
                dp_ = mm(values, grads[h], NT)
                ds = (p * (dp_ - delta_ref[0, h : h + 1, rows])).astype(BF16)
                gv = mm(p.astype(BF16), grads[h])
                gk = mm(ds, queries[h])
                grad_v = gv if grad_v is None else grad_v + gv
                grad_k = gk if grad_k is None else grad_k + gk
                kt = kt_ref[pl.ds(h * HD, HD), span]
                res.append(carry[h] + mm(kt, ds))
            dk_ref[span, :] += grad_k
            dv_ref[span, :] += grad_v
            return tuple(res)

        carry = lax.fori_loop(
            first_ref[j], (first_q + QB) // KB, step, (jnp.zeros((HD, QB), F32),) * 2
        )
        for h in range(2):
            dq_ref[pl.ds(h * HD, HD), rows] = carry[h] * 0.125


def attend_back(first, doc, q, k, kt, v, do, lse, delta, halo):
    tokens, width = q.shape
    keys = k.shape[0]
    pairs = width // 128
    q_spec = pl.BlockSpec((tokens, 128), lambda p, f: (0, p))
    k_spec = pl.BlockSpec((keys, 128), lambda p, f: (0, p))
    stat = pl.BlockSpec((1, 2, tokens), lambda p, f: (p, 0, 0))
    return pl.pallas_call(
        functools.partial(attend_back_kernel, halo),
        out_shape=[
            jax.ShapeDtypeStruct((width, tokens), F32),
            jax.ShapeDtypeStruct((keys, width), F32),
            jax.ShapeDtypeStruct((keys, width), F32),
        ],
        grid_spec=pltpu.PrefetchScalarGridSpec(
            num_scalar_prefetch=1,
            grid=(pairs,),
            in_specs=[
                pl.BlockSpec((1, tokens), lambda p, f: (0, 0)),
                q_spec,
                k_spec,
                pl.BlockSpec((128, keys), lambda p, f: (p, 0)),
                k_spec,
                q_spec,
                stat,
                stat,
            ],
            out_specs=[pl.BlockSpec((128, tokens), lambda p, f: (p, 0)), k_spec, k_spec],
        ),
        name="attend_back",
    )(first, doc, q, k, kt, v, do, lse, delta)


def gelu_tanh(values_in):
    return (
        0.5
        * values_in
        * (
            1.0
            + jnp.tanh(TANH_SLOPE * (values_in + CUBIC_TERM * values_in * values_in * values_in))
        )
    )


def plain_device(
    block_input,
    teacher,
    segment_ids,
    valid_mask,
    ln1_gain,
    ln1_bias,
    qkv_weight,
    qv_bias,
    out_weight,
    out_bias,
    ln2_gain,
    ln2_bias,
    fc_weight,
    fc_bias,
    proj_weight,
    proj_bias,
):
    dp, ts = lax.axis_size("dp"), lax.axis_size("tensor")
    me, mt = lax.axis_index("dp"), lax.axis_index("tensor")
    tokens, width = block_input.shape[1:]
    total_tokens = tokens * ts * dp
    halo = -(-(DOC_MOST - 1) // KB) * KB
    e = qkv_weight.shape[2]
    x = block_input[0]
    valid_rows = valid_mask[0].astype(F32)

    qkvo = jnp.concatenate([qkv_weight[0], qkv_weight[1], qkv_weight[2], out_weight.T], axis=1)
    local_count = jnp.sum(valid_mask[0])
    mine = jnp.arange(dp) == me

    def spread(v):
        return jnp.where(mine[:, None], v[..., None, :], jnp.zeros((), v.dtype))

    vectors = jnp.stack([ln1_gain, ln1_bias, out_bias, ln2_gain, ln2_bias, proj_bias])
    tail = jnp.stack([local_count // 16, local_count % 16]).astype(BF16)
    small = jnp.concatenate(
        [
            spread(vectors).reshape(6, width),
            spread(fc_bias).reshape(1, -1),
            jnp.concatenate(
                [spread(qv_bias).reshape(-1), tail, jnp.zeros((width - 2 * e - 2,), BF16)]
            )[None],
        ]
    )
    seg_rows = jnp.broadcast_to(segment_ids, (8, tokens))
    small_all, w_qkvo, w_fc, w_proj, x_halo, seg_halo = gather(
        [small, qkvo, fc_weight, proj_weight.T], x, seg_rows, dp, ts, halo
    )
    small_all = jnp.sum(small_all.astype(F32), axis=1)
    gain_one, bias_one, b_out, gain_two, bias_two, b_proj = [small_all[0, i] for i in range(6)]
    b_fc = small_all[:, 6].reshape(-1)
    b_q = small_all[:, 7, :e].reshape(-1)
    b_v = small_all[:, 7, e : 2 * e].reshape(-1)
    valid_count = jnp.sum(small_all[:, 7, 2 * e] * 16 + small_all[:, 7, 2 * e + 1])
    w_qkvo = w_qkvo.reshape(ts, width, 4, e)
    wq, wk, wv, wo = [w_qkvo[:, :, i].transpose(1, 0, 2).reshape(width, width) for i in range(4)]
    wf = w_fc.reshape(ts, width, -1)
    wp = w_proj.reshape(ts, width, -1)

    seg = segment_ids[0]
    pieces = []
    for i, (back, count) in enumerate(halo_parts(tokens, ts)):
        pieces.insert(0, seg_halo[i, 0, tokens - count :])
    filled = sum(p.shape[0] for p in pieces)
    seg_window = jnp.concatenate([jnp.full((halo - filled,), -1, jnp.int32)] + pieces)
    position = jnp.sum((seg_window[:, None] < seg[None, :]).astype(jnp.int32), axis=0)
    own = jnp.sum((seg[:, None] < seg[None, :]).astype(jnp.int32), axis=0)
    doc = (position + own)[None]
    first = doc[0, ::QB] // KB

    inputs = x.astype(F32)
    window = jnp.concatenate([x_halo, x]).astype(F32)
    unit_window, scale_window = normalize(window)
    normed_window = (unit_window * gain_one + bias_one).astype(BF16)
    unit_one, scale_one = unit_window[halo:], scale_window[halo:]
    normed_one = normed_window[halo:]
    q = ((mm(normed_one, wq) + b_q).astype(BF16) * 0.125).astype(BF16)
    k = mm(normed_window, wk).astype(BF16)
    v = (mm(normed_window, wv) + b_v).astype(BF16)
    mixed_t, lse = attend(first, doc, q, k, v.T, halo)
    mixed = mixed_t.T.astype(BF16)
    hidden = inputs + mm(mixed, wo, NT) + b_out
    unit_two, scale_two = normalize(hidden)
    normed_two = (unit_two * gain_two + bias_two).astype(BF16)
    pre_act = jnp.einsum("sd,tdf->stf", normed_two, wf, preferred_element_type=F32) + b_fc.reshape(ts, -1)
    activated = gelu_tanh(pre_act).astype(BF16)
    output = hidden + jnp.einsum("stf,tdf->sd", activated, wp, preferred_element_type=F32) + b_proj
    residual_error = output - teacher[0].astype(F32)
    squares = jnp.sum(valid_rows[:, None] * residual_error * residual_error)
    grad_output = valid_rows[:, None] * residual_error * (total_tokens / valid_count)
    low_output = grad_output.astype(BF16)
    grad_act = jnp.einsum("sd,tdf->stf", low_output, wp, preferred_element_type=F32)
    grad_proj_w = jnp.einsum("sd,stf->tdf", low_output, activated, preferred_element_type=F32)
    _, gelu_back = jax.vjp(gelu_tanh, pre_act)
    grad_pre = gelu_back(grad_act)[0].astype(BF16)
    grad_fc_w = jnp.einsum("sd,stf->tdf", normed_two, grad_pre, preferred_element_type=F32)
    grad_fc_b = jnp.sum(grad_pre, axis=0, dtype=F32)
    grad_normed_two = jnp.einsum("stf,tdf->sd", grad_pre, wf, preferred_element_type=F32)
    grad_gain_two = jnp.sum(grad_normed_two * unit_two, axis=0)
    grad_bias_two = jnp.sum(grad_normed_two, axis=0)
    grad_hidden = grad_output + norm_back(grad_normed_two, gain_two, unit_two, scale_two)
    low_hidden = grad_hidden.astype(BF16)
    grad_mixed = mm(low_hidden, wo).astype(BF16)
    grad_out_w = jnp.einsum("sd,se->de", low_hidden, mixed, preferred_element_type=F32)
    heads = width // HD
    delta = jnp.sum((grad_mixed.T.astype(F32) * mixed_t).reshape(heads // 2, 2, HD, tokens), axis=2)
    dq_t, dk, dv = attend_back(first, doc, q, k, k.T, v, grad_mixed, lse, delta, halo)
    dq, dk, dv = dq_t.T.astype(BF16), dk.astype(BF16), dv.astype(BF16)
    sd_se = lambda a, b: jnp.einsum("sd,se->de", a, b, preferred_element_type=F32)
    g_q, g_k, g_v = sd_se(normed_one, dq), sd_se(normed_window, dk), sd_se(normed_window, dv)
    grad_window = mm(dk, wk, NT) + mm(dv, wv, NT)
    grad_normed_one = grad_window[halo:] + mm(dq, wq, NT)
    end = halo
    for back, count in halo_parts(tokens, ts):
        end -= count
        part = lax.ppermute(
            grad_window[end : end + count].astype(BF16), "tensor", [(t, t - back) for t in range(back, ts)]
        )
        grad_normed_one = grad_normed_one.at[tokens - count :].add(part.astype(F32))
    grad_input = grad_hidden + norm_back(grad_normed_one, gain_one, unit_one, scale_one)

    def by_t(g):
        return g.reshape(width, ts, e)

    g_qkvo = jnp.stack([by_t(g_q), by_t(g_k), by_t(g_v), by_t(grad_out_w)], axis=2)
    g_qkvo = g_qkvo.transpose(1, 0, 2, 3).reshape(ts, width, 4 * e)
    grads = jnp.stack([grad_proj_w, grad_fc_w, g_qkvo]).astype(BF16)
    grads = grads.reshape(3, ts, dp, width // dp, -1)
    r_proj, r_fc, r_qkvo = reduce(grads, dp, ts)
    smalls = [
        jnp.sum(grad_normed_one * unit_one, axis=0),
        jnp.sum(grad_normed_one, axis=0),
        jnp.sum(grad_hidden, axis=0),
        grad_gain_two,
        grad_bias_two,
        jnp.sum(grad_output, axis=0),
        grad_fc_b.reshape(-1),
        jnp.sum(dq, axis=0, dtype=F32),
        jnp.sum(dv, axis=0, dtype=F32),
        squares[None],
    ]
    summed = lax.psum(jnp.concatenate(smalls), ("dp", "tensor"))
    rows = width // dp
    own_rows = lambda i: lax.dynamic_slice_in_dim(summed, i * width + me * rows, rows)
    fc_b = summed[6 * width : 6 * width + fc_bias.size * dp * ts].reshape(ts, -1, dp, fc_bias.shape[1])
    qv0 = 6 * width + fc_bias.size * dp * ts
    qv_b = summed[qv0 : qv0 + 2 * width].reshape(2, ts, -1, dp, qv_bias.shape[2])
    loss = summed[-1] / (width * valid_count)
    pick = lambda a, i, ax: lax.dynamic_index_in_dim(a, i, ax, keepdims=False)
    return (
        output.astype(BF16)[None],
        loss,
        grad_input[None],
        own_rows(0),
        own_rows(1),
        jnp.stack([r_qkvo[:, i * e : (i + 1) * e] for i in range(3)]),
        pick(pick(qv_b, mt, 1), me, 2),
        r_qkvo[:, 3 * e :].T,
        own_rows(2),
        own_rows(3),
        own_rows(4),
        r_fc,
        pick(pick(fc_b, mt, 0), me, 1),
        r_proj.T,
        own_rows(5),
    )


def on_device(
    block_input,
    teacher,
    segment_ids,
    valid_mask,
    ln1_gain,
    ln1_bias,
    qkv_weight,
    qv_bias,
    out_weight,
    out_bias,
    ln2_gain,
    ln2_bias,
    fc_weight,
    fc_bias,
    proj_weight,
    proj_bias,
):
    dp, ts = lax.axis_size("dp"), lax.axis_size("tensor")
    me, mt = lax.axis_index("dp"), lax.axis_index("tensor")
    tokens, width = block_input.shape[1:]
    total_tokens = tokens * ts * dp
    e = qkv_weight.shape[2]
    x = block_input[0]
    valid_rows = valid_mask[0].astype(F32)

    cuts = [qkv_weight[0], qkv_weight[1], qkv_weight[2], out_weight.T]
    qkvo = jnp.concatenate([c[:, : 2 * HD] for c in cuts] + [c[:, 2 * HD :] for c in cuts], axis=1)
    mine = jnp.arange(dp) == me

    def spread(v):
        return jnp.where(mine[:, None], v[..., None, :], jnp.zeros((), v.dtype)).astype(F32)

    vectors = jnp.stack([ln1_gain, ln1_bias, out_bias, ln2_gain, ln2_bias, proj_bias])
    qv = spread(qv_bias).reshape(2, e)
    small = jnp.concatenate(
        [
            spread(vectors).reshape(6, width),
            spread(fc_bias).reshape(1, -1),
            jnp.concatenate(
                [qv[0, : 2 * HD], qv[1, : 2 * HD], qv[0, 2 * HD :], qv[1, 2 * HD :], jnp.sum(valid_rows)[None]]
                + [jnp.zeros((width - 2 * e - 1,), F32)]
            )[None],
        ]
    )
    seg_rows = jnp.broadcast_to(segment_ids, (8, tokens))
    qkvo_all, w_fc, w_proj, vec, kseg, qseg, normed_t, halo_x, q, k, v, ot, lse, mixed, hidden = front(
        x, seg_rows, small, qkvo, fc_weight, proj_weight.T, dp, ts, HALO
    )
    gain_two, bias_two, b_proj = [vec[0, i] for i in (3, 4, 5)]
    b_fc = vec[:, 6]
    valid_count = jnp.sum(vec[:, 7, 2 * e])
    wf = w_fc.reshape(ts, width, -1)
    wp = w_proj.reshape(ts, width, -1)

    unit_two, scale_two = normalize(hidden)
    normed_two = (unit_two * gain_two + bias_two).astype(BF16)
    pre_act = jnp.einsum("sd,tdf->stf", normed_two, wf, preferred_element_type=F32) + b_fc
    activated = gelu_tanh(pre_act).astype(BF16)
    output = hidden + jnp.einsum("stf,tdf->sd", activated, wp, preferred_element_type=F32) + b_proj
    residual_error = output - teacher[0].astype(F32)
    squares = jnp.sum(valid_rows[:, None] * residual_error * residual_error)
    grad_output = valid_rows[:, None] * residual_error * (total_tokens / valid_count)
    low_output = grad_output.astype(BF16)
    grad_act = jnp.einsum("sd,tdf->stf", low_output, wp, preferred_element_type=F32)
    grad_proj_w = jnp.einsum("sd,stf->tdf", low_output, activated, preferred_element_type=F32)
    _, gelu_back = jax.vjp(gelu_tanh, pre_act)
    grad_pre = gelu_back(grad_act)[0].astype(BF16)
    grad_fc_w = jnp.einsum("sd,stf->tdf", normed_two, grad_pre, preferred_element_type=F32)
    grad_normed_two = jnp.einsum("stf,tdf->sd", grad_pre, wf, preferred_element_type=F32)
    grad_hidden = grad_output + norm_back(grad_normed_two, gain_two, unit_two, scale_two)
    small_grads = jnp.concatenate(
        [
            jnp.sum(grad_hidden, axis=0)[None],
            jnp.sum(grad_normed_two * unit_two, axis=0)[None],
            jnp.sum(grad_normed_two, axis=0)[None],
            jnp.sum(grad_output, axis=0)[None],
            jnp.sum(grad_pre, axis=0, dtype=F32),
            jnp.full((1, width), squares),
            jnp.zeros((-(5 + ts) % 8, width), F32),
        ]
    )
    blocks = lambda g: g.astype(BF16).reshape(ts, dp // 2, 2, width // dp, width)
    input_grad, sums, small_sums, late_sums = back(
        x, halo_x, vec, kseg, qseg, normed_t, q, k, v, ot, lse, mixed, grad_hidden, small_grads,
        blocks(grad_proj_w), blocks(grad_fc_w), qkvo_all,
    )
    r_proj, r_fc, r_qkvo = sums
    own = lambda a: lax.dynamic_slice_in_dim(a, me * (width // dp), width // dp, 1)
    own_late, own_small = own(late_sums), own(small_sums)
    fc_b = small_sums[4 : 4 + ts].reshape(ts, -1, dp, fc_bias.shape[1])
    fc_b = lax.dynamic_index_in_dim(lax.dynamic_index_in_dim(fc_b, mt, 0, False), me, 1, False)

    def by_head(v):
        low = lax.dynamic_slice_in_dim(v, mt * 2 * HD, 2 * HD, 1)
        last = lax.dynamic_slice_in_dim(v, ts * 2 * HD + mt * HD, HD, 1)
        v = jnp.concatenate([low, last], axis=1).reshape(2, -1, dp, qv_bias.shape[2])
        return lax.dynamic_index_in_dim(v, me, 2, False)

    def columns(i):
        return jnp.concatenate(
            [r_qkvo[:, i * 128 : (i + 1) * 128], r_qkvo[:, 512 + i * HD : 512 + (i + 1) * HD]], axis=1
        )

    return (
        output.astype(BF16)[None],
        small_sums[4 + ts, 0] / (width * valid_count),
        input_grad[None],
        own_late[0],
        own_late[1],
        jnp.stack([columns(i) for i in range(3)]),
        by_head(late_sums[2:4]),
        columns(3).T,
        own_small[0],
        own_small[1],
        own_small[2],
        r_fc,
        fc_b,
        r_proj.T,
        own_small[3],
    )


def solution(mesh):
    placed = (
        P("dp", "tensor", None),
        P("dp", "tensor", None),
        P("dp", "tensor"),
        P("dp", "tensor"),
        P("dp"),
        P("dp"),
        P(None, "dp", "tensor"),
        P(None, "tensor", "dp"),
        P("tensor", "dp"),
        P("dp"),
        P("dp"),
        P("dp"),
        P("dp", "tensor"),
        P("tensor", "dp"),
        P("tensor", "dp"),
        P("dp"),
    )
    def fits(qkv_weight, block_input):
        rows = block_input.shape[2] // mesh.shape["dp"]
        wide = qkv_weight.shape[2] // mesh.shape["tensor"]
        return rows % 16 == 0 and wide == 3 * HD and mesh.shape["tensor"] % 2 == 0

    def step(*args):
        return placed_step(on_device if fits(args[6], args[0]) else plain_device)(*args)

    placed_step = lambda body: jax.shard_map(
        body,
        mesh=mesh,
        in_specs=placed,
        out_specs=(
            P("dp", "tensor", None),
            P(),
            P("dp", "tensor", None),
            P("dp"),
            P("dp"),
            P(None, "dp", "tensor"),
            P(None, "tensor", "dp"),
            P("tensor", "dp"),
            P("dp"),
            P("dp"),
            P("dp"),
            P("dp", "tensor"),
            P("tensor", "dp"),
            P("tensor", "dp"),
            P("dp"),
        ),
        check_vma=False,
    )
    return step
```

```python
import functools

import jax
import jax.numpy as jnp
from jax import lax
from jax.experimental import pallas as pl
from jax.experimental.pallas import tpu as pltpu
from jax.sharding import PartitionSpec as P

HD = 64
DOC_MOST = 800
KB = 128
QB = 256
DOCS = 8
HALO = -(-(DOC_MOST - 1) // KB) * KB
LEAD = (HALO - DOC_MOST + 1) // 32 * 32
CHUNKS = ([(LEAD, KB - LEAD)] if LEAD else [(0, KB)]) + [(r, KB) for r in range(KB, HALO + QB, KB)]
Q_SCALE = 0.125 * 1.4426950408889634
EPSILON = 1e-05
LAG = 2
TANH_SLOPE = 0.7978845608028654
CUBIC_TERM = 0.044715
MESH = pl.DeviceIdType.MESH
F32 = jnp.float32
BF16 = jnp.bfloat16
NN = (((1,), (0,)), ((), ()))
NT = (((1,), (1,)), ((), ()))


def mm(a, b, dims=NN):
    return lax.dot_general(a, b, dims, preferred_element_type=F32)


def halo_parts(tokens, ts):
    parts, left, back = [], DOC_MOST, 1
    while left > 0 and back < ts:
        parts.append((back, min(tokens, left)))
        left -= tokens
        back += 1
    return parts


class Gather:
    def __init__(self, dp, ts, ins, outs, z_send, z_recv, send_sem, recv_sem):
        self.dp, self.ts, self.ins, self.outs = dp, ts, ins, outs
        self.z_send, self.z_recv, self.send_sem, self.recv_sem = z_send, z_recv, send_sem, recv_sem
        self.me, self.mt = lax.axis_index("dp"), lax.axis_index("tensor")
        self.far = [1 << k for k in range(1, dp.bit_length() - 1)]
        self.keys = {}
        self.flight = []
        self.near = [sorted(range(ts), key=lambda t: (abs(t - m), t)) for m in range(ts)]

    @staticmethod
    def copies(dp, ts, parts):
        return parts * ts * (dp - 1)

    def t_of(self, k):
        t = jnp.int32(self.near[0][k])
        for m in range(1, self.ts):
            t = jnp.where(self.mt == m, self.near[m][k], t)
        return t

    def order(self, t):
        flip = t * 2 >= self.ts
        return [jnp.where(flip, b, a) for a, b in zip(self.far, self.far[::-1])]

    def place(self, c, t, dp_index):
        return self.outs[c].at[t, dp_index]

    def along(self, c, t, up):
        src = self.ins[c] if t is None else self.place(c, t, self.me)
        t = self.mt if t is None else t
        return pltpu.make_async_remote_copy(
            src_ref=src,
            dst_ref=self.place(c, t, self.me),
            send_sem=self.z_send.at[c, t, int(up)],
            recv_sem=self.z_recv.at[c, t],
            device_id={"tensor": self.mt + (1 if up else -1)},
            device_id_type=MESH,
        )

    def desc(self, key):
        c, k, known, i = key
        t = self.t_of(k)
        order = self.order(t)
        mask = jnp.int32(0)
        for b in known:
            mask = mask ^ order[b]
        ref = self.place(c, t, self.me ^ mask)
        own = k == 0 and not known
        n = self.keys.setdefault(key, len(self.keys))
        return pltpu.make_async_remote_copy(
            src_ref=self.ins[c] if own else ref,
            dst_ref=ref,
            send_sem=self.send_sem.at[n],
            recv_sem=self.recv_sem.at[n],
            device_id={"dp": self.me ^ (1 if i < 0 else order[i])},
            device_id_type=MESH,
        )

    def here(self, c, k, known):
        first = max(known) + 1 if known else 0
        for i in list(range(first, len(self.far))) + [-1]:
            key = (c, k, known, i)
            self.desc(key).start()
            self.flight.append(key)

    def start(self, c):
        @pl.when(self.mt + 1 < self.ts)
        def _():
            self.along(c, None, True).start()

        @pl.when(self.mt >= 1)
        def _():
            self.along(c, None, False).start()

        self.here(c, 0, ())

    def z_step(self, c, k):
        t = self.t_of(k)
        self.along(c, t, True).wait_recv()

        @pl.when((t < self.mt) & (self.mt + 1 < self.ts))
        def _():
            self.along(c, t, True).start()

        @pl.when((t > self.mt) & (self.mt >= 1))
        def _():
            self.along(c, t, False).start()

        self.here(c, k, ())

    def far_step(self, c, k, i):
        for key in [q for q in self.flight if q[:2] == (c, k) and q[3] == i]:
            self.desc(key).wait_recv()
            self.here(c, k, key[2] + (i,))

    def core_step(self, c, k):
        for key in [q for q in self.flight if q[:2] == (c, k) and q[3] < 0]:
            self.desc(key).wait_recv()

    def finish(self):
        for c in range(len(self.ins)):
            for k in range(self.ts):
                t = self.t_of(k)

                @pl.when((t <= self.mt) & (self.mt + 1 < self.ts))
                def _():
                    self.along(c, t, True).wait_send()

                @pl.when((t >= self.mt) & (self.mt >= 1))
                def _():
                    self.along(c, t, False).wait_send()

        for key in self.flight:
            self.desc(key).wait_send()


def meet(dp, ts):
    me, mt = lax.axis_index("dp"), lax.axis_index("tensor")
    barrier = pltpu.get_barrier_semaphore()
    for k in range(1, ts):
        pl.semaphore_signal(barrier, inc=1, device_id={"tensor": lax.rem(mt + k, ts)}, device_id_type=MESH)
    for b in range(1, dp):
        pl.semaphore_signal(barrier, inc=1, device_id={"dp": me ^ b}, device_id_type=MESH)
    pl.semaphore_wait(barrier, ts - 1 + dp - 1)


def keep_lanes(block, head):
    lanes = lax.broadcasted_iota(jnp.int32, block.shape, 1)
    return jnp.where((lanes < HD) == (head == 0), block, jnp.zeros_like(block))


def fold_rows(block, op):
    return op(block.reshape(block.shape[0] // 8, 8, block.shape[1]), axis=0)


def swap_halves(block):
    return jnp.concatenate([block[:, HD:], block[:, :HD]], axis=1)


def lanes_of(low, high):
    lanes = lax.broadcasted_iota(jnp.int32, low.shape, 1)
    return jnp.where(lanes < HD, low, high)


def causal(s, row):
    ahead = row - HALO
    if ahead < 0:
        return s
    key = lax.broadcasted_iota(jnp.int32, s.shape, 0)
    query = lax.broadcasted_iota(jnp.int32, s.shape, 1)
    return jnp.where(key + ahead <= query, s, -1e30)


def segment_lanes(seg_row, same):
    shape = (128, seg_row.shape[1])
    value = lax.rem(lax.broadcasted_iota(jnp.int32, shape, 0), HD)
    hit = (seg_row == value) if same else (seg_row != value)
    level = -1e30 if same else 1.0
    return jnp.where(hit & (value < DOCS), level, 0.0).T.astype(BF16)


def normalize(values_in):
    center = values_in - jnp.mean(values_in, axis=-1, keepdims=True)
    scaler = lax.rsqrt(jnp.mean(center * center, axis=-1, keepdims=True) + EPSILON)
    return (center * scaler, scaler)


def merge_pairs(w_ref, h2_ref, ts):
    for a in range(ts // 2):
        tiles = []
        for t in (2 * a, 2 * a + 1):
            block = h2_ref[t, :, :, 0:256].reshape(-1, 256)
            tiles.append((block[:, :128], block[:, 128:]))
        (qk0, vo0), (qk1, vo1) = tiles
        merged = [
            lanes_of(qk0, swap_halves(qk1)),
            lanes_of(swap_halves(qk0), qk1),
            lanes_of(vo0, swap_halves(vo1)),
            lanes_of(swap_halves(vo0), vo1),
        ]
        for i, m in enumerate(merged):
            w_ref[ts + a, :, :, i * 128 : (i + 1) * 128] = m.reshape(w_ref.shape[1], w_ref.shape[2], 128)


def weight_loads(qkvo_all, w_ref, h2_ref, sem, ts):
    res = []
    for t in range(ts):
        res.append(pltpu.make_async_copy(qkvo_all.at[t, :, :, pl.ds(0, 512)], w_ref.at[t], sem.at[2 * t]))
        res.append(pltpu.make_async_copy(qkvo_all.at[t, :, :, pl.ds(512, 256)], h2_ref.at[t, :, :, pl.ds(0, 256)], sem.at[2 * t + 1]))
    return res


def front_kernel(
    dp,
    ts,
    x_ref,
    seg_ref,
    small_ref,
    qkvo_ref,
    fc_ref,
    proj_ref,
    qkvo_all,
    fc_all,
    proj_all,
    vec_ref,
    kseg_ref,
    qseg_ref,
    normed_t_ref,
    halo_ref,
    q_ref,
    k_ref,
    v_ref,
    ot_ref,
    lse_ref,
    mixed_ref,
    hidden_ref,
    small_all,
    w_ref,
    h2_ref,
    hseg_ref,
    normed_ref,
    ka_ref,
    vt_ref,
    s_ref,
    local_sem,
    z_send,
    z_recv,
    send_sem,
    recv_sem,
    halo_send,
    halo_recv,
):
    me, mt = lax.axis_index("dp"), lax.axis_index("tensor")
    tokens, width = x_ref.shape
    halo = halo_ref.shape[0]
    ins = [small_ref, qkvo_ref, fc_ref, proj_ref]
    outs = [small_all, qkvo_all, fc_all, proj_all]
    halo_ref[...] = jnp.zeros_like(halo_ref)
    hseg_ref[...] = jnp.full_like(hseg_ref, -1)
    meet(dp, ts)
    net = Gather(dp, ts, ins, outs, z_send, z_recv, send_sem, recv_sem)
    stages = len(net.far)
    parts = halo_parts(tokens, ts)

    far = parts[1][1]
    near_at, cut = halo - tokens, tokens - far

    def hop(src, dst, n, back):
        return pltpu.make_async_remote_copy(
            src_ref=src,
            dst_ref=dst,
            send_sem=halo_send.at[n],
            recv_sem=halo_recv.at[n],
            device_id={"tensor": lax.rem(mt + back, ts)},
            device_id_type=MESH,
        )

    late_rows = hop(x_ref.at[pl.ds(cut, far)], halo_ref.at[pl.ds(near_at + cut, far)], 0, 1)
    early_rows = hop(x_ref.at[pl.ds(0, cut)], halo_ref.at[pl.ds(near_at, cut)], 1, 1)
    passed_rows = hop(halo_ref.at[pl.ds(near_at + cut, far)], halo_ref.at[pl.ds(near_at - far, far)], 2, 1)
    segs = [hop(seg_ref, hseg_ref.at[i], 3 + i, back) for i, (back, _) in enumerate(parts)]

    own = [
        pltpu.make_async_copy(ins[c], outs[c].at[mt, me], local_sem.at[2 * ts + c]) for c in range(4)
    ]
    net.start(0)
    net.start(1)
    for c in own:
        c.start()
    for k in range(1, ts):
        net.z_step(0, k)
    for k in range(1, ts - 1):
        net.z_step(1, k)
    for i, (back, _) in enumerate(parts):

        @pl.when(mt + back < ts)
        def _():
            segs[i].start()

    @pl.when(mt + 1 < ts)
    def _():
        late_rows.start()
        early_rows.start()

    net.z_step(1, ts - 1)
    for i in range(stages):
        for k in range(ts):
            net.far_step(0, k, i)
    for k in range(ts):
        net.far_step(1, k, 0)

    @pl.when(mt >= 1)
    def _():
        late_rows.wait_recv()

    @pl.when((mt >= 1) & (mt + 1 < ts))
    def _():
        passed_rows.start()

    net.start(2)
    net.start(3)
    own[0].wait()
    for k in range(ts):
        net.core_step(0, k)
    for t in range(ts):
        vec_ref[t] = jnp.sum(small_all[t], axis=0)

    def norm_rows(src, i, at):
        unit, _ = normalize(src[pl.ds(i * KB, KB), :].astype(F32))
        rows = pl.ds(pl.multiple_of(at + i * KB, KB), KB)
        normed = (unit * vec_ref[0, 0:1, :] + vec_ref[0, 1:2, :]).astype(BF16)
        normed_ref[rows, :] = normed
        for n in range(width // KB):
            normed_t_ref[n * KB : (n + 1) * KB, rows] = normed[:, n * KB : (n + 1) * KB].T

    def own_rows(i, carry):
        norm_rows(x_ref, i, halo)
        return carry

    lax.fori_loop(0, tokens // KB, own_rows, 0)
    qseg_ref[...] = segment_lanes(seg_ref[0:1, :], True)
    kseg_ref[pl.ds(halo, tokens), :] = segment_lanes(seg_ref[0:1, :], False)
    for i in range(1, stages):
        for k in range(ts):
            net.far_step(1, k, i)
    own[1].wait()
    for k in range(ts):
        net.core_step(1, k)
    loads = weight_loads(qkvo_all, w_ref, h2_ref, local_sem, ts)
    for load in loads:
        load.start()
    for load in loads:
        load.wait()
    merge_pairs(w_ref, h2_ref, ts)

    def biases(p):
        t = jnp.minimum(p, ts - 1)
        a = jnp.maximum(p - ts, 0)
        low, high = vec_ref[2 * a, 7:8, 256:384], vec_ref[2 * a + 1, 7:8, 256:384]
        bias_q = jnp.where(p < ts, vec_ref[t, 7:8, 0:128], lanes_of(low, swap_halves(high)))
        bias_v = jnp.where(p < ts, vec_ref[t, 7:8, 128:256], lanes_of(swap_halves(low), high))
        return bias_q, bias_v

    own_span = pl.ds(halo, tokens)

    def project_own(p, carry):
        cols = pl.ds(pl.multiple_of(p * 128, 128), 128)
        bias_q, bias_v = biases(p)
        y = mm(normed_ref[own_span, :], w_ref[p, :, :, 0:384].reshape(width, 384))
        q_ref[:, cols] = ((y[:, :128] + bias_q) * Q_SCALE).astype(BF16)
        k_ref[own_span, cols] = y[:, 128:256].astype(BF16)
        v_ref[own_span, cols] = (y[:, 256:] + bias_v).astype(BF16)
        return carry

    lax.fori_loop(0, width // 128, project_own, 0)
    net.far_step(2, 0, 0)
    for i, (back, _) in enumerate(parts):

        @pl.when(mt >= back)
        def _():
            segs[i].wait_recv()

    @pl.when(mt >= 1)
    def _():
        early_rows.wait_recv()

    @pl.when(mt >= 2)
    def _():
        passed_rows.wait_recv()

    def halo_rows(i, carry):
        norm_rows(halo_ref, i, 0)
        return carry

    lax.fori_loop(0, halo // KB, halo_rows, 0)
    lanes = lax.rem(lax.broadcasted_iota(jnp.int32, (halo, 128), 1), HD)
    kseg_ref[pl.ds(0, halo), :] = jnp.where(lanes < DOCS, 1.0, 0.0).astype(BF16)
    end = halo
    for i, (_, count) in enumerate(parts):
        kseg_ref[pl.ds(end - count, count), :] = segment_lanes(hseg_ref[i, 0:1, :], False)[tokens - count :]
        end -= count

    plan = {0: [(3, 0, 0)]}
    for n, (k, c) in enumerate((k, c) for k in range(1, ts) for c in (2, 3)):
        plan.setdefault(n, []).append((c, k, "z"))
        plan.setdefault(n + 2, []).append((c, k, 0))
        plan.setdefault(n + 4, []).append((c, k, 1))
    plan.setdefault(2, []).extend([(2, 0, 1), (3, 0, 1)])

    def steps_at(p, place):
        for slot, items in plan.items():
            if slot % 2 != place:
                continue

            @pl.when(p == slot // 2)
            def _():
                for item in items:
                    c, k, what = item
                    if what == "z":
                        net.z_step(c, k)
                    elif what < stages:
                        net.far_step(c, k, what)

    def one_pair(p, carry):
        cols = pl.ds(pl.multiple_of(p * 128, 128), 128)
        _, bias_v = biases(p)

        def project(i, c):
            rows = pl.ds(pl.multiple_of(i * (halo // 2), 16), halo // 2)
            kv = mm(normed_ref[rows, :], w_ref[p, :, :, 128:384].reshape(width, 256))
            k_ref[rows, cols] = kv[:, :128].astype(BF16)
            v_ref[rows, cols] = (kv[:, 128:] + bias_v).astype(BF16)
            return c

        lax.fori_loop(0, 2, project, 0)

        def turn(i, c):
            rows = pl.ds(pl.multiple_of(i * KB, KB), KB)
            vt_ref[:, rows] = v_ref[rows, cols].T
            k, aux = k_ref[rows, cols], kseg_ref[rows, :]
            ka_ref[0, rows, :] = lanes_of(k, aux)
            ka_ref[1, rows, :] = lanes_of(aux, k)
            return c

        lax.fori_loop(0, (halo + tokens) // KB, turn, 0)
        steps_at(p, 0)

        def one_block(j, c):
            rows = pl.ds(pl.multiple_of(j * QB, QB), QB)
            q_block, aux = q_ref[rows, cols], qseg_ref[rows, :]
            base = j * QB
            spans = [(row, size, pl.ds(pl.multiple_of(base + row, 16), size)) for row, size in CHUNKS]
            for h in range(2):
                query = lanes_of(q_block, aux) if h == 0 else lanes_of(aux, q_block)
                top = jnp.full((8, QB), -1e30, F32)
                for row, size, span in spans:
                    s = causal(mm(ka_ref[h, span, :], query, NT), row)
                    s_ref[h, row : row + size, :] = s
                    top = jnp.maximum(top, fold_rows(s, jnp.max))
                top = jnp.max(top, axis=0, keepdims=True)
                total = jnp.zeros((8, QB), F32)
                acc = jnp.zeros((HD, QB), F32)
                for row, size, span in spans:
                    e = jnp.exp2(s_ref[h, row : row + size, :] - top)
                    total = total + fold_rows(e, jnp.sum)
                    if size < KB:
                        wide = pl.ds(pl.multiple_of(base + row // KB * KB, KB), KB)
                        e = jnp.concatenate([jnp.zeros((KB - size, QB), F32), e], axis=0)
                    else:
                        wide = pl.ds(pl.multiple_of(base + row, KB), KB)
                    acc = acc + mm(vt_ref[h * HD : (h + 1) * HD, wide], e.astype(BF16))
                total = jnp.sum(total, axis=0, keepdims=True)
                ot_ref[pl.ds(pl.multiple_of(p * 128 + h * HD, HD), HD), rows] = acc / total
                lse_ref[p, h : h + 1, rows] = top + jnp.log2(total)
            o = ot_ref[pl.ds(pl.multiple_of(p * 128, 128), 128), rows]
            mixed_ref[rows, cols] = o.T.astype(BF16)
            return c

        lax.fori_loop(0, tokens // QB, one_block, 0)
        w_o = w_ref[p, :, :, 384:512].reshape(width, 128)
        start = jnp.where(p == 0, x_ref[...].astype(F32) + vec_ref[0, 2:3, :], hidden_ref[...])
        hidden_ref[...] = start + mm(mixed_ref[:, cols], w_o, NT)
        steps_at(p, 1)
        return carry

    hidden_ref[...] = jnp.zeros_like(hidden_ref)
    lax.fori_loop(0, width // 128, one_pair, 0)
    for c in (2, 3):
        for k in range(ts):
            net.core_step(c, k)
    for c in own[2:]:
        c.wait()
    for i, (back, _) in enumerate(parts):

        @pl.when(mt + back < ts)
        def _():
            segs[i].wait_send()

    @pl.when(mt + 1 < ts)
    def _():
        late_rows.wait_send()
        early_rows.wait_send()

    @pl.when((mt >= 1) & (mt + 1 < ts))
    def _():
        passed_rows.wait_send()

    net.finish()


def front(x, seg, small, qkvo, fc, proj, dp, ts, halo):
    tokens, width = x.shape
    rows = fc.shape[0]
    window = halo + tokens
    pairs = width // 128
    copies = Gather.copies(dp, ts, 4)
    n_halo = len(halo_parts(tokens, ts))
    any_spec = pl.BlockSpec(memory_space=pl.ANY)
    vmem = pl.BlockSpec(memory_space=pltpu.VMEM)
    big = jax.ShapeDtypeStruct((ts, dp, rows, width), BF16)
    s = jax.ShapeDtypeStruct
    dma = pltpu.SemaphoreType.DMA
    return pl.pallas_call(
        functools.partial(front_kernel, dp, ts),
        out_shape=[
            big,
            big,
            big,
            s((ts, 8, width), F32),
            s((window, 128), BF16),
            s((tokens, 128), BF16),
            s((width, window), BF16),
            s((halo, width), BF16),
            s((tokens, width), BF16),
            s((window, width), BF16),
            s((window, width), BF16),
            s((width, tokens), F32),
            s((pairs, 2, tokens), F32),
            s((tokens, width), BF16),
            s((tokens, width), F32),
        ],
        in_specs=[vmem, vmem] + [any_spec] * 4,
        out_specs=[any_spec] * 3 + [vmem] * 12,
        scratch_shapes=[
            pltpu.VMEM((ts, dp, 8, width), F32),
            pltpu.VMEM((pairs, dp, rows, 512), BF16),
            pltpu.VMEM((ts, dp, rows, 256), BF16),
            pltpu.VMEM((n_halo, 8, tokens), jnp.int32),
            pltpu.VMEM((window, width), BF16),
            pltpu.VMEM((2, window, 128), BF16),
            pltpu.VMEM((128, window), BF16),
            pltpu.VMEM((2, HALO + QB, QB), F32),
            dma((2 * ts + 4,)),
            dma((4, ts, 2)),
            dma((4, ts)),
            dma((copies,)),
            dma((copies,)),
            dma((3 + n_halo,)),
            dma((3 + n_halo,)),
        ],
        compiler_params=pltpu.CompilerParams(
            collective_id=1, has_side_effects=True, vmem_limit_bytes=62 << 20
        ),
        name="front",
    )(x, seg, small, qkvo, fc, proj)


class Scatter:
    def __init__(self, dp, ts, srcs, local, in_core, in_far, in_z, sems):
        self.dp, self.ts, self.srcs, self.local = dp, ts, srcs, local
        self.in_core, self.in_far, self.in_z = in_core, in_far, in_z
        self.core_send, self.core_recv, self.far_send, self.far_recv, self.z_send, self.z_recv = sems
        self.me, self.mt = lax.axis_index("dp"), lax.axis_index("tensor")
        self.far = [1 << k for k in range(1, dp.bit_length() - 1)]
        self.evens = list(range(0, dp, 2))

    def block(self, c, t, to):
        if c < 2:
            return self.srcs[c].at[t, to // 2, lax.rem(to, 2)]
        return self.srcs[c].at[t, to]

    def order(self, t):
        return self.far[::-1] if 2 * t < self.ts else self.far

    def core(self, c, t, m):
        return pltpu.make_async_remote_copy(
            src_ref=self.block(c, t, self.me ^ 1 ^ m),
            dst_ref=self.in_core.at[c, t, m >> 1],
            send_sem=self.core_send.at[c, t, m >> 1],
            recv_sem=self.core_recv.at[c, t, m >> 1],
            device_id={"dp": self.me ^ 1},
            device_id_type=MESH,
        )

    def far_moves(self, t, s):
        order = self.order(t)
        done = sum(order[:s])
        first = sum(len(self.evens) >> (i + 1) for i in range(s))
        masks = [m for m in self.evens if m & order[s] and not m & done]
        return [(m, first + i) for i, m in enumerate(masks)]

    def far_copy(self, c, t, s, m, slot):
        return pltpu.make_async_remote_copy(
            src_ref=self.in_core.at[c, t, m >> 1],
            dst_ref=self.in_far.at[c, t, slot],
            send_sem=self.far_send.at[c, t, slot],
            recv_sem=self.far_recv.at[c, t, slot],
            device_id={"dp": self.me ^ self.order(t)[s]},
            device_id_type=MESH,
        )

    def z_copy(self, c, t):
        back = lax.rem(self.mt + self.ts - t, self.ts) - 1
        return pltpu.make_async_remote_copy(
            src_ref=self.in_core.at[c, t, 0],
            dst_ref=self.in_z.at[c, back],
            send_sem=self.z_send.at[c, t],
            recv_sem=self.z_recv.at[c, back],
            device_id={"tensor": t},
            device_id_type=MESH,
        )

    def start(self, c, t):
        for m in self.evens[::-1]:
            self.core(c, t, m).start()

    def step(self, c, t, s):
        if s == 0:
            for m in self.evens[::-1]:
                self.core(c, t, m).wait_recv()
                to = self.me ^ m
                mine = self.local[c, t, to // 2] if c < 2 else self.srcs[c][t, to]
                self.in_core[c, t, m >> 1] = self.in_core[c, t, m >> 1] + mine
        else:
            bit = self.order(t)[s - 1]
            for m, slot in self.far_moves(t, s - 1):
                self.far_copy(c, t, s - 1, m, slot).wait_recv()
                to = (m ^ bit) >> 1
                self.in_core[c, t, to] = self.in_core[c, t, to] + self.in_far[c, t, slot]
        if s < len(self.far):
            for m, slot in self.far_moves(t, s):
                self.far_copy(c, t, s, m, slot).start()
        else:

            @pl.when(self.mt != t)
            def _():
                self.z_copy(c, t).start()

    def final(self, c):
        total = self.in_core[c, self.mt, 0].astype(F32)
        for k in range(self.ts - 1):
            pltpu.make_async_remote_copy(
                src_ref=self.in_core.at[c, 0, 0],
                dst_ref=self.in_z.at[c, k],
                send_sem=self.z_send.at[c, 0],
                recv_sem=self.z_recv.at[c, k],
                device_id={"tensor": self.mt},
                device_id_type=MESH,
            ).wait_recv()
            total = total + self.in_z[c, k].astype(F32)
        return total

    def finish(self):
        for c in range(len(self.srcs)):
            for t in range(self.ts):
                for m in self.evens:
                    self.core(c, t, m).wait_send()
                for s in range(len(self.far)):
                    for m, slot in self.far_moves(t, s):
                        self.far_copy(c, t, s, m, slot).wait_send()

                @pl.when(self.mt != t)
                def _():
                    self.z_copy(c, t).wait_send()


def norm_back(grad_in, gain_vec, unit_rows, scaler):
    scaled = grad_in * gain_vec
    return scaler * (
        scaled
        - jnp.mean(scaled, axis=-1, keepdims=True)
        - unit_rows * jnp.mean(scaled * unit_rows, axis=-1, keepdims=True)
    )


class Total:
    def __init__(self, dp, ts, mine, dp_in, z_in, sends, recvs):
        self.dp, self.ts, self.mine, self.dp_in, self.z_in = dp, ts, mine, dp_in, z_in
        self.sends, self.recvs = sends, recvs
        self.me, self.mt = lax.axis_index("dp"), lax.axis_index("tensor")

    def over_dp(self, m):
        return pltpu.make_async_remote_copy(
            src_ref=self.mine,
            dst_ref=self.dp_in.at[m],
            send_sem=self.sends.at[m],
            recv_sem=self.recvs.at[m],
            device_id={"dp": self.me ^ m},
            device_id_type=MESH,
        )

    def over_z(self, k):
        return pltpu.make_async_remote_copy(
            src_ref=self.z_in.at[0],
            dst_ref=self.z_in.at[self.ts - k],
            send_sem=self.sends.at[self.dp + k],
            recv_sem=self.recvs.at[self.dp + self.ts - k],
            device_id={"tensor": lax.rem(self.mt + k, self.ts)},
            device_id_type=MESH,
        )

    def start(self):
        for m in range(1, self.dp):
            self.over_dp(m).start()

    def turn(self):
        total = self.mine[...]
        for m in range(1, self.dp):
            self.over_dp(m).wait_recv()
            total = total + self.dp_in[m]
        self.z_in[0] = total
        for k in range(1, self.ts):
            self.over_z(k).start()

    def end(self):
        total = self.z_in[0]
        for k in range(1, self.ts):
            self.over_z(k).wait_recv()
            total = total + self.z_in[self.ts - k]
        return total

    def finish(self):
        for m in range(1, self.dp):
            self.over_dp(m).wait_send()
        for k in range(1, self.ts):
            self.over_z(k).wait_send()


def back_kernel(
    dp,
    ts,
    x_ref,
    halo_ref,
    vec_ref,
    kseg_ref,
    qseg_ref,
    normed_t_ref,
    q_ref,
    k_ref,
    v_ref,
    ot_ref,
    lse_ref,
    mixed_ref,
    grad_hidden_ref,
    small_ref,
    g_proj,
    g_fc,
    qkvo_all,
    input_grad_ref,
    loss_out,
    gain_one_out,
    bias_one_out,
    qkv_out,
    qv_bias_out,
    out_out,
    out_bias_out,
    gain_two_out,
    bias_two_out,
    fc_out,
    fc_bias_out,
    proj_out,
    proj_bias_out,
    w_ref,
    g_qkvo,
    low_ref,
    low_t_ref,
    ka_ref,
    kt_ref,
    dk_ref,
    dv_ref,
    gm_ref,
    delta_ref,
    dqkv_ref,
    dkv_ref,
    give_ref,
    take_ref,
    far_ref,
    gh_ref,
    gw_ref,
    g_local,
    small_in,
    small_z,
    late_own,
    late_in,
    late_z,
    in_core,
    in_far,
    in_z,
    local_sem,
    core_send,
    core_recv,
    far_send,
    far_recv,
    z_send,
    z_recv,
    halo_send,
    halo_recv,
    small_send,
    small_recv,
    late_send,
    late_recv,
):
    me, mt = lax.axis_index("dp"), lax.axis_index("tensor")
    tokens, width = x_ref.shape
    halo = halo_ref.shape[0]
    pairs = width // 128
    parts = halo_parts(tokens, ts)
    meet(dp, ts)
    sems = (core_send, core_recv, far_send, far_recv, z_send, z_recv)
    net = Scatter(dp, ts, [g_proj, g_fc, g_qkvo], g_local, in_core, in_far, in_z, sems)
    early = Total(dp, ts, small_ref, small_in, small_z, small_send, small_recv)
    late = Total(dp, ts, late_own, late_in, late_z, late_send, late_recv)
    stages = len(net.far) + 1
    zigzag = [t for pair in zip(range(ts // 2), range(ts - 1, ts // 2 - 1, -1)) for t in pair]
    for c in (0, 1):
        for t in zigzag:
            net.start(c, t)
    early.start()
    loads = weight_loads(qkvo_all, w_ref, g_qkvo, local_sem, ts)
    loads += [
        pltpu.make_async_copy(g.at[:, :, lax.rem(me, 2)], g_local.at[c], local_sem.at[2 * ts + c])
        for c, g in enumerate((g_proj, g_fc))
    ]
    for load in loads:
        load.start()

    def low_rows(i, c):
        rows = pl.ds(pl.multiple_of(i * KB, KB), KB)
        low = grad_hidden_ref[rows, :].astype(BF16)
        low_ref[rows, :] = low
        for n in range(pairs):
            low_t_ref[n * KB : (n + 1) * KB, rows] = low[:, n * KB : (n + 1) * KB].T
        return c

    lax.fori_loop(0, tokens // KB, low_rows, 0)
    for load in loads:
        load.wait()
    merge_pairs(w_ref, g_qkvo, ts)
    late_own[...] = jnp.zeros_like(late_own)
    gw_ref[...] = jnp.zeros_like(gw_ref)
    gh_ref[...] = jnp.zeros_like(gh_ref)

    turns = pairs + LAG
    order = list(range(ts, pairs)) + zigzag

    def pair_of(n):
        p = jnp.int32(order[0])
        for i in range(1, pairs):
            p = jnp.where(n == i, order[i], p)
        return p

    last = 4 * turns
    plan = {5: ["turn"], 9: ["end"], 4 * pairs + 3: ["final0", "final1"]}
    units = [(c, t) for c in (0, 1) for t in zigzag]
    for n, (c, t) in enumerate(units):
        for s in range(stages):
            plan.setdefault(2 * n + 1 + 3 * s, []).append((c, t, s))

    def after(slot):
        slot += 2
        return slot if slot < 4 * pairs else -(-(slot - 3) // 4) * 4 + 3 if slot < last else slot

    for i, t in enumerate(zigzag):
        at = 4 * (pairs - ts + i + LAG) + 3
        plan.setdefault(at, []).insert(0, (2, t, "start"))
        for s in range(stages):
            at = after(at) if at < last - 1 else max(at, last - 1) + 1
            plan.setdefault(at, []).append((2, t, s))

    def turned(block):
        pad = jnp.zeros((128 - block.shape[0], 128), F32)
        return jnp.concatenate([block, pad], axis=0).T[:, : block.shape[0]]

    def write_final(c):
        total = net.final(c)
        if c == 0:
            proj_out[...] = total
        elif c == 1:
            fc_out[...] = total
        else:
            for i in range(3):
                qkv_out[i, :, 0:128] = total[:, i * 128 : (i + 1) * 128]
                qkv_out[i, :, 128:192] = total[:, 512 + i * HD : 512 + (i + 1) * HD]
            out_out[0:128, :] = turned(total[:, 384:512])
            out_out[128:192, :] = turned(total[:, 640:768])[HD:, :]

    def at_lane(block, lane):
        return pltpu.roll(block, lax.rem(width - lane, width), 1)

    def write_small(block):
        rows = at_lane(block[0:8, :], me * (width // dp))
        for i, ref in enumerate((out_bias_out, gain_two_out, bias_two_out, proj_bias_out)):
            ref[...] = rows[i : i + 1, : width // dp]
        mine = block[4:5, :]
        for t in range(1, ts):
            mine = jnp.where(mt == t, block[4 + t : 5 + t, :], mine)
        mine = at_lane(jnp.broadcast_to(mine, (8, width)), me * (HD // dp))
        for i in range(width // HD):
            fc_bias_out[i : i + 1, :] = mine[0:1, i * HD : i * HD + HD // dp]
        count = vec_ref[0, 7:8, 384:385]
        for t in range(1, ts):
            count = count + vec_ref[t, 7:8, 384:385]
        loss_out[...] = block[4 + ts : 5 + ts, 0:1] / (width * count)

    def write_late(block):
        rows = at_lane(block, me * (width // dp))
        gain_one_out[...] = rows[0:1, : width // dp]
        bias_one_out[...] = rows[1:2, : width // dp]
        rows = at_lane(block, me * (HD // dp))
        for h in range(3):
            for i in range(2):
                value = None
                for t in range(ts):
                    lane = t * 128 + h * HD if h < 2 else ts * 128 + t * HD
                    here = rows[2 + i : 3 + i, lane : lane + HD // dp]
                    value = here if value is None else jnp.where(mt == t, here, value)
                qv_bias_out[h, i : i + 1, :] = value

    def run(items):
        for item in items:
            if item == "turn":
                early.turn()
            elif item == "end":
                write_small(early.end())
            elif item in ("final0", "final1"):
                write_final(int(item[-1]))
            elif item[2] == "start":
                net.start(item[0], item[1])
            else:
                net.step(*item)

    def steps_at(n, place):
        for slot, items in sorted(plan.items()):
            if slot % 4 == place and slot < (last if place == 3 else 4 * pairs):

                @pl.when(n == slot // 4)
                def _():
                    run(items)

    far = parts[1][1]
    near_at, cut = halo - tokens, tokens - far

    def hop(src, dst, n):
        return pltpu.make_async_remote_copy(
            src_ref=src,
            dst_ref=dst,
            send_sem=halo_send.at[n],
            recv_sem=halo_recv.at[n],
            device_id={"tensor": lax.rem(mt + ts - 1, ts)},
            device_id_type=MESH,
        )

    far_rows = hop(give_ref.at[pl.ds(near_at - far, far)], far_ref, 0)
    early_rows = hop(give_ref.at[pl.ds(near_at, cut)], take_ref.at[pl.ds(0, cut)], 1)
    late_rows = hop(give_ref.at[pl.ds(near_at + cut, far)], take_ref.at[pl.ds(cut, far)], 2)

    def attend_back(n):
        p = pair_of(n)
        cols = pl.ds(pl.multiple_of(p * 128, 128), 128)
        w_o = w_ref[p, :, :, 384:512].reshape(width, 128)
        rounded = mm(low_ref[...], w_o).astype(BF16)
        gm_ref[...] = rounded
        weighted = rounded.astype(F32).T * ot_ref[pl.ds(pl.multiple_of(p * 128, 128), 128), :]
        for h in range(2):
            delta_ref[h : h + 1, :] = jnp.sum(weighted[h * HD : (h + 1) * HD], axis=0, keepdims=True)

        def turn(i, c):
            rows = pl.ds(pl.multiple_of(i * KB, KB), KB)
            k, aux = k_ref[rows, cols], kseg_ref[rows, :]
            kt_ref[:, rows] = k.T
            ka_ref[0, rows, :] = lanes_of(k, aux)
            ka_ref[1, rows, :] = lanes_of(aux, k)
            dk_ref[rows, :] = jnp.zeros((KB, 128), F32)
            dv_ref[rows, :] = jnp.zeros((KB, 128), F32)
            return c

        lax.fori_loop(0, (halo + tokens) // KB, turn, 0)
        steps_at(n, 0)

        def one_block(j, c):
            base = j * QB
            at = pl.ds(pl.multiple_of(base, QB), QB)
            q_block, aux, do_block = q_ref[at, cols], qseg_ref[at, :], gm_ref[at, :]
            asks = [lanes_of(q_block, aux), lanes_of(aux, q_block)]
            q_cat = jnp.concatenate([keep_lanes(q_block, h) for h in range(2)], axis=0)
            do_cat = jnp.concatenate([keep_lanes(do_block, h) for h in range(2)], axis=0)
            lse = [lse_ref[p, h : h + 1, at] for h in range(2)]
            delta = [delta_ref[h : h + 1, at] for h in range(2)]
            dq_t = [jnp.zeros((HD, QB), F32) for h in range(2)]
            for row, size in CHUNKS:
                span = pl.ds(pl.multiple_of(base + row, 16), size)
                values = v_ref[span, cols]
                ps, dss = [], []
                for h in range(2):
                    s = causal(mm(ka_ref[h, span, :], asks[h], NT), row)
                    e = jnp.exp2(s - lse[h])
                    grad_e = mm(values, do_cat[h * QB : (h + 1) * QB], NT)
                    ds = (e * (grad_e - delta[h])).astype(BF16)
                    wide = pl.ds(pl.multiple_of(base + row // KB * KB, KB), KB)
                    tall = ds
                    if size < KB:
                        tall = jnp.concatenate([jnp.zeros((KB - size, QB), BF16), ds], axis=0)
                    dq_t[h] = dq_t[h] + mm(kt_ref[h * HD : (h + 1) * HD, wide], tall)
                    ps.append(e.astype(BF16))
                    dss.append(ds)
                dv_ref[span, :] += mm(jnp.concatenate(ps, axis=1), do_cat)
                dk_ref[span, :] += mm(jnp.concatenate(dss, axis=1), q_cat)
            dqkv_ref[n, at, 0:128] = (jnp.concatenate(dq_t, axis=0) * 0.125).T.astype(BF16)
            for place in range(tokens // QB):

                @pl.when(j == place)
                def _():
                    steps_at(n, 1 + place)
            return c

        lax.fori_loop(0, tokens // QB, one_block, 0)

        dkv_ref[n, :, 0:128] = (dk_ref[:halo, :] * (0.125 / Q_SCALE)).astype(BF16)
        dkv_ref[n, :, 128:256] = dv_ref[:halo, :].astype(BF16)
        dqkv_ref[n, :, 128:256] = (dk_ref[halo:, :] * (0.125 / Q_SCALE)).astype(BF16)
        dqkv_ref[n, :, 256:384] = dv_ref[halo:, :].astype(BF16)

        def halo_grad(i, c):
            rows = pl.ds(pl.multiple_of(i * (halo // 2), 16), halo // 2)
            gh_ref[rows, :] += mm(dkv_ref[n, rows, :], w_ref[p, :, :, 128:384].reshape(width, 256), NT)
            return c

        lax.fori_loop(0, 2, halo_grad, 0)

        @pl.when(n == pairs - 1)
        def _():
            give_ref[: near_at + cut, :] = gh_ref[: near_at + cut, :].astype(BF16)

            @pl.when(mt >= 2)
            def _():
                far_rows.start()

            @pl.when(mt >= 1)
            def _():
                early_rows.start()

    def store(tile, value, t):
        g_qkvo[t, :, :, tile * 128 : (tile + 1) * 128] = value.astype(BF16).reshape(dp, -1, 128)

    def weights_back(n):
        p = pair_of(n)
        cols = pl.ds(pl.multiple_of(p * 128, 128), 128)
        grad_o = mm(low_t_ref[...], mixed_ref[:, cols])
        dqkv = dqkv_ref[n]
        own = mm(normed_t_ref[:, halo:], dqkv)
        far = mm(normed_t_ref[:, :halo], dkv_ref[n])
        four = [own[:, 0:128], own[:, 128:256] + far[:, 0:128], own[:, 256:384] + far[:, 128:256], grad_o]

        @pl.when(p < ts)
        def _():
            for i, g in enumerate(four):
                store(i, g, p)

        for a in range(pairs - ts):

            @pl.when(p == ts + a)
            def _():
                for i in range(2):
                    low_half, high_half = four[2 * i], four[2 * i + 1]
                    store(4 + i, lanes_of(low_half, swap_halves(high_half)), 2 * a)
                    store(4 + i, lanes_of(swap_halves(low_half), high_half), 2 * a + 1)

        gw_ref[...] += mm(dqkv, w_ref[p, :, :, 0:384].reshape(width, 384), NT)
        grad_v = jnp.sum(dqkv[:, 256:384].astype(F32), axis=0, keepdims=True)
        late_own[2:3, cols] = jnp.sum(dqkv[:, 0:128].astype(F32), axis=0, keepdims=True)
        late_own[3:4, cols] = grad_v + jnp.sum(dkv_ref[n, :, 128:256].astype(F32), axis=0, keepdims=True)

    def one_turn(n, carry):
        @pl.when(n < pairs)
        def _():
            attend_back(n)

        @pl.when(n >= LAG)
        def _():
            weights_back(n - LAG)

        steps_at(n, 3)
        return carry

    lax.fori_loop(0, turns, one_turn, 0)

    def halo_sums(i, carry):
        rows = pl.ds(pl.multiple_of(i * KB, KB), KB)
        unit, _ = normalize(halo_ref[rows, :].astype(F32))
        g = gh_ref[rows, :]
        return carry[0] + fold_rows(g * unit, jnp.sum), carry[1] + fold_rows(g, jnp.sum)

    def own_sums(i, carry):
        rows = pl.ds(pl.multiple_of(i * KB, KB), KB)
        unit, _ = normalize(x_ref[rows, :].astype(F32))
        g = gw_ref[rows, :]
        return carry[0] + fold_rows(g * unit, jnp.sum), carry[1] + fold_rows(g, jnp.sum)

    zero = jnp.zeros((8, width), F32)
    carry = lax.fori_loop(0, halo // KB, halo_sums, (zero, zero))
    passed = (mt >= 1) & (mt + 1 < ts)

    @pl.when(passed)
    def _():
        far_rows.wait_recv()
        gh_ref[near_at + cut :, :] += far_ref[...].astype(F32)

    @pl.when(mt >= 1)
    def _():
        give_ref[near_at + cut :, :] = gh_ref[near_at + cut :, :].astype(BF16)
        late_rows.start()

    tail = [item for slot, items in sorted(plan.items()) if slot >= last for item in items]
    first = [item for item in tail if item[2] == 0] + [item for item in tail if item[1] == zigzag[-3]]
    tail = [item for item in tail if item not in first]
    run(first)
    gains, shifts = lax.fori_loop(0, tokens // KB, own_sums, carry)
    late_own[0:1, :] = jnp.sum(gains, axis=0, keepdims=True)
    late_own[1:2, :] = jnp.sum(shifts, axis=0, keepdims=True)
    late.start()
    tail.sort(key=lambda item: (item[2], -zigzag.index(item[1])))
    run(tail[:1])
    late.turn()
    run(tail[1:])

    @pl.when(mt + 1 < ts)
    def _():
        early_rows.wait_recv()
        late_rows.wait_recv()
        gw_ref[...] += take_ref[...].astype(F32)

    def own_grad(i, carry):
        rows = pl.ds(pl.multiple_of(i * KB, KB), KB)
        unit, scaler = normalize(x_ref[rows, :].astype(F32))
        g = gw_ref[rows, :]
        input_grad_ref[rows, :] = grad_hidden_ref[rows, :] + norm_back(g, vec_ref[0, 0:1, :], unit, scaler)
        return carry

    lax.fori_loop(0, tokens // KB, own_grad, 0)
    write_late(late.end())
    write_final(2)
    early.finish()
    late.finish()

    @pl.when(mt >= 2)
    def _():
        far_rows.wait_send()

    @pl.when(mt >= 1)
    def _():
        early_rows.wait_send()
        late_rows.wait_send()

    net.finish()


def back(x, halo_x, vec, kseg, qseg, normed_t, q, k, v, ot, lse, mixed, grad_hidden, small, g_proj, g_fc, qkvo_all):
    tokens, width = x.shape
    halo = halo_x.shape[0]
    window = halo + tokens
    ts, dp, rows = qkvo_all.shape[:3]
    pairs = width // 128
    n_far = dp // 2 - 1
    any_spec = pl.BlockSpec(memory_space=pl.ANY)
    vmem = pl.BlockSpec(memory_space=pltpu.VMEM)
    s = jax.ShapeDtypeStruct
    dma = pltpu.SemaphoreType.DMA
    return pl.pallas_call(
        functools.partial(back_kernel, dp, ts),
        out_shape=[
            s((tokens, width), F32),
            s((1, 1), F32),
            s((1, rows), F32),
            s((1, rows), F32),
            s((3, rows, 3 * HD), F32),
            s((3, 2, HD // dp), F32),
            s((3 * HD, rows), F32),
            s((1, rows), F32),
            s((1, rows), F32),
            s((1, rows), F32),
            s((rows, width), F32),
            s((width // HD, HD // dp), F32),
            s((rows, width), F32),
            s((1, rows), F32),
        ],
        in_specs=[vmem] * 14 + [any_spec] * 3,
        out_specs=[vmem] * 14,
        scratch_shapes=[
            pltpu.VMEM((pairs, dp, rows, 512), BF16),
            pltpu.VMEM((ts, dp, rows, width), BF16),
            pltpu.VMEM((tokens, width), BF16),
            pltpu.VMEM((width, tokens), BF16),
            pltpu.VMEM((2, window, 128), BF16),
            pltpu.VMEM((128, window), BF16),
            pltpu.VMEM((window, 128), F32),
            pltpu.VMEM((window, 128), F32),
            pltpu.VMEM((tokens, 128), BF16),
            pltpu.VMEM((8, tokens), F32),
            pltpu.VMEM((pairs, tokens, 384), BF16),
            pltpu.VMEM((pairs, halo, 256), BF16),
            pltpu.VMEM((halo, width), BF16),
            pltpu.VMEM((tokens, width), BF16),
            pltpu.VMEM((halo_parts(tokens, ts)[1][1], width), BF16),
            pltpu.VMEM((halo, width), F32),
            pltpu.VMEM((tokens, width), F32),
            pltpu.VMEM((2, ts, dp // 2, rows, width), BF16),
            pltpu.VMEM((dp,) + small.shape, F32),
            pltpu.VMEM((ts,) + small.shape, F32),
            pltpu.VMEM((8, width), F32),
            pltpu.VMEM((dp, 8, width), F32),
            pltpu.VMEM((ts, 8, width), F32),
            pltpu.VMEM((3, ts, dp // 2, rows, width), BF16),
            pltpu.VMEM((3, ts, n_far, rows, width), BF16),
            pltpu.VMEM((3, ts - 1, rows, width), BF16),
            dma((2 * ts + 2,)),
            dma((3, ts, dp // 2)),
            dma((3, ts, dp // 2)),
            dma((3, ts, n_far)),
            dma((3, ts, n_far)),
            dma((3, ts)),
            dma((3, ts - 1)),
            dma((3,)),
            dma((3,)),
            dma((dp + ts,)),
            dma((dp + ts,)),
            dma((dp + ts,)),
            dma((dp + ts,)),
        ],
        compiler_params=pltpu.CompilerParams(
            collective_id=2, has_side_effects=True, vmem_limit_bytes=63 << 20
        ),
        name="back",
    )(x, halo_x, vec, kseg, qseg, normed_t, q, k, v, ot, lse, mixed, grad_hidden, small, g_proj, g_fc, qkvo_all)


def gather_kernel(dp, ts, tokens, n_in, *refs):
    w_refs, (x_ref, seg_ref) = refs[:n_in], refs[n_in : n_in + 2]
    outs = refs[n_in + 2 : 2 * n_in + 2]
    halo_ref, hseg_ref = refs[2 * n_in + 2 : 2 * n_in + 4]
    local_sem, send_sem, recv_sem, halo_send, halo_recv = refs[2 * n_in + 4 :]
    me = lax.axis_index("dp")
    mt = lax.axis_index("tensor")
    bits = [1 << k for k in range(dp.bit_length() - 1)]
    far = bits[1:]
    halo_ref[...] = jnp.zeros_like(halo_ref)
    hseg_ref[...] = jnp.full_like(hseg_ref, -1)
    barrier = pltpu.get_barrier_semaphore()
    peers_t = [lax.rem(mt + k, ts) for k in range(1, ts)]
    for t in peers_t:
        pl.semaphore_signal(barrier, inc=1, device_id={"tensor": t}, device_id_type=MESH)
    for b in bits:
        pl.semaphore_signal(barrier, inc=1, device_id={"dp": me ^ b}, device_id_type=MESH)
    pl.semaphore_wait(barrier, len(peers_t) + len(bits))
    started = []

    def rcopy(src, dst, dev):
        i = len(started)
        c = pltpu.make_async_remote_copy(
            src_ref=src,
            dst_ref=dst,
            send_sem=send_sem.at[i],
            recv_sem=recv_sem.at[i],
            device_id=dev,
            device_id_type=MESH,
        )
        c.start()
        started.append(c)
        return c

    locals_, over_z = [], []
    for c in range(n_in):
        copy = pltpu.make_async_copy(w_refs[c], outs[c].at[mt, me], local_sem.at[c])
        copy.start()
        locals_.append(copy)
        over_z.append([rcopy(w_refs[c], outs[c].at[mt, me], {"tensor": t}) for t in peers_t])
        if c == min(1, n_in - 1):
            end = halo_ref.shape[0]
            halos = []
            for i, (back, count) in enumerate(halo_parts(tokens, ts)):
                end -= count
                pair = [
                    pltpu.make_async_remote_copy(
                        src_ref=src,
                        dst_ref=dst,
                        send_sem=halo_send.at[2 * i + k],
                        recv_sem=halo_recv.at[2 * i + k],
                        device_id={"tensor": lax.rem(mt + back, ts)},
                        device_id_type=MESH,
                    )
                    for k, (src, dst) in enumerate(
                        [
                            (x_ref.at[pl.ds(tokens - count, count)], halo_ref.at[pl.ds(end, count)]),
                            (seg_ref, hseg_ref.at[i]),
                        ]
                    )
                ]
                halos.append((back, pair))

                @pl.when(mt + back < ts)
                def _():
                    for h in pair:
                        h.start()

    half = max(ts // 2, 1)
    groups = [(0, half, far)] + ([(half, ts - half, far[::-1])] if ts > half else [])

    def spread(c, group, masks, later):
        res = {}
        for b in later + [1]:
            res[b] = []
            for m in masks:
                ref = outs[c].at[pl.ds(group[0], group[1]), me ^ m]
                res[b].append((m, rcopy(ref, ref, {"dp": me ^ b})))
        return res

    stages = len(far) + 1
    pending = {}
    for step in range(n_in + stages - 1):
        for s in range(stages):
            c = step - s
            if not 0 <= c < n_in:
                continue
            if s == 0:
                locals_[c].wait()
                for k in over_z[c]:
                    k.wait_recv()
            for gi, group in enumerate(groups):
                if s == 0:
                    pending[c, gi] = [spread(c, group, [0], group[2])]
                else:
                    b = group[2][s - 1]
                    masks = []
                    for res in pending[c, gi]:
                        for m, k in res.get(b, []):
                            k.wait_recv()
                            masks.append(m ^ b)
                    pending[c, gi].append(spread(c, group, masks, group[2][s:]))
    for c in range(n_in):
        for gi in range(len(groups)):
            for res in pending[c, gi]:
                for m, k in res[1]:
                    k.wait_recv()
    for back, pair in halos:

        @pl.when(mt >= back)
        def _():
            for h in pair:
                h.wait_recv()

        @pl.when(mt + back < ts)
        def _():
            for h in pair:
                h.wait_send()

    for k in started:
        k.wait_send()


def gather(parts, x, seg, dp, ts, halo):
    n_in = len(parts)
    tokens = x.shape[0]
    copies = n_in * ((ts - 1) + (2 if ts > 1 else 1) * (dp - 1))
    n_halo = len(halo_parts(tokens, ts))
    any_spec = pl.BlockSpec(memory_space=pl.ANY)
    vmem = pl.BlockSpec(memory_space=pltpu.VMEM)
    return pl.pallas_call(
        functools.partial(gather_kernel, dp, ts, tokens, n_in),
        out_shape=[jax.ShapeDtypeStruct((ts, dp) + p.shape, p.dtype) for p in parts]
        + [
            jax.ShapeDtypeStruct((halo, x.shape[1]), x.dtype),
            jax.ShapeDtypeStruct((n_halo,) + seg.shape, seg.dtype),
        ],
        in_specs=[any_spec] * (n_in + 2),
        out_specs=[any_spec] * n_in + [vmem, vmem],
        scratch_shapes=[
            pltpu.SemaphoreType.DMA((n_in,)),
            pltpu.SemaphoreType.DMA((copies,)),
            pltpu.SemaphoreType.DMA((copies,)),
            pltpu.SemaphoreType.DMA((2 * n_halo,)),
            pltpu.SemaphoreType.DMA((2 * n_halo,)),
        ],
        compiler_params=pltpu.CompilerParams(collective_id=1, has_side_effects=True),
        name="gather",
    )(*parts, x, seg)


def reduce_kernel(dp, ts, g_ref, out_ref, in_core, in_far, in_z, send_sem, recv_sem):
    n_c = g_ref.shape[0]
    me = lax.axis_index("dp")
    mt = lax.axis_index("tensor")
    bits = [1 << k for k in range(dp.bit_length() - 1)]
    far = bits[1:]
    barrier = pltpu.get_barrier_semaphore()
    peers_t = [lax.rem(mt + k, ts) for k in range(1, ts)]
    for t in peers_t:
        pl.semaphore_signal(barrier, inc=1, device_id={"tensor": t}, device_id_type=MESH)
    for b in bits:
        pl.semaphore_signal(barrier, inc=1, device_id={"dp": me ^ b}, device_id_type=MESH)
    pl.semaphore_wait(barrier, len(peers_t) + len(bits))
    started = []

    def rcopy(src, dst, dev):
        i = len(started)
        c = pltpu.make_async_remote_copy(
            src_ref=src,
            dst_ref=dst,
            send_sem=send_sem.at[i],
            recv_sem=recv_sem.at[i],
            device_id=dev,
            device_id_type=MESH,
        )
        c.start()
        started.append(c)
        return c

    half = max(ts // 2, 1)
    groups = [(0, half, far[::-1])] + ([(half, ts - half, far)] if ts > half else [])
    evens = list(range(0, dp, 2))
    core = []
    for c in range(n_c):
        core.append(
            {
                m: rcopy(g_ref.at[c, :, me ^ 1 ^ m], in_core.at[c, m >> 1], {"dp": me ^ 1})
                for m in evens[::-1]
            }
        )

    def add_into(dst, src, base, count):
        def one(i, carry):
            dst[base + i] = (dst[base + i].astype(F32) + src[i].astype(F32)).astype(BF16)
            return carry

        lax.fori_loop(0, count, one, 0)

    stages = len(far) + 2
    pending = {}
    slots = {}
    for step in range(n_c + stages - 1):
        for s in range(stages):
            c = step - s
            if not 0 <= c < n_c:
                continue
            if s == 0:
                for m in evens[::-1]:
                    core[c][m].wait_recv()

                    def one(i, carry, m=m):
                        in_core[c, m >> 1, i] = (
                            in_core[c, m >> 1, i].astype(F32) + g_ref[c, i, me ^ m].astype(F32)
                        ).astype(BF16)
                        return carry

                    lax.fori_loop(0, ts, one, 0)
            for gi, (t0, tn, order) in enumerate(groups):
                if s > 0:
                    for m, slot, k in pending.pop((c, gi)):
                        k.wait_recv()
                        add_into(in_core.at[c, m >> 1], in_far.at[c, slot, pl.ds(t0, tn)], t0, tn)
                if s < len(far):
                    b = order[s]
                    done = sum(order[:s])
                    masks = [m for m in evens if m & b and not m & done]
                    sent = []
                    for m in masks:
                        slot = slots.get((c, gi), 0)
                        slots[c, gi] = slot + 1
                        k = rcopy(
                            in_core.at[c, m >> 1, pl.ds(t0, tn)],
                            in_far.at[c, slot, pl.ds(t0, tn)],
                            {"dp": me ^ b},
                        )
                        sent.append((m ^ b, slot, k))
                    pending[c, gi] = sent
                elif s == len(far):
                    pending[c, gi] = []
            if s == len(far):
                pending[c, "z"] = [
                    rcopy(in_core.at[c, 0, lax.rem(mt + k, ts)], in_z.at[c, k - 1], {"tensor": lax.rem(mt + k, ts)})
                    for k in range(1, ts)
                ]
            if s == len(far) + 1:
                total = in_core[c, 0, mt].astype(F32)
                for k in pending[c, "z"]:
                    k.wait_recv()
                for k in range(ts - 1):
                    total = total + in_z[c, k].astype(F32)
                out_ref[c] = total
    for k in started:
        k.wait_send()


def reduce(grads, dp, ts):
    n_c, _, _, rows, width = grads.shape
    n_far = dp // 2 - 1
    groups = 2 if ts > 1 else 1
    copies = n_c * (dp // 2 + groups * n_far + ts - 1)
    vmem = pl.BlockSpec(memory_space=pltpu.VMEM)
    return pl.pallas_call(
        functools.partial(reduce_kernel, dp, ts),
        out_shape=jax.ShapeDtypeStruct((n_c, rows, width), F32),
        in_specs=[vmem],
        out_specs=vmem,
        scratch_shapes=[
            pltpu.VMEM((n_c, dp // 2, ts, rows, width), BF16),
            pltpu.VMEM((n_c, n_far, ts, rows, width), BF16),
            pltpu.VMEM((n_c, ts - 1, rows, width), BF16),
            pltpu.SemaphoreType.DMA((copies,)),
            pltpu.SemaphoreType.DMA((copies,)),
        ],
        compiler_params=pltpu.CompilerParams(
            collective_id=2, has_side_effects=True, vmem_limit_bytes=62 << 20
        ),
        name="reduce",
    )(grads)


def allowed_at(chunk, doc_row, first_q):
    key = chunk * KB + lax.broadcasted_iota(jnp.int32, (KB, QB), 0)
    query = first_q + lax.broadcasted_iota(jnp.int32, (KB, QB), 1)
    return (key >= doc_row) & (key <= query)


def attend_kernel(halo, first_ref, doc_ref, q_ref, k_ref, vt_ref, o_ref, lse_ref, s_ref):
    for j in range(q_ref.shape[0] // QB):
        rows = pl.ds(j * QB, QB)
        q_block = q_ref[rows, :]
        queries = [keep_lanes(q_block, h) for h in range(2)]
        doc_row = doc_ref[0:1, rows]
        first_q = halo + j * QB
        begin = first_ref[j]
        end = (first_q + QB) // KB

        def score(c, tops):
            keys = k_ref[pl.ds(pl.multiple_of(c * KB, KB), KB), :]
            ok = allowed_at(c, doc_row, first_q)
            res = []
            for h in range(2):
                s = jnp.where(ok, mm(keys, queries[h], NT), -1e30)
                s_ref[h, c] = s
                res.append(jnp.maximum(tops[h], fold_rows(s, jnp.max)))
            return tuple(res)

        tops = lax.fori_loop(begin, end, score, (jnp.full((8, QB), -1e30, F32),) * 2)
        tops = [jnp.max(t, axis=0, keepdims=True) for t in tops]

        def mix(c, carry):
            res = []
            for h in range(2):
                total, acc = carry[h]
                p = jnp.exp(s_ref[h, c] - tops[h])
                total = total + fold_rows(p, jnp.sum)
                vt = vt_ref[pl.ds(h * HD, HD), pl.ds(pl.multiple_of(c * KB, KB), KB)]
                acc = acc + mm(vt, p.astype(BF16))
                res.append((total, acc))
            return tuple(res)

        carry = lax.fori_loop(
            begin, end, mix, ((jnp.zeros((8, QB), F32), jnp.zeros((HD, QB), F32)),) * 2
        )
        for h in range(2):
            total = jnp.sum(carry[h][0], axis=0, keepdims=True)
            o_ref[pl.ds(h * HD, HD), rows] = carry[h][1] / total
            lse_ref[0, h : h + 1, rows] = tops[h] + jnp.log(total)


def attend(first, doc, q, k, vt, halo):
    tokens, width = q.shape
    keys = k.shape[0]
    pairs = width // 128
    return pl.pallas_call(
        functools.partial(attend_kernel, halo),
        out_shape=[
            jax.ShapeDtypeStruct((width, tokens), F32),
            jax.ShapeDtypeStruct((pairs, 2, tokens), F32),
        ],
        grid_spec=pltpu.PrefetchScalarGridSpec(
            num_scalar_prefetch=1,
            grid=(pairs,),
            in_specs=[
                pl.BlockSpec((1, tokens), lambda p, f: (0, 0)),
                pl.BlockSpec((tokens, 128), lambda p, f: (0, p)),
                pl.BlockSpec((keys, 128), lambda p, f: (0, p)),
                pl.BlockSpec((128, keys), lambda p, f: (p, 0)),
            ],
            out_specs=[
                pl.BlockSpec((128, tokens), lambda p, f: (p, 0)),
                pl.BlockSpec((1, 2, tokens), lambda p, f: (p, 0, 0)),
            ],
            scratch_shapes=[pltpu.VMEM((2, keys // KB, KB, QB), F32)],
        ),
        name="attend",
    )(first, doc, q, k, vt)


def attend_back_kernel(
    halo, first_ref, doc_ref, q_ref, k_ref, kt_ref, v_ref, do_ref, lse_ref, delta_ref, dq_ref, dk_ref, dv_ref
):
    dk_ref[...] = jnp.zeros_like(dk_ref)
    dv_ref[...] = jnp.zeros_like(dv_ref)
    for j in range(q_ref.shape[0] // QB):
        rows = pl.ds(j * QB, QB)
        q_block, do_block = q_ref[rows, :], do_ref[rows, :]
        queries = [keep_lanes(q_block, h) for h in range(2)]
        grads = [keep_lanes(do_block, h) for h in range(2)]
        doc_row = doc_ref[0:1, rows]
        first_q = halo + j * QB

        def step(c, carry):
            span = pl.ds(pl.multiple_of(c * KB, KB), KB)
            keys, values = k_ref[span, :], v_ref[span, :]
            ok = allowed_at(c, doc_row, first_q)
            res = []
            grad_k = grad_v = None
            for h in range(2):
                s = jnp.where(ok, mm(keys, queries[h], NT), -1e30)
                p = jnp.exp(s - lse_ref[0, h : h + 1, rows])
                dp_ = mm(values, grads[h], NT)
                ds = (p * (dp_ - delta_ref[0, h : h + 1, rows])).astype(BF16)
                gv = mm(p.astype(BF16), grads[h])
                gk = mm(ds, queries[h])
                grad_v = gv if grad_v is None else grad_v + gv
                grad_k = gk if grad_k is None else grad_k + gk
                kt = kt_ref[pl.ds(h * HD, HD), span]
                res.append(carry[h] + mm(kt, ds))
            dk_ref[span, :] += grad_k
            dv_ref[span, :] += grad_v
            return tuple(res)

        carry = lax.fori_loop(
            first_ref[j], (first_q + QB) // KB, step, (jnp.zeros((HD, QB), F32),) * 2
        )
        for h in range(2):
            dq_ref[pl.ds(h * HD, HD), rows] = carry[h] * 0.125


def attend_back(first, doc, q, k, kt, v, do, lse, delta, halo):
    tokens, width = q.shape
    keys = k.shape[0]
    pairs = width // 128
    q_spec = pl.BlockSpec((tokens, 128), lambda p, f: (0, p))
    k_spec = pl.BlockSpec((keys, 128), lambda p, f: (0, p))
    stat = pl.BlockSpec((1, 2, tokens), lambda p, f: (p, 0, 0))
    return pl.pallas_call(
        functools.partial(attend_back_kernel, halo),
        out_shape=[
            jax.ShapeDtypeStruct((width, tokens), F32),
            jax.ShapeDtypeStruct((keys, width), F32),
            jax.ShapeDtypeStruct((keys, width), F32),
        ],
        grid_spec=pltpu.PrefetchScalarGridSpec(
            num_scalar_prefetch=1,
            grid=(pairs,),
            in_specs=[
                pl.BlockSpec((1, tokens), lambda p, f: (0, 0)),
                q_spec,
                k_spec,
                pl.BlockSpec((128, keys), lambda p, f: (p, 0)),
                k_spec,
                q_spec,
                stat,
                stat,
            ],
            out_specs=[pl.BlockSpec((128, tokens), lambda p, f: (p, 0)), k_spec, k_spec],
        ),
        name="attend_back",
    )(first, doc, q, k, kt, v, do, lse, delta)


def gelu_tanh(values_in):
    return (
        0.5
        * values_in
        * (
            1.0
            + jnp.tanh(TANH_SLOPE * (values_in + CUBIC_TERM * values_in * values_in * values_in))
        )
    )


def plain_device(
    block_input,
    teacher,
    segment_ids,
    valid_mask,
    ln1_gain,
    ln1_bias,
    qkv_weight,
    qv_bias,
    out_weight,
    out_bias,
    ln2_gain,
    ln2_bias,
    fc_weight,
    fc_bias,
    proj_weight,
    proj_bias,
):
    dp, ts = lax.axis_size("dp"), lax.axis_size("tensor")
    me, mt = lax.axis_index("dp"), lax.axis_index("tensor")
    tokens, width = block_input.shape[1:]
    total_tokens = tokens * ts * dp
    halo = -(-(DOC_MOST - 1) // KB) * KB
    e = qkv_weight.shape[2]
    x = block_input[0]
    valid_rows = valid_mask[0].astype(F32)

    qkvo = jnp.concatenate([qkv_weight[0], qkv_weight[1], qkv_weight[2], out_weight.T], axis=1)
    local_count = jnp.sum(valid_mask[0])
    mine = jnp.arange(dp) == me

    def spread(v):
        return jnp.where(mine[:, None], v[..., None, :], jnp.zeros((), v.dtype))

    vectors = jnp.stack([ln1_gain, ln1_bias, out_bias, ln2_gain, ln2_bias, proj_bias])
    tail = jnp.stack([local_count // 16, local_count % 16]).astype(BF16)
    small = jnp.concatenate(
        [
            spread(vectors).reshape(6, width),
            spread(fc_bias).reshape(1, -1),
            jnp.concatenate(
                [spread(qv_bias).reshape(-1), tail, jnp.zeros((width - 2 * e - 2,), BF16)]
            )[None],
        ]
    )
    seg_rows = jnp.broadcast_to(segment_ids, (8, tokens))
    small_all, w_qkvo, w_fc, w_proj, x_halo, seg_halo = gather(
        [small, qkvo, fc_weight, proj_weight.T], x, seg_rows, dp, ts, halo
    )
    small_all = jnp.sum(small_all.astype(F32), axis=1)
    gain_one, bias_one, b_out, gain_two, bias_two, b_proj = [small_all[0, i] for i in range(6)]
    b_fc = small_all[:, 6].reshape(-1)
    b_q = small_all[:, 7, :e].reshape(-1)
    b_v = small_all[:, 7, e : 2 * e].reshape(-1)
    valid_count = jnp.sum(small_all[:, 7, 2 * e] * 16 + small_all[:, 7, 2 * e + 1])
    w_qkvo = w_qkvo.reshape(ts, width, 4, e)
    wq, wk, wv, wo = [w_qkvo[:, :, i].transpose(1, 0, 2).reshape(width, width) for i in range(4)]
    wf = w_fc.reshape(ts, width, -1)
    wp = w_proj.reshape(ts, width, -1)

    seg = segment_ids[0]
    pieces = []
    for i, (back, count) in enumerate(halo_parts(tokens, ts)):
        pieces.insert(0, seg_halo[i, 0, tokens - count :])
    filled = sum(p.shape[0] for p in pieces)
    seg_window = jnp.concatenate([jnp.full((halo - filled,), -1, jnp.int32)] + pieces)
    position = jnp.sum((seg_window[:, None] < seg[None, :]).astype(jnp.int32), axis=0)
    own = jnp.sum((seg[:, None] < seg[None, :]).astype(jnp.int32), axis=0)
    doc = (position + own)[None]
    first = doc[0, ::QB] // KB

    inputs = x.astype(F32)
    window = jnp.concatenate([x_halo, x]).astype(F32)
    unit_window, scale_window = normalize(window)
    normed_window = (unit_window * gain_one + bias_one).astype(BF16)
    unit_one, scale_one = unit_window[halo:], scale_window[halo:]
    normed_one = normed_window[halo:]
    q = ((mm(normed_one, wq) + b_q).astype(BF16) * 0.125).astype(BF16)
    k = mm(normed_window, wk).astype(BF16)
    v = (mm(normed_window, wv) + b_v).astype(BF16)
    mixed_t, lse = attend(first, doc, q, k, v.T, halo)
    mixed = mixed_t.T.astype(BF16)
    hidden = inputs + mm(mixed, wo, NT) + b_out
    unit_two, scale_two = normalize(hidden)
    normed_two = (unit_two * gain_two + bias_two).astype(BF16)
    pre_act = jnp.einsum("sd,tdf->stf", normed_two, wf, preferred_element_type=F32) + b_fc.reshape(ts, -1)
    activated = gelu_tanh(pre_act).astype(BF16)
    output = hidden + jnp.einsum("stf,tdf->sd", activated, wp, preferred_element_type=F32) + b_proj
    residual_error = output - teacher[0].astype(F32)
    squares = jnp.sum(valid_rows[:, None] * residual_error * residual_error)
    grad_output = valid_rows[:, None] * residual_error * (total_tokens / valid_count)
    low_output = grad_output.astype(BF16)
    grad_act = jnp.einsum("sd,tdf->stf", low_output, wp, preferred_element_type=F32)
    grad_proj_w = jnp.einsum("sd,stf->tdf", low_output, activated, preferred_element_type=F32)
    _, gelu_back = jax.vjp(gelu_tanh, pre_act)
    grad_pre = gelu_back(grad_act)[0].astype(BF16)
    grad_fc_w = jnp.einsum("sd,stf->tdf", normed_two, grad_pre, preferred_element_type=F32)
    grad_fc_b = jnp.sum(grad_pre, axis=0, dtype=F32)
    grad_normed_two = jnp.einsum("stf,tdf->sd", grad_pre, wf, preferred_element_type=F32)
    grad_gain_two = jnp.sum(grad_normed_two * unit_two, axis=0)
    grad_bias_two = jnp.sum(grad_normed_two, axis=0)
    grad_hidden = grad_output + norm_back(grad_normed_two, gain_two, unit_two, scale_two)
    low_hidden = grad_hidden.astype(BF16)
    grad_mixed = mm(low_hidden, wo).astype(BF16)
    grad_out_w = jnp.einsum("sd,se->de", low_hidden, mixed, preferred_element_type=F32)
    heads = width // HD
    delta = jnp.sum((grad_mixed.T.astype(F32) * mixed_t).reshape(heads // 2, 2, HD, tokens), axis=2)
    dq_t, dk, dv = attend_back(first, doc, q, k, k.T, v, grad_mixed, lse, delta, halo)
    dq, dk, dv = dq_t.T.astype(BF16), dk.astype(BF16), dv.astype(BF16)
    sd_se = lambda a, b: jnp.einsum("sd,se->de", a, b, preferred_element_type=F32)
    g_q, g_k, g_v = sd_se(normed_one, dq), sd_se(normed_window, dk), sd_se(normed_window, dv)
    grad_window = mm(dk, wk, NT) + mm(dv, wv, NT)
    grad_normed_one = grad_window[halo:] + mm(dq, wq, NT)
    end = halo
    for back, count in halo_parts(tokens, ts):
        end -= count
        part = lax.ppermute(
            grad_window[end : end + count].astype(BF16), "tensor", [(t, t - back) for t in range(back, ts)]
        )
        grad_normed_one = grad_normed_one.at[tokens - count :].add(part.astype(F32))
    grad_input = grad_hidden + norm_back(grad_normed_one, gain_one, unit_one, scale_one)

    def by_t(g):
        return g.reshape(width, ts, e)

    g_qkvo = jnp.stack([by_t(g_q), by_t(g_k), by_t(g_v), by_t(grad_out_w)], axis=2)
    g_qkvo = g_qkvo.transpose(1, 0, 2, 3).reshape(ts, width, 4 * e)
    grads = jnp.stack([grad_proj_w, grad_fc_w, g_qkvo]).astype(BF16)
    grads = grads.reshape(3, ts, dp, width // dp, -1)
    r_proj, r_fc, r_qkvo = reduce(grads, dp, ts)
    smalls = [
        jnp.sum(grad_normed_one * unit_one, axis=0),
        jnp.sum(grad_normed_one, axis=0),
        jnp.sum(grad_hidden, axis=0),
        grad_gain_two,
        grad_bias_two,
        jnp.sum(grad_output, axis=0),
        grad_fc_b.reshape(-1),
        jnp.sum(dq, axis=0, dtype=F32),
        jnp.sum(dv, axis=0, dtype=F32),
        squares[None],
    ]
    summed = lax.psum(jnp.concatenate(smalls), ("dp", "tensor"))
    rows = width // dp
    own_rows = lambda i: lax.dynamic_slice_in_dim(summed, i * width + me * rows, rows)
    fc_b = summed[6 * width : 6 * width + fc_bias.size * dp * ts].reshape(ts, -1, dp, fc_bias.shape[1])
    qv0 = 6 * width + fc_bias.size * dp * ts
    qv_b = summed[qv0 : qv0 + 2 * width].reshape(2, ts, -1, dp, qv_bias.shape[2])
    loss = summed[-1] / (width * valid_count)
    pick = lambda a, i, ax: lax.dynamic_index_in_dim(a, i, ax, keepdims=False)
    return (
        output.astype(BF16)[None],
        loss,
        grad_input[None],
        own_rows(0),
        own_rows(1),
        jnp.stack([r_qkvo[:, i * e : (i + 1) * e] for i in range(3)]),
        pick(pick(qv_b, mt, 1), me, 2),
        r_qkvo[:, 3 * e :].T,
        own_rows(2),
        own_rows(3),
        own_rows(4),
        r_fc,
        pick(pick(fc_b, mt, 0), me, 1),
        r_proj.T,
        own_rows(5),
    )


def on_device(
    block_input,
    teacher,
    segment_ids,
    valid_mask,
    ln1_gain,
    ln1_bias,
    qkv_weight,
    qv_bias,
    out_weight,
    out_bias,
    ln2_gain,
    ln2_bias,
    fc_weight,
    fc_bias,
    proj_weight,
    proj_bias,
):
    dp, ts = lax.axis_size("dp"), lax.axis_size("tensor")
    me, mt = lax.axis_index("dp"), lax.axis_index("tensor")
    tokens, width = block_input.shape[1:]
    total_tokens = tokens * ts * dp
    e = qkv_weight.shape[2]
    x = block_input[0]
    valid_rows = valid_mask[0].astype(F32)

    cuts = [qkv_weight[0], qkv_weight[1], qkv_weight[2], out_weight.T]
    qkvo = jnp.concatenate([c[:, : 2 * HD] for c in cuts] + [c[:, 2 * HD :] for c in cuts], axis=1)
    mine = jnp.arange(dp) == me

    def spread(v):
        return jnp.where(mine[:, None], v[..., None, :], jnp.zeros((), v.dtype)).astype(F32)

    vectors = jnp.stack([ln1_gain, ln1_bias, out_bias, ln2_gain, ln2_bias, proj_bias])
    qv = spread(qv_bias).reshape(2, e)
    small = jnp.concatenate(
        [
            spread(vectors).reshape(6, width),
            spread(fc_bias).reshape(1, -1),
            jnp.concatenate(
                [qv[0, : 2 * HD], qv[1, : 2 * HD], qv[0, 2 * HD :], qv[1, 2 * HD :], jnp.sum(valid_rows)[None]]
                + [jnp.zeros((width - 2 * e - 1,), F32)]
            )[None],
        ]
    )
    seg_rows = jnp.broadcast_to(segment_ids, (8, tokens))
    qkvo_all, w_fc, w_proj, vec, kseg, qseg, normed_t, halo_x, q, k, v, ot, lse, mixed, hidden = front(
        x, seg_rows, small, qkvo, fc_weight, proj_weight.T, dp, ts, HALO
    )
    gain_two, bias_two, b_proj = [vec[0, i] for i in (3, 4, 5)]
    b_fc = vec[:, 6]
    valid_count = jnp.sum(vec[:, 7, 2 * e])
    wf = w_fc.reshape(ts, width, -1)
    wp = w_proj.reshape(ts, width, -1)

    unit_two, scale_two = normalize(hidden)
    normed_two = (unit_two * gain_two + bias_two).astype(BF16)
    pre_act = jnp.einsum("sd,tdf->stf", normed_two, wf, preferred_element_type=F32) + b_fc
    activated = gelu_tanh(pre_act).astype(BF16)
    output = hidden + jnp.einsum("stf,tdf->sd", activated, wp, preferred_element_type=F32) + b_proj
    residual_error = output - teacher[0].astype(F32)
    squares = jnp.sum(valid_rows[:, None] * residual_error * residual_error)
    grad_output = valid_rows[:, None] * residual_error * (total_tokens / valid_count)
    low_output = grad_output.astype(BF16)
    grad_act = jnp.einsum("sd,tdf->stf", low_output, wp, preferred_element_type=F32)
    grad_proj_w = jnp.einsum("sd,stf->tdf", low_output, activated, preferred_element_type=F32)
    _, gelu_back = jax.vjp(gelu_tanh, pre_act)
    grad_pre = gelu_back(grad_act)[0].astype(BF16)
    grad_fc_w = jnp.einsum("sd,stf->tdf", normed_two, grad_pre, preferred_element_type=F32)
    grad_normed_two = jnp.einsum("stf,tdf->sd", grad_pre, wf, preferred_element_type=F32)
    grad_hidden = grad_output + norm_back(grad_normed_two, gain_two, unit_two, scale_two)
    small_grads = jnp.concatenate(
        [
            jnp.sum(grad_hidden, axis=0)[None],
            jnp.sum(grad_normed_two * unit_two, axis=0)[None],
            jnp.sum(grad_normed_two, axis=0)[None],
            jnp.sum(grad_output, axis=0)[None],
            jnp.sum(grad_pre, axis=0, dtype=F32),
            jnp.full((1, width), squares),
            jnp.zeros((-(5 + ts) % 8, width), F32),
        ]
    )
    blocks = lambda g: g.astype(BF16).reshape(ts, dp // 2, 2, width // dp, width)
    grads = back(
        x, halo_x, vec, kseg, qseg, normed_t, q, k, v, ot, lse, mixed, grad_hidden, small_grads,
        blocks(grad_proj_w), blocks(grad_fc_w), qkvo_all,
    )
    input_grad, loss, gain_one, bias_one, g_qkv, g_qv_bias, g_out, *others = grads
    out_bias_, gain_two_, bias_two_, g_fc, g_fc_bias, g_proj, proj_bias_ = others
    return (
        output.astype(BF16)[None],
        loss[0, 0],
        input_grad[None],
        gain_one[0],
        bias_one[0],
        g_qkv,
        g_qv_bias.transpose(1, 0, 2),
        g_out,
        out_bias_[0],
        gain_two_[0],
        bias_two_[0],
        g_fc,
        g_fc_bias,
        g_proj.T,
        proj_bias_[0],
    )


def solution(mesh):
    placed = (
        P("dp", "tensor", None),
        P("dp", "tensor", None),
        P("dp", "tensor"),
        P("dp", "tensor"),
        P("dp"),
        P("dp"),
        P(None, "dp", "tensor"),
        P(None, "tensor", "dp"),
        P("tensor", "dp"),
        P("dp"),
        P("dp"),
        P("dp"),
        P("dp", "tensor"),
        P("tensor", "dp"),
        P("tensor", "dp"),
        P("dp"),
    )
    def fits(qkv_weight, block_input):
        rows = block_input.shape[2] // mesh.shape["dp"]
        wide = qkv_weight.shape[2] // mesh.shape["tensor"]
        parts = halo_parts(block_input.shape[1] // mesh.shape["tensor"], mesh.shape["tensor"])
        return rows % 16 == 0 and wide == 3 * HD and mesh.shape["tensor"] % 2 == 0 and len(parts) == 2

    def step(*args):
        return placed_step(on_device if fits(args[6], args[0]) else plain_device)(*args)

    placed_step = lambda body: jax.shard_map(
        body,
        mesh=mesh,
        in_specs=placed,
        out_specs=(
            P("dp", "tensor", None),
            P(),
            P("dp", "tensor", None),
            P("dp"),
            P("dp"),
            P(None, "dp", "tensor"),
            P(None, "tensor", "dp"),
            P("tensor", "dp"),
            P("dp"),
            P("dp"),
            P("dp"),
            P("dp", "tensor"),
            P("tensor", "dp"),
            P("tensor", "dp"),
            P("dp"),
        ),
        check_vma=False,
    )
    return step
```

```python
import functools

import jax
import jax.numpy as jnp
from jax import lax
from jax.experimental import pallas as pl
from jax.experimental.pallas import tpu as pltpu
from jax.sharding import PartitionSpec as P

HD = 64
DOC_MOST = 800
KB = 128
QB = 256
DOCS = 8
HALO = -(-(DOC_MOST - 1) // KB) * KB
LEAD = (HALO - DOC_MOST + 1) // 32 * 32
CHUNKS = ([(LEAD, KB - LEAD)] if LEAD else [(0, KB)]) + [(r, KB) for r in range(KB, HALO + QB, KB)]
Q_SCALE = 0.125 * 1.4426950408889634
EPSILON = 1e-05
LAG = 2
TANH_SLOPE = 0.7978845608028654
CUBIC_TERM = 0.044715
MESH = pl.DeviceIdType.MESH
F32 = jnp.float32
BF16 = jnp.bfloat16
NN = (((1,), (0,)), ((), ()))
NT = (((1,), (1,)), ((), ()))


def mm(a, b, dims=NN):
    return lax.dot_general(a, b, dims, preferred_element_type=F32)


def halo_parts(tokens, ts):
    parts, left, back = [], DOC_MOST, 1
    while left > 0 and back < ts:
        parts.append((back, min(tokens, left)))
        left -= tokens
        back += 1
    return parts


class Gather:
    def __init__(self, dp, ts, ins, outs, z_send, z_recv, send_sem, recv_sem):
        self.dp, self.ts, self.ins, self.outs = dp, ts, ins, outs
        self.z_send, self.z_recv, self.send_sem, self.recv_sem = z_send, z_recv, send_sem, recv_sem
        self.me, self.mt = lax.axis_index("dp"), lax.axis_index("tensor")
        self.far = [1 << k for k in range(1, dp.bit_length() - 1)]
        self.keys = {}
        self.flight = []
        self.near = [sorted(range(ts), key=lambda t: (abs(t - m), t)) for m in range(ts)]

    @staticmethod
    def copies(dp, ts, parts):
        return parts * ts * (dp - 1)

    def t_of(self, k):
        t = jnp.int32(self.near[0][k])
        for m in range(1, self.ts):
            t = jnp.where(self.mt == m, self.near[m][k], t)
        return t

    def order(self, t):
        flip = t * 2 >= self.ts
        return [jnp.where(flip, b, a) for a, b in zip(self.far, self.far[::-1])]

    def place(self, c, t, dp_index):
        return self.outs[c].at[t, dp_index]

    def along(self, c, t, up):
        src = self.ins[c] if t is None else self.place(c, t, self.me)
        t = self.mt if t is None else t
        return pltpu.make_async_remote_copy(
            src_ref=src,
            dst_ref=self.place(c, t, self.me),
            send_sem=self.z_send.at[c, t, int(up)],
            recv_sem=self.z_recv.at[c, t],
            device_id={"tensor": self.mt + (1 if up else -1)},
            device_id_type=MESH,
        )

    def desc(self, key):
        c, k, known, i = key
        t = self.t_of(k)
        order = self.order(t)
        mask = jnp.int32(0)
        for b in known:
            mask = mask ^ order[b]
        ref = self.place(c, t, self.me ^ mask)
        own = k == 0 and not known
        n = self.keys.setdefault(key, len(self.keys))
        return pltpu.make_async_remote_copy(
            src_ref=self.ins[c] if own else ref,
            dst_ref=ref,
            send_sem=self.send_sem.at[n],
            recv_sem=self.recv_sem.at[n],
            device_id={"dp": self.me ^ (1 if i < 0 else order[i])},
            device_id_type=MESH,
        )

    def here(self, c, k, known):
        first = max(known) + 1 if known else 0
        for i in list(range(first, len(self.far))) + [-1]:
            key = (c, k, known, i)
            self.desc(key).start()
            self.flight.append(key)

    def start(self, c):
        @pl.when(self.mt + 1 < self.ts)
        def _():
            self.along(c, None, True).start()

        @pl.when(self.mt >= 1)
        def _():
            self.along(c, None, False).start()

        self.here(c, 0, ())

    def z_step(self, c, k):
        t = self.t_of(k)
        self.along(c, t, True).wait_recv()

        @pl.when((t < self.mt) & (self.mt + 1 < self.ts))
        def _():
            self.along(c, t, True).start()

        @pl.when((t > self.mt) & (self.mt >= 1))
        def _():
            self.along(c, t, False).start()

        self.here(c, k, ())

    def far_step(self, c, k, i):
        for key in [q for q in self.flight if q[:2] == (c, k) and q[3] == i]:
            self.desc(key).wait_recv()
            self.here(c, k, key[2] + (i,))

    def core_step(self, c, k):
        for key in [q for q in self.flight if q[:2] == (c, k) and q[3] < 0]:
            self.desc(key).wait_recv()

    def finish(self):
        for c in range(len(self.ins)):
            for k in range(self.ts):
                t = self.t_of(k)

                @pl.when((t <= self.mt) & (self.mt + 1 < self.ts))
                def _():
                    self.along(c, t, True).wait_send()

                @pl.when((t >= self.mt) & (self.mt >= 1))
                def _():
                    self.along(c, t, False).wait_send()

        for key in self.flight:
            self.desc(key).wait_send()


def meet(dp, ts):
    me, mt = lax.axis_index("dp"), lax.axis_index("tensor")
    barrier = pltpu.get_barrier_semaphore()
    for k in range(1, ts):
        pl.semaphore_signal(barrier, inc=1, device_id={"tensor": lax.rem(mt + k, ts)}, device_id_type=MESH)
    for b in range(1, dp):
        pl.semaphore_signal(barrier, inc=1, device_id={"dp": me ^ b}, device_id_type=MESH)
    pl.semaphore_wait(barrier, ts - 1 + dp - 1)


def keep_lanes(block, head):
    lanes = lax.broadcasted_iota(jnp.int32, block.shape, 1)
    return jnp.where((lanes < HD) == (head == 0), block, jnp.zeros_like(block))


def fold_rows(block, op):
    return op(block.reshape(block.shape[0] // 8, 8, block.shape[1]), axis=0)


def swap_halves(block):
    return jnp.concatenate([block[:, HD:], block[:, :HD]], axis=1)


def lanes_of(low, high):
    lanes = lax.broadcasted_iota(jnp.int32, low.shape, 1)
    return jnp.where(lanes < HD, low, high)


def causal(s, row):
    ahead = row - HALO
    if ahead < 0:
        return s
    key = lax.broadcasted_iota(jnp.int32, s.shape, 0)
    query = lax.broadcasted_iota(jnp.int32, s.shape, 1)
    return jnp.where(key + ahead <= query, s, -1e30)


def segment_lanes(seg_row, same):
    shape = (128, seg_row.shape[1])
    value = lax.rem(lax.broadcasted_iota(jnp.int32, shape, 0), HD)
    hit = (seg_row == value) if same else (seg_row != value)
    level = -1e30 if same else 1.0
    return jnp.where(hit & (value < DOCS), level, 0.0).T.astype(BF16)


def normalize(values_in):
    center = values_in - jnp.mean(values_in, axis=-1, keepdims=True)
    scaler = lax.rsqrt(jnp.mean(center * center, axis=-1, keepdims=True) + EPSILON)
    return (center * scaler, scaler)


def merge_pairs(w_ref, h2_ref, ts):
    for a in range(ts // 2):
        tiles = []
        for t in (2 * a, 2 * a + 1):
            block = h2_ref[t, :, :, 0:256].reshape(-1, 256)
            tiles.append((block[:, :128], block[:, 128:]))
        (qk0, vo0), (qk1, vo1) = tiles
        merged = [
            lanes_of(qk0, swap_halves(qk1)),
            lanes_of(swap_halves(qk0), qk1),
            lanes_of(vo0, swap_halves(vo1)),
            lanes_of(swap_halves(vo0), vo1),
        ]
        for i, m in enumerate(merged):
            w_ref[ts + a, :, :, i * 128 : (i + 1) * 128] = m.reshape(w_ref.shape[1], w_ref.shape[2], 128)


def weight_loads(qkvo_all, w_ref, h2_ref, sem, ts):
    res = []
    for t in range(ts):
        res.append(pltpu.make_async_copy(qkvo_all.at[t, :, :, pl.ds(0, 512)], w_ref.at[t], sem.at[2 * t]))
        res.append(pltpu.make_async_copy(qkvo_all.at[t, :, :, pl.ds(512, 256)], h2_ref.at[t, :, :, pl.ds(0, 256)], sem.at[2 * t + 1]))
    return res


def front_kernel(
    dp,
    ts,
    x_ref,
    seg_ref,
    small_ref,
    qkvo_ref,
    fc_ref,
    proj_ref,
    qkvo_all,
    fc_all,
    proj_all,
    vec_ref,
    kseg_ref,
    qseg_ref,
    normed_t_ref,
    halo_ref,
    q_ref,
    k_ref,
    v_ref,
    ot_ref,
    lse_ref,
    mixed_ref,
    hidden_ref,
    small_all,
    w_ref,
    h2_ref,
    hseg_ref,
    normed_ref,
    ka_ref,
    vt_ref,
    s_ref,
    local_sem,
    z_send,
    z_recv,
    send_sem,
    recv_sem,
    halo_send,
    halo_recv,
):
    me, mt = lax.axis_index("dp"), lax.axis_index("tensor")
    tokens, width = x_ref.shape
    halo = halo_ref.shape[0]
    ins = [small_ref, qkvo_ref, fc_ref, proj_ref]
    outs = [small_all, qkvo_all, fc_all, proj_all]
    halo_ref[...] = jnp.zeros_like(halo_ref)
    hseg_ref[...] = jnp.full_like(hseg_ref, -1)
    meet(dp, ts)
    net = Gather(dp, ts, ins, outs, z_send, z_recv, send_sem, recv_sem)
    stages = len(net.far)
    parts = halo_parts(tokens, ts)

    far = parts[1][1]
    near_at, cut = halo - tokens, tokens - far

    def hop(src, dst, n, back):
        return pltpu.make_async_remote_copy(
            src_ref=src,
            dst_ref=dst,
            send_sem=halo_send.at[n],
            recv_sem=halo_recv.at[n],
            device_id={"tensor": lax.rem(mt + back, ts)},
            device_id_type=MESH,
        )

    late_rows = hop(x_ref.at[pl.ds(cut, far)], halo_ref.at[pl.ds(near_at + cut, far)], 0, 1)
    early_rows = hop(x_ref.at[pl.ds(0, cut)], halo_ref.at[pl.ds(near_at, cut)], 1, 1)
    passed_rows = hop(halo_ref.at[pl.ds(near_at + cut, far)], halo_ref.at[pl.ds(near_at - far, far)], 2, 1)
    segs = [hop(seg_ref, hseg_ref.at[i], 3 + i, back) for i, (back, _) in enumerate(parts)]

    own = [
        pltpu.make_async_copy(ins[c], outs[c].at[mt, me], local_sem.at[2 * ts + c]) for c in range(4)
    ]
    net.start(0)
    net.start(1)
    for c in own:
        c.start()
    for k in range(1, ts):
        net.z_step(0, k)
    for k in range(1, ts):
        net.z_step(1, k)
    for i, (back, _) in enumerate(parts):

        @pl.when(mt + back < ts)
        def _():
            segs[i].start()

    @pl.when(mt + 1 < ts)
    def _():
        late_rows.start()
        early_rows.start()

    for i in range(stages):
        for k in range(ts):
            net.far_step(0, k, i)
    for k in range(ts):
        net.far_step(1, k, 0)

    @pl.when(mt >= 1)
    def _():
        late_rows.wait_recv()

    @pl.when((mt >= 1) & (mt + 1 < ts))
    def _():
        passed_rows.start()

    net.start(2)
    net.start(3)
    own[0].wait()
    for k in range(ts):
        net.core_step(0, k)
    for t in range(ts):
        vec_ref[t] = jnp.sum(small_all[t], axis=0)

    def norm_rows(src, i, at):
        unit, _ = normalize(src[pl.ds(i * KB, KB), :].astype(F32))
        rows = pl.ds(pl.multiple_of(at + i * KB, KB), KB)
        normed = (unit * vec_ref[0, 0:1, :] + vec_ref[0, 1:2, :]).astype(BF16)
        normed_ref[rows, :] = normed
        for n in range(width // KB):
            normed_t_ref[n * KB : (n + 1) * KB, rows] = normed[:, n * KB : (n + 1) * KB].T

    def own_rows(i, carry):
        norm_rows(x_ref, i, halo)
        return carry

    lax.fori_loop(0, tokens // KB, own_rows, 0)
    qseg_ref[...] = segment_lanes(seg_ref[0:1, :], True)
    kseg_ref[pl.ds(halo, tokens), :] = segment_lanes(seg_ref[0:1, :], False)
    for i in range(1, stages):
        for k in range(ts):
            net.far_step(1, k, i)
    own[1].wait()
    for k in range(ts):
        net.core_step(1, k)
    loads = weight_loads(qkvo_all, w_ref, h2_ref, local_sem, ts)
    for load in loads:
        load.start()
    for load in loads:
        load.wait()
    merge_pairs(w_ref, h2_ref, ts)

    def biases(p):
        t = jnp.minimum(p, ts - 1)
        a = jnp.maximum(p - ts, 0)
        low, high = vec_ref[2 * a, 7:8, 256:384], vec_ref[2 * a + 1, 7:8, 256:384]
        bias_q = jnp.where(p < ts, vec_ref[t, 7:8, 0:128], lanes_of(low, swap_halves(high)))
        bias_v = jnp.where(p < ts, vec_ref[t, 7:8, 128:256], lanes_of(swap_halves(low), high))
        return bias_q, bias_v

    own_span = pl.ds(halo, tokens)

    def project_own(p, carry):
        cols = pl.ds(pl.multiple_of(p * 128, 128), 128)
        bias_q, bias_v = biases(p)
        y = mm(normed_ref[own_span, :], w_ref[p, :, :, 0:384].reshape(width, 384))
        q_ref[:, cols] = ((y[:, :128] + bias_q) * Q_SCALE).astype(BF16)
        k_ref[own_span, cols] = y[:, 128:256].astype(BF16)
        v_ref[own_span, cols] = (y[:, 256:] + bias_v).astype(BF16)
        return carry

    lax.fori_loop(0, width // 128, project_own, 0)
    net.far_step(2, 0, 0)
    for i, (back, _) in enumerate(parts):

        @pl.when(mt >= back)
        def _():
            segs[i].wait_recv()

    @pl.when(mt >= 1)
    def _():
        early_rows.wait_recv()

    @pl.when(mt >= 2)
    def _():
        passed_rows.wait_recv()

    def halo_rows(i, carry):
        norm_rows(halo_ref, i, 0)
        return carry

    lax.fori_loop(0, halo // KB, halo_rows, 0)
    lanes = lax.rem(lax.broadcasted_iota(jnp.int32, (halo, 128), 1), HD)
    kseg_ref[pl.ds(0, halo), :] = jnp.where(lanes < DOCS, 1.0, 0.0).astype(BF16)
    end = halo
    for i, (_, count) in enumerate(parts):
        kseg_ref[pl.ds(end - count, count), :] = segment_lanes(hseg_ref[i, 0:1, :], False)[tokens - count :]
        end -= count

    plan = {0: [(3, 0, 0)]}
    for n, (k, c) in enumerate((k, c) for k in range(1, ts) for c in (2, 3)):
        plan.setdefault(n, []).append((c, k, "z"))
        plan.setdefault(n + 2, []).append((c, k, 0))
        plan.setdefault(n + 4, []).append((c, k, 1))
    plan.setdefault(2, []).extend([(2, 0, 1), (3, 0, 1)])

    def steps_at(p, place):
        for slot, items in plan.items():
            if slot % 2 != place:
                continue

            @pl.when(p == slot // 2)
            def _():
                for item in items:
                    c, k, what = item
                    if what == "z":
                        net.z_step(c, k)
                    elif what < stages:
                        net.far_step(c, k, what)

    def one_pair(p, carry):
        cols = pl.ds(pl.multiple_of(p * 128, 128), 128)
        _, bias_v = biases(p)

        def project(i, c):
            rows = pl.ds(pl.multiple_of(i * (halo // 2), 16), halo // 2)
            kv = mm(normed_ref[rows, :], w_ref[p, :, :, 128:384].reshape(width, 256))
            k_ref[rows, cols] = kv[:, :128].astype(BF16)
            v_ref[rows, cols] = (kv[:, 128:] + bias_v).astype(BF16)
            return c

        lax.fori_loop(0, 2, project, 0)

        def turn(i, c):
            rows = pl.ds(pl.multiple_of(i * KB, KB), KB)
            vt_ref[:, rows] = v_ref[rows, cols].T
            k, aux = k_ref[rows, cols], kseg_ref[rows, :]
            ka_ref[0, rows, :] = lanes_of(k, aux)
            ka_ref[1, rows, :] = lanes_of(aux, k)
            return c

        lax.fori_loop(0, (halo + tokens) // KB, turn, 0)
        steps_at(p, 0)

        def one_block(j, c):
            rows = pl.ds(pl.multiple_of(j * QB, QB), QB)
            q_block, aux = q_ref[rows, cols], qseg_ref[rows, :]
            base = j * QB
            spans = [(row, size, pl.ds(pl.multiple_of(base + row, 16), size)) for row, size in CHUNKS]
            for h in range(2):
                query = lanes_of(q_block, aux) if h == 0 else lanes_of(aux, q_block)
                top = jnp.full((8, QB), -1e30, F32)
                for row, size, span in spans:
                    s = causal(mm(ka_ref[h, span, :], query, NT), row)
                    s_ref[h, row : row + size, :] = s
                    top = jnp.maximum(top, fold_rows(s, jnp.max))
                top = jnp.max(top, axis=0, keepdims=True)
                total = jnp.zeros((8, QB), F32)
                acc = jnp.zeros((HD, QB), F32)
                for row, size, span in spans:
                    e = jnp.exp2(s_ref[h, row : row + size, :] - top)
                    total = total + fold_rows(e, jnp.sum)
                    if size < KB:
                        wide = pl.ds(pl.multiple_of(base + row // KB * KB, KB), KB)
                        e = jnp.concatenate([jnp.zeros((KB - size, QB), F32), e], axis=0)
                    else:
                        wide = pl.ds(pl.multiple_of(base + row, KB), KB)
                    acc = acc + mm(vt_ref[h * HD : (h + 1) * HD, wide], e.astype(BF16))
                total = jnp.sum(total, axis=0, keepdims=True)
                ot_ref[pl.ds(pl.multiple_of(p * 128 + h * HD, HD), HD), rows] = acc / total
                lse_ref[p, h : h + 1, rows] = top + jnp.log2(total)
            o = ot_ref[pl.ds(pl.multiple_of(p * 128, 128), 128), rows]
            mixed_ref[rows, cols] = o.T.astype(BF16)
            return c

        lax.fori_loop(0, tokens // QB, one_block, 0)
        w_o = w_ref[p, :, :, 384:512].reshape(width, 128)
        start = jnp.where(p == 0, x_ref[...].astype(F32) + vec_ref[0, 2:3, :], hidden_ref[...])
        hidden_ref[...] = start + mm(mixed_ref[:, cols], w_o, NT)
        steps_at(p, 1)
        return carry

    hidden_ref[...] = jnp.zeros_like(hidden_ref)
    lax.fori_loop(0, width // 128, one_pair, 0)
    for c in (2, 3):
        for k in range(ts):
            net.core_step(c, k)
    for c in own[2:]:
        c.wait()
    for i, (back, _) in enumerate(parts):

        @pl.when(mt + back < ts)
        def _():
            segs[i].wait_send()

    @pl.when(mt + 1 < ts)
    def _():
        late_rows.wait_send()
        early_rows.wait_send()

    @pl.when((mt >= 1) & (mt + 1 < ts))
    def _():
        passed_rows.wait_send()

    net.finish()


def front(x, seg, small, qkvo, fc, proj, dp, ts, halo):
    tokens, width = x.shape
    rows = fc.shape[0]
    window = halo + tokens
    pairs = width // 128
    copies = Gather.copies(dp, ts, 4)
    n_halo = len(halo_parts(tokens, ts))
    any_spec = pl.BlockSpec(memory_space=pl.ANY)
    vmem = pl.BlockSpec(memory_space=pltpu.VMEM)
    big = jax.ShapeDtypeStruct((ts, dp, rows, width), BF16)
    s = jax.ShapeDtypeStruct
    dma = pltpu.SemaphoreType.DMA
    return pl.pallas_call(
        functools.partial(front_kernel, dp, ts),
        out_shape=[
            big,
            big,
            big,
            s((ts, 8, width), F32),
            s((window, 128), BF16),
            s((tokens, 128), BF16),
            s((width, window), BF16),
            s((halo, width), BF16),
            s((tokens, width), BF16),
            s((window, width), BF16),
            s((window, width), BF16),
            s((width, tokens), F32),
            s((pairs, 2, tokens), F32),
            s((tokens, width), BF16),
            s((tokens, width), F32),
        ],
        in_specs=[vmem, vmem] + [any_spec] * 4,
        out_specs=[any_spec] * 3 + [vmem] * 12,
        scratch_shapes=[
            pltpu.VMEM((ts, dp, 8, width), F32),
            pltpu.VMEM((pairs, dp, rows, 512), BF16),
            pltpu.VMEM((ts, dp, rows, 256), BF16),
            pltpu.VMEM((n_halo, 1, tokens), jnp.int32),
            pltpu.VMEM((window, width), BF16),
            pltpu.VMEM((2, window, 128), BF16),
            pltpu.VMEM((128, window), BF16),
            pltpu.VMEM((2, HALO + QB, QB), F32),
            dma((2 * ts + 4,)),
            dma((4, ts, 2)),
            dma((4, ts)),
            dma((copies,)),
            dma((copies,)),
            dma((3 + n_halo,)),
            dma((3 + n_halo,)),
        ],
        compiler_params=pltpu.CompilerParams(
            collective_id=1, has_side_effects=True, vmem_limit_bytes=62 << 20
        ),
        name="front",
    )(x, seg, small, qkvo, fc, proj)


class Scatter:
    def __init__(self, dp, ts, srcs, local, in_core, in_far, in_z, sems):
        self.dp, self.ts, self.srcs, self.local = dp, ts, srcs, local
        self.in_core, self.in_far, self.in_z = in_core, in_far, in_z
        self.core_send, self.core_recv, self.far_send, self.far_recv, self.z_send, self.z_recv = sems
        self.me, self.mt = lax.axis_index("dp"), lax.axis_index("tensor")
        self.far = [1 << k for k in range(1, dp.bit_length() - 1)]
        self.evens = list(range(0, dp, 2))

    def block(self, c, t, to):
        if c < 2:
            return self.srcs[c].at[t, to // 2, lax.rem(to, 2)]
        return self.srcs[c].at[t, to]

    def order(self, t):
        return self.far[::-1] if 2 * t < self.ts else self.far

    def core(self, c, t, m):
        return pltpu.make_async_remote_copy(
            src_ref=self.block(c, t, self.me ^ 1 ^ m),
            dst_ref=self.in_core.at[c, t, m >> 1],
            send_sem=self.core_send.at[c, t, m >> 1],
            recv_sem=self.core_recv.at[c, t, m >> 1],
            device_id={"dp": self.me ^ 1},
            device_id_type=MESH,
        )

    def far_moves(self, t, s):
        order = self.order(t)
        done = sum(order[:s])
        first = sum(len(self.evens) >> (i + 1) for i in range(s))
        masks = [m for m in self.evens if m & order[s] and not m & done]
        return [(m, first + i) for i, m in enumerate(masks)]

    def far_copy(self, c, t, s, m, slot):
        return pltpu.make_async_remote_copy(
            src_ref=self.in_core.at[c, t, m >> 1],
            dst_ref=self.in_far.at[c, t, slot],
            send_sem=self.far_send.at[c, t, slot],
            recv_sem=self.far_recv.at[c, t, slot],
            device_id={"dp": self.me ^ self.order(t)[s]},
            device_id_type=MESH,
        )

    def z_copy(self, c, t):
        back = lax.rem(self.mt + self.ts - t, self.ts) - 1
        return pltpu.make_async_remote_copy(
            src_ref=self.in_core.at[c, t, 0],
            dst_ref=self.in_z.at[c, back],
            send_sem=self.z_send.at[c, t],
            recv_sem=self.z_recv.at[c, back],
            device_id={"tensor": t},
            device_id_type=MESH,
        )

    def start(self, c, t):
        for m in self.evens[::-1]:
            self.core(c, t, m).start()

    def step(self, c, t, s):
        if s == 0:
            for m in self.evens[::-1]:
                self.core(c, t, m).wait_recv()
                to = self.me ^ m
                mine = self.local[c, t, to // 2] if c < 2 else self.srcs[c][t, to]
                self.in_core[c, t, m >> 1] = self.in_core[c, t, m >> 1] + mine
        else:
            bit = self.order(t)[s - 1]
            for m, slot in self.far_moves(t, s - 1):
                self.far_copy(c, t, s - 1, m, slot).wait_recv()
                to = (m ^ bit) >> 1
                self.in_core[c, t, to] = self.in_core[c, t, to] + self.in_far[c, t, slot]
        if s < len(self.far):
            for m, slot in self.far_moves(t, s):
                self.far_copy(c, t, s, m, slot).start()
        else:

            @pl.when(self.mt != t)
            def _():
                self.z_copy(c, t).start()

    def final(self, c):
        total = self.in_core[c, self.mt, 0].astype(F32)
        for k in range(self.ts - 1):
            pltpu.make_async_remote_copy(
                src_ref=self.in_core.at[c, 0, 0],
                dst_ref=self.in_z.at[c, k],
                send_sem=self.z_send.at[c, 0],
                recv_sem=self.z_recv.at[c, k],
                device_id={"tensor": self.mt},
                device_id_type=MESH,
            ).wait_recv()
            total = total + self.in_z[c, k].astype(F32)
        return total

    def finish(self):
        for c in range(len(self.srcs)):
            for t in range(self.ts):
                for m in self.evens:
                    self.core(c, t, m).wait_send()
                for s in range(len(self.far)):
                    for m, slot in self.far_moves(t, s):
                        self.far_copy(c, t, s, m, slot).wait_send()

                @pl.when(self.mt != t)
                def _():
                    self.z_copy(c, t).wait_send()


def norm_back(grad_in, gain_vec, unit_rows, scaler):
    scaled = grad_in * gain_vec
    return scaler * (
        scaled
        - jnp.mean(scaled, axis=-1, keepdims=True)
        - unit_rows * jnp.mean(scaled * unit_rows, axis=-1, keepdims=True)
    )


class Total:
    def __init__(self, dp, ts, mine, dp_in, z_in, sends, recvs):
        self.dp, self.ts, self.mine, self.dp_in, self.z_in = dp, ts, mine, dp_in, z_in
        self.sends, self.recvs = sends, recvs
        self.me, self.mt = lax.axis_index("dp"), lax.axis_index("tensor")

    def over_dp(self, m):
        return pltpu.make_async_remote_copy(
            src_ref=self.mine,
            dst_ref=self.dp_in.at[m],
            send_sem=self.sends.at[m],
            recv_sem=self.recvs.at[m],
            device_id={"dp": self.me ^ m},
            device_id_type=MESH,
        )

    def over_z(self, k):
        return pltpu.make_async_remote_copy(
            src_ref=self.z_in.at[0],
            dst_ref=self.z_in.at[self.ts - k],
            send_sem=self.sends.at[self.dp + k],
            recv_sem=self.recvs.at[self.dp + self.ts - k],
            device_id={"tensor": lax.rem(self.mt + k, self.ts)},
            device_id_type=MESH,
        )

    def start(self):
        for m in range(1, self.dp):
            self.over_dp(m).start()

    def turn(self):
        total = self.mine[...]
        for m in range(1, self.dp):
            self.over_dp(m).wait_recv()
            total = total + self.dp_in[m]
        self.z_in[0] = total
        for k in range(1, self.ts):
            self.over_z(k).start()

    def end(self):
        total = self.z_in[0]
        for k in range(1, self.ts):
            self.over_z(k).wait_recv()
            total = total + self.z_in[self.ts - k]
        return total

    def finish(self):
        for m in range(1, self.dp):
            self.over_dp(m).wait_send()
        for k in range(1, self.ts):
            self.over_z(k).wait_send()


def back_kernel(
    dp,
    ts,
    x_ref,
    halo_ref,
    vec_ref,
    kseg_ref,
    qseg_ref,
    normed_t_ref,
    q_ref,
    k_ref,
    v_ref,
    ot_ref,
    lse_ref,
    mixed_ref,
    grad_hidden_ref,
    small_ref,
    g_proj,
    g_fc,
    qkvo_all,
    input_grad_ref,
    loss_out,
    gain_one_out,
    bias_one_out,
    qkv_out,
    qv_bias_out,
    out_out,
    out_bias_out,
    gain_two_out,
    bias_two_out,
    fc_out,
    fc_bias_out,
    proj_out,
    proj_bias_out,
    w_ref,
    g_qkvo,
    low_ref,
    low_t_ref,
    ka_ref,
    kt_ref,
    dk_ref,
    dv_ref,
    gm_ref,
    delta_ref,
    dqkv_ref,
    dkv_ref,
    give_ref,
    take_ref,
    far_ref,
    gh_ref,
    gw_ref,
    g_local,
    small_in,
    small_z,
    late_own,
    late_in,
    late_z,
    in_core,
    in_far,
    in_z,
    local_sem,
    core_send,
    core_recv,
    far_send,
    far_recv,
    z_send,
    z_recv,
    halo_send,
    halo_recv,
    small_send,
    small_recv,
    late_send,
    late_recv,
):
    me, mt = lax.axis_index("dp"), lax.axis_index("tensor")
    tokens, width = x_ref.shape
    halo = halo_ref.shape[0]
    pairs = width // 128
    parts = halo_parts(tokens, ts)
    meet(dp, ts)
    sems = (core_send, core_recv, far_send, far_recv, z_send, z_recv)
    net = Scatter(dp, ts, [g_proj, g_fc, g_qkvo], g_local, in_core, in_far, in_z, sems)
    early = Total(dp, ts, small_ref, small_in, small_z, small_send, small_recv)
    late = Total(dp, ts, late_own, late_in, late_z, late_send, late_recv)
    stages = len(net.far) + 1
    zigzag = [t for pair in zip(range(ts // 2), range(ts - 1, ts // 2 - 1, -1)) for t in pair]
    for c in (0, 1):
        for t in zigzag:
            net.start(c, t)
    early.start()
    loads = weight_loads(qkvo_all, w_ref, g_qkvo, local_sem, ts)
    loads += [
        pltpu.make_async_copy(g.at[:, :, lax.rem(me, 2)], g_local.at[c], local_sem.at[2 * ts + c])
        for c, g in enumerate((g_proj, g_fc))
    ]
    for load in loads:
        load.start()

    def low_rows(i, c):
        rows = pl.ds(pl.multiple_of(i * KB, KB), KB)
        low = grad_hidden_ref[rows, :].astype(BF16)
        low_ref[rows, :] = low
        for n in range(pairs):
            low_t_ref[n * KB : (n + 1) * KB, rows] = low[:, n * KB : (n + 1) * KB].T
        return c

    lax.fori_loop(0, tokens // KB, low_rows, 0)
    for load in loads:
        load.wait()
    merge_pairs(w_ref, g_qkvo, ts)
    late_own[...] = jnp.zeros_like(late_own)
    gw_ref[...] = jnp.zeros_like(gw_ref)
    gh_ref[...] = jnp.zeros_like(gh_ref)

    turns = pairs + LAG
    order = list(range(ts, pairs)) + zigzag

    def pair_of(n):
        p = jnp.int32(order[0])
        for i in range(1, pairs):
            p = jnp.where(n == i, order[i], p)
        return p

    last = 4 * turns
    plan = {5: ["turn"], 9: ["end"], 4 * pairs + 3: ["final0", "final1"]}
    units = [(c, t) for c in (0, 1) for t in zigzag]
    for n, (c, t) in enumerate(units):
        for s in range(stages):
            plan.setdefault(2 * n + 1 + 3 * s, []).append((c, t, s))

    def after(slot):
        slot += 2
        return slot if slot < 4 * pairs else -(-(slot - 3) // 4) * 4 + 3 if slot < last else slot

    for i, t in enumerate(zigzag):
        at = 4 * (pairs - ts + i + LAG) + 3
        plan.setdefault(at, []).insert(0, (2, t, "start"))
        for s in range(stages):
            at = after(at) if at < last - 1 else max(at, last - 1) + 1
            plan.setdefault(at, []).append((2, t, s))

    def turned(block):
        pad = jnp.zeros((128 - block.shape[0], 128), F32)
        return jnp.concatenate([block, pad], axis=0).T[:, : block.shape[0]]

    def write_final(c):
        total = net.final(c)
        if c == 0:
            proj_out[...] = total
        elif c == 1:
            fc_out[...] = total
        else:
            for i in range(3):
                qkv_out[i, :, 0:128] = total[:, i * 128 : (i + 1) * 128]
                qkv_out[i, :, 128:192] = total[:, 512 + i * HD : 512 + (i + 1) * HD]
            out_out[0:128, :] = turned(total[:, 384:512])
            out_out[128:192, :] = turned(total[:, 640:768])[HD:, :]

    def at_lane(block, lane):
        return pltpu.roll(block, lax.rem(width - lane, width), 1)

    def write_small(block):
        rows = at_lane(block[0:8, :], me * (width // dp))
        for i, ref in enumerate((out_bias_out, gain_two_out, bias_two_out, proj_bias_out)):
            ref[...] = rows[i : i + 1, : width // dp]
        mine = block[4:5, :]
        for t in range(1, ts):
            mine = jnp.where(mt == t, block[4 + t : 5 + t, :], mine)
        mine = at_lane(jnp.broadcast_to(mine, (8, width)), me * (HD // dp))
        for i in range(width // HD):
            fc_bias_out[i : i + 1, :] = mine[0:1, i * HD : i * HD + HD // dp]
        count = vec_ref[0, 7:8, 384:385]
        for t in range(1, ts):
            count = count + vec_ref[t, 7:8, 384:385]
        loss_out[...] = block[4 + ts : 5 + ts, 0:1] / (width * count)

    def write_late(block):
        rows = at_lane(block, me * (width // dp))
        gain_one_out[...] = rows[0:1, : width // dp]
        bias_one_out[...] = rows[1:2, : width // dp]
        rows = at_lane(block, me * (HD // dp))
        for h in range(3):
            for i in range(2):
                value = None
                for t in range(ts):
                    lane = t * 128 + h * HD if h < 2 else ts * 128 + t * HD
                    here = rows[2 + i : 3 + i, lane : lane + HD // dp]
                    value = here if value is None else jnp.where(mt == t, here, value)
                qv_bias_out[h, i : i + 1, :] = value

    def run(items):
        for item in items:
            if item == "turn":
                early.turn()
            elif item == "end":
                write_small(early.end())
            elif item in ("final0", "final1"):
                write_final(int(item[-1]))
            elif item[2] == "start":
                net.start(item[0], item[1])
            else:
                net.step(*item)

    def steps_at(n, place):
        for slot, items in sorted(plan.items()):
            if slot % 4 == place and slot < (last if place == 3 else 4 * pairs):

                @pl.when(n == slot // 4)
                def _():
                    run(items)

    far = parts[1][1]
    near_at, cut = halo - tokens, tokens - far

    def hop(src, dst, n):
        return pltpu.make_async_remote_copy(
            src_ref=src,
            dst_ref=dst,
            send_sem=halo_send.at[n],
            recv_sem=halo_recv.at[n],
            device_id={"tensor": lax.rem(mt + ts - 1, ts)},
            device_id_type=MESH,
        )

    far_rows = hop(give_ref.at[pl.ds(near_at - far, far)], far_ref, 0)
    early_rows = hop(give_ref.at[pl.ds(near_at, cut)], take_ref.at[pl.ds(0, cut)], 1)
    late_rows = hop(give_ref.at[pl.ds(near_at + cut, far)], take_ref.at[pl.ds(cut, far)], 2)

    def attend_back(n):
        p = pair_of(n)
        cols = pl.ds(pl.multiple_of(p * 128, 128), 128)
        w_o = w_ref[p, :, :, 384:512].reshape(width, 128)
        rounded = mm(low_ref[...], w_o).astype(BF16)
        gm_ref[...] = rounded
        weighted = rounded.astype(F32).T * ot_ref[pl.ds(pl.multiple_of(p * 128, 128), 128), :]
        for h in range(2):
            delta_ref[h : h + 1, :] = jnp.sum(weighted[h * HD : (h + 1) * HD], axis=0, keepdims=True)

        def turn(i, c):
            rows = pl.ds(pl.multiple_of(i * KB, KB), KB)
            k, aux = k_ref[rows, cols], kseg_ref[rows, :]
            kt_ref[:, rows] = k.T
            ka_ref[0, rows, :] = lanes_of(k, aux)
            ka_ref[1, rows, :] = lanes_of(aux, k)
            dk_ref[rows, :] = jnp.zeros((KB, 128), F32)
            dv_ref[rows, :] = jnp.zeros((KB, 128), F32)
            return c

        lax.fori_loop(0, (halo + tokens) // KB, turn, 0)
        steps_at(n, 0)

        def one_block(j, c):
            base = j * QB
            at = pl.ds(pl.multiple_of(base, QB), QB)
            q_block, aux, do_block = q_ref[at, cols], qseg_ref[at, :], gm_ref[at, :]
            asks = [lanes_of(q_block, aux), lanes_of(aux, q_block)]
            q_cat = jnp.concatenate([keep_lanes(q_block, h) for h in range(2)], axis=0)
            do_cat = jnp.concatenate([keep_lanes(do_block, h) for h in range(2)], axis=0)
            lse = [lse_ref[p, h : h + 1, at] for h in range(2)]
            delta = [delta_ref[h : h + 1, at] for h in range(2)]
            dq_t = [jnp.zeros((HD, QB), F32) for h in range(2)]
            for row, size in CHUNKS:
                span = pl.ds(pl.multiple_of(base + row, 16), size)
                values = v_ref[span, cols]
                ps, dss = [], []
                for h in range(2):
                    s = causal(mm(ka_ref[h, span, :], asks[h], NT), row)
                    e = jnp.exp2(s - lse[h])
                    grad_e = mm(values, do_cat[h * QB : (h + 1) * QB], NT)
                    ds = (e * (grad_e - delta[h])).astype(BF16)
                    wide = pl.ds(pl.multiple_of(base + row // KB * KB, KB), KB)
                    tall = ds
                    if size < KB:
                        tall = jnp.concatenate([jnp.zeros((KB - size, QB), BF16), ds], axis=0)
                    dq_t[h] = dq_t[h] + mm(kt_ref[h * HD : (h + 1) * HD, wide], tall)
                    ps.append(e.astype(BF16))
                    dss.append(ds)
                dv_ref[span, :] += mm(jnp.concatenate(ps, axis=1), do_cat)
                dk_ref[span, :] += mm(jnp.concatenate(dss, axis=1), q_cat)
            dqkv_ref[n, at, 0:128] = (jnp.concatenate(dq_t, axis=0) * 0.125).T.astype(BF16)
            for place in range(tokens // QB):

                @pl.when(j == place)
                def _():
                    steps_at(n, 1 + place)
            return c

        lax.fori_loop(0, tokens // QB, one_block, 0)

        dkv_ref[n, :, 0:128] = (dk_ref[:halo, :] * (0.125 / Q_SCALE)).astype(BF16)
        dkv_ref[n, :, 128:256] = dv_ref[:halo, :].astype(BF16)
        dqkv_ref[n, :, 128:256] = (dk_ref[halo:, :] * (0.125 / Q_SCALE)).astype(BF16)
        dqkv_ref[n, :, 256:384] = dv_ref[halo:, :].astype(BF16)

        def halo_grad(i, c):
            rows = pl.ds(pl.multiple_of(i * (halo // 2), 16), halo // 2)
            gh_ref[rows, :] += mm(dkv_ref[n, rows, :], w_ref[p, :, :, 128:384].reshape(width, 256), NT)
            return c

        lax.fori_loop(0, 2, halo_grad, 0)

        @pl.when(n == pairs - 1)
        def _():
            give_ref[: near_at + cut, :] = gh_ref[: near_at + cut, :].astype(BF16)

            @pl.when(mt >= 2)
            def _():
                far_rows.start()

            @pl.when(mt >= 1)
            def _():
                early_rows.start()

    def store(tile, value, t):
        g_qkvo[t, :, :, tile * 128 : (tile + 1) * 128] = value.astype(BF16).reshape(dp, -1, 128)

    def weights_back(n):
        p = pair_of(n)
        cols = pl.ds(pl.multiple_of(p * 128, 128), 128)
        grad_o = mm(low_t_ref[...], mixed_ref[:, cols])
        dqkv = dqkv_ref[n]
        own = mm(normed_t_ref[:, halo:], dqkv)
        far = mm(normed_t_ref[:, :halo], dkv_ref[n])
        four = [own[:, 0:128], own[:, 128:256] + far[:, 0:128], own[:, 256:384] + far[:, 128:256], grad_o]

        @pl.when(p < ts)
        def _():
            for i, g in enumerate(four):
                store(i, g, p)

        for a in range(pairs - ts):

            @pl.when(p == ts + a)
            def _():
                for i in range(2):
                    low_half, high_half = four[2 * i], four[2 * i + 1]
                    store(4 + i, lanes_of(low_half, swap_halves(high_half)), 2 * a)
                    store(4 + i, lanes_of(swap_halves(low_half), high_half), 2 * a + 1)

        gw_ref[...] += mm(dqkv, w_ref[p, :, :, 0:384].reshape(width, 384), NT)
        grad_v = jnp.sum(dqkv[:, 256:384].astype(F32), axis=0, keepdims=True)
        late_own[2:3, cols] = jnp.sum(dqkv[:, 0:128].astype(F32), axis=0, keepdims=True)
        late_own[3:4, cols] = grad_v + jnp.sum(dkv_ref[n, :, 128:256].astype(F32), axis=0, keepdims=True)

    def one_turn(n, carry):
        @pl.when(n < pairs)
        def _():
            attend_back(n)

        @pl.when(n >= LAG)
        def _():
            weights_back(n - LAG)

        steps_at(n, 3)
        return carry

    lax.fori_loop(0, turns, one_turn, 0)

    def halo_sums(i, carry):
        rows = pl.ds(pl.multiple_of(i * KB, KB), KB)
        unit, _ = normalize(halo_ref[rows, :].astype(F32))
        g = gh_ref[rows, :]
        return carry[0] + fold_rows(g * unit, jnp.sum), carry[1] + fold_rows(g, jnp.sum)

    def own_sums(i, carry):
        rows = pl.ds(pl.multiple_of(i * KB, KB), KB)
        unit, _ = normalize(x_ref[rows, :].astype(F32))
        g = gw_ref[rows, :]
        return carry[0] + fold_rows(g * unit, jnp.sum), carry[1] + fold_rows(g, jnp.sum)

    zero = jnp.zeros((8, width), F32)
    carry = lax.fori_loop(0, halo // KB, halo_sums, (zero, zero))
    passed = (mt >= 1) & (mt + 1 < ts)

    @pl.when(passed)
    def _():
        far_rows.wait_recv()
        gh_ref[near_at + cut :, :] += far_ref[...].astype(F32)

    @pl.when(mt >= 1)
    def _():
        give_ref[near_at + cut :, :] = gh_ref[near_at + cut :, :].astype(BF16)
        late_rows.start()

    tail = [item for slot, items in sorted(plan.items()) if slot >= last for item in items]
    first = [item for item in tail if item[2] == 0] + [item for item in tail if item[1] == zigzag[-3]]
    tail = [item for item in tail if item not in first]
    run(first)
    gains, shifts = lax.fori_loop(0, tokens // KB, own_sums, carry)
    late_own[0:1, :] = jnp.sum(gains, axis=0, keepdims=True)
    late_own[1:2, :] = jnp.sum(shifts, axis=0, keepdims=True)
    late.start()
    tail.sort(key=lambda item: (item[2], -zigzag.index(item[1])))
    run(tail[:1])
    late.turn()
    run(tail[1:])

    @pl.when(mt + 1 < ts)
    def _():
        early_rows.wait_recv()
        late_rows.wait_recv()
        gw_ref[...] += take_ref[...].astype(F32)

    def own_grad(i, carry):
        rows = pl.ds(pl.multiple_of(i * KB, KB), KB)
        unit, scaler = normalize(x_ref[rows, :].astype(F32))
        g = gw_ref[rows, :]
        input_grad_ref[rows, :] = grad_hidden_ref[rows, :] + norm_back(g, vec_ref[0, 0:1, :], unit, scaler)
        return carry

    lax.fori_loop(0, tokens // KB, own_grad, 0)
    write_late(late.end())
    write_final(2)
    early.finish()
    late.finish()

    @pl.when(mt >= 2)
    def _():
        far_rows.wait_send()

    @pl.when(mt >= 1)
    def _():
        early_rows.wait_send()
        late_rows.wait_send()

    net.finish()


def back(x, halo_x, vec, kseg, qseg, normed_t, q, k, v, ot, lse, mixed, grad_hidden, small, g_proj, g_fc, qkvo_all):
    tokens, width = x.shape
    halo = halo_x.shape[0]
    window = halo + tokens
    ts, dp, rows = qkvo_all.shape[:3]
    pairs = width // 128
    n_far = dp // 2 - 1
    any_spec = pl.BlockSpec(memory_space=pl.ANY)
    vmem = pl.BlockSpec(memory_space=pltpu.VMEM)
    s = jax.ShapeDtypeStruct
    dma = pltpu.SemaphoreType.DMA
    return pl.pallas_call(
        functools.partial(back_kernel, dp, ts),
        out_shape=[
            s((tokens, width), F32),
            s((1, 1), F32),
            s((1, rows), F32),
            s((1, rows), F32),
            s((3, rows, 3 * HD), F32),
            s((3, 2, HD // dp), F32),
            s((3 * HD, rows), F32),
            s((1, rows), F32),
            s((1, rows), F32),
            s((1, rows), F32),
            s((rows, width), F32),
            s((width // HD, HD // dp), F32),
            s((rows, width), F32),
            s((1, rows), F32),
        ],
        in_specs=[vmem] * 14 + [any_spec] * 3,
        out_specs=[vmem] * 14,
        scratch_shapes=[
            pltpu.VMEM((pairs, dp, rows, 512), BF16),
            pltpu.VMEM((ts, dp, rows, width), BF16),
            pltpu.VMEM((tokens, width), BF16),
            pltpu.VMEM((width, tokens), BF16),
            pltpu.VMEM((2, window, 128), BF16),
            pltpu.VMEM((128, window), BF16),
            pltpu.VMEM((window, 128), F32),
            pltpu.VMEM((window, 128), F32),
            pltpu.VMEM((tokens, 128), BF16),
            pltpu.VMEM((8, tokens), F32),
            pltpu.VMEM((pairs, tokens, 384), BF16),
            pltpu.VMEM((pairs, halo, 256), BF16),
            pltpu.VMEM((halo, width), BF16),
            pltpu.VMEM((tokens, width), BF16),
            pltpu.VMEM((halo_parts(tokens, ts)[1][1], width), BF16),
            pltpu.VMEM((halo, width), F32),
            pltpu.VMEM((tokens, width), F32),
            pltpu.VMEM((2, ts, dp // 2, rows, width), BF16),
            pltpu.VMEM((dp,) + small.shape, F32),
            pltpu.VMEM((ts,) + small.shape, F32),
            pltpu.VMEM((8, width), F32),
            pltpu.VMEM((dp, 8, width), F32),
            pltpu.VMEM((ts, 8, width), F32),
            pltpu.VMEM((3, ts, dp // 2, rows, width), BF16),
            pltpu.VMEM((3, ts, n_far, rows, width), BF16),
            pltpu.VMEM((3, ts - 1, rows, width), BF16),
            dma((2 * ts + 2,)),
            dma((3, ts, dp // 2)),
            dma((3, ts, dp // 2)),
            dma((3, ts, n_far)),
            dma((3, ts, n_far)),
            dma((3, ts)),
            dma((3, ts - 1)),
            dma((3,)),
            dma((3,)),
            dma((dp + ts,)),
            dma((dp + ts,)),
            dma((dp + ts,)),
            dma((dp + ts,)),
        ],
        compiler_params=pltpu.CompilerParams(
            collective_id=2, has_side_effects=True, vmem_limit_bytes=63 << 20
        ),
        name="back",
    )(x, halo_x, vec, kseg, qseg, normed_t, q, k, v, ot, lse, mixed, grad_hidden, small, g_proj, g_fc, qkvo_all)


def gather_kernel(dp, ts, tokens, n_in, *refs):
    w_refs, (x_ref, seg_ref) = refs[:n_in], refs[n_in : n_in + 2]
    outs = refs[n_in + 2 : 2 * n_in + 2]
    halo_ref, hseg_ref = refs[2 * n_in + 2 : 2 * n_in + 4]
    local_sem, send_sem, recv_sem, halo_send, halo_recv = refs[2 * n_in + 4 :]
    me = lax.axis_index("dp")
    mt = lax.axis_index("tensor")
    bits = [1 << k for k in range(dp.bit_length() - 1)]
    far = bits[1:]
    halo_ref[...] = jnp.zeros_like(halo_ref)
    hseg_ref[...] = jnp.full_like(hseg_ref, -1)
    barrier = pltpu.get_barrier_semaphore()
    peers_t = [lax.rem(mt + k, ts) for k in range(1, ts)]
    for t in peers_t:
        pl.semaphore_signal(barrier, inc=1, device_id={"tensor": t}, device_id_type=MESH)
    for b in bits:
        pl.semaphore_signal(barrier, inc=1, device_id={"dp": me ^ b}, device_id_type=MESH)
    pl.semaphore_wait(barrier, len(peers_t) + len(bits))
    started = []

    def rcopy(src, dst, dev):
        i = len(started)
        c = pltpu.make_async_remote_copy(
            src_ref=src,
            dst_ref=dst,
            send_sem=send_sem.at[i],
            recv_sem=recv_sem.at[i],
            device_id=dev,
            device_id_type=MESH,
        )
        c.start()
        started.append(c)
        return c

    locals_, over_z = [], []
    for c in range(n_in):
        copy = pltpu.make_async_copy(w_refs[c], outs[c].at[mt, me], local_sem.at[c])
        copy.start()
        locals_.append(copy)
        over_z.append([rcopy(w_refs[c], outs[c].at[mt, me], {"tensor": t}) for t in peers_t])
        if c == min(1, n_in - 1):
            end = halo_ref.shape[0]
            halos = []
            for i, (back, count) in enumerate(halo_parts(tokens, ts)):
                end -= count
                pair = [
                    pltpu.make_async_remote_copy(
                        src_ref=src,
                        dst_ref=dst,
                        send_sem=halo_send.at[2 * i + k],
                        recv_sem=halo_recv.at[2 * i + k],
                        device_id={"tensor": lax.rem(mt + back, ts)},
                        device_id_type=MESH,
                    )
                    for k, (src, dst) in enumerate(
                        [
                            (x_ref.at[pl.ds(tokens - count, count)], halo_ref.at[pl.ds(end, count)]),
                            (seg_ref, hseg_ref.at[i]),
                        ]
                    )
                ]
                halos.append((back, pair))

                @pl.when(mt + back < ts)
                def _():
                    for h in pair:
                        h.start()

    half = max(ts // 2, 1)
    groups = [(0, half, far)] + ([(half, ts - half, far[::-1])] if ts > half else [])

    def spread(c, group, masks, later):
        res = {}
        for b in later + [1]:
            res[b] = []
            for m in masks:
                ref = outs[c].at[pl.ds(group[0], group[1]), me ^ m]
                res[b].append((m, rcopy(ref, ref, {"dp": me ^ b})))
        return res

    stages = len(far) + 1
    pending = {}
    for step in range(n_in + stages - 1):
        for s in range(stages):
            c = step - s
            if not 0 <= c < n_in:
                continue
            if s == 0:
                locals_[c].wait()
                for k in over_z[c]:
                    k.wait_recv()
            for gi, group in enumerate(groups):
                if s == 0:
                    pending[c, gi] = [spread(c, group, [0], group[2])]
                else:
                    b = group[2][s - 1]
                    masks = []
                    for res in pending[c, gi]:
                        for m, k in res.get(b, []):
                            k.wait_recv()
                            masks.append(m ^ b)
                    pending[c, gi].append(spread(c, group, masks, group[2][s:]))
    for c in range(n_in):
        for gi in range(len(groups)):
            for res in pending[c, gi]:
                for m, k in res[1]:
                    k.wait_recv()
    for back, pair in halos:

        @pl.when(mt >= back)
        def _():
            for h in pair:
                h.wait_recv()

        @pl.when(mt + back < ts)
        def _():
            for h in pair:
                h.wait_send()

    for k in started:
        k.wait_send()


def gather(parts, x, seg, dp, ts, halo):
    n_in = len(parts)
    tokens = x.shape[0]
    copies = n_in * ((ts - 1) + (2 if ts > 1 else 1) * (dp - 1))
    n_halo = len(halo_parts(tokens, ts))
    any_spec = pl.BlockSpec(memory_space=pl.ANY)
    vmem = pl.BlockSpec(memory_space=pltpu.VMEM)
    return pl.pallas_call(
        functools.partial(gather_kernel, dp, ts, tokens, n_in),
        out_shape=[jax.ShapeDtypeStruct((ts, dp) + p.shape, p.dtype) for p in parts]
        + [
            jax.ShapeDtypeStruct((halo, x.shape[1]), x.dtype),
            jax.ShapeDtypeStruct((n_halo,) + seg.shape, seg.dtype),
        ],
        in_specs=[any_spec] * (n_in + 2),
        out_specs=[any_spec] * n_in + [vmem, vmem],
        scratch_shapes=[
            pltpu.SemaphoreType.DMA((n_in,)),
            pltpu.SemaphoreType.DMA((copies,)),
            pltpu.SemaphoreType.DMA((copies,)),
            pltpu.SemaphoreType.DMA((2 * n_halo,)),
            pltpu.SemaphoreType.DMA((2 * n_halo,)),
        ],
        compiler_params=pltpu.CompilerParams(collective_id=1, has_side_effects=True),
        name="gather",
    )(*parts, x, seg)


def reduce_kernel(dp, ts, g_ref, out_ref, in_core, in_far, in_z, send_sem, recv_sem):
    n_c = g_ref.shape[0]
    me = lax.axis_index("dp")
    mt = lax.axis_index("tensor")
    bits = [1 << k for k in range(dp.bit_length() - 1)]
    far = bits[1:]
    barrier = pltpu.get_barrier_semaphore()
    peers_t = [lax.rem(mt + k, ts) for k in range(1, ts)]
    for t in peers_t:
        pl.semaphore_signal(barrier, inc=1, device_id={"tensor": t}, device_id_type=MESH)
    for b in bits:
        pl.semaphore_signal(barrier, inc=1, device_id={"dp": me ^ b}, device_id_type=MESH)
    pl.semaphore_wait(barrier, len(peers_t) + len(bits))
    started = []

    def rcopy(src, dst, dev):
        i = len(started)
        c = pltpu.make_async_remote_copy(
            src_ref=src,
            dst_ref=dst,
            send_sem=send_sem.at[i],
            recv_sem=recv_sem.at[i],
            device_id=dev,
            device_id_type=MESH,
        )
        c.start()
        started.append(c)
        return c

    half = max(ts // 2, 1)
    groups = [(0, half, far[::-1])] + ([(half, ts - half, far)] if ts > half else [])
    evens = list(range(0, dp, 2))
    core = []
    for c in range(n_c):
        core.append(
            {
                m: rcopy(g_ref.at[c, :, me ^ 1 ^ m], in_core.at[c, m >> 1], {"dp": me ^ 1})
                for m in evens[::-1]
            }
        )

    def add_into(dst, src, base, count):
        def one(i, carry):
            dst[base + i] = (dst[base + i].astype(F32) + src[i].astype(F32)).astype(BF16)
            return carry

        lax.fori_loop(0, count, one, 0)

    stages = len(far) + 2
    pending = {}
    slots = {}
    for step in range(n_c + stages - 1):
        for s in range(stages):
            c = step - s
            if not 0 <= c < n_c:
                continue
            if s == 0:
                for m in evens[::-1]:
                    core[c][m].wait_recv()

                    def one(i, carry, m=m):
                        in_core[c, m >> 1, i] = (
                            in_core[c, m >> 1, i].astype(F32) + g_ref[c, i, me ^ m].astype(F32)
                        ).astype(BF16)
                        return carry

                    lax.fori_loop(0, ts, one, 0)
            for gi, (t0, tn, order) in enumerate(groups):
                if s > 0:
                    for m, slot, k in pending.pop((c, gi)):
                        k.wait_recv()
                        add_into(in_core.at[c, m >> 1], in_far.at[c, slot, pl.ds(t0, tn)], t0, tn)
                if s < len(far):
                    b = order[s]
                    done = sum(order[:s])
                    masks = [m for m in evens if m & b and not m & done]
                    sent = []
                    for m in masks:
                        slot = slots.get((c, gi), 0)
                        slots[c, gi] = slot + 1
                        k = rcopy(
                            in_core.at[c, m >> 1, pl.ds(t0, tn)],
                            in_far.at[c, slot, pl.ds(t0, tn)],
                            {"dp": me ^ b},
                        )
                        sent.append((m ^ b, slot, k))
                    pending[c, gi] = sent
                elif s == len(far):
                    pending[c, gi] = []
            if s == len(far):
                pending[c, "z"] = [
                    rcopy(in_core.at[c, 0, lax.rem(mt + k, ts)], in_z.at[c, k - 1], {"tensor": lax.rem(mt + k, ts)})
                    for k in range(1, ts)
                ]
            if s == len(far) + 1:
                total = in_core[c, 0, mt].astype(F32)
                for k in pending[c, "z"]:
                    k.wait_recv()
                for k in range(ts - 1):
                    total = total + in_z[c, k].astype(F32)
                out_ref[c] = total
    for k in started:
        k.wait_send()


def reduce(grads, dp, ts):
    n_c, _, _, rows, width = grads.shape
    n_far = dp // 2 - 1
    groups = 2 if ts > 1 else 1
    copies = n_c * (dp // 2 + groups * n_far + ts - 1)
    vmem = pl.BlockSpec(memory_space=pltpu.VMEM)
    return pl.pallas_call(
        functools.partial(reduce_kernel, dp, ts),
        out_shape=jax.ShapeDtypeStruct((n_c, rows, width), F32),
        in_specs=[vmem],
        out_specs=vmem,
        scratch_shapes=[
            pltpu.VMEM((n_c, dp // 2, ts, rows, width), BF16),
            pltpu.VMEM((n_c, n_far, ts, rows, width), BF16),
            pltpu.VMEM((n_c, ts - 1, rows, width), BF16),
            pltpu.SemaphoreType.DMA((copies,)),
            pltpu.SemaphoreType.DMA((copies,)),
        ],
        compiler_params=pltpu.CompilerParams(
            collective_id=2, has_side_effects=True, vmem_limit_bytes=62 << 20
        ),
        name="reduce",
    )(grads)


def allowed_at(chunk, doc_row, first_q):
    key = chunk * KB + lax.broadcasted_iota(jnp.int32, (KB, QB), 0)
    query = first_q + lax.broadcasted_iota(jnp.int32, (KB, QB), 1)
    return (key >= doc_row) & (key <= query)


def attend_kernel(halo, first_ref, doc_ref, q_ref, k_ref, vt_ref, o_ref, lse_ref, s_ref):
    for j in range(q_ref.shape[0] // QB):
        rows = pl.ds(j * QB, QB)
        q_block = q_ref[rows, :]
        queries = [keep_lanes(q_block, h) for h in range(2)]
        doc_row = doc_ref[0:1, rows]
        first_q = halo + j * QB
        begin = first_ref[j]
        end = (first_q + QB) // KB

        def score(c, tops):
            keys = k_ref[pl.ds(pl.multiple_of(c * KB, KB), KB), :]
            ok = allowed_at(c, doc_row, first_q)
            res = []
            for h in range(2):
                s = jnp.where(ok, mm(keys, queries[h], NT), -1e30)
                s_ref[h, c] = s
                res.append(jnp.maximum(tops[h], fold_rows(s, jnp.max)))
            return tuple(res)

        tops = lax.fori_loop(begin, end, score, (jnp.full((8, QB), -1e30, F32),) * 2)
        tops = [jnp.max(t, axis=0, keepdims=True) for t in tops]

        def mix(c, carry):
            res = []
            for h in range(2):
                total, acc = carry[h]
                p = jnp.exp(s_ref[h, c] - tops[h])
                total = total + fold_rows(p, jnp.sum)
                vt = vt_ref[pl.ds(h * HD, HD), pl.ds(pl.multiple_of(c * KB, KB), KB)]
                acc = acc + mm(vt, p.astype(BF16))
                res.append((total, acc))
            return tuple(res)

        carry = lax.fori_loop(
            begin, end, mix, ((jnp.zeros((8, QB), F32), jnp.zeros((HD, QB), F32)),) * 2
        )
        for h in range(2):
            total = jnp.sum(carry[h][0], axis=0, keepdims=True)
            o_ref[pl.ds(h * HD, HD), rows] = carry[h][1] / total
            lse_ref[0, h : h + 1, rows] = tops[h] + jnp.log(total)


def attend(first, doc, q, k, vt, halo):
    tokens, width = q.shape
    keys = k.shape[0]
    pairs = width // 128
    return pl.pallas_call(
        functools.partial(attend_kernel, halo),
        out_shape=[
            jax.ShapeDtypeStruct((width, tokens), F32),
            jax.ShapeDtypeStruct((pairs, 2, tokens), F32),
        ],
        grid_spec=pltpu.PrefetchScalarGridSpec(
            num_scalar_prefetch=1,
            grid=(pairs,),
            in_specs=[
                pl.BlockSpec((1, tokens), lambda p, f: (0, 0)),
                pl.BlockSpec((tokens, 128), lambda p, f: (0, p)),
                pl.BlockSpec((keys, 128), lambda p, f: (0, p)),
                pl.BlockSpec((128, keys), lambda p, f: (p, 0)),
            ],
            out_specs=[
                pl.BlockSpec((128, tokens), lambda p, f: (p, 0)),
                pl.BlockSpec((1, 2, tokens), lambda p, f: (p, 0, 0)),
            ],
            scratch_shapes=[pltpu.VMEM((2, keys // KB, KB, QB), F32)],
        ),
        name="attend",
    )(first, doc, q, k, vt)


def attend_back_kernel(
    halo, first_ref, doc_ref, q_ref, k_ref, kt_ref, v_ref, do_ref, lse_ref, delta_ref, dq_ref, dk_ref, dv_ref
):
    dk_ref[...] = jnp.zeros_like(dk_ref)
    dv_ref[...] = jnp.zeros_like(dv_ref)
    for j in range(q_ref.shape[0] // QB):
        rows = pl.ds(j * QB, QB)
        q_block, do_block = q_ref[rows, :], do_ref[rows, :]
        queries = [keep_lanes(q_block, h) for h in range(2)]
        grads = [keep_lanes(do_block, h) for h in range(2)]
        doc_row = doc_ref[0:1, rows]
        first_q = halo + j * QB

        def step(c, carry):
            span = pl.ds(pl.multiple_of(c * KB, KB), KB)
            keys, values = k_ref[span, :], v_ref[span, :]
            ok = allowed_at(c, doc_row, first_q)
            res = []
            grad_k = grad_v = None
            for h in range(2):
                s = jnp.where(ok, mm(keys, queries[h], NT), -1e30)
                p = jnp.exp(s - lse_ref[0, h : h + 1, rows])
                dp_ = mm(values, grads[h], NT)
                ds = (p * (dp_ - delta_ref[0, h : h + 1, rows])).astype(BF16)
                gv = mm(p.astype(BF16), grads[h])
                gk = mm(ds, queries[h])
                grad_v = gv if grad_v is None else grad_v + gv
                grad_k = gk if grad_k is None else grad_k + gk
                kt = kt_ref[pl.ds(h * HD, HD), span]
                res.append(carry[h] + mm(kt, ds))
            dk_ref[span, :] += grad_k
            dv_ref[span, :] += grad_v
            return tuple(res)

        carry = lax.fori_loop(
            first_ref[j], (first_q + QB) // KB, step, (jnp.zeros((HD, QB), F32),) * 2
        )
        for h in range(2):
            dq_ref[pl.ds(h * HD, HD), rows] = carry[h] * 0.125


def attend_back(first, doc, q, k, kt, v, do, lse, delta, halo):
    tokens, width = q.shape
    keys = k.shape[0]
    pairs = width // 128
    q_spec = pl.BlockSpec((tokens, 128), lambda p, f: (0, p))
    k_spec = pl.BlockSpec((keys, 128), lambda p, f: (0, p))
    stat = pl.BlockSpec((1, 2, tokens), lambda p, f: (p, 0, 0))
    return pl.pallas_call(
        functools.partial(attend_back_kernel, halo),
        out_shape=[
            jax.ShapeDtypeStruct((width, tokens), F32),
            jax.ShapeDtypeStruct((keys, width), F32),
            jax.ShapeDtypeStruct((keys, width), F32),
        ],
        grid_spec=pltpu.PrefetchScalarGridSpec(
            num_scalar_prefetch=1,
            grid=(pairs,),
            in_specs=[
                pl.BlockSpec((1, tokens), lambda p, f: (0, 0)),
                q_spec,
                k_spec,
                pl.BlockSpec((128, keys), lambda p, f: (p, 0)),
                k_spec,
                q_spec,
                stat,
                stat,
            ],
            out_specs=[pl.BlockSpec((128, tokens), lambda p, f: (p, 0)), k_spec, k_spec],
        ),
        name="attend_back",
    )(first, doc, q, k, kt, v, do, lse, delta)


def gelu_tanh(values_in):
    return (
        0.5
        * values_in
        * (
            1.0
            + jnp.tanh(TANH_SLOPE * (values_in + CUBIC_TERM * values_in * values_in * values_in))
        )
    )


def plain_device(
    block_input,
    teacher,
    segment_ids,
    valid_mask,
    ln1_gain,
    ln1_bias,
    qkv_weight,
    qv_bias,
    out_weight,
    out_bias,
    ln2_gain,
    ln2_bias,
    fc_weight,
    fc_bias,
    proj_weight,
    proj_bias,
):
    dp, ts = lax.axis_size("dp"), lax.axis_size("tensor")
    me, mt = lax.axis_index("dp"), lax.axis_index("tensor")
    tokens, width = block_input.shape[1:]
    total_tokens = tokens * ts * dp
    halo = -(-(DOC_MOST - 1) // KB) * KB
    e = qkv_weight.shape[2]
    x = block_input[0]
    valid_rows = valid_mask[0].astype(F32)

    qkvo = jnp.concatenate([qkv_weight[0], qkv_weight[1], qkv_weight[2], out_weight.T], axis=1)
    local_count = jnp.sum(valid_mask[0])
    mine = jnp.arange(dp) == me

    def spread(v):
        return jnp.where(mine[:, None], v[..., None, :], jnp.zeros((), v.dtype))

    vectors = jnp.stack([ln1_gain, ln1_bias, out_bias, ln2_gain, ln2_bias, proj_bias])
    tail = jnp.stack([local_count // 16, local_count % 16]).astype(BF16)
    small = jnp.concatenate(
        [
            spread(vectors).reshape(6, width),
            spread(fc_bias).reshape(1, -1),
            jnp.concatenate(
                [spread(qv_bias).reshape(-1), tail, jnp.zeros((width - 2 * e - 2,), BF16)]
            )[None],
        ]
    )
    seg_rows = jnp.broadcast_to(segment_ids, (8, tokens))
    small_all, w_qkvo, w_fc, w_proj, x_halo, seg_halo = gather(
        [small, qkvo, fc_weight, proj_weight.T], x, seg_rows, dp, ts, halo
    )
    small_all = jnp.sum(small_all.astype(F32), axis=1)
    gain_one, bias_one, b_out, gain_two, bias_two, b_proj = [small_all[0, i] for i in range(6)]
    b_fc = small_all[:, 6].reshape(-1)
    b_q = small_all[:, 7, :e].reshape(-1)
    b_v = small_all[:, 7, e : 2 * e].reshape(-1)
    valid_count = jnp.sum(small_all[:, 7, 2 * e] * 16 + small_all[:, 7, 2 * e + 1])
    w_qkvo = w_qkvo.reshape(ts, width, 4, e)
    wq, wk, wv, wo = [w_qkvo[:, :, i].transpose(1, 0, 2).reshape(width, width) for i in range(4)]
    wf = w_fc.reshape(ts, width, -1)
    wp = w_proj.reshape(ts, width, -1)

    seg = segment_ids[0]
    pieces = []
    for i, (back, count) in enumerate(halo_parts(tokens, ts)):
        pieces.insert(0, seg_halo[i, 0, tokens - count :])
    filled = sum(p.shape[0] for p in pieces)
    seg_window = jnp.concatenate([jnp.full((halo - filled,), -1, jnp.int32)] + pieces)
    position = jnp.sum((seg_window[:, None] < seg[None, :]).astype(jnp.int32), axis=0)
    own = jnp.sum((seg[:, None] < seg[None, :]).astype(jnp.int32), axis=0)
    doc = (position + own)[None]
    first = doc[0, ::QB] // KB

    inputs = x.astype(F32)
    window = jnp.concatenate([x_halo, x]).astype(F32)
    unit_window, scale_window = normalize(window)
    normed_window = (unit_window * gain_one + bias_one).astype(BF16)
    unit_one, scale_one = unit_window[halo:], scale_window[halo:]
    normed_one = normed_window[halo:]
    q = ((mm(normed_one, wq) + b_q).astype(BF16) * 0.125).astype(BF16)
    k = mm(normed_window, wk).astype(BF16)
    v = (mm(normed_window, wv) + b_v).astype(BF16)
    mixed_t, lse = attend(first, doc, q, k, v.T, halo)
    mixed = mixed_t.T.astype(BF16)
    hidden = inputs + mm(mixed, wo, NT) + b_out
    unit_two, scale_two = normalize(hidden)
    normed_two = (unit_two * gain_two + bias_two).astype(BF16)
    pre_act = jnp.einsum("sd,tdf->stf", normed_two, wf, preferred_element_type=F32) + b_fc.reshape(ts, -1)
    activated = gelu_tanh(pre_act).astype(BF16)
    output = hidden + jnp.einsum("stf,tdf->sd", activated, wp, preferred_element_type=F32) + b_proj
    residual_error = output - teacher[0].astype(F32)
    squares = jnp.sum(valid_rows[:, None] * residual_error * residual_error)
    grad_output = valid_rows[:, None] * residual_error * (total_tokens / valid_count)
    low_output = grad_output.astype(BF16)
    grad_act = jnp.einsum("sd,tdf->stf", low_output, wp, preferred_element_type=F32)
    grad_proj_w = jnp.einsum("sd,stf->tdf", low_output, activated, preferred_element_type=F32)
    _, gelu_back = jax.vjp(gelu_tanh, pre_act)
    grad_pre = gelu_back(grad_act)[0].astype(BF16)
    grad_fc_w = jnp.einsum("sd,stf->tdf", normed_two, grad_pre, preferred_element_type=F32)
    grad_fc_b = jnp.sum(grad_pre, axis=0, dtype=F32)
    grad_normed_two = jnp.einsum("stf,tdf->sd", grad_pre, wf, preferred_element_type=F32)
    grad_gain_two = jnp.sum(grad_normed_two * unit_two, axis=0)
    grad_bias_two = jnp.sum(grad_normed_two, axis=0)
    grad_hidden = grad_output + norm_back(grad_normed_two, gain_two, unit_two, scale_two)
    low_hidden = grad_hidden.astype(BF16)
    grad_mixed = mm(low_hidden, wo).astype(BF16)
    grad_out_w = jnp.einsum("sd,se->de", low_hidden, mixed, preferred_element_type=F32)
    heads = width // HD
    delta = jnp.sum((grad_mixed.T.astype(F32) * mixed_t).reshape(heads // 2, 2, HD, tokens), axis=2)
    dq_t, dk, dv = attend_back(first, doc, q, k, k.T, v, grad_mixed, lse, delta, halo)
    dq, dk, dv = dq_t.T.astype(BF16), dk.astype(BF16), dv.astype(BF16)
    sd_se = lambda a, b: jnp.einsum("sd,se->de", a, b, preferred_element_type=F32)
    g_q, g_k, g_v = sd_se(normed_one, dq), sd_se(normed_window, dk), sd_se(normed_window, dv)
    grad_window = mm(dk, wk, NT) + mm(dv, wv, NT)
    grad_normed_one = grad_window[halo:] + mm(dq, wq, NT)
    end = halo
    for back, count in halo_parts(tokens, ts):
        end -= count
        part = lax.ppermute(
            grad_window[end : end + count].astype(BF16), "tensor", [(t, t - back) for t in range(back, ts)]
        )
        grad_normed_one = grad_normed_one.at[tokens - count :].add(part.astype(F32))
    grad_input = grad_hidden + norm_back(grad_normed_one, gain_one, unit_one, scale_one)

    def by_t(g):
        return g.reshape(width, ts, e)

    g_qkvo = jnp.stack([by_t(g_q), by_t(g_k), by_t(g_v), by_t(grad_out_w)], axis=2)
    g_qkvo = g_qkvo.transpose(1, 0, 2, 3).reshape(ts, width, 4 * e)
    grads = jnp.stack([grad_proj_w, grad_fc_w, g_qkvo]).astype(BF16)
    grads = grads.reshape(3, ts, dp, width // dp, -1)
    r_proj, r_fc, r_qkvo = reduce(grads, dp, ts)
    smalls = [
        jnp.sum(grad_normed_one * unit_one, axis=0),
        jnp.sum(grad_normed_one, axis=0),
        jnp.sum(grad_hidden, axis=0),
        grad_gain_two,
        grad_bias_two,
        jnp.sum(grad_output, axis=0),
        grad_fc_b.reshape(-1),
        jnp.sum(dq, axis=0, dtype=F32),
        jnp.sum(dv, axis=0, dtype=F32),
        squares[None],
    ]
    summed = lax.psum(jnp.concatenate(smalls), ("dp", "tensor"))
    rows = width // dp
    own_rows = lambda i: lax.dynamic_slice_in_dim(summed, i * width + me * rows, rows)
    fc_b = summed[6 * width : 6 * width + fc_bias.size * dp * ts].reshape(ts, -1, dp, fc_bias.shape[1])
    qv0 = 6 * width + fc_bias.size * dp * ts
    qv_b = summed[qv0 : qv0 + 2 * width].reshape(2, ts, -1, dp, qv_bias.shape[2])
    loss = summed[-1] / (width * valid_count)
    pick = lambda a, i, ax: lax.dynamic_index_in_dim(a, i, ax, keepdims=False)
    return (
        output.astype(BF16)[None],
        loss,
        grad_input[None],
        own_rows(0),
        own_rows(1),
        jnp.stack([r_qkvo[:, i * e : (i + 1) * e] for i in range(3)]),
        pick(pick(qv_b, mt, 1), me, 2),
        r_qkvo[:, 3 * e :].T,
        own_rows(2),
        own_rows(3),
        own_rows(4),
        r_fc,
        pick(pick(fc_b, mt, 0), me, 1),
        r_proj.T,
        own_rows(5),
    )


def on_device(
    block_input,
    teacher,
    segment_ids,
    valid_mask,
    ln1_gain,
    ln1_bias,
    qkv_weight,
    qv_bias,
    out_weight,
    out_bias,
    ln2_gain,
    ln2_bias,
    fc_weight,
    fc_bias,
    proj_weight,
    proj_bias,
):
    dp, ts = lax.axis_size("dp"), lax.axis_size("tensor")
    me, mt = lax.axis_index("dp"), lax.axis_index("tensor")
    tokens, width = block_input.shape[1:]
    total_tokens = tokens * ts * dp
    e = qkv_weight.shape[2]
    x = block_input[0]
    valid_rows = valid_mask[0].astype(F32)

    cuts = [qkv_weight[0], qkv_weight[1], qkv_weight[2], out_weight.T]
    qkvo = jnp.concatenate([c[:, : 2 * HD] for c in cuts] + [c[:, 2 * HD :] for c in cuts], axis=1)
    mine = jnp.arange(dp) == me

    def spread(v):
        return jnp.where(mine[:, None], v[..., None, :], jnp.zeros((), v.dtype)).astype(F32)

    vectors = jnp.stack([ln1_gain, ln1_bias, out_bias, ln2_gain, ln2_bias, proj_bias])
    qv = spread(qv_bias).reshape(2, e)
    small = jnp.concatenate(
        [
            spread(vectors).reshape(6, width),
            spread(fc_bias).reshape(1, -1),
            jnp.concatenate(
                [qv[0, : 2 * HD], qv[1, : 2 * HD], qv[0, 2 * HD :], qv[1, 2 * HD :], jnp.sum(valid_rows)[None]]
                + [jnp.zeros((width - 2 * e - 1,), F32)]
            )[None],
        ]
    )
    qkvo_all, w_fc, w_proj, vec, kseg, qseg, normed_t, halo_x, q, k, v, ot, lse, mixed, hidden = front(
        x, segment_ids, small, qkvo, fc_weight, proj_weight.T, dp, ts, HALO
    )
    gain_two, bias_two, b_proj = [vec[0, i] for i in (3, 4, 5)]
    b_fc = vec[:, 6]
    valid_count = jnp.sum(vec[:, 7, 2 * e])
    wf = w_fc.reshape(ts, width, -1)
    wp = w_proj.reshape(ts, width, -1)

    unit_two, scale_two = normalize(hidden)
    normed_two = (unit_two * gain_two + bias_two).astype(BF16)
    pre_act = jnp.einsum("sd,tdf->stf", normed_two, wf, preferred_element_type=F32) + b_fc
    activated = gelu_tanh(pre_act).astype(BF16)
    output = hidden + jnp.einsum("stf,tdf->sd", activated, wp, preferred_element_type=F32) + b_proj
    residual_error = output - teacher[0].astype(F32)
    squares = jnp.sum(valid_rows[:, None] * residual_error * residual_error)
    grad_output = valid_rows[:, None] * residual_error * (total_tokens / valid_count)
    low_output = grad_output.astype(BF16)
    grad_act = jnp.einsum("sd,tdf->stf", low_output, wp, preferred_element_type=F32)
    grad_proj_w = jnp.einsum("sd,stf->tdf", low_output, activated, preferred_element_type=F32)
    _, gelu_back = jax.vjp(gelu_tanh, pre_act)
    grad_pre = gelu_back(grad_act)[0].astype(BF16)
    grad_fc_w = jnp.einsum("sd,stf->tdf", normed_two, grad_pre, preferred_element_type=F32)
    grad_normed_two = jnp.einsum("stf,tdf->sd", grad_pre, wf, preferred_element_type=F32)
    grad_hidden = grad_output + norm_back(grad_normed_two, gain_two, unit_two, scale_two)
    small_grads = jnp.concatenate(
        [
            jnp.sum(grad_hidden, axis=0)[None],
            jnp.sum(grad_normed_two * unit_two, axis=0)[None],
            jnp.sum(grad_normed_two, axis=0)[None],
            jnp.sum(grad_output, axis=0)[None],
            jnp.sum(grad_pre, axis=0, dtype=F32),
            jnp.full((1, width), squares),
            jnp.zeros((-(5 + ts) % 8, width), F32),
        ]
    )
    blocks = lambda g: g.astype(BF16).reshape(ts, dp // 2, 2, width // dp, width)
    grads = back(
        x, halo_x, vec, kseg, qseg, normed_t, q, k, v, ot, lse, mixed, grad_hidden, small_grads,
        blocks(grad_proj_w), blocks(grad_fc_w), qkvo_all,
    )
    input_grad, loss, gain_one, bias_one, g_qkv, g_qv_bias, g_out, *others = grads
    out_bias_, gain_two_, bias_two_, g_fc, g_fc_bias, g_proj, proj_bias_ = others
    return (
        output.astype(BF16)[None],
        loss[0, 0],
        input_grad[None],
        gain_one[0],
        bias_one[0],
        g_qkv,
        g_qv_bias.transpose(1, 0, 2),
        g_out,
        out_bias_[0],
        gain_two_[0],
        bias_two_[0],
        g_fc,
        g_fc_bias,
        g_proj.T,
        proj_bias_[0],
    )


def solution(mesh):
    placed = (
        P("dp", "tensor", None),
        P("dp", "tensor", None),
        P("dp", "tensor"),
        P("dp", "tensor"),
        P("dp"),
        P("dp"),
        P(None, "dp", "tensor"),
        P(None, "tensor", "dp"),
        P("tensor", "dp"),
        P("dp"),
        P("dp"),
        P("dp"),
        P("dp", "tensor"),
        P("tensor", "dp"),
        P("tensor", "dp"),
        P("dp"),
    )
    def fits(qkv_weight, block_input):
        rows = block_input.shape[2] // mesh.shape["dp"]
        wide = qkv_weight.shape[2] // mesh.shape["tensor"]
        parts = halo_parts(block_input.shape[1] // mesh.shape["tensor"], mesh.shape["tensor"])
        return rows % 16 == 0 and wide == 3 * HD and mesh.shape["tensor"] % 2 == 0 and len(parts) == 2

    def step(*args):
        return placed_step(on_device if fits(args[6], args[0]) else plain_device)(*args)

    placed_step = lambda body: jax.shard_map(
        body,
        mesh=mesh,
        in_specs=placed,
        out_specs=(
            P("dp", "tensor", None),
            P(),
            P("dp", "tensor", None),
            P("dp"),
            P("dp"),
            P(None, "dp", "tensor"),
            P(None, "tensor", "dp"),
            P("tensor", "dp"),
            P("dp"),
            P("dp"),
            P("dp"),
            P("dp", "tensor"),
            P("tensor", "dp"),
            P("tensor", "dp"),
            P("dp"),
        ),
        check_vma=False,
    )
    return step
```

```python
import functools

import jax
import jax.numpy as jnp
from jax import lax
from jax.experimental import pallas as pl
from jax.experimental.pallas import tpu as pltpu
from jax.sharding import PartitionSpec as P

HD = 64
DOC_MOST = 800
KB = 128
QB = 256
DOCS = 8
HALO = -(-(DOC_MOST - 1) // KB) * KB
LEAD = (HALO - DOC_MOST + 1) // 32 * 32
CHUNKS = ([(LEAD, KB - LEAD)] if LEAD else [(0, KB)]) + [(r, KB) for r in range(KB, HALO + QB, KB)]
Q_SCALE = 0.125 * 1.4426950408889634
EPSILON = 1e-05
LAG = 2
TANH_SLOPE = 0.7978845608028654
CUBIC_TERM = 0.044715
MESH = pl.DeviceIdType.MESH
F32 = jnp.float32
BF16 = jnp.bfloat16
NN = (((1,), (0,)), ((), ()))
NT = (((1,), (1,)), ((), ()))


def mm(a, b, dims=NN):
    return lax.dot_general(a, b, dims, preferred_element_type=F32)


def halo_parts(tokens, ts):
    parts, left, back = [], DOC_MOST, 1
    while left > 0 and back < ts:
        parts.append((back, min(tokens, left)))
        left -= tokens
        back += 1
    return parts


class Gather:
    def __init__(self, dp, ts, ins, outs, z_send, z_recv, send_sem, recv_sem):
        self.dp, self.ts, self.ins, self.outs = dp, ts, ins, outs
        self.z_send, self.z_recv, self.send_sem, self.recv_sem = z_send, z_recv, send_sem, recv_sem
        self.me, self.mt = lax.axis_index("dp"), lax.axis_index("tensor")
        self.far = [1 << k for k in range(1, dp.bit_length() - 1)]
        self.keys = {}
        self.flight = []
        self.near = [sorted(range(ts), key=lambda t: (abs(t - m), t)) for m in range(ts)]

    @staticmethod
    def copies(dp, ts, parts):
        return parts * ts * (dp - 1)

    def t_of(self, k):
        t = jnp.int32(self.near[0][k])
        for m in range(1, self.ts):
            t = jnp.where(self.mt == m, self.near[m][k], t)
        return t

    def order(self, t):
        flip = t * 2 >= self.ts
        return [jnp.where(flip, b, a) for a, b in zip(self.far, self.far[::-1])]

    def place(self, c, t, dp_index):
        return self.outs[c].at[t, dp_index]

    def along(self, c, t, up):
        src = self.ins[c] if t is None else self.place(c, t, self.me)
        t = self.mt if t is None else t
        return pltpu.make_async_remote_copy(
            src_ref=src,
            dst_ref=self.place(c, t, self.me),
            send_sem=self.z_send.at[c, t, int(up)],
            recv_sem=self.z_recv.at[c, t],
            device_id={"tensor": self.mt + (1 if up else -1)},
            device_id_type=MESH,
        )

    def desc(self, key):
        c, k, known, i = key
        t = self.t_of(k)
        order = self.order(t)
        mask = jnp.int32(0)
        for b in known:
            mask = mask ^ order[b]
        ref = self.place(c, t, self.me ^ mask)
        own = k == 0 and not known
        n = self.keys.setdefault(key, len(self.keys))
        return pltpu.make_async_remote_copy(
            src_ref=self.ins[c] if own else ref,
            dst_ref=ref,
            send_sem=self.send_sem.at[n],
            recv_sem=self.recv_sem.at[n],
            device_id={"dp": self.me ^ (1 if i < 0 else order[i])},
            device_id_type=MESH,
        )

    def here(self, c, k, known):
        first = max(known) + 1 if known else 0
        for i in list(range(first, len(self.far))) + [-1]:
            key = (c, k, known, i)
            self.desc(key).start()
            self.flight.append(key)

    def start(self, c):
        @pl.when(self.mt + 1 < self.ts)
        def _():
            self.along(c, None, True).start()

        @pl.when(self.mt >= 1)
        def _():
            self.along(c, None, False).start()

        self.here(c, 0, ())

    def z_step(self, c, k):
        t = self.t_of(k)
        self.along(c, t, True).wait_recv()

        @pl.when((t < self.mt) & (self.mt + 1 < self.ts))
        def _():
            self.along(c, t, True).start()

        @pl.when((t > self.mt) & (self.mt >= 1))
        def _():
            self.along(c, t, False).start()

        self.here(c, k, ())

    def far_step(self, c, k, i):
        for key in [q for q in self.flight if q[:2] == (c, k) and q[3] == i]:
            self.desc(key).wait_recv()
            self.here(c, k, key[2] + (i,))

    def core_step(self, c, k):
        for key in [q for q in self.flight if q[:2] == (c, k) and q[3] < 0]:
            self.desc(key).wait_recv()

    def finish(self):
        for c in range(len(self.ins)):
            for k in range(self.ts):
                t = self.t_of(k)

                @pl.when((t <= self.mt) & (self.mt + 1 < self.ts))
                def _():
                    self.along(c, t, True).wait_send()

                @pl.when((t >= self.mt) & (self.mt >= 1))
                def _():
                    self.along(c, t, False).wait_send()

        for key in self.flight:
            self.desc(key).wait_send()


def meet(dp, ts):
    me, mt = lax.axis_index("dp"), lax.axis_index("tensor")
    barrier = pltpu.get_barrier_semaphore()
    for k in range(1, ts):
        pl.semaphore_signal(barrier, inc=1, device_id={"tensor": lax.rem(mt + k, ts)}, device_id_type=MESH)
    for b in range(1, dp):
        pl.semaphore_signal(barrier, inc=1, device_id={"dp": me ^ b}, device_id_type=MESH)
    pl.semaphore_wait(barrier, ts - 1 + dp - 1)


def keep_lanes(block, head):
    lanes = lax.broadcasted_iota(jnp.int32, block.shape, 1)
    return jnp.where((lanes < HD) == (head == 0), block, jnp.zeros_like(block))


def fold_rows(block, op):
    return op(block.reshape(block.shape[0] // 8, 8, block.shape[1]), axis=0)


def swap_halves(block):
    return jnp.concatenate([block[:, HD:], block[:, :HD]], axis=1)


def lanes_of(low, high):
    lanes = lax.broadcasted_iota(jnp.int32, low.shape, 1)
    return jnp.where(lanes < HD, low, high)


def causal(s, row):
    ahead = row - HALO
    if ahead < 0:
        return s
    key = lax.broadcasted_iota(jnp.int32, s.shape, 0)
    query = lax.broadcasted_iota(jnp.int32, s.shape, 1)
    return jnp.where(key + ahead <= query, s, -1e30)


def segment_lanes(seg_row, same):
    shape = (128, seg_row.shape[1])
    value = lax.rem(lax.broadcasted_iota(jnp.int32, shape, 0), HD)
    hit = (seg_row == value) if same else (seg_row != value)
    level = -1e30 if same else 1.0
    return jnp.where(hit & (value < DOCS), level, 0.0).T.astype(BF16)


def normalize(values_in):
    center = values_in - jnp.mean(values_in, axis=-1, keepdims=True)
    scaler = lax.rsqrt(jnp.mean(center * center, axis=-1, keepdims=True) + EPSILON)
    return (center * scaler, scaler)


def merge_pairs(w_ref, h2_ref, ts):
    for a in range(ts // 2):
        tiles = []
        for t in (2 * a, 2 * a + 1):
            block = h2_ref[t, :, :, 0:256].reshape(-1, 256)
            tiles.append((block[:, :128], block[:, 128:]))
        (qk0, vo0), (qk1, vo1) = tiles
        merged = [
            lanes_of(qk0, swap_halves(qk1)),
            lanes_of(swap_halves(qk0), qk1),
            lanes_of(vo0, swap_halves(vo1)),
            lanes_of(swap_halves(vo0), vo1),
        ]
        for i, m in enumerate(merged):
            w_ref[ts + a, :, :, i * 128 : (i + 1) * 128] = m.reshape(w_ref.shape[1], w_ref.shape[2], 128)


def weight_loads(qkvo_all, w_ref, h2_ref, sem, ts):
    res = []
    for t in range(ts):
        res.append(pltpu.make_async_copy(qkvo_all.at[t, :, :, pl.ds(0, 512)], w_ref.at[t], sem.at[2 * t]))
        res.append(pltpu.make_async_copy(qkvo_all.at[t, :, :, pl.ds(512, 256)], h2_ref.at[t, :, :, pl.ds(0, 256)], sem.at[2 * t + 1]))
    return res


def front_kernel(
    dp,
    ts,
    x_ref,
    seg_ref,
    valid_ref,
    small_in,
    qkvo_ref,
    fc_ref,
    proj_ref,
    qkvo_all,
    fc_all,
    proj_all,
    vec_ref,
    kseg_ref,
    qseg_ref,
    normed_t_ref,
    halo_ref,
    q_ref,
    k_ref,
    v_ref,
    ot_ref,
    lse_ref,
    mixed_ref,
    hidden_ref,
    small_ref,
    small_all,
    w_ref,
    h2_ref,
    hseg_ref,
    normed_ref,
    ka_ref,
    vt_ref,
    s_ref,
    local_sem,
    z_send,
    z_recv,
    send_sem,
    recv_sem,
    halo_send,
    halo_recv,
):
    me, mt = lax.axis_index("dp"), lax.axis_index("tensor")
    tokens, width = x_ref.shape
    halo = halo_ref.shape[0]
    ins = [small_ref, qkvo_ref, fc_ref, proj_ref]
    outs = [small_all, qkvo_all, fc_all, proj_all]
    halo_ref[...] = jnp.zeros_like(halo_ref)
    hseg_ref[...] = jnp.full_like(hseg_ref, -1)
    row = lax.broadcasted_iota(jnp.int32, small_ref.shape, 0)
    lane = lax.broadcasted_iota(jnp.int32, small_ref.shape, 1)
    count = jnp.sum(valid_ref[...].astype(F32), axis=1, keepdims=True)
    small_ref[...] = jnp.where((row == 7) & (lane == 6 * HD), count, small_in[...])
    meet(dp, ts)
    net = Gather(dp, ts, ins, outs, z_send, z_recv, send_sem, recv_sem)
    stages = len(net.far)
    parts = halo_parts(tokens, ts)

    far = parts[1][1]
    near_at, cut = halo - tokens, tokens - far

    def hop(src, dst, n, back):
        return pltpu.make_async_remote_copy(
            src_ref=src,
            dst_ref=dst,
            send_sem=halo_send.at[n],
            recv_sem=halo_recv.at[n],
            device_id={"tensor": lax.rem(mt + back, ts)},
            device_id_type=MESH,
        )

    late_rows = hop(x_ref.at[pl.ds(cut, far)], halo_ref.at[pl.ds(near_at + cut, far)], 0, 1)
    early_rows = hop(x_ref.at[pl.ds(0, cut)], halo_ref.at[pl.ds(near_at, cut)], 1, 1)
    passed_rows = hop(halo_ref.at[pl.ds(near_at + cut, far)], halo_ref.at[pl.ds(near_at - far, far)], 2, 1)
    segs = [hop(seg_ref, hseg_ref.at[i], 3 + i, back) for i, (back, _) in enumerate(parts)]

    own = [
        pltpu.make_async_copy(ins[c], outs[c].at[mt, me], local_sem.at[2 * ts + c]) for c in range(4)
    ]
    net.start(0)
    net.start(1)
    for c in own:
        c.start()
    for k in range(1, ts):
        net.z_step(0, k)
    for k in range(1, ts):
        net.z_step(1, k)
    for i, (back, _) in enumerate(parts):

        @pl.when(mt + back < ts)
        def _():
            segs[i].start()

    @pl.when(mt + 1 < ts)
    def _():
        late_rows.start()
        early_rows.start()

    for i in range(stages):
        for k in range(ts):
            net.far_step(0, k, i)
    for k in range(ts):
        net.far_step(1, k, 0)

    @pl.when(mt >= 1)
    def _():
        late_rows.wait_recv()

    @pl.when((mt >= 1) & (mt + 1 < ts))
    def _():
        passed_rows.start()

    net.start(2)
    net.start(3)
    own[0].wait()
    for k in range(ts):
        net.core_step(0, k)
    for t in range(ts):
        vec_ref[t] = jnp.sum(small_all[t], axis=0)

    def norm_rows(src, i, at):
        unit, _ = normalize(src[pl.ds(i * KB, KB), :].astype(F32))
        rows = pl.ds(pl.multiple_of(at + i * KB, KB), KB)
        normed = (unit * vec_ref[0, 0:1, :] + vec_ref[0, 1:2, :]).astype(BF16)
        normed_ref[rows, :] = normed
        for n in range(width // KB):
            normed_t_ref[n * KB : (n + 1) * KB, rows] = normed[:, n * KB : (n + 1) * KB].T

    def own_rows(i, carry):
        norm_rows(x_ref, i, halo)
        return carry

    lax.fori_loop(0, tokens // KB, own_rows, 0)
    qseg_ref[...] = segment_lanes(seg_ref[0:1, :], True)
    kseg_ref[pl.ds(halo, tokens), :] = segment_lanes(seg_ref[0:1, :], False)
    for i in range(1, stages):
        for k in range(ts):
            net.far_step(1, k, i)
    own[1].wait()
    for k in range(ts):
        net.core_step(1, k)
    loads = weight_loads(qkvo_all, w_ref, h2_ref, local_sem, ts)
    for load in loads:
        load.start()
    for load in loads:
        load.wait()
    merge_pairs(w_ref, h2_ref, ts)

    def biases(p):
        t = jnp.minimum(p, ts - 1)
        a = jnp.maximum(p - ts, 0)
        low, high = vec_ref[2 * a, 7:8, 256:384], vec_ref[2 * a + 1, 7:8, 256:384]
        bias_q = jnp.where(p < ts, vec_ref[t, 7:8, 0:128], lanes_of(low, swap_halves(high)))
        bias_v = jnp.where(p < ts, vec_ref[t, 7:8, 128:256], lanes_of(swap_halves(low), high))
        return bias_q, bias_v

    own_span = pl.ds(halo, tokens)

    def project_own(p, carry):
        cols = pl.ds(pl.multiple_of(p * 128, 128), 128)
        bias_q, bias_v = biases(p)
        y = mm(normed_ref[own_span, :], w_ref[p, :, :, 0:384].reshape(width, 384))
        q_ref[:, cols] = ((y[:, :128] + bias_q) * Q_SCALE).astype(BF16)
        k_ref[own_span, cols] = y[:, 128:256].astype(BF16)
        v_ref[own_span, cols] = (y[:, 256:] + bias_v).astype(BF16)
        return carry

    lax.fori_loop(0, width // 128, project_own, 0)
    net.far_step(2, 0, 0)
    for i, (back, _) in enumerate(parts):

        @pl.when(mt >= back)
        def _():
            segs[i].wait_recv()

    @pl.when(mt >= 1)
    def _():
        early_rows.wait_recv()

    @pl.when(mt >= 2)
    def _():
        passed_rows.wait_recv()

    def halo_rows(i, carry):
        norm_rows(halo_ref, i, 0)
        return carry

    lax.fori_loop(0, halo // KB, halo_rows, 0)
    lanes = lax.rem(lax.broadcasted_iota(jnp.int32, (halo, 128), 1), HD)
    kseg_ref[pl.ds(0, halo), :] = jnp.where(lanes < DOCS, 1.0, 0.0).astype(BF16)
    end = halo
    for i, (_, count) in enumerate(parts):
        kseg_ref[pl.ds(end - count, count), :] = segment_lanes(hseg_ref[i, 0:1, :], False)[tokens - count :]
        end -= count

    plan = {0: [(3, 0, 0)]}
    for n, (k, c) in enumerate((k, c) for k in range(1, ts) for c in (2, 3)):
        plan.setdefault(n, []).append((c, k, "z"))
        plan.setdefault(n + 2, []).append((c, k, 0))
        plan.setdefault(n + 4, []).append((c, k, 1))
    plan.setdefault(2, []).extend([(2, 0, 1), (3, 0, 1)])

    def steps_at(p, place):
        for slot, items in plan.items():
            if slot % 2 != place:
                continue

            @pl.when(p == slot // 2)
            def _():
                for item in items:
                    c, k, what = item
                    if what == "z":
                        net.z_step(c, k)
                    elif what < stages:
                        net.far_step(c, k, what)

    def one_pair(p, carry):
        cols = pl.ds(pl.multiple_of(p * 128, 128), 128)
        _, bias_v = biases(p)

        def project(i, c):
            rows = pl.ds(pl.multiple_of(i * (halo // 2), 16), halo // 2)
            kv = mm(normed_ref[rows, :], w_ref[p, :, :, 128:384].reshape(width, 256))
            k_ref[rows, cols] = kv[:, :128].astype(BF16)
            v_ref[rows, cols] = (kv[:, 128:] + bias_v).astype(BF16)
            return c

        lax.fori_loop(0, 2, project, 0)

        def turn(i, c):
            rows = pl.ds(pl.multiple_of(i * KB, KB), KB)
            vt_ref[:, rows] = v_ref[rows, cols].T
            k, aux = k_ref[rows, cols], kseg_ref[rows, :]
            ka_ref[0, rows, :] = lanes_of(k, aux)
            ka_ref[1, rows, :] = lanes_of(aux, k)
            return c

        lax.fori_loop(0, (halo + tokens) // KB, turn, 0)
        steps_at(p, 0)

        def one_block(j, c):
            rows = pl.ds(pl.multiple_of(j * QB, QB), QB)
            q_block, aux = q_ref[rows, cols], qseg_ref[rows, :]
            base = j * QB
            spans = [(row, size, pl.ds(pl.multiple_of(base + row, 16), size)) for row, size in CHUNKS]
            for h in range(2):
                query = lanes_of(q_block, aux) if h == 0 else lanes_of(aux, q_block)
                top = jnp.full((8, QB), -1e30, F32)
                for row, size, span in spans:
                    s = causal(mm(ka_ref[h, span, :], query, NT), row)
                    s_ref[h, row : row + size, :] = s
                    top = jnp.maximum(top, fold_rows(s, jnp.max))
                top = jnp.max(top, axis=0, keepdims=True)
                total = jnp.zeros((8, QB), F32)
                acc = jnp.zeros((HD, QB), F32)
                for row, size, span in spans:
                    e = jnp.exp2(s_ref[h, row : row + size, :] - top)
                    total = total + fold_rows(e, jnp.sum)
                    if size < KB:
                        wide = pl.ds(pl.multiple_of(base + row // KB * KB, KB), KB)
                        e = jnp.concatenate([jnp.zeros((KB - size, QB), F32), e], axis=0)
                    else:
                        wide = pl.ds(pl.multiple_of(base + row, KB), KB)
                    acc = acc + mm(vt_ref[h * HD : (h + 1) * HD, wide], e.astype(BF16))
                total = jnp.sum(total, axis=0, keepdims=True)
                ot_ref[pl.ds(pl.multiple_of(p * 128 + h * HD, HD), HD), rows] = acc / total
                lse_ref[p, h : h + 1, rows] = top + jnp.log2(total)
            o = ot_ref[pl.ds(pl.multiple_of(p * 128, 128), 128), rows]
            mixed_ref[rows, cols] = o.T.astype(BF16)
            return c

        lax.fori_loop(0, tokens // QB, one_block, 0)
        w_o = w_ref[p, :, :, 384:512].reshape(width, 128)
        start = jnp.where(p == 0, x_ref[...].astype(F32) + vec_ref[0, 2:3, :], hidden_ref[...])
        hidden_ref[...] = start + mm(mixed_ref[:, cols], w_o, NT)
        steps_at(p, 1)
        return carry

    hidden_ref[...] = jnp.zeros_like(hidden_ref)
    lax.fori_loop(0, width // 128, one_pair, 0)
    for c in (2, 3):
        for k in range(ts):
            net.core_step(c, k)
    for c in own[2:]:
        c.wait()
    for i, (back, _) in enumerate(parts):

        @pl.when(mt + back < ts)
        def _():
            segs[i].wait_send()

    @pl.when(mt + 1 < ts)
    def _():
        late_rows.wait_send()
        early_rows.wait_send()

    @pl.when((mt >= 1) & (mt + 1 < ts))
    def _():
        passed_rows.wait_send()

    net.finish()


def front(x, seg, valid, small, qkvo, fc, proj, dp, ts, halo):
    tokens, width = x.shape
    rows = fc.shape[0]
    window = halo + tokens
    pairs = width // 128
    copies = Gather.copies(dp, ts, 4)
    n_halo = len(halo_parts(tokens, ts))
    any_spec = pl.BlockSpec(memory_space=pl.ANY)
    vmem = pl.BlockSpec(memory_space=pltpu.VMEM)
    big = jax.ShapeDtypeStruct((ts, dp, rows, width), BF16)
    s = jax.ShapeDtypeStruct
    dma = pltpu.SemaphoreType.DMA
    return pl.pallas_call(
        functools.partial(front_kernel, dp, ts),
        out_shape=[
            big,
            big,
            big,
            s((ts, 8, width), F32),
            s((window, 128), BF16),
            s((tokens, 128), BF16),
            s((width, window), BF16),
            s((halo, width), BF16),
            s((tokens, width), BF16),
            s((window, width), BF16),
            s((window, width), BF16),
            s((width, tokens), F32),
            s((pairs, 2, tokens), F32),
            s((tokens, width), BF16),
            s((tokens, width), F32),
        ],
        in_specs=[vmem] * 4 + [any_spec] * 3,
        out_specs=[any_spec] * 3 + [vmem] * 12,
        scratch_shapes=[
            pltpu.VMEM((8, width), F32),
            pltpu.VMEM((ts, dp, 8, width), F32),
            pltpu.VMEM((pairs, dp, rows, 512), BF16),
            pltpu.VMEM((ts, dp, rows, 256), BF16),
            pltpu.VMEM((n_halo, 1, tokens), jnp.int32),
            pltpu.VMEM((window, width), BF16),
            pltpu.VMEM((2, window, 128), BF16),
            pltpu.VMEM((128, window), BF16),
            pltpu.VMEM((2, HALO + QB, QB), F32),
            dma((2 * ts + 4,)),
            dma((4, ts, 2)),
            dma((4, ts)),
            dma((copies,)),
            dma((copies,)),
            dma((3 + n_halo,)),
            dma((3 + n_halo,)),
        ],
        compiler_params=pltpu.CompilerParams(
            collective_id=1, has_side_effects=True, vmem_limit_bytes=62 << 20
        ),
        name="front",
    )(x, seg, valid, small, qkvo, fc, proj)


class Scatter:
    def __init__(self, dp, ts, srcs, local, in_core, in_far, in_z, sems):
        self.dp, self.ts, self.srcs, self.local = dp, ts, srcs, local
        self.in_core, self.in_far, self.in_z = in_core, in_far, in_z
        self.core_send, self.core_recv, self.far_send, self.far_recv, self.z_send, self.z_recv = sems
        self.me, self.mt = lax.axis_index("dp"), lax.axis_index("tensor")
        self.far = [1 << k for k in range(1, dp.bit_length() - 1)]
        self.evens = list(range(0, dp, 2))

    def block(self, c, t, to):
        if c < 2:
            return self.srcs[c].at[t, to // 2, lax.rem(to, 2)]
        return self.srcs[c].at[t, to]

    def order(self, t):
        return self.far[::-1] if 2 * t < self.ts else self.far

    def core(self, c, t, m):
        return pltpu.make_async_remote_copy(
            src_ref=self.block(c, t, self.me ^ 1 ^ m),
            dst_ref=self.in_core.at[c, t, m >> 1],
            send_sem=self.core_send.at[c, t, m >> 1],
            recv_sem=self.core_recv.at[c, t, m >> 1],
            device_id={"dp": self.me ^ 1},
            device_id_type=MESH,
        )

    def far_moves(self, t, s):
        order = self.order(t)
        done = sum(order[:s])
        first = sum(len(self.evens) >> (i + 1) for i in range(s))
        masks = [m for m in self.evens if m & order[s] and not m & done]
        return [(m, first + i) for i, m in enumerate(masks)]

    def far_copy(self, c, t, s, m, slot):
        return pltpu.make_async_remote_copy(
            src_ref=self.in_core.at[c, t, m >> 1],
            dst_ref=self.in_far.at[c, t, slot],
            send_sem=self.far_send.at[c, t, slot],
            recv_sem=self.far_recv.at[c, t, slot],
            device_id={"dp": self.me ^ self.order(t)[s]},
            device_id_type=MESH,
        )

    def z_copy(self, c, t):
        back = lax.rem(self.mt + self.ts - t, self.ts) - 1
        return pltpu.make_async_remote_copy(
            src_ref=self.in_core.at[c, t, 0],
            dst_ref=self.in_z.at[c, back],
            send_sem=self.z_send.at[c, t],
            recv_sem=self.z_recv.at[c, back],
            device_id={"tensor": t},
            device_id_type=MESH,
        )

    def start(self, c, t):
        for m in self.evens[::-1]:
            self.core(c, t, m).start()

    def step(self, c, t, s):
        if s == 0:
            for m in self.evens[::-1]:
                self.core(c, t, m).wait_recv()
                to = self.me ^ m
                mine = self.local[c, t, to // 2] if c < 2 else self.srcs[c][t, to]
                self.in_core[c, t, m >> 1] = self.in_core[c, t, m >> 1] + mine
        else:
            bit = self.order(t)[s - 1]
            for m, slot in self.far_moves(t, s - 1):
                self.far_copy(c, t, s - 1, m, slot).wait_recv()
                to = (m ^ bit) >> 1
                self.in_core[c, t, to] = self.in_core[c, t, to] + self.in_far[c, t, slot]
        if s < len(self.far):
            for m, slot in self.far_moves(t, s):
                self.far_copy(c, t, s, m, slot).start()
        else:

            @pl.when(self.mt != t)
            def _():
                self.z_copy(c, t).start()

    def final(self, c):
        total = self.in_core[c, self.mt, 0].astype(F32)
        for k in range(self.ts - 1):
            pltpu.make_async_remote_copy(
                src_ref=self.in_core.at[c, 0, 0],
                dst_ref=self.in_z.at[c, k],
                send_sem=self.z_send.at[c, 0],
                recv_sem=self.z_recv.at[c, k],
                device_id={"tensor": self.mt},
                device_id_type=MESH,
            ).wait_recv()
            total = total + self.in_z[c, k].astype(F32)
        return total

    def finish(self):
        for c in range(len(self.srcs)):
            for t in range(self.ts):
                for m in self.evens:
                    self.core(c, t, m).wait_send()
                for s in range(len(self.far)):
                    for m, slot in self.far_moves(t, s):
                        self.far_copy(c, t, s, m, slot).wait_send()

                @pl.when(self.mt != t)
                def _():
                    self.z_copy(c, t).wait_send()


def norm_back(grad_in, gain_vec, unit_rows, scaler):
    scaled = grad_in * gain_vec
    return scaler * (
        scaled
        - jnp.mean(scaled, axis=-1, keepdims=True)
        - unit_rows * jnp.mean(scaled * unit_rows, axis=-1, keepdims=True)
    )


class Total:
    def __init__(self, dp, ts, mine, dp_in, z_in, sends, recvs):
        self.dp, self.ts, self.mine, self.dp_in, self.z_in = dp, ts, mine, dp_in, z_in
        self.sends, self.recvs = sends, recvs
        self.me, self.mt = lax.axis_index("dp"), lax.axis_index("tensor")

    def over_dp(self, m):
        return pltpu.make_async_remote_copy(
            src_ref=self.mine,
            dst_ref=self.dp_in.at[m],
            send_sem=self.sends.at[m],
            recv_sem=self.recvs.at[m],
            device_id={"dp": self.me ^ m},
            device_id_type=MESH,
        )

    def over_z(self, k):
        return pltpu.make_async_remote_copy(
            src_ref=self.z_in.at[0],
            dst_ref=self.z_in.at[self.ts - k],
            send_sem=self.sends.at[self.dp + k],
            recv_sem=self.recvs.at[self.dp + self.ts - k],
            device_id={"tensor": lax.rem(self.mt + k, self.ts)},
            device_id_type=MESH,
        )

    def start(self):
        for m in range(1, self.dp):
            self.over_dp(m).start()

    def turn(self):
        total = self.mine[...]
        for m in range(1, self.dp):
            self.over_dp(m).wait_recv()
            total = total + self.dp_in[m]
        self.z_in[0] = total
        for k in range(1, self.ts):
            self.over_z(k).start()

    def end(self):
        total = self.z_in[0]
        for k in range(1, self.ts):
            self.over_z(k).wait_recv()
            total = total + self.z_in[self.ts - k]
        return total

    def finish(self):
        for m in range(1, self.dp):
            self.over_dp(m).wait_send()
        for k in range(1, self.ts):
            self.over_z(k).wait_send()


def back_kernel(
    dp,
    ts,
    x_ref,
    halo_ref,
    vec_ref,
    kseg_ref,
    qseg_ref,
    normed_t_ref,
    q_ref,
    k_ref,
    v_ref,
    ot_ref,
    lse_ref,
    mixed_ref,
    grad_hidden_ref,
    small_ref,
    g_proj,
    g_fc,
    qkvo_all,
    input_grad_ref,
    loss_out,
    gain_one_out,
    bias_one_out,
    qkv_out,
    qv_bias_out,
    out_out,
    out_bias_out,
    gain_two_out,
    bias_two_out,
    fc_out,
    fc_bias_out,
    proj_out,
    proj_bias_out,
    w_ref,
    g_qkvo,
    low_ref,
    low_t_ref,
    ka_ref,
    kt_ref,
    dk_ref,
    dv_ref,
    gm_ref,
    delta_ref,
    dqkv_ref,
    dkv_ref,
    give_ref,
    take_ref,
    far_ref,
    gh_ref,
    gw_ref,
    g_local,
    small_in,
    small_z,
    late_own,
    late_in,
    late_z,
    in_core,
    in_far,
    in_z,
    local_sem,
    core_send,
    core_recv,
    far_send,
    far_recv,
    z_send,
    z_recv,
    halo_send,
    halo_recv,
    small_send,
    small_recv,
    late_send,
    late_recv,
):
    me, mt = lax.axis_index("dp"), lax.axis_index("tensor")
    tokens, width = x_ref.shape
    halo = halo_ref.shape[0]
    pairs = width // 128
    parts = halo_parts(tokens, ts)
    meet(dp, ts)
    sems = (core_send, core_recv, far_send, far_recv, z_send, z_recv)
    net = Scatter(dp, ts, [g_proj, g_fc, g_qkvo], g_local, in_core, in_far, in_z, sems)
    early = Total(dp, ts, small_ref, small_in, small_z, small_send, small_recv)
    late = Total(dp, ts, late_own, late_in, late_z, late_send, late_recv)
    stages = len(net.far) + 1
    zigzag = [t for pair in zip(range(ts // 2), range(ts - 1, ts // 2 - 1, -1)) for t in pair]
    for c in (0, 1):
        for t in zigzag:
            net.start(c, t)
    early.start()
    loads = weight_loads(qkvo_all, w_ref, g_qkvo, local_sem, ts)
    loads += [
        pltpu.make_async_copy(g.at[:, :, lax.rem(me, 2)], g_local.at[c], local_sem.at[2 * ts + c])
        for c, g in enumerate((g_proj, g_fc))
    ]
    for load in loads:
        load.start()

    def low_rows(i, c):
        rows = pl.ds(pl.multiple_of(i * KB, KB), KB)
        low = grad_hidden_ref[rows, :].astype(BF16)
        low_ref[rows, :] = low
        for n in range(pairs):
            low_t_ref[n * KB : (n + 1) * KB, rows] = low[:, n * KB : (n + 1) * KB].T
        return c

    lax.fori_loop(0, tokens // KB, low_rows, 0)
    for load in loads:
        load.wait()
    merge_pairs(w_ref, g_qkvo, ts)
    late_own[...] = jnp.zeros_like(late_own)
    gw_ref[...] = jnp.zeros_like(gw_ref)
    gh_ref[...] = jnp.zeros_like(gh_ref)

    turns = pairs + LAG
    order = list(range(ts, pairs)) + zigzag

    def pair_of(n):
        p = jnp.int32(order[0])
        for i in range(1, pairs):
            p = jnp.where(n == i, order[i], p)
        return p

    last = 4 * turns
    plan = {5: ["turn"], 9: ["end"], 4 * pairs + 3: ["final0", "final1"]}
    units = [(c, t) for c in (0, 1) for t in zigzag]
    for n, (c, t) in enumerate(units):
        for s in range(stages):
            plan.setdefault(2 * n + 1 + 3 * s, []).append((c, t, s))

    def after(slot):
        slot += 2
        return slot if slot < 4 * pairs else -(-(slot - 3) // 4) * 4 + 3 if slot < last else slot

    for i, t in enumerate(zigzag):
        at = 4 * (pairs - ts + i + LAG) + 3
        plan.setdefault(at, []).insert(0, (2, t, "start"))
        for s in range(stages):
            at = after(at) if at < last - 1 else max(at, last - 1) + 1
            plan.setdefault(at, []).append((2, t, s))

    def turned(block):
        pad = jnp.zeros((128 - block.shape[0], 128), F32)
        return jnp.concatenate([block, pad], axis=0).T[:, : block.shape[0]]

    def write_final(c):
        total = net.final(c)
        if c == 0:
            proj_out[...] = total
        elif c == 1:
            fc_out[...] = total
        else:
            for i in range(3):
                qkv_out[i, :, 0:128] = total[:, i * 128 : (i + 1) * 128]
                qkv_out[i, :, 128:192] = total[:, 512 + i * HD : 512 + (i + 1) * HD]
            out_out[0:128, :] = turned(total[:, 384:512])
            out_out[128:192, :] = turned(total[:, 640:768])[HD:, :]

    def at_lane(block, lane):
        return pltpu.roll(block, lax.rem(width - lane, width), 1)

    def write_small(block):
        rows = at_lane(block[0:8, :], me * (width // dp))
        for i, ref in enumerate((out_bias_out, gain_two_out, bias_two_out, proj_bias_out)):
            ref[...] = rows[i : i + 1, : width // dp]
        mine = block[4:5, :]
        for t in range(1, ts):
            mine = jnp.where(mt == t, block[4 + t : 5 + t, :], mine)
        mine = at_lane(jnp.broadcast_to(mine, (8, width)), me * (HD // dp))
        for i in range(width // HD):
            fc_bias_out[i : i + 1, :] = mine[0:1, i * HD : i * HD + HD // dp]
        count = vec_ref[0, 7:8, 384:385]
        for t in range(1, ts):
            count = count + vec_ref[t, 7:8, 384:385]
        loss_out[...] = block[4 + ts : 5 + ts, 0:1] / (width * count)

    def write_late(block):
        rows = at_lane(block, me * (width // dp))
        gain_one_out[...] = rows[0:1, : width // dp]
        bias_one_out[...] = rows[1:2, : width // dp]
        rows = at_lane(block, me * (HD // dp))
        for h in range(3):
            for i in range(2):
                value = None
                for t in range(ts):
                    lane = t * 128 + h * HD if h < 2 else ts * 128 + t * HD
                    here = rows[2 + i : 3 + i, lane : lane + HD // dp]
                    value = here if value is None else jnp.where(mt == t, here, value)
                qv_bias_out[h, i : i + 1, :] = value

    def run(items):
        for item in items:
            if item == "turn":
                early.turn()
            elif item == "end":
                write_small(early.end())
            elif item in ("final0", "final1"):
                write_final(int(item[-1]))
            elif item[2] == "start":
                net.start(item[0], item[1])
            else:
                net.step(*item)

    def steps_at(n, place):
        for slot, items in sorted(plan.items()):
            if slot % 4 == place and slot < (last if place == 3 else 4 * pairs):

                @pl.when(n == slot // 4)
                def _():
                    run(items)

    far = parts[1][1]
    near_at, cut = halo - tokens, tokens - far

    def hop(src, dst, n):
        return pltpu.make_async_remote_copy(
            src_ref=src,
            dst_ref=dst,
            send_sem=halo_send.at[n],
            recv_sem=halo_recv.at[n],
            device_id={"tensor": lax.rem(mt + ts - 1, ts)},
            device_id_type=MESH,
        )

    far_rows = hop(give_ref.at[pl.ds(near_at - far, far)], far_ref, 0)
    early_rows = hop(give_ref.at[pl.ds(near_at, cut)], take_ref.at[pl.ds(0, cut)], 1)
    late_rows = hop(give_ref.at[pl.ds(near_at + cut, far)], take_ref.at[pl.ds(cut, far)], 2)

    def attend_back(n):
        p = pair_of(n)
        cols = pl.ds(pl.multiple_of(p * 128, 128), 128)
        w_o = w_ref[p, :, :, 384:512].reshape(width, 128)
        rounded = mm(low_ref[...], w_o).astype(BF16)
        gm_ref[...] = rounded
        weighted = rounded.astype(F32).T * ot_ref[pl.ds(pl.multiple_of(p * 128, 128), 128), :]
        for h in range(2):
            delta_ref[h : h + 1, :] = jnp.sum(weighted[h * HD : (h + 1) * HD], axis=0, keepdims=True)

        def turn(i, c):
            rows = pl.ds(pl.multiple_of(i * KB, KB), KB)
            k, aux = k_ref[rows, cols], kseg_ref[rows, :]
            kt_ref[:, rows] = k.T
            ka_ref[0, rows, :] = lanes_of(k, aux)
            ka_ref[1, rows, :] = lanes_of(aux, k)
            dk_ref[rows, :] = jnp.zeros((KB, 128), F32)
            dv_ref[rows, :] = jnp.zeros((KB, 128), F32)
            return c

        lax.fori_loop(0, (halo + tokens) // KB, turn, 0)
        steps_at(n, 0)

        def one_block(j, c):
            base = j * QB
            at = pl.ds(pl.multiple_of(base, QB), QB)
            q_block, aux, do_block = q_ref[at, cols], qseg_ref[at, :], gm_ref[at, :]
            asks = [lanes_of(q_block, aux), lanes_of(aux, q_block)]
            q_cat = jnp.concatenate([keep_lanes(q_block, h) for h in range(2)], axis=0)
            do_cat = jnp.concatenate([keep_lanes(do_block, h) for h in range(2)], axis=0)
            lse = [lse_ref[p, h : h + 1, at] for h in range(2)]
            delta = [delta_ref[h : h + 1, at] for h in range(2)]
            dq_t = [jnp.zeros((HD, QB), F32) for h in range(2)]
            for row, size in CHUNKS:
                span = pl.ds(pl.multiple_of(base + row, 16), size)
                values = v_ref[span, cols]
                ps, dss = [], []
                for h in range(2):
                    s = causal(mm(ka_ref[h, span, :], asks[h], NT), row)
                    e = jnp.exp2(s - lse[h])
                    grad_e = mm(values, do_cat[h * QB : (h + 1) * QB], NT)
                    ds = (e * (grad_e - delta[h])).astype(BF16)
                    wide = pl.ds(pl.multiple_of(base + row // KB * KB, KB), KB)
                    tall = ds
                    if size < KB:
                        tall = jnp.concatenate([jnp.zeros((KB - size, QB), BF16), ds], axis=0)
                    dq_t[h] = dq_t[h] + mm(kt_ref[h * HD : (h + 1) * HD, wide], tall)
                    ps.append(e.astype(BF16))
                    dss.append(ds)
                dv_ref[span, :] += mm(jnp.concatenate(ps, axis=1), do_cat)
                dk_ref[span, :] += mm(jnp.concatenate(dss, axis=1), q_cat)
            dqkv_ref[n, at, 0:128] = (jnp.concatenate(dq_t, axis=0) * 0.125).T.astype(BF16)
            for place in range(tokens // QB):

                @pl.when(j == place)
                def _():
                    steps_at(n, 1 + place)
            return c

        lax.fori_loop(0, tokens // QB, one_block, 0)

        dkv_ref[n, :, 0:128] = (dk_ref[:halo, :] * (0.125 / Q_SCALE)).astype(BF16)
        dkv_ref[n, :, 128:256] = dv_ref[:halo, :].astype(BF16)
        dqkv_ref[n, :, 128:256] = (dk_ref[halo:, :] * (0.125 / Q_SCALE)).astype(BF16)
        dqkv_ref[n, :, 256:384] = dv_ref[halo:, :].astype(BF16)

        def halo_grad(i, c):
            rows = pl.ds(pl.multiple_of(i * (halo // 2), 16), halo // 2)
            gh_ref[rows, :] += mm(dkv_ref[n, rows, :], w_ref[p, :, :, 128:384].reshape(width, 256), NT)
            return c

        lax.fori_loop(0, 2, halo_grad, 0)

        @pl.when(n == pairs - 1)
        def _():
            give_ref[: near_at + cut, :] = gh_ref[: near_at + cut, :].astype(BF16)

            @pl.when(mt >= 2)
            def _():
                far_rows.start()

            @pl.when(mt >= 1)
            def _():
                early_rows.start()

    def store(tile, value, t):
        g_qkvo[t, :, :, tile * 128 : (tile + 1) * 128] = value.astype(BF16).reshape(dp, -1, 128)

    def weights_back(n):
        p = pair_of(n)
        cols = pl.ds(pl.multiple_of(p * 128, 128), 128)
        grad_o = mm(low_t_ref[...], mixed_ref[:, cols])
        dqkv = dqkv_ref[n]
        own = mm(normed_t_ref[:, halo:], dqkv)
        far = mm(normed_t_ref[:, :halo], dkv_ref[n])
        four = [own[:, 0:128], own[:, 128:256] + far[:, 0:128], own[:, 256:384] + far[:, 128:256], grad_o]

        @pl.when(p < ts)
        def _():
            for i, g in enumerate(four):
                store(i, g, p)

        for a in range(pairs - ts):

            @pl.when(p == ts + a)
            def _():
                for i in range(2):
                    low_half, high_half = four[2 * i], four[2 * i + 1]
                    store(4 + i, lanes_of(low_half, swap_halves(high_half)), 2 * a)
                    store(4 + i, lanes_of(swap_halves(low_half), high_half), 2 * a + 1)

        gw_ref[...] += mm(dqkv, w_ref[p, :, :, 0:384].reshape(width, 384), NT)
        grad_v = jnp.sum(dqkv[:, 256:384].astype(F32), axis=0, keepdims=True)
        late_own[2:3, cols] = jnp.sum(dqkv[:, 0:128].astype(F32), axis=0, keepdims=True)
        late_own[3:4, cols] = grad_v + jnp.sum(dkv_ref[n, :, 128:256].astype(F32), axis=0, keepdims=True)

    def one_turn(n, carry):
        @pl.when(n < pairs)
        def _():
            attend_back(n)

        @pl.when(n >= LAG)
        def _():
            weights_back(n - LAG)

        steps_at(n, 3)
        return carry

    lax.fori_loop(0, turns, one_turn, 0)

    def halo_sums(i, carry):
        rows = pl.ds(pl.multiple_of(i * KB, KB), KB)
        unit, _ = normalize(halo_ref[rows, :].astype(F32))
        g = gh_ref[rows, :]
        return carry[0] + fold_rows(g * unit, jnp.sum), carry[1] + fold_rows(g, jnp.sum)

    def own_sums(i, carry):
        rows = pl.ds(pl.multiple_of(i * KB, KB), KB)
        unit, _ = normalize(x_ref[rows, :].astype(F32))
        g = gw_ref[rows, :]
        return carry[0] + fold_rows(g * unit, jnp.sum), carry[1] + fold_rows(g, jnp.sum)

    zero = jnp.zeros((8, width), F32)
    carry = lax.fori_loop(0, halo // KB, halo_sums, (zero, zero))
    passed = (mt >= 1) & (mt + 1 < ts)

    @pl.when(passed)
    def _():
        far_rows.wait_recv()
        gh_ref[near_at + cut :, :] += far_ref[...].astype(F32)

    @pl.when(mt >= 1)
    def _():
        give_ref[near_at + cut :, :] = gh_ref[near_at + cut :, :].astype(BF16)
        late_rows.start()

    tail = [item for slot, items in sorted(plan.items()) if slot >= last for item in items]
    first = [item for item in tail if item[2] == 0] + [item for item in tail if item[1] == zigzag[-3]]
    tail = [item for item in tail if item not in first]
    run(first)
    gains, shifts = lax.fori_loop(0, tokens // KB, own_sums, carry)
    late_own[0:1, :] = jnp.sum(gains, axis=0, keepdims=True)
    late_own[1:2, :] = jnp.sum(shifts, axis=0, keepdims=True)
    late.start()
    tail.sort(key=lambda item: (item[2], -zigzag.index(item[1])))
    run(tail[:1])
    late.turn()
    run(tail[1:])

    @pl.when(mt + 1 < ts)
    def _():
        early_rows.wait_recv()
        late_rows.wait_recv()
        gw_ref[...] += take_ref[...].astype(F32)

    def own_grad(i, carry):
        rows = pl.ds(pl.multiple_of(i * KB, KB), KB)
        unit, scaler = normalize(x_ref[rows, :].astype(F32))
        g = gw_ref[rows, :]
        input_grad_ref[rows, :] = grad_hidden_ref[rows, :] + norm_back(g, vec_ref[0, 0:1, :], unit, scaler)
        return carry

    lax.fori_loop(0, tokens // KB, own_grad, 0)
    write_late(late.end())
    write_final(2)
    early.finish()
    late.finish()

    @pl.when(mt >= 2)
    def _():
        far_rows.wait_send()

    @pl.when(mt >= 1)
    def _():
        early_rows.wait_send()
        late_rows.wait_send()

    net.finish()


def back(x, halo_x, vec, kseg, qseg, normed_t, q, k, v, ot, lse, mixed, grad_hidden, small, g_proj, g_fc, qkvo_all):
    tokens, width = x.shape
    halo = halo_x.shape[0]
    window = halo + tokens
    ts, dp, rows = qkvo_all.shape[:3]
    pairs = width // 128
    n_far = dp // 2 - 1
    any_spec = pl.BlockSpec(memory_space=pl.ANY)
    vmem = pl.BlockSpec(memory_space=pltpu.VMEM)
    s = jax.ShapeDtypeStruct
    dma = pltpu.SemaphoreType.DMA
    return pl.pallas_call(
        functools.partial(back_kernel, dp, ts),
        out_shape=[
            s((tokens, width), F32),
            s((1, 1), F32),
            s((1, rows), F32),
            s((1, rows), F32),
            s((3, rows, 3 * HD), F32),
            s((3, 2, HD // dp), F32),
            s((3 * HD, rows), F32),
            s((1, rows), F32),
            s((1, rows), F32),
            s((1, rows), F32),
            s((rows, width), F32),
            s((width // HD, HD // dp), F32),
            s((rows, width), F32),
            s((1, rows), F32),
        ],
        in_specs=[vmem] * 14 + [any_spec] * 3,
        out_specs=[vmem] * 14,
        scratch_shapes=[
            pltpu.VMEM((pairs, dp, rows, 512), BF16),
            pltpu.VMEM((ts, dp, rows, width), BF16),
            pltpu.VMEM((tokens, width), BF16),
            pltpu.VMEM((width, tokens), BF16),
            pltpu.VMEM((2, window, 128), BF16),
            pltpu.VMEM((128, window), BF16),
            pltpu.VMEM((window, 128), F32),
            pltpu.VMEM((window, 128), F32),
            pltpu.VMEM((tokens, 128), BF16),
            pltpu.VMEM((8, tokens), F32),
            pltpu.VMEM((pairs, tokens, 384), BF16),
            pltpu.VMEM((pairs, halo, 256), BF16),
            pltpu.VMEM((halo, width), BF16),
            pltpu.VMEM((tokens, width), BF16),
            pltpu.VMEM((halo_parts(tokens, ts)[1][1], width), BF16),
            pltpu.VMEM((halo, width), F32),
            pltpu.VMEM((tokens, width), F32),
            pltpu.VMEM((2, ts, dp // 2, rows, width), BF16),
            pltpu.VMEM((dp,) + small.shape, F32),
            pltpu.VMEM((ts,) + small.shape, F32),
            pltpu.VMEM((8, width), F32),
            pltpu.VMEM((dp, 8, width), F32),
            pltpu.VMEM((ts, 8, width), F32),
            pltpu.VMEM((3, ts, dp // 2, rows, width), BF16),
            pltpu.VMEM((3, ts, n_far, rows, width), BF16),
            pltpu.VMEM((3, ts - 1, rows, width), BF16),
            dma((2 * ts + 2,)),
            dma((3, ts, dp // 2)),
            dma((3, ts, dp // 2)),
            dma((3, ts, n_far)),
            dma((3, ts, n_far)),
            dma((3, ts)),
            dma((3, ts - 1)),
            dma((3,)),
            dma((3,)),
            dma((dp + ts,)),
            dma((dp + ts,)),
            dma((dp + ts,)),
            dma((dp + ts,)),
        ],
        compiler_params=pltpu.CompilerParams(
            collective_id=2, has_side_effects=True, vmem_limit_bytes=63 << 20
        ),
        name="back",
    )(x, halo_x, vec, kseg, qseg, normed_t, q, k, v, ot, lse, mixed, grad_hidden, small, g_proj, g_fc, qkvo_all)


def gather_kernel(dp, ts, tokens, n_in, *refs):
    w_refs, (x_ref, seg_ref) = refs[:n_in], refs[n_in : n_in + 2]
    outs = refs[n_in + 2 : 2 * n_in + 2]
    halo_ref, hseg_ref = refs[2 * n_in + 2 : 2 * n_in + 4]
    local_sem, send_sem, recv_sem, halo_send, halo_recv = refs[2 * n_in + 4 :]
    me = lax.axis_index("dp")
    mt = lax.axis_index("tensor")
    bits = [1 << k for k in range(dp.bit_length() - 1)]
    far = bits[1:]
    halo_ref[...] = jnp.zeros_like(halo_ref)
    hseg_ref[...] = jnp.full_like(hseg_ref, -1)
    barrier = pltpu.get_barrier_semaphore()
    peers_t = [lax.rem(mt + k, ts) for k in range(1, ts)]
    for t in peers_t:
        pl.semaphore_signal(barrier, inc=1, device_id={"tensor": t}, device_id_type=MESH)
    for b in bits:
        pl.semaphore_signal(barrier, inc=1, device_id={"dp": me ^ b}, device_id_type=MESH)
    pl.semaphore_wait(barrier, len(peers_t) + len(bits))
    started = []

    def rcopy(src, dst, dev):
        i = len(started)
        c = pltpu.make_async_remote_copy(
            src_ref=src,
            dst_ref=dst,
            send_sem=send_sem.at[i],
            recv_sem=recv_sem.at[i],
            device_id=dev,
            device_id_type=MESH,
        )
        c.start()
        started.append(c)
        return c

    locals_, over_z = [], []
    for c in range(n_in):
        copy = pltpu.make_async_copy(w_refs[c], outs[c].at[mt, me], local_sem.at[c])
        copy.start()
        locals_.append(copy)
        over_z.append([rcopy(w_refs[c], outs[c].at[mt, me], {"tensor": t}) for t in peers_t])
        if c == min(1, n_in - 1):
            end = halo_ref.shape[0]
            halos = []
            for i, (back, count) in enumerate(halo_parts(tokens, ts)):
                end -= count
                pair = [
                    pltpu.make_async_remote_copy(
                        src_ref=src,
                        dst_ref=dst,
                        send_sem=halo_send.at[2 * i + k],
                        recv_sem=halo_recv.at[2 * i + k],
                        device_id={"tensor": lax.rem(mt + back, ts)},
                        device_id_type=MESH,
                    )
                    for k, (src, dst) in enumerate(
                        [
                            (x_ref.at[pl.ds(tokens - count, count)], halo_ref.at[pl.ds(end, count)]),
                            (seg_ref, hseg_ref.at[i]),
                        ]
                    )
                ]
                halos.append((back, pair))

                @pl.when(mt + back < ts)
                def _():
                    for h in pair:
                        h.start()

    half = max(ts // 2, 1)
    groups = [(0, half, far)] + ([(half, ts - half, far[::-1])] if ts > half else [])

    def spread(c, group, masks, later):
        res = {}
        for b in later + [1]:
            res[b] = []
            for m in masks:
                ref = outs[c].at[pl.ds(group[0], group[1]), me ^ m]
                res[b].append((m, rcopy(ref, ref, {"dp": me ^ b})))
        return res

    stages = len(far) + 1
    pending = {}
    for step in range(n_in + stages - 1):
        for s in range(stages):
            c = step - s
            if not 0 <= c < n_in:
                continue
            if s == 0:
                locals_[c].wait()
                for k in over_z[c]:
                    k.wait_recv()
            for gi, group in enumerate(groups):
                if s == 0:
                    pending[c, gi] = [spread(c, group, [0], group[2])]
                else:
                    b = group[2][s - 1]
                    masks = []
                    for res in pending[c, gi]:
                        for m, k in res.get(b, []):
                            k.wait_recv()
                            masks.append(m ^ b)
                    pending[c, gi].append(spread(c, group, masks, group[2][s:]))
    for c in range(n_in):
        for gi in range(len(groups)):
            for res in pending[c, gi]:
                for m, k in res[1]:
                    k.wait_recv()
    for back, pair in halos:

        @pl.when(mt >= back)
        def _():
            for h in pair:
                h.wait_recv()

        @pl.when(mt + back < ts)
        def _():
            for h in pair:
                h.wait_send()

    for k in started:
        k.wait_send()


def gather(parts, x, seg, dp, ts, halo):
    n_in = len(parts)
    tokens = x.shape[0]
    copies = n_in * ((ts - 1) + (2 if ts > 1 else 1) * (dp - 1))
    n_halo = len(halo_parts(tokens, ts))
    any_spec = pl.BlockSpec(memory_space=pl.ANY)
    vmem = pl.BlockSpec(memory_space=pltpu.VMEM)
    return pl.pallas_call(
        functools.partial(gather_kernel, dp, ts, tokens, n_in),
        out_shape=[jax.ShapeDtypeStruct((ts, dp) + p.shape, p.dtype) for p in parts]
        + [
            jax.ShapeDtypeStruct((halo, x.shape[1]), x.dtype),
            jax.ShapeDtypeStruct((n_halo,) + seg.shape, seg.dtype),
        ],
        in_specs=[any_spec] * (n_in + 2),
        out_specs=[any_spec] * n_in + [vmem, vmem],
        scratch_shapes=[
            pltpu.SemaphoreType.DMA((n_in,)),
            pltpu.SemaphoreType.DMA((copies,)),
            pltpu.SemaphoreType.DMA((copies,)),
            pltpu.SemaphoreType.DMA((2 * n_halo,)),
            pltpu.SemaphoreType.DMA((2 * n_halo,)),
        ],
        compiler_params=pltpu.CompilerParams(collective_id=1, has_side_effects=True),
        name="gather",
    )(*parts, x, seg)


def reduce_kernel(dp, ts, g_ref, out_ref, in_core, in_far, in_z, send_sem, recv_sem):
    n_c = g_ref.shape[0]
    me = lax.axis_index("dp")
    mt = lax.axis_index("tensor")
    bits = [1 << k for k in range(dp.bit_length() - 1)]
    far = bits[1:]
    barrier = pltpu.get_barrier_semaphore()
    peers_t = [lax.rem(mt + k, ts) for k in range(1, ts)]
    for t in peers_t:
        pl.semaphore_signal(barrier, inc=1, device_id={"tensor": t}, device_id_type=MESH)
    for b in bits:
        pl.semaphore_signal(barrier, inc=1, device_id={"dp": me ^ b}, device_id_type=MESH)
    pl.semaphore_wait(barrier, len(peers_t) + len(bits))
    started = []

    def rcopy(src, dst, dev):
        i = len(started)
        c = pltpu.make_async_remote_copy(
            src_ref=src,
            dst_ref=dst,
            send_sem=send_sem.at[i],
            recv_sem=recv_sem.at[i],
            device_id=dev,
            device_id_type=MESH,
        )
        c.start()
        started.append(c)
        return c

    half = max(ts // 2, 1)
    groups = [(0, half, far[::-1])] + ([(half, ts - half, far)] if ts > half else [])
    evens = list(range(0, dp, 2))
    core = []
    for c in range(n_c):
        core.append(
            {
                m: rcopy(g_ref.at[c, :, me ^ 1 ^ m], in_core.at[c, m >> 1], {"dp": me ^ 1})
                for m in evens[::-1]
            }
        )

    def add_into(dst, src, base, count):
        def one(i, carry):
            dst[base + i] = (dst[base + i].astype(F32) + src[i].astype(F32)).astype(BF16)
            return carry

        lax.fori_loop(0, count, one, 0)

    stages = len(far) + 2
    pending = {}
    slots = {}
    for step in range(n_c + stages - 1):
        for s in range(stages):
            c = step - s
            if not 0 <= c < n_c:
                continue
            if s == 0:
                for m in evens[::-1]:
                    core[c][m].wait_recv()

                    def one(i, carry, m=m):
                        in_core[c, m >> 1, i] = (
                            in_core[c, m >> 1, i].astype(F32) + g_ref[c, i, me ^ m].astype(F32)
                        ).astype(BF16)
                        return carry

                    lax.fori_loop(0, ts, one, 0)
            for gi, (t0, tn, order) in enumerate(groups):
                if s > 0:
                    for m, slot, k in pending.pop((c, gi)):
                        k.wait_recv()
                        add_into(in_core.at[c, m >> 1], in_far.at[c, slot, pl.ds(t0, tn)], t0, tn)
                if s < len(far):
                    b = order[s]
                    done = sum(order[:s])
                    masks = [m for m in evens if m & b and not m & done]
                    sent = []
                    for m in masks:
                        slot = slots.get((c, gi), 0)
                        slots[c, gi] = slot + 1
                        k = rcopy(
                            in_core.at[c, m >> 1, pl.ds(t0, tn)],
                            in_far.at[c, slot, pl.ds(t0, tn)],
                            {"dp": me ^ b},
                        )
                        sent.append((m ^ b, slot, k))
                    pending[c, gi] = sent
                elif s == len(far):
                    pending[c, gi] = []
            if s == len(far):
                pending[c, "z"] = [
                    rcopy(in_core.at[c, 0, lax.rem(mt + k, ts)], in_z.at[c, k - 1], {"tensor": lax.rem(mt + k, ts)})
                    for k in range(1, ts)
                ]
            if s == len(far) + 1:
                total = in_core[c, 0, mt].astype(F32)
                for k in pending[c, "z"]:
                    k.wait_recv()
                for k in range(ts - 1):
                    total = total + in_z[c, k].astype(F32)
                out_ref[c] = total
    for k in started:
        k.wait_send()


def reduce(grads, dp, ts):
    n_c, _, _, rows, width = grads.shape
    n_far = dp // 2 - 1
    groups = 2 if ts > 1 else 1
    copies = n_c * (dp // 2 + groups * n_far + ts - 1)
    vmem = pl.BlockSpec(memory_space=pltpu.VMEM)
    return pl.pallas_call(
        functools.partial(reduce_kernel, dp, ts),
        out_shape=jax.ShapeDtypeStruct((n_c, rows, width), F32),
        in_specs=[vmem],
        out_specs=vmem,
        scratch_shapes=[
            pltpu.VMEM((n_c, dp // 2, ts, rows, width), BF16),
            pltpu.VMEM((n_c, n_far, ts, rows, width), BF16),
            pltpu.VMEM((n_c, ts - 1, rows, width), BF16),
            pltpu.SemaphoreType.DMA((copies,)),
            pltpu.SemaphoreType.DMA((copies,)),
        ],
        compiler_params=pltpu.CompilerParams(
            collective_id=2, has_side_effects=True, vmem_limit_bytes=62 << 20
        ),
        name="reduce",
    )(grads)


def allowed_at(chunk, doc_row, first_q):
    key = chunk * KB + lax.broadcasted_iota(jnp.int32, (KB, QB), 0)
    query = first_q + lax.broadcasted_iota(jnp.int32, (KB, QB), 1)
    return (key >= doc_row) & (key <= query)


def attend_kernel(halo, first_ref, doc_ref, q_ref, k_ref, vt_ref, o_ref, lse_ref, s_ref):
    for j in range(q_ref.shape[0] // QB):
        rows = pl.ds(j * QB, QB)
        q_block = q_ref[rows, :]
        queries = [keep_lanes(q_block, h) for h in range(2)]
        doc_row = doc_ref[0:1, rows]
        first_q = halo + j * QB
        begin = first_ref[j]
        end = (first_q + QB) // KB

        def score(c, tops):
            keys = k_ref[pl.ds(pl.multiple_of(c * KB, KB), KB), :]
            ok = allowed_at(c, doc_row, first_q)
            res = []
            for h in range(2):
                s = jnp.where(ok, mm(keys, queries[h], NT), -1e30)
                s_ref[h, c] = s
                res.append(jnp.maximum(tops[h], fold_rows(s, jnp.max)))
            return tuple(res)

        tops = lax.fori_loop(begin, end, score, (jnp.full((8, QB), -1e30, F32),) * 2)
        tops = [jnp.max(t, axis=0, keepdims=True) for t in tops]

        def mix(c, carry):
            res = []
            for h in range(2):
                total, acc = carry[h]
                p = jnp.exp(s_ref[h, c] - tops[h])
                total = total + fold_rows(p, jnp.sum)
                vt = vt_ref[pl.ds(h * HD, HD), pl.ds(pl.multiple_of(c * KB, KB), KB)]
                acc = acc + mm(vt, p.astype(BF16))
                res.append((total, acc))
            return tuple(res)

        carry = lax.fori_loop(
            begin, end, mix, ((jnp.zeros((8, QB), F32), jnp.zeros((HD, QB), F32)),) * 2
        )
        for h in range(2):
            total = jnp.sum(carry[h][0], axis=0, keepdims=True)
            o_ref[pl.ds(h * HD, HD), rows] = carry[h][1] / total
            lse_ref[0, h : h + 1, rows] = tops[h] + jnp.log(total)


def attend(first, doc, q, k, vt, halo):
    tokens, width = q.shape
    keys = k.shape[0]
    pairs = width // 128
    return pl.pallas_call(
        functools.partial(attend_kernel, halo),
        out_shape=[
            jax.ShapeDtypeStruct((width, tokens), F32),
            jax.ShapeDtypeStruct((pairs, 2, tokens), F32),
        ],
        grid_spec=pltpu.PrefetchScalarGridSpec(
            num_scalar_prefetch=1,
            grid=(pairs,),
            in_specs=[
                pl.BlockSpec((1, tokens), lambda p, f: (0, 0)),
                pl.BlockSpec((tokens, 128), lambda p, f: (0, p)),
                pl.BlockSpec((keys, 128), lambda p, f: (0, p)),
                pl.BlockSpec((128, keys), lambda p, f: (p, 0)),
            ],
            out_specs=[
                pl.BlockSpec((128, tokens), lambda p, f: (p, 0)),
                pl.BlockSpec((1, 2, tokens), lambda p, f: (p, 0, 0)),
            ],
            scratch_shapes=[pltpu.VMEM((2, keys // KB, KB, QB), F32)],
        ),
        name="attend",
    )(first, doc, q, k, vt)


def attend_back_kernel(
    halo, first_ref, doc_ref, q_ref, k_ref, kt_ref, v_ref, do_ref, lse_ref, delta_ref, dq_ref, dk_ref, dv_ref
):
    dk_ref[...] = jnp.zeros_like(dk_ref)
    dv_ref[...] = jnp.zeros_like(dv_ref)
    for j in range(q_ref.shape[0] // QB):
        rows = pl.ds(j * QB, QB)
        q_block, do_block = q_ref[rows, :], do_ref[rows, :]
        queries = [keep_lanes(q_block, h) for h in range(2)]
        grads = [keep_lanes(do_block, h) for h in range(2)]
        doc_row = doc_ref[0:1, rows]
        first_q = halo + j * QB

        def step(c, carry):
            span = pl.ds(pl.multiple_of(c * KB, KB), KB)
            keys, values = k_ref[span, :], v_ref[span, :]
            ok = allowed_at(c, doc_row, first_q)
            res = []
            grad_k = grad_v = None
            for h in range(2):
                s = jnp.where(ok, mm(keys, queries[h], NT), -1e30)
                p = jnp.exp(s - lse_ref[0, h : h + 1, rows])
                dp_ = mm(values, grads[h], NT)
                ds = (p * (dp_ - delta_ref[0, h : h + 1, rows])).astype(BF16)
                gv = mm(p.astype(BF16), grads[h])
                gk = mm(ds, queries[h])
                grad_v = gv if grad_v is None else grad_v + gv
                grad_k = gk if grad_k is None else grad_k + gk
                kt = kt_ref[pl.ds(h * HD, HD), span]
                res.append(carry[h] + mm(kt, ds))
            dk_ref[span, :] += grad_k
            dv_ref[span, :] += grad_v
            return tuple(res)

        carry = lax.fori_loop(
            first_ref[j], (first_q + QB) // KB, step, (jnp.zeros((HD, QB), F32),) * 2
        )
        for h in range(2):
            dq_ref[pl.ds(h * HD, HD), rows] = carry[h] * 0.125


def attend_back(first, doc, q, k, kt, v, do, lse, delta, halo):
    tokens, width = q.shape
    keys = k.shape[0]
    pairs = width // 128
    q_spec = pl.BlockSpec((tokens, 128), lambda p, f: (0, p))
    k_spec = pl.BlockSpec((keys, 128), lambda p, f: (0, p))
    stat = pl.BlockSpec((1, 2, tokens), lambda p, f: (p, 0, 0))
    return pl.pallas_call(
        functools.partial(attend_back_kernel, halo),
        out_shape=[
            jax.ShapeDtypeStruct((width, tokens), F32),
            jax.ShapeDtypeStruct((keys, width), F32),
            jax.ShapeDtypeStruct((keys, width), F32),
        ],
        grid_spec=pltpu.PrefetchScalarGridSpec(
            num_scalar_prefetch=1,
            grid=(pairs,),
            in_specs=[
                pl.BlockSpec((1, tokens), lambda p, f: (0, 0)),
                q_spec,
                k_spec,
                pl.BlockSpec((128, keys), lambda p, f: (p, 0)),
                k_spec,
                q_spec,
                stat,
                stat,
            ],
            out_specs=[pl.BlockSpec((128, tokens), lambda p, f: (p, 0)), k_spec, k_spec],
        ),
        name="attend_back",
    )(first, doc, q, k, kt, v, do, lse, delta)


def gelu_tanh(values_in):
    return (
        0.5
        * values_in
        * (
            1.0
            + jnp.tanh(TANH_SLOPE * (values_in + CUBIC_TERM * values_in * values_in * values_in))
        )
    )


def plain_device(
    block_input,
    teacher,
    segment_ids,
    valid_mask,
    ln1_gain,
    ln1_bias,
    qkv_weight,
    qv_bias,
    out_weight,
    out_bias,
    ln2_gain,
    ln2_bias,
    fc_weight,
    fc_bias,
    proj_weight,
    proj_bias,
):
    dp, ts = lax.axis_size("dp"), lax.axis_size("tensor")
    me, mt = lax.axis_index("dp"), lax.axis_index("tensor")
    tokens, width = block_input.shape[1:]
    total_tokens = tokens * ts * dp
    halo = -(-(DOC_MOST - 1) // KB) * KB
    e = qkv_weight.shape[2]
    x = block_input[0]
    valid_rows = valid_mask[0].astype(F32)

    qkvo = jnp.concatenate([qkv_weight[0], qkv_weight[1], qkv_weight[2], out_weight.T], axis=1)
    local_count = jnp.sum(valid_mask[0])
    mine = jnp.arange(dp) == me

    def spread(v):
        return jnp.where(mine[:, None], v[..., None, :], jnp.zeros((), v.dtype))

    vectors = jnp.stack([ln1_gain, ln1_bias, out_bias, ln2_gain, ln2_bias, proj_bias])
    tail = jnp.stack([local_count // 16, local_count % 16]).astype(BF16)
    small = jnp.concatenate(
        [
            spread(vectors).reshape(6, width),
            spread(fc_bias).reshape(1, -1),
            jnp.concatenate(
                [spread(qv_bias).reshape(-1), tail, jnp.zeros((width - 2 * e - 2,), BF16)]
            )[None],
        ]
    )
    seg_rows = jnp.broadcast_to(segment_ids, (8, tokens))
    small_all, w_qkvo, w_fc, w_proj, x_halo, seg_halo = gather(
        [small, qkvo, fc_weight, proj_weight.T], x, seg_rows, dp, ts, halo
    )
    small_all = jnp.sum(small_all.astype(F32), axis=1)
    gain_one, bias_one, b_out, gain_two, bias_two, b_proj = [small_all[0, i] for i in range(6)]
    b_fc = small_all[:, 6].reshape(-1)
    b_q = small_all[:, 7, :e].reshape(-1)
    b_v = small_all[:, 7, e : 2 * e].reshape(-1)
    valid_count = jnp.sum(small_all[:, 7, 2 * e] * 16 + small_all[:, 7, 2 * e + 1])
    w_qkvo = w_qkvo.reshape(ts, width, 4, e)
    wq, wk, wv, wo = [w_qkvo[:, :, i].transpose(1, 0, 2).reshape(width, width) for i in range(4)]
    wf = w_fc.reshape(ts, width, -1)
    wp = w_proj.reshape(ts, width, -1)

    seg = segment_ids[0]
    pieces = []
    for i, (back, count) in enumerate(halo_parts(tokens, ts)):
        pieces.insert(0, seg_halo[i, 0, tokens - count :])
    filled = sum(p.shape[0] for p in pieces)
    seg_window = jnp.concatenate([jnp.full((halo - filled,), -1, jnp.int32)] + pieces)
    position = jnp.sum((seg_window[:, None] < seg[None, :]).astype(jnp.int32), axis=0)
    own = jnp.sum((seg[:, None] < seg[None, :]).astype(jnp.int32), axis=0)
    doc = (position + own)[None]
    first = doc[0, ::QB] // KB

    inputs = x.astype(F32)
    window = jnp.concatenate([x_halo, x]).astype(F32)
    unit_window, scale_window = normalize(window)
    normed_window = (unit_window * gain_one + bias_one).astype(BF16)
    unit_one, scale_one = unit_window[halo:], scale_window[halo:]
    normed_one = normed_window[halo:]
    q = ((mm(normed_one, wq) + b_q).astype(BF16) * 0.125).astype(BF16)
    k = mm(normed_window, wk).astype(BF16)
    v = (mm(normed_window, wv) + b_v).astype(BF16)
    mixed_t, lse = attend(first, doc, q, k, v.T, halo)
    mixed = mixed_t.T.astype(BF16)
    hidden = inputs + mm(mixed, wo, NT) + b_out
    unit_two, scale_two = normalize(hidden)
    normed_two = (unit_two * gain_two + bias_two).astype(BF16)
    pre_act = jnp.einsum("sd,tdf->stf", normed_two, wf, preferred_element_type=F32) + b_fc.reshape(ts, -1)
    activated = gelu_tanh(pre_act).astype(BF16)
    output = hidden + jnp.einsum("stf,tdf->sd", activated, wp, preferred_element_type=F32) + b_proj
    residual_error = output - teacher[0].astype(F32)
    squares = jnp.sum(valid_rows[:, None] * residual_error * residual_error)
    grad_output = valid_rows[:, None] * residual_error * (total_tokens / valid_count)
    low_output = grad_output.astype(BF16)
    grad_act = jnp.einsum("sd,tdf->stf", low_output, wp, preferred_element_type=F32)
    grad_proj_w = jnp.einsum("sd,stf->tdf", low_output, activated, preferred_element_type=F32)
    _, gelu_back = jax.vjp(gelu_tanh, pre_act)
    grad_pre = gelu_back(grad_act)[0].astype(BF16)
    grad_fc_w = jnp.einsum("sd,stf->tdf", normed_two, grad_pre, preferred_element_type=F32)
    grad_fc_b = jnp.sum(grad_pre, axis=0, dtype=F32)
    grad_normed_two = jnp.einsum("stf,tdf->sd", grad_pre, wf, preferred_element_type=F32)
    grad_gain_two = jnp.sum(grad_normed_two * unit_two, axis=0)
    grad_bias_two = jnp.sum(grad_normed_two, axis=0)
    grad_hidden = grad_output + norm_back(grad_normed_two, gain_two, unit_two, scale_two)
    low_hidden = grad_hidden.astype(BF16)
    grad_mixed = mm(low_hidden, wo).astype(BF16)
    grad_out_w = jnp.einsum("sd,se->de", low_hidden, mixed, preferred_element_type=F32)
    heads = width // HD
    delta = jnp.sum((grad_mixed.T.astype(F32) * mixed_t).reshape(heads // 2, 2, HD, tokens), axis=2)
    dq_t, dk, dv = attend_back(first, doc, q, k, k.T, v, grad_mixed, lse, delta, halo)
    dq, dk, dv = dq_t.T.astype(BF16), dk.astype(BF16), dv.astype(BF16)
    sd_se = lambda a, b: jnp.einsum("sd,se->de", a, b, preferred_element_type=F32)
    g_q, g_k, g_v = sd_se(normed_one, dq), sd_se(normed_window, dk), sd_se(normed_window, dv)
    grad_window = mm(dk, wk, NT) + mm(dv, wv, NT)
    grad_normed_one = grad_window[halo:] + mm(dq, wq, NT)
    end = halo
    for back, count in halo_parts(tokens, ts):
        end -= count
        part = lax.ppermute(
            grad_window[end : end + count].astype(BF16), "tensor", [(t, t - back) for t in range(back, ts)]
        )
        grad_normed_one = grad_normed_one.at[tokens - count :].add(part.astype(F32))
    grad_input = grad_hidden + norm_back(grad_normed_one, gain_one, unit_one, scale_one)

    def by_t(g):
        return g.reshape(width, ts, e)

    g_qkvo = jnp.stack([by_t(g_q), by_t(g_k), by_t(g_v), by_t(grad_out_w)], axis=2)
    g_qkvo = g_qkvo.transpose(1, 0, 2, 3).reshape(ts, width, 4 * e)
    grads = jnp.stack([grad_proj_w, grad_fc_w, g_qkvo]).astype(BF16)
    grads = grads.reshape(3, ts, dp, width // dp, -1)
    r_proj, r_fc, r_qkvo = reduce(grads, dp, ts)
    smalls = [
        jnp.sum(grad_normed_one * unit_one, axis=0),
        jnp.sum(grad_normed_one, axis=0),
        jnp.sum(grad_hidden, axis=0),
        grad_gain_two,
        grad_bias_two,
        jnp.sum(grad_output, axis=0),
        grad_fc_b.reshape(-1),
        jnp.sum(dq, axis=0, dtype=F32),
        jnp.sum(dv, axis=0, dtype=F32),
        squares[None],
    ]
    summed = lax.psum(jnp.concatenate(smalls), ("dp", "tensor"))
    rows = width // dp
    own_rows = lambda i: lax.dynamic_slice_in_dim(summed, i * width + me * rows, rows)
    fc_b = summed[6 * width : 6 * width + fc_bias.size * dp * ts].reshape(ts, -1, dp, fc_bias.shape[1])
    qv0 = 6 * width + fc_bias.size * dp * ts
    qv_b = summed[qv0 : qv0 + 2 * width].reshape(2, ts, -1, dp, qv_bias.shape[2])
    loss = summed[-1] / (width * valid_count)
    pick = lambda a, i, ax: lax.dynamic_index_in_dim(a, i, ax, keepdims=False)
    return (
        output.astype(BF16)[None],
        loss,
        grad_input[None],
        own_rows(0),
        own_rows(1),
        jnp.stack([r_qkvo[:, i * e : (i + 1) * e] for i in range(3)]),
        pick(pick(qv_b, mt, 1), me, 2),
        r_qkvo[:, 3 * e :].T,
        own_rows(2),
        own_rows(3),
        own_rows(4),
        r_fc,
        pick(pick(fc_b, mt, 0), me, 1),
        r_proj.T,
        own_rows(5),
    )


def on_device(
    block_input,
    teacher,
    segment_ids,
    valid_mask,
    ln1_gain,
    ln1_bias,
    qkv_weight,
    qv_bias,
    out_weight,
    out_bias,
    ln2_gain,
    ln2_bias,
    fc_weight,
    fc_bias,
    proj_weight,
    proj_bias,
):
    dp, ts = lax.axis_size("dp"), lax.axis_size("tensor")
    me, mt = lax.axis_index("dp"), lax.axis_index("tensor")
    tokens, width = block_input.shape[1:]
    total_tokens = tokens * ts * dp
    e = qkv_weight.shape[2]
    x = block_input[0]
    valid_rows = valid_mask[0].astype(F32)

    cuts = [qkv_weight[0], qkv_weight[1], qkv_weight[2], out_weight.T]
    qkvo = jnp.concatenate([c[:, : 2 * HD] for c in cuts] + [c[:, 2 * HD :] for c in cuts], axis=1)
    mine = jnp.arange(dp) == me

    def spread(v):
        return jnp.where(mine[:, None], v[..., None, :], jnp.zeros((), v.dtype)).astype(F32)

    vectors = jnp.stack([ln1_gain, ln1_bias, out_bias, ln2_gain, ln2_bias, proj_bias])
    qv = spread(qv_bias).reshape(2, e)
    small = jnp.concatenate(
        [
            spread(vectors).reshape(6, width),
            spread(fc_bias).reshape(1, -1),
            jnp.concatenate(
                [qv[0, : 2 * HD], qv[1, : 2 * HD], qv[0, 2 * HD :], qv[1, 2 * HD :], jnp.zeros((width - 2 * e,), F32)]
            )[None],
        ]
    )
    qkvo_all, w_fc, w_proj, vec, kseg, qseg, normed_t, halo_x, q, k, v, ot, lse, mixed, hidden = front(
        x, segment_ids, valid_mask, small, qkvo, fc_weight, proj_weight.T, dp, ts, HALO
    )
    gain_two, bias_two, b_proj = [vec[0, i] for i in (3, 4, 5)]
    b_fc = vec[:, 6]
    valid_count = jnp.sum(vec[:, 7, 2 * e])
    wf = w_fc.reshape(ts, width, -1)
    wp = w_proj.reshape(ts, width, -1)

    unit_two, scale_two = normalize(hidden)
    normed_two = (unit_two * gain_two + bias_two).astype(BF16)
    pre_act = jnp.einsum("sd,tdf->stf", normed_two, wf, preferred_element_type=F32) + b_fc
    activated = gelu_tanh(pre_act).astype(BF16)
    output = hidden + jnp.einsum("stf,tdf->sd", activated, wp, preferred_element_type=F32) + b_proj
    residual_error = output - teacher[0].astype(F32)
    squares = jnp.sum(valid_rows[:, None] * residual_error * residual_error)
    grad_output = valid_rows[:, None] * residual_error * (total_tokens / valid_count)
    low_output = grad_output.astype(BF16)
    grad_act = jnp.einsum("sd,tdf->stf", low_output, wp, preferred_element_type=F32)
    grad_proj_w = jnp.einsum("sd,stf->tdf", low_output, activated, preferred_element_type=F32)
    _, gelu_back = jax.vjp(gelu_tanh, pre_act)
    grad_pre = gelu_back(grad_act)[0].astype(BF16)
    grad_fc_w = jnp.einsum("sd,stf->tdf", normed_two, grad_pre, preferred_element_type=F32)
    grad_normed_two = jnp.einsum("stf,tdf->sd", grad_pre, wf, preferred_element_type=F32)
    grad_hidden = grad_output + norm_back(grad_normed_two, gain_two, unit_two, scale_two)
    small_grads = jnp.concatenate(
        [
            jnp.sum(grad_hidden, axis=0)[None],
            jnp.sum(grad_normed_two * unit_two, axis=0)[None],
            jnp.sum(grad_normed_two, axis=0)[None],
            jnp.sum(grad_output, axis=0)[None],
            jnp.sum(grad_pre, axis=0, dtype=F32),
            jnp.full((1, width), squares),
            jnp.zeros((-(5 + ts) % 8, width), F32),
        ]
    )
    blocks = lambda g: g.astype(BF16).reshape(ts, dp // 2, 2, width // dp, width)
    grads = back(
        x, halo_x, vec, kseg, qseg, normed_t, q, k, v, ot, lse, mixed, grad_hidden, small_grads,
        blocks(grad_proj_w), blocks(grad_fc_w), qkvo_all,
    )
    input_grad, loss, gain_one, bias_one, g_qkv, g_qv_bias, g_out, *others = grads
    out_bias_, gain_two_, bias_two_, g_fc, g_fc_bias, g_proj, proj_bias_ = others
    return (
        output.astype(BF16)[None],
        loss[0, 0],
        input_grad[None],
        gain_one[0],
        bias_one[0],
        g_qkv,
        g_qv_bias.transpose(1, 0, 2),
        g_out,
        out_bias_[0],
        gain_two_[0],
        bias_two_[0],
        g_fc,
        g_fc_bias,
        g_proj.T,
        proj_bias_[0],
    )


def solution(mesh):
    placed = (
        P("dp", "tensor", None),
        P("dp", "tensor", None),
        P("dp", "tensor"),
        P("dp", "tensor"),
        P("dp"),
        P("dp"),
        P(None, "dp", "tensor"),
        P(None, "tensor", "dp"),
        P("tensor", "dp"),
        P("dp"),
        P("dp"),
        P("dp"),
        P("dp", "tensor"),
        P("tensor", "dp"),
        P("tensor", "dp"),
        P("dp"),
    )
    def fits(qkv_weight, block_input):
        rows = block_input.shape[2] // mesh.shape["dp"]
        wide = qkv_weight.shape[2] // mesh.shape["tensor"]
        parts = halo_parts(block_input.shape[1] // mesh.shape["tensor"], mesh.shape["tensor"])
        return rows % 16 == 0 and wide == 3 * HD and mesh.shape["tensor"] % 2 == 0 and len(parts) == 2

    def step(*args):
        return placed_step(on_device if fits(args[6], args[0]) else plain_device)(*args)

    placed_step = lambda body: jax.shard_map(
        body,
        mesh=mesh,
        in_specs=placed,
        out_specs=(
            P("dp", "tensor", None),
            P(),
            P("dp", "tensor", None),
            P("dp"),
            P("dp"),
            P(None, "dp", "tensor"),
            P(None, "tensor", "dp"),
            P("tensor", "dp"),
            P("dp"),
            P("dp"),
            P("dp"),
            P("dp", "tensor"),
            P("tensor", "dp"),
            P("tensor", "dp"),
            P("dp"),
        ),
        check_vma=False,
    )
    return step
```
